32 devices in a mesh: dp: 8 (over z, x), tensor: 4 (over y, core).
Axes of the slice: x: 2, y: 2, z: 4, core: 2. Of those that a mesh axis runs over, the one named last changes fastest.
Arguments:
- x_in: bfloat16 [20480, 768], P(('dp', 'tensor')), may hold values from -6 to 6
- tags: int32 [128], P('dp'), may hold values from 0 to 1, as said below
- lengths: int32 [128], P('dp'), may hold values from 95 to 160, as said below
- w_qkv: bfloat16 [2, 768, 3, 768], P(None, 'dp', None, 'tensor'), may hold values from -0.3125 to 0.3125
- w_out: bfloat16 [2, 768, 768], P(None, 'dp', 'tensor'), may hold values from -1.5 to 1.5
- w_up: bfloat16 [2, 768, 3072], P(None, 'dp', 'tensor'), may hold values from -0.21875 to 0.21875
- w_down: bfloat16 [2, 768, 3072], P(None, 'dp', 'tensor'), may hold values from -0.109375 to 0.109375
- norm_gain: float32 [2, 2, 768], P(None, None, ('dp', 'tensor')), may hold values from 0.5 to 1.5
- norm_bias: float32 [2, 2, 768], P(None, None, ('dp', 'tensor')), may hold values from -2 to 2
- cotangent: bfloat16 [20480, 768], P(('dp', 'tensor')), may hold values from -6 to 6
Outputs:
- y_out: bfloat16 [20480, 768], P(('dp', 'tensor'))
- x_grad: float32 [20480, 768], P(('dp', 'tensor'))
- qkv_grad: float32 [2, 768, 3, 768], P(None, 'dp', None, 'tensor')
- out_grad: float32 [2, 768, 768], P(None, 'dp', 'tensor')
- up_grad: float32 [2, 768, 3072], P(None, 'dp', 'tensor')
- down_grad: float32 [2, 768, 3072], P(None, 'dp', 'tensor')
- gain_grad: float32 [2, 2, 768], P(None, None, ('dp', 'tensor'))
- bias_grad: float32 [2, 2, 768], P(None, None, ('dp', 'tensor'))
The draws below stay inside these ranges and needn't reach their ends.
Inputs may be any that keep to these rules, and one draw needn't show every extreme that they name: `tags`: within the chains of each index of dp (a block of 16 in order), all heavy chains (0) come before all light ones (1); each block holds at least a quarter of either type. `lengths`: each device's chains (blocks of 4 in order) include one of length 160.
All inputs are finite; a program needn't handle non-finite values.
Results may differ from the reference program's by a relative error of at most 0.02.
Values may be sent and summed in bfloat16 or wider, within the bound.
A program may use at most 192 MiB of HBM per device.

```python
import jax
import jax.numpy as jnp
from jax import lax

D = 768
HEADS = 12
HEAD_DIM = 64
FF = 3072
LENGTH = 160
MICRO = 4
CHAINS_PART = 1
CHAINS = 128
TOKENS = 20480
N_DP = 8
N_TENSOR = 4


def draw_tags(key, part):
    block = CHAINS // N_DP
    heavy = jax.random.randint(key, (N_DP, 1), block // 4, block - block // 4 + 1)
    places = jnp.arange(block)[None, :]
    return (places >= heavy).astype(jnp.int32).reshape(CHAINS)


def draw_lengths(key, part):
    per_device = MICRO * CHAINS_PART
    devices = CHAINS // per_device
    base = jax.random.randint(jax.random.fold_in(key, 1), (devices, per_device), LENGTH * 19 // 32, LENGTH + 1)
    spot = jax.random.randint(jax.random.fold_in(key, 2), (devices, 1), 0, per_device)
    places = jnp.arange(per_device)[None, :]
    return jnp.where(places == spot, LENGTH, base).astype(jnp.int32).reshape(CHAINS)


def raised(values, own_key, source, target, shards_of, factor):
    def block_of(position):
        return (jnp.arange(values.shape[position]) // (values.shape[position] // shards_of)).reshape((-1,) + (1,) * (values.ndim - 1 - position))

    one_side = jax.random.permutation(own_key, shards_of)[block_of(target)]
    far = (block_of(target) + shards_of // 2) % shards_of
    return jnp.where((block_of(source) == one_side) | (block_of(source) == far), factor * values, values)


def level_of(own_key, dims, split, least, largest):
    level = 1.0
    for position, blocks in split:
        heights = jax.random.uniform(jax.random.fold_in(jax.random.fold_in(own_key, 6), position), (blocks,), jnp.float32, least / len(split), largest / len(split))
        level = level * jnp.repeat(jnp.exp(heights), dims[position] // blocks).reshape((-1,) + (1,) * (len(dims) - 1 - position))
    return level


def centred(stream_key, dims, scale, reach, pieces=(), held_as=jnp.bfloat16):
    entries = scale * jax.random.normal(stream_key, dims, jnp.float32)
    if pieces:
        entries = entries * level_of(stream_key, dims, pieces, -0.22, 0.18)
    return jnp.clip(entries, -reach, reach).astype(held_as)


def noise_with(stream_key, dims, deviation, reach, cuts, heavy, kind=jnp.bfloat16):
    entries = deviation * jax.random.normal(stream_key, dims, jnp.float32)
    if cuts:
        entries = entries * level_of(stream_key, dims, cuts, -0.22, 0.18)
    return jnp.clip(raised(entries, jax.random.fold_in(stream_key, 3), *heavy), -reach, reach).astype(kind)


def setup_inputs(seed: int = 0) -> dict:
    key_list = jax.random.split(jax.random.key(seed), 11)
    x_in = centred(key_list[0], (TOKENS, D), 1.0, 6.0, ((0, 32),))
    tags = draw_tags(jax.random.fold_in(key_list[10], 71), 0)
    lengths = draw_lengths(jax.random.fold_in(key_list[10], 71), 0)
    w_qkv = centred(key_list[3], (2, D, 3, D), (D // 2) ** -0.5, 0.3125, ((1, 8), (3, 4)))
    w_out = centred(key_list[4], (2, D, D), (D // 48) ** -0.5, 1.5, ((1, 8), (2, 4)))
    w_up = centred(key_list[5], (2, D, FF), D ** -0.5, 0.21875, ((1, 8), (2, 4)))
    w_down = centred(key_list[6], (2, D, FF), FF ** -0.5, 0.109375, ((1, 8), (2, 4)))
    norm_gain = jnp.clip(1.0 + 0.1 * jax.random.normal(key_list[7], (2, 2, D), jnp.float32), 0.5, 1.5)
    norm_bias = centred(key_list[8], (2, 2, D), 0.3, 2.0, ((2, 32),), jnp.float32)
    cotangent = noise_with(key_list[9], (TOKENS, D), 1.0, 6.0, ((0, 32),), (0, 1, 32, 2.75))
    return dict(x_in=x_in, tags=tags, lengths=lengths, w_qkv=w_qkv, w_out=w_out, w_up=w_up, w_down=w_down, norm_gain=norm_gain, norm_bias=norm_bias, cotangent=cotangent)


@jax.custom_vjp
def low(v):
    return lax.optimization_barrier(v.astype(jnp.bfloat16)).astype(jnp.float32)

@jax.custom_vjp
def low_back(v):
    return v

def low_keep(v):
    return (low(v), None)

def low_pass(kept, grad):
    return (grad,)

def back_keep(v):
    return (v, None)

def back_low(kept, grad):
    return (low(grad),)
low.defvjp(low_keep, low_pass)
low_back.defvjp(back_keep, back_low)
EPS = 1e-12
NEG = -1e+30
HIGH = lax.Precision.HIGHEST

def dense(left_side, right_side):
    return jnp.dot(left_side, right_side, precision=HIGH, preferred_element_type=jnp.float32)

def layer_norm(values, gain, shift):
    center = values - lax.optimization_barrier(jnp.mean(values, -1, keepdims=True))
    spread = lax.optimization_barrier(jnp.mean(center * center, -1, keepdims=True))
    return center * lax.rsqrt(spread + EPS) * gain + shift

def chain_forward(chain, length, qkv_w, out_w, up_w, down_w, gains, shifts):
    group = HEADS // N_TENSOR * HEAD_DIM
    hidden_part = FF // N_TENSOR
    valid = jnp.arange(LENGTH) < length
    attn = jnp.zeros((LENGTH, D), jnp.float32)
    for part_index in range(N_TENSOR):
        cols = slice(part_index * group, (part_index + 1) * group)
        proj = jnp.einsum('ld,dkh->lkh', chain, qkv_w[:, :, cols], precision=HIGH)
        proj = low_back(low(proj)).reshape(LENGTH, 3, HEADS // N_TENSOR, HEAD_DIM)
        query = proj[:, 0]
        keys = proj[:, 1]
        values = proj[:, 2]
        scores = low_back(jnp.einsum('qhe,khe->hqk', query, keys, precision=HIGH) * 0.125)
        scores = jnp.where(valid[None, None, :], scores, NEG)
        probs = low(jax.nn.softmax(scores, axis=-1))
        heads = jnp.einsum('hqk,khe->qhe', probs, values, precision=HIGH).reshape(LENGTH, group)
        heads = low_back(low(heads))
        attn = attn + low(dense(heads, out_w[:, cols].T))
    attn = low_back(attn)
    mid = layer_norm(chain + attn, gains[0], shifts[0])
    mid_low = low(mid)
    ffn = jnp.zeros((LENGTH, D), jnp.float32)
    for part_index in range(N_TENSOR):
        cols = slice(part_index * hidden_part, (part_index + 1) * hidden_part)
        up_value = low_back(dense(mid_low, up_w[:, cols]))
        act = low(jax.nn.gelu(up_value, approximate=False))
        ffn = ffn + low(dense(act, down_w[:, cols].T))
    ffn = low_back(ffn)
    return layer_norm(ffn + mid, gains[1], shifts[1])

def reference(x_in, tags, lengths, w_qkv, w_out, w_up, w_down, norm_gain, norm_bias, cotangent):
    weights = (w_qkv.astype(jnp.float32), w_out.astype(jnp.float32), w_up.astype(jnp.float32), w_down.astype(jnp.float32), norm_gain.astype(jnp.float32), norm_bias.astype(jnp.float32))
    chains = x_in.astype(jnp.float32).reshape(CHAINS, LENGTH, D)

    def single_chain(chain, kind, length, params):
        picked = [lax.dynamic_index_in_dim(p, kind, 0, keepdims=False) for p in params]
        return chain_forward(chain, length, *picked)
    saved = jax.checkpoint(single_chain)

    def whole(chain_rows, params):

        def advance(carry, element):
            return (carry, saved(element[0], element[1], element[2], params))
        return lax.scan(advance, None, (chain_rows, tags, lengths))[1]
    outputs, pull = jax.vjp(whole, chains, weights)
    grad_chains, grad_weights = pull(cotangent.astype(jnp.float32).reshape(CHAINS, LENGTH, D))
    return (outputs.reshape(TOKENS, D).astype(jnp.bfloat16), grad_chains.reshape(TOKENS, D), grad_weights[0], grad_weights[1], grad_weights[2], grad_weights[3], grad_weights[4], grad_weights[5])
```

```python
from functools import partial

import jax
import jax.numpy as jnp
from jax import lax
from jax.experimental import pallas as pl
from jax.experimental.pallas import tpu as pltpu
from jax.sharding import Mesh
from jax.sharding import PartitionSpec as P

D = 768
HEADS = 12
HEAD_DIM = 64
MICRO = 4
CHAINS_PART = 1
LENGTH = 160
GROUPS = 4
OWN = 4
EXTRA = 2
SLOTS = OWN + EXTRA
EXT_ROWS = EXTRA * LENGTH
OWN_ROWS = OWN * LENGTH
ROWS = SLOTS * LENGTH

EPS = 1e-12
NEG = -1e30
HIGH = lax.Precision.HIGHEST
BF = jnp.bfloat16
F32 = jnp.float32
MESH = pl.DeviceIdType.MESH
ANY = pl.BlockSpec(memory_space=pl.ANY)
AXES = ("z", "x", "y", "c")


def place():
    return tuple(lax.axis_index(a) for a in AXES)


def meet(nz, z, x, y, c):
    barrier = pltpu.get_barrier_semaphore()
    friends = [{"c": 1 - c}, {"y": 1 - y}, {"y": 1 - y, "c": 1 - c}, {"x": 1 - x}]
    friends += [{"z": lax.rem(z + dz, nz)} for dz in range(1, nz)]
    for friend in friends:
        pl.semaphore_signal(barrier, inc=1, device_id=friend, device_id_type=MESH)
    pl.semaphore_wait(barrier, len(friends))


def gather_kernel(nz, rows, x_in, cot, qo, up, dn, norms, w, x_ext, cot_ext, n_all,
                  y_s, y_r, z_s, z_r, x_s, x_r, c_s, c_r, e_s, e_r, n_s, n_r, l_s):
    z, x, y, c = place()
    mats = (qo, up, dn)

    def block(m, t, zz, xx):
        off = pl.multiple_of((zz * 2 + xx) * rows, rows)
        return w.at[m, t, pl.ds(off, rows)]

    def send(src, dst, s_sem, r_sem, who):
        return pltpu.make_async_remote_copy(
            src_ref=src, dst_ref=dst, send_sem=s_sem, recv_sem=r_sem, device_id=who, device_id_type=MESH
        )

    meet(nz, z, x, y, c)
    sent = []

    def go(copy):
        copy.start()
        sent.append(copy)

    groups = (2 * y + c, 2 * (1 - y) + c)
    locals_ = []
    for m in range(3):
        go(send(mats[m].at[1 - y], block(m, groups[0], z, x), y_s.at[m], y_r.at[m], {"y": 1 - y}))
    me = ((z * 2 + x) * 2 + y) * 2 + c
    copy = pltpu.make_async_copy(norms, n_all.at[me], l_s.at[3])
    copy.start()
    for m in range(3):
        cp = pltpu.make_async_copy(mats[m].at[y], block(m, groups[0], z, x), l_s.at[m])
        cp.start()
        locals_.append(cp)

    @pl.when(y != c)
    def _():
        for i, arr in enumerate((x_in, cot)):
            out = (x_ext, cot_ext)[i]
            for j, (who, part) in enumerate((({"y": 1 - y}, c), ({"y": 1 - y, "c": 1 - c}, 1 - c))):
                src = arr.at[pl.ds(pl.multiple_of(part * EXT_ROWS, EXT_ROWS), EXT_ROWS)]
                send(src, out, e_s.at[i, j], e_r.at[i], who).start()

    def spread(m, g, src):
        t = groups[g]
        for dz in range(1, nz):
            go(send(src, block(m, t, z, x), z_s.at[m, g, dz], z_r.at[m, g, dz], {"z": lax.rem(z + dz, nz)}))
        go(send(src, block(m, t, z, x), x_s.at[m, g, 0], x_r.at[m, g, 0], {"x": 1 - x}))
        go(send(src, block(m, t, z, x), c_s.at[m, g, 0, 0], c_r.at[m, g, 0, 0], {"c": 1 - c}))

    def arrived(m, g, dz, xx, sem):
        zz = lax.rem(z + nz - dz, nz)
        ref = block(m, groups[g], zz, xx)
        send(ref, ref, sem, sem, {"c": 1 - c}).wait_recv()
        return ref

    for m in range(3):
        spread(m, 0, mats[m].at[y])
    copy.wait()
    n1 = send(n_all.at[me], n_all.at[me], n_s.at[0], n_r.at[0], {"c": 1 - c})
    go(n1)
    n1.wait_recv()
    base = pl.multiple_of(me - c, 2)
    n2 = send(n_all.at[pl.ds(base, 2)], n_all.at[pl.ds(base, 2)], n_s.at[1], n_r.at[1], {"y": 1 - y})
    go(n2)
    n2.wait_recv()
    base = pl.multiple_of((z * 2 + x) * 4, 4)
    n3 = send(n_all.at[pl.ds(base, 4)], n_all.at[pl.ds(base, 4)], n_s.at[2], n_r.at[2], {"x": 1 - x})
    go(n3)
    n3.wait_recv()
    base = pl.multiple_of(z * 8, 8)
    for dz in range(1, nz):
        go(send(n_all.at[pl.ds(base, 8)], n_all.at[pl.ds(base, 8)], n_s.at[2 + dz], n_r.at[2 + dz], {"z": lax.rem(z + dz, nz)}))
    for m in range(3):
        ref = block(m, groups[1], z, x)
        send(ref, ref, y_r.at[m], y_r.at[m], {"y": 1 - y}).wait_recv()
        spread(m, 1, ref)
    for m in range(3):
        for g in range(2):
            for dz in range(1, nz):
                ref = arrived(m, g, dz, x, z_r.at[m, g, dz])
                go(send(ref, ref, x_s.at[m, g, dz], x_r.at[m, g, dz], {"x": 1 - x}))
                go(send(ref, ref, c_s.at[m, g, dz, 0], c_r.at[m, g, dz, 0], {"c": 1 - c}))
        for g in range(2):
            for dz in range(nz):
                ref = arrived(m, g, dz, 1 - x, x_r.at[m, g, dz])
                go(send(ref, ref, c_s.at[m, g, dz, 1], c_r.at[m, g, dz, 1], {"c": 1 - c}))
    for m in range(3):
        for g in range(2):
            for dz in range(nz):
                zz = lax.rem(z + nz - dz, nz)
                for q, xx in enumerate((x, 1 - x)):
                    ref = block(m, (1 - 2 * c) + groups[g], zz, xx)
                    send(ref, ref, c_r.at[m, g, dz, q], c_r.at[m, g, dz, q], {"c": 1 - c}).wait_recv()
    for dz in range(1, nz):
        zz = lax.rem(z + nz - dz, nz)
        ref = n_all.at[pl.ds(pl.multiple_of(zz * 8, 8), 8)]
        send(ref, ref, n_r.at[2 + dz], n_r.at[2 + dz], {"x": 1 - x}).wait_recv()
    for i, out in enumerate((x_ext, cot_ext)):
        send(out, out, e_r.at[i], e_r.at[i], {"y": 1 - y}).wait_recv()
    for cp in locals_:
        cp.wait()
    for cp in sent:
        cp.wait_send()

    @pl.when(y != c)
    def _():
        for i in range(2):
            for j in range(2):
                src = x_in.at[pl.ds(0, EXT_ROWS)]
                send(src, src, e_s.at[i, j], e_r.at[i], {"y": 1 - y}).wait_send()


def gather_all(nz, x_in, cot, qo, up, dn, norms):
    rows = qo.shape[1]
    sem = pltpu.SemaphoreType.DMA
    return pl.pallas_call(
        partial(gather_kernel, nz, rows),
        out_shape=(
            jax.ShapeDtypeStruct((3, GROUPS, D, D), BF),
            jax.ShapeDtypeStruct((EXT_ROWS, D), BF),
            jax.ShapeDtypeStruct((EXT_ROWS, D), BF),
            jax.ShapeDtypeStruct((nz * 8, 8, 128), F32),
        ),
        in_specs=[ANY] * 6,
        out_specs=(ANY,) * 4,
        scratch_shapes=[
            sem((3,)), sem((3,)),
            sem((3, 2, nz)), sem((3, 2, nz)),
            sem((3, 2, nz)), sem((3, 2, nz)),
            sem((3, 2, nz, 2)), sem((3, 2, nz, 2)),
            sem((2, 2)), sem((2,)),
            sem((nz + 2,)), sem((nz + 2,)),
            sem((4,)),
        ],
        compiler_params=pltpu.CompilerParams(collective_id=0, has_side_effects=True),
        name="gather_weights",
    )(x_in, cot, qo, up, dn, norms)


def scatter_kernel(nz, rows, grads, ngrad, y_ext, g_ext, own_out, oth_out, n_out, y_back, g_back,
                   own, r_c, r_x, r_z, half, nbuf, n_c, n_x, n_z, nsum,
                   c_s, c_r, x_s, x_r, z_s, z_r, y_s, y_r, e_s, e_r, n_s, n_r, l_s):
    z, x, y, c = place()

    def send(src, dst, s_sem, r_sem, who):
        return pltpu.make_async_remote_copy(
            src_ref=src, dst_ref=dst, send_sem=s_sem, recv_sem=r_sem, device_id=who, device_id_type=MESH
        )

    def part(zz, xx):
        return pl.ds(pl.multiple_of((zz * 2 + xx) * rows, rows), rows)

    meet(nz, z, x, y, c)
    sent = []

    def go(copy):
        copy.start()
        sent.append(copy)

    order = [(m, g) for m in (2, 1, 0) for g in range(2)]
    loads = {}
    for m, g in order:
        go(send(grads.at[m, 2 * g + 1 - c], r_c.at[m, g], c_s.at[m, g], c_r.at[m, g], {"c": 1 - c}))
        loads[m, g] = pltpu.make_async_copy(grads.at[m, 2 * g + c], own.at[m, g], l_s.at[m, g])
        loads[m, g].start()

    for i, (src, dst) in enumerate(((y_ext, y_back), (g_ext, g_back))):
        dst = dst.at[pl.ds(pl.multiple_of(c * EXT_ROWS, EXT_ROWS), EXT_ROWS)]

        @pl.when(c == y)
        def _():
            send(src, dst, e_s.at[i], e_r.at[i, c], {"y": 1 - y}).start()

        @pl.when(c != y)
        def _():
            send(src, dst, e_s.at[i], e_r.at[i, c], {"y": 1 - y, "c": 1 - c}).start()

    nbuf[...] = ngrad[...]
    a = send(nbuf, n_c, n_s.at[0], n_r.at[0], {"c": 1 - c})
    go(a)
    a.wait_recv()
    nsum[0] = nbuf[...] + n_c[...]
    b = send(nsum.at[0], n_x, n_s.at[1], n_r.at[1], {"x": 1 - x})
    go(b)
    b.wait_recv()
    nsum[1] = nsum[0] + n_x[...]
    for dz in range(1, nz):
        go(send(nsum.at[1], n_z.at[dz], n_s.at[1 + dz], n_r.at[1 + dz], {"z": lax.rem(z + dz, nz)}))

    for m, g in order:
        loads[m, g].wait()
        send(r_c.at[m, g], r_c.at[m, g], c_r.at[m, g], c_r.at[m, g], {"c": 1 - c}).wait_recv()

        def add(zz, _):
            for xx in (1 - x, x):
                p = part(zz, xx)
                own[m, g, p] = (own[m, g, p].astype(F32) + r_c[m, g, p].astype(F32)).astype(BF)
            return 0

        lax.fori_loop(0, nz, add, 0)
        for zz in range(nz):
            go(send(own.at[m, g, part(zz, 1 - x)], r_x.at[m, g, zz], x_s.at[m, g, zz], x_r.at[m, g, zz], {"x": 1 - x}))
    for m, g in order:
        for dz in range(1, nz + 1):
            zz = lax.rem(z + dz, nz)
            send(r_x.at[m, g, zz], r_x.at[m, g, zz], x_r.at[m, g, zz], x_r.at[m, g, zz], {"x": 1 - x}).wait_recv()
            p = part(zz, x)
            own[m, g, p] = (own[m, g, p].astype(F32) + r_x[m, g, zz].astype(F32)).astype(BF)
            if dz < nz:
                go(send(own.at[m, g, p], r_z.at[m, g, dz], z_s.at[m, g, dz], z_r.at[m, g, dz], {"z": zz}))
    total = nsum[1]
    for dz in range(1, nz):
        send(n_z.at[dz], n_z.at[dz], n_r.at[1 + dz], n_r.at[1 + dz], {"x": 1 - x}).wait_recv()
        total = total + n_z[dz]
    n_out[y] = total
    nd = send(n_out.at[y], n_out.at[y], n_s.at[nz + 1], n_r.at[nz + 1], {"y": 1 - y})
    go(nd)
    for m, g in order:
        p = part(z, x)
        total = own[m, g, p].astype(F32)
        for dz in range(1, nz):
            send(r_z.at[m, g, dz], r_z.at[m, g, dz], z_r.at[m, g, dz], z_r.at[m, g, dz], {"x": 1 - x}).wait_recv()
            total = total + r_z[m, g, dz].astype(F32)

        @pl.when(y == g)
        def _():
            own_out[m] = total

        @pl.when(y != g)
        def _():
            half[m] = total.astype(BF)
            send(half.at[m], oth_out.at[m], y_s.at[m], y_r.at[m], {"y": 1 - y}).start()
    for m in range(3):
        send(half.at[m], oth_out.at[m], y_s.at[m], y_r.at[m], {"y": 1 - y}).wait()
    nd.wait_recv()

    @pl.when(y != c)
    def _():
        for i, dst in enumerate((y_back, g_back)):
            for j in range(2):
                ref = dst.at[pl.ds(j * EXT_ROWS, EXT_ROWS)]
                send(ref, ref, e_s.at[i], e_r.at[i, j], {"y": 1 - y}).wait_recv()

    for i in range(2):
        send(y_ext, y_ext, e_s.at[i], e_s.at[i], {"y": 1 - y}).wait_send()
    for cp in sent:
        cp.wait_send()


def scatter_all(nz, rows, grads, ngrad, y_ext, g_ext):
    sem = pltpu.SemaphoreType.DMA
    V = pl.BlockSpec(memory_space=pltpu.VMEM)
    return pl.pallas_call(
        partial(scatter_kernel, nz, rows),
        out_shape=(
            jax.ShapeDtypeStruct((3, rows, D), F32),
            jax.ShapeDtypeStruct((3, rows, D), BF),
            jax.ShapeDtypeStruct((2, 8, D), F32),
            jax.ShapeDtypeStruct((OWN_ROWS, D), BF),
            jax.ShapeDtypeStruct((OWN_ROWS, D), BF),
        ),
        in_specs=[ANY, V, ANY, ANY],
        out_specs=(V, ANY, V, ANY, ANY),
        scratch_shapes=[
            pltpu.VMEM((3, 2, D, D), BF),
            pltpu.VMEM((3, 2, D, D), BF),
            pltpu.VMEM((3, 2, nz, rows, D), BF),
            pltpu.VMEM((3, 2, nz, rows, D), BF),
            pltpu.VMEM((3, rows, D), BF),
            pltpu.VMEM((8, D), F32),
            pltpu.VMEM((8, D), F32),
            pltpu.VMEM((8, D), F32),
            pltpu.VMEM((nz, 8, D), F32),
            pltpu.VMEM((2, 8, D), F32),
            sem((3, 2)), sem((3, 2)),
            sem((3, 2, nz)), sem((3, 2, nz)),
            sem((3, 2, nz)), sem((3, 2, nz)),
            sem((3,)), sem((3,)),
            sem((2,)), sem((2, 2)),
            sem((nz + 2,)), sem((nz + 2,)),
            sem((3, 2)),
        ],
        compiler_params=pltpu.CompilerParams(
            collective_id=1, has_side_effects=True, vmem_limit_bytes=48 * 1024 * 1024
        ),
        name="scatter_grads",
    )(grads, ngrad, y_ext, g_ext)


def norm_forward(values, gain, shift):
    center = values - jnp.mean(values, -1, keepdims=True)
    factor = lax.rsqrt(jnp.mean(center * center, -1, keepdims=True) + EPS)
    normed = center * factor
    return normed * gain + shift, normed, factor


def norm_backward(grad_out, normed, factor, gain):
    scaled = grad_out * gain
    mean_plain = jnp.mean(scaled, -1, keepdims=True)
    mean_normed = jnp.mean(scaled * normed, -1, keepdims=True)
    return factor * (scaled - mean_plain - normed * mean_normed)


def ein(pattern, *operands):
    return jnp.einsum(pattern, *operands, preferred_element_type=F32)


def layer(x, cot, lens, w, gains, shifts):
    heads = HEADS // GROUPS
    qkv_w = w[0][:, :, : 3 * heads * HEAD_DIM]
    out_w = w[0][:, :, 3 * heads * HEAD_DIM :]
    up_w, down_w = w[1], w[2]
    proj = ein("nd,tdk->tnk", x, qkv_w).astype(BF)
    parts = proj.reshape(GROUPS, SLOTS, LENGTH, 3, heads, HEAD_DIM)
    query, key, value = parts[:, :, :, 0], parts[:, :, :, 1], parts[:, :, :, 2]
    valid = lax.broadcasted_iota(jnp.int32, (SLOTS, LENGTH), 1) < lens[:, None]
    scores = ein("tcqhe,tckhe->tchqk", query, key) * 0.125
    scores = jnp.where(valid[None, :, None, None, :], scores, NEG)
    probs = jax.nn.softmax(scores, axis=-1)
    low = probs.astype(BF)
    hout = ein("tchqk,tckhe->tcqhe", low, value).astype(BF).reshape(GROUPS, ROWS, heads * HEAD_DIM)
    attn = ein("tnh,tdh->nd", hout, out_w)
    mid, n1, s1 = norm_forward(x.astype(F32) + attn, gains[0], shifts[0])
    mid_low = mid.astype(BF)
    up = ein("nd,tdf->tnf", mid_low, up_w)
    act, pull = jax.vjp(partial(jax.nn.gelu, approximate=False), up)
    act = act.astype(BF)
    ffn = ein("tnf,tdf->nd", act, down_w)
    final, n2, s2 = norm_forward(ffn + mid, gains[1], shifts[1])
    y = final.astype(BF)
    dr2 = norm_backward(cot, n2, s2, gains[1])
    ngrad = [None, jnp.sum(cot * n2, 0), None, jnp.sum(cot, 0)]
    d_ffn = dr2.astype(BF)
    d_act = ein("nd,tdf->tnf", d_ffn, down_w)
    d_up = pull(d_act)[0].astype(BF)
    g_down = ein("nd,tnf->tdf", d_ffn, act)
    g_up = ein("nd,tnf->tdf", mid_low, d_up)
    d_mid = dr2 + ein("tnf,tdf->nd", d_up, up_w)
    dr1 = norm_backward(d_mid, n1, s1, gains[0])
    ngrad[0] = jnp.sum(d_mid * n1, 0)
    ngrad[2] = jnp.sum(d_mid, 0)
    d_attn = dr1.astype(BF)
    d_heads = ein("nd,tdh->tnh", d_attn, out_w).astype(BF)
    g_out = ein("nd,tnh->tdh", d_attn, hout)
    d_heads = d_heads.reshape(GROUPS, SLOTS, LENGTH, heads, HEAD_DIM)
    d_probs = ein("tcqhe,tckhe->tchqk", d_heads, value)
    d_scores = (probs * (d_probs - jnp.sum(d_probs * probs, -1, keepdims=True))).astype(BF)
    d_q = (ein("tchqk,tckhe->tcqhe", d_scores, key) * 0.125).astype(BF)
    d_k = (ein("tchqk,tcqhe->tckhe", d_scores, query) * 0.125).astype(BF)
    d_v = ein("tchqk,tcqhe->tckhe", low, d_heads).astype(BF)
    d_proj = jnp.stack([d_q, d_k, d_v], 3).reshape(GROUPS, ROWS, 3 * heads * HEAD_DIM)
    g_qkv = ein("nd,tnk->tdk", x, d_proj)
    x_grad = dr1 + ein("tnk,tdk->nd", d_proj, qkv_w)
    grads = jnp.stack([jnp.concatenate([g_qkv, g_out], -1), g_up, g_down]).astype(BF)
    ngrad = jnp.pad(jnp.stack(ngrad), ((0, 4), (0, 0)))
    return y, x_grad, grads, ngrad


def split_local(nz, x_in, tags, lengths, w_qkv, w_out, w_up, w_down, norm_gain, norm_bias, cotangent):
    z, x, y, c = place()
    rows = w_up.shape[1]
    cols = norm_gain.shape[2]
    own = 2 * y + c
    qo = jnp.concatenate([w_qkv.reshape(2, rows, -1), w_out], -1)
    norms = jnp.concatenate([norm_gain.reshape(4, cols), norm_bias.reshape(4, cols)], 0)
    norms = jnp.pad(norms, ((0, 0), (0, 128 - cols)))
    w, x_ext, cot_ext, n_all = gather_all(nz, x_in, cotangent, qo, w_up, w_down, norms)
    params = n_all[:, :, :cols].transpose(1, 0, 2).reshape(2, 2, 2, D)
    params = lax.dynamic_index_in_dim(params, y, 1, keepdims=False)

    def slots(values):
        mine = lax.dynamic_slice_in_dim(values, own * OWN, OWN)
        lent = lax.dynamic_slice_in_dim(values, (2 - y) * OWN + c * EXTRA, EXTRA)
        return jnp.concatenate([mine, lent])

    kinds = slots(tags)
    lens = slots(lengths)
    mine = jnp.repeat(kinds == y, LENGTH)[:, None]
    rows_x = jnp.concatenate([x_in, x_ext])
    rows_cot = jnp.concatenate([cotangent, cot_ext]).astype(F32)
    rows_cot = jnp.where(mine, rows_cot, 0.0)
    y_rows, g_rows, grads, ngrad = layer(rows_x, rows_cot, lens, w, params[0], params[1])
    own_g, oth_g, n_sum, y_back, g_back = scatter_all(
        nz, rows, grads, ngrad, y_rows[OWN_ROWS:], g_rows[OWN_ROWS:].astype(BF)
    )
    y_out = jnp.where(mine[:OWN_ROWS], y_rows[:OWN_ROWS], y_back)
    x_grad = jnp.where(mine[:OWN_ROWS], g_rows[:OWN_ROWS], g_back.astype(F32))
    oth_g = oth_g.astype(F32)
    both = jnp.stack([jnp.where(y == 0, own_g, oth_g), jnp.where(y == 0, oth_g, own_g)])
    width = w_qkv.shape[2] * w_qkv.shape[3]
    me = ((z * 2 + x) * 2 + y) * 2 + c
    n_mine = lax.dynamic_slice_in_dim(n_sum, me * cols, cols, 2)
    return (
        y_out,
        x_grad,
        both[:, 0, :, :width].reshape(w_qkv.shape),
        both[:, 0, :, width:],
        both[:, 1],
        both[:, 2],
        n_mine[:, :2],
        n_mine[:, 2:4],
    )


def typed_map(operand, stacked, chain_kinds, pattern):

    def single(element):
        weight = lax.dynamic_index_in_dim(stacked, element[1], 0, keepdims=False)
        return jnp.einsum(pattern, element[0], weight, preferred_element_type=jnp.float32)

    return lax.map(single, (operand, chain_kinds))


def typed_grads(running, operand, partner, chain_kinds, pattern):

    def single(carry, element):
        product_term = jnp.einsum(
            pattern, element[0], element[1], preferred_element_type=jnp.float32
        )
        previous = lax.dynamic_index_in_dim(carry, element[2], 0, keepdims=False)
        return (
            lax.dynamic_update_index_in_dim(carry, previous + product_term, element[2], 0),
            None,
        )

    return lax.scan(single, running, (operand, partner, chain_kinds))[0]


def row_terms(operand, stacked, chain_kinds, pattern, row_count):
    result = typed_map(operand, stacked, chain_kinds, pattern)
    return result.reshape(row_count, result.shape[-1])


def old_norm_forward(values, gain_rows, shift_rows):
    center = values - jnp.mean(values, -1, keepdims=True)
    factor = lax.rsqrt(jnp.mean(center * center, -1, keepdims=True) + EPS)
    normed = center * factor
    return (normed * gain_rows + shift_rows, normed, factor)


def old_norm_backward(grad_out, normed, factor, gain_rows):
    scaled = grad_out * gain_rows
    mean_plain = jnp.mean(scaled, -1, keepdims=True)
    mean_normed = jnp.mean(scaled * normed, -1, keepdims=True)
    return factor * (scaled - mean_plain - normed * mean_normed)


def type_sums(onehot, values):
    return jnp.dot(onehot.T, values, precision=HIGH, preferred_element_type=jnp.float32)


def general_local(x_in, tags, lengths, w_qkv, w_out, w_up, w_down, norm_gain, norm_bias, cotangent):
    tp_count = lax.axis_size("tensor")
    tp_index = lax.axis_index("tensor")
    local_rows = CHAINS_PART * LENGTH
    batch_chains = tp_count * CHAINS_PART
    head_cols = w_qkv.shape[3]
    local_heads = head_cols // HEAD_DIM
    tag_grid = tags.reshape(tp_count, MICRO, CHAINS_PART)
    len_grid = lengths.reshape(tp_count, MICRO, CHAINS_PART)
    own_tags = lax.dynamic_index_in_dim(tag_grid, tp_index, 0, keepdims=False)
    gains, shifts = (
        lax.all_gather(norm_gain, ("dp", "tensor"), axis=2, tiled=True),
        lax.all_gather(norm_bias, ("dp", "tensor"), axis=2, tiled=True),
    )
    grad_full = (
        jnp.zeros((2, D, 3, head_cols), jnp.float32),
        jnp.zeros((2, D, head_cols), jnp.float32),
        jnp.zeros((2, D, w_up.shape[2]), jnp.float32),
        jnp.zeros((2, D, w_down.shape[2]), jnp.float32),
    )
    shards = (
        jnp.zeros(w_qkv.shape, jnp.float32),
        jnp.zeros(w_out.shape, jnp.float32),
        jnp.zeros(w_up.shape, jnp.float32),
        jnp.zeros(w_down.shape, jnp.float32),
    )
    gain_acc = jnp.zeros((2, 2, D), jnp.float32)
    shift_acc = jnp.zeros((2, 2, D), jnp.float32)
    outputs = []
    input_grads = []
    for micro_index in range(MICRO):
        held = (
            lax.all_gather(w_qkv, "dp", axis=1, tiled=True),
            lax.all_gather(w_out, "dp", axis=1, tiled=True),
            lax.all_gather(w_up, "dp", axis=1, tiled=True),
            lax.all_gather(w_down, "dp", axis=1, tiled=True),
        )
        qkv_w, out_w, up_w, down_w = held
        chain_kinds = tag_grid[:, micro_index].reshape(batch_chains)
        chain_lens = len_grid[:, micro_index].reshape(batch_chains)
        own_rows = x_in[micro_index * local_rows : (micro_index + 1) * local_rows]
        kinds_rows = jnp.repeat(own_tags[micro_index], LENGTH)
        heavy_rows = (kinds_rows == 0)[:, None]
        onehot = (kinds_rows[:, None] == jnp.arange(2)[None, :]).astype(jnp.float32)
        gain_mid = jnp.where(heavy_rows, gains[0, 0], gains[1, 0])
        shift_mid = jnp.where(heavy_rows, shifts[0, 0], shifts[1, 0])
        gain_end = jnp.where(heavy_rows, gains[0, 1], gains[1, 1])
        shift_end = jnp.where(heavy_rows, shifts[0, 1], shifts[1, 1])
        gathered = lax.all_gather(own_rows, "tensor", axis=0, tiled=True).reshape(
            batch_chains, LENGTH, D
        )
        projected = typed_map(gathered, qkv_w, chain_kinds, "ld,dkh->lkh").astype(jnp.bfloat16)
        query = projected[:, :, 0].reshape(batch_chains, LENGTH, local_heads, HEAD_DIM)
        keys_low = projected[:, :, 1].reshape(batch_chains, LENGTH, local_heads, HEAD_DIM)
        values_low = projected[:, :, 2].reshape(batch_chains, LENGTH, local_heads, HEAD_DIM)
        valid = (
            lax.broadcasted_iota(jnp.int32, (batch_chains, 1, 1, LENGTH), 3)
            < chain_lens[:, None, None, None]
        )
        scores = (
            jnp.einsum("cqhe,ckhe->chqk", query, keys_low, preferred_element_type=jnp.float32)
            * 0.125
        )
        scores = jnp.where(valid, scores, NEG)
        highest = jnp.max(scores, -1, keepdims=True)
        expo = jnp.exp(scores - highest)
        totals = jnp.sum(expo, -1, keepdims=True)
        probs = expo / totals
        log_total = highest + jnp.log(totals)
        heads_low = jnp.einsum(
            "chqk,ckhe->cqhe",
            probs.astype(jnp.bfloat16),
            values_low,
            preferred_element_type=jnp.float32,
        ).astype(jnp.bfloat16)
        heads_low = heads_low.reshape(batch_chains, LENGTH, head_cols)
        attn_sum = lax.psum_scatter(
            row_terms(
                heads_low, out_w, chain_kinds, "lh,dh->ld", lax.axis_size("tensor") * local_rows
            ).astype(jnp.bfloat16),
            "tensor",
            scatter_dimension=0,
            tiled=True,
        ).astype(jnp.float32)
        mid, normed_mid, factor_mid = old_norm_forward(
            own_rows.astype(jnp.float32) + attn_sum, gain_mid, shift_mid
        )
        mid_all = lax.all_gather(mid.astype(jnp.bfloat16), "tensor", axis=0, tiled=True).reshape(
            batch_chains, LENGTH, D
        )
        up_value = typed_map(mid_all, up_w, chain_kinds, "ld,df->lf")
        act_low = jax.nn.gelu(up_value, approximate=False).astype(jnp.bfloat16)
        ffn_sum = lax.psum_scatter(
            row_terms(
                act_low, down_w, chain_kinds, "lf,df->ld", lax.axis_size("tensor") * local_rows
            ).astype(jnp.bfloat16),
            "tensor",
            scatter_dimension=0,
            tiled=True,
        ).astype(jnp.float32)
        final, normed_end, factor_end = old_norm_forward(ffn_sum + mid, gain_end, shift_end)
        outputs.append(final.astype(jnp.bfloat16))
        base = grad_full
        grad_final = cotangent[micro_index * local_rows : (micro_index + 1) * local_rows].astype(
            jnp.float32
        )
        gain_acc = gain_acc.at[:, 1].add(type_sums(onehot, grad_final * normed_end))
        shift_acc = shift_acc.at[:, 1].add(type_sums(onehot, grad_final))
        grad_resid2 = old_norm_backward(grad_final, normed_end, factor_end, gain_end)
        grad_ffn = lax.all_gather(
            grad_resid2.astype(jnp.bfloat16), "tensor", axis=0, tiled=True
        ).reshape(batch_chains, LENGTH, D)
        grad_act = typed_map(grad_ffn, down_w, chain_kinds, "ld,df->lf")
        unused_value, gelu_back = jax.vjp(partial(jax.nn.gelu, approximate=False), up_value)
        grad_up = gelu_back(grad_act)[0].astype(jnp.bfloat16)
        down_acc = typed_grads(base[3], grad_ffn, act_low, chain_kinds, "ld,lf->df")
        up_acc = typed_grads(base[2], mid_all, grad_up, chain_kinds, "ld,lf->df")
        grad_mid = grad_resid2 + lax.psum_scatter(
            row_terms(
                grad_up, up_w, chain_kinds, "lf,df->ld", lax.axis_size("tensor") * local_rows
            ).astype(jnp.bfloat16),
            "tensor",
            scatter_dimension=0,
            tiled=True,
        ).astype(jnp.float32)
        gain_acc = gain_acc.at[:, 0].add(type_sums(onehot, grad_mid * normed_mid))
        shift_acc = shift_acc.at[:, 0].add(type_sums(onehot, grad_mid))
        grad_resid1 = old_norm_backward(grad_mid, normed_mid, factor_mid, gain_mid)
        grad_attn = lax.all_gather(
            grad_resid1.astype(jnp.bfloat16), "tensor", axis=0, tiled=True
        ).reshape(batch_chains, LENGTH, D)
        grad_heads = typed_map(grad_attn, out_w, chain_kinds, "ld,dh->lh").astype(jnp.bfloat16)
        out_acc = typed_grads(base[1], grad_attn, heads_low, chain_kinds, "ld,lh->dh")
        grad_heads = grad_heads.reshape(batch_chains, LENGTH, local_heads, HEAD_DIM)
        again = (
            jnp.einsum("cqhe,ckhe->chqk", query, keys_low, preferred_element_type=jnp.float32)
            * 0.125
        )
        probs_again = jnp.exp(jnp.where(valid, again, NEG) - log_total)
        grad_probs = jnp.einsum(
            "cqhe,ckhe->chqk", grad_heads, values_low, preferred_element_type=jnp.float32
        )
        inner = jnp.sum(grad_probs * probs_again, -1, keepdims=True)
        grad_scores = (probs_again * (grad_probs - inner)).astype(jnp.bfloat16)
        grad_query = (
            jnp.einsum("chqk,ckhe->cqhe", grad_scores, keys_low, preferred_element_type=jnp.float32)
            * 0.125
        ).astype(jnp.bfloat16)
        grad_keys = (
            jnp.einsum("chqk,cqhe->ckhe", grad_scores, query, preferred_element_type=jnp.float32)
            * 0.125
        ).astype(jnp.bfloat16)
        grad_values = jnp.einsum(
            "chqk,cqhe->ckhe",
            probs_again.astype(jnp.bfloat16),
            grad_heads,
            preferred_element_type=jnp.float32,
        ).astype(jnp.bfloat16)
        grad_proj = jnp.stack([grad_query, grad_keys, grad_values], 2).reshape(
            batch_chains, LENGTH, 3, head_cols
        )
        qkv_acc = typed_grads(base[0], gathered, grad_proj, chain_kinds, "ld,lkh->dkh")
        grad_input = grad_resid1 + lax.psum_scatter(
            row_terms(
                grad_proj, qkv_w, chain_kinds, "lkh,dkh->ld", lax.axis_size("tensor") * local_rows
            ).astype(jnp.bfloat16),
            "tensor",
            scatter_dimension=0,
            tiled=True,
        ).astype(jnp.float32)
        input_grads.append(grad_input)
        updated = (qkv_acc, out_acc, up_acc, down_acc)
        grad_full = updated
    shards = (
        lax.psum_scatter(grad_full[0], "dp", scatter_dimension=1, tiled=True),
        lax.psum_scatter(grad_full[1], "dp", scatter_dimension=1, tiled=True),
        lax.psum_scatter(grad_full[2], "dp", scatter_dimension=1, tiled=True),
        lax.psum_scatter(grad_full[3], "dp", scatter_dimension=1, tiled=True),
    )
    gain_grad, shift_grad = (
        lax.psum_scatter(gain_acc, ("dp", "tensor"), scatter_dimension=2, tiled=True),
        lax.psum_scatter(shift_acc, ("dp", "tensor"), scatter_dimension=2, tiled=True),
    )
    return (
        jnp.concatenate(outputs, 0),
        jnp.concatenate(input_grads, 0),
        shards[0],
        shards[1],
        shards[2],
        shards[3],
        gain_grad,
        shift_grad,
    )


def solution(mesh):
    placed = (
        P(("dp", "tensor"), None),
        P("dp"),
        P("dp"),
        P(None, "dp", None, "tensor"),
        P(None, "dp", "tensor"),
        P(None, "dp", "tensor"),
        P(None, "dp", "tensor"),
        P(None, None, ("dp", "tensor")),
        P(None, None, ("dp", "tensor")),
        P(("dp", "tensor"), None),
    )
    results = (
        P(("dp", "tensor"), None),
        P(("dp", "tensor"), None),
        P(None, "dp", None, "tensor"),
        P(None, "dp", "tensor"),
        P(None, "dp", "tensor"),
        P(None, "dp", "tensor"),
        P(None, None, ("dp", "tensor")),
        P(None, None, ("dp", "tensor")),
    )
    n_dp, n_tensor = mesh.shape["dp"], mesh.shape["tensor"]
    if n_tensor != GROUPS or n_dp % 2 or D % (16 * n_dp):
        return jax.shard_map(
            general_local, mesh=mesh, in_specs=placed, out_specs=results, check_vma=False
        )
    fine = Mesh(mesh.devices.reshape(n_dp // 2, 2, 2, 2), AXES)
    names = {"dp": ("z", "x"), "tensor": ("y", "c")}

    def refine(spec):
        parts = []
        for entry in spec:
            entry = (entry,) if isinstance(entry, str) else entry
            parts.append(entry and sum((names[a] for a in entry), ()))
        return P(*parts)

    return jax.shard_map(
        partial(split_local, n_dp // 2),
        mesh=fine,
        in_specs=tuple(refine(s) for s in placed),
        out_specs=tuple(refine(s) for s in results),
        check_vma=False,
    )
```

```python
from functools import partial

import jax
import jax.numpy as jnp
from jax import lax
from jax.experimental import pallas as pl
from jax.experimental.pallas import tpu as pltpu
from jax.sharding import Mesh
from jax.sharding import PartitionSpec as P

D = 768
HEADS = 12
HEAD_DIM = 64
MICRO = 4
CHAINS_PART = 1
LENGTH = 160
GROUPS = 4
OWN = 4
EXTRA = 2
SLOTS = OWN + EXTRA
EXT_ROWS = EXTRA * LENGTH
OWN_ROWS = OWN * LENGTH
ROWS = SLOTS * LENGTH

EPS = 1e-12
NEG = -1e30
HIGH = lax.Precision.HIGHEST
BF = jnp.bfloat16
F32 = jnp.float32
MESH = pl.DeviceIdType.MESH
ANY = pl.BlockSpec(memory_space=pl.ANY)
AXES = ("z", "x", "y", "c")


def place():
    return tuple(lax.axis_index(a) for a in AXES)


def meet(nz, z, x, y, c):
    barrier = pltpu.get_barrier_semaphore()
    friends = [{"c": 1 - c}, {"y": 1 - y}, {"y": 1 - y, "c": 1 - c}, {"x": 1 - x}]
    friends += [{"z": lax.rem(z + dz, nz)} for dz in range(1, nz)]
    for friend in friends:
        pl.semaphore_signal(barrier, inc=1, device_id=friend, device_id_type=MESH)
    pl.semaphore_wait(barrier, len(friends))


def gather_kernel(nz, rows, x_in, cot, qo, up, dn, norms, w, x_ext, cot_ext, n_all,
                  y_s, y_r, z_s, z_r, x_s, x_r, c_s, c_r, e_s, e_r, n_s, n_r, l_s):
    z, x, y, c = place()
    mats = (qo, up, dn)

    def block(m, t, zz, xx):
        off = pl.multiple_of((zz * 2 + xx) * rows, rows)
        return w.at[m, t, pl.ds(off, rows)]

    def send(src, dst, s_sem, r_sem, who):
        return pltpu.make_async_remote_copy(
            src_ref=src, dst_ref=dst, send_sem=s_sem, recv_sem=r_sem, device_id=who, device_id_type=MESH
        )

    meet(nz, z, x, y, c)
    sent = []

    def go(copy):
        copy.start()
        sent.append(copy)

    groups = (2 * y + c, 2 * (1 - y) + c)
    locals_ = []
    for m in range(3):
        go(send(mats[m].at[1 - y], block(m, groups[0], z, x), y_s.at[m], y_r.at[m], {"y": 1 - y}))
    me = ((z * 2 + x) * 2 + y) * 2 + c
    copy = pltpu.make_async_copy(norms, n_all.at[me], l_s.at[3])
    copy.start()
    for m in range(3):
        cp = pltpu.make_async_copy(mats[m].at[y], block(m, groups[0], z, x), l_s.at[m])
        cp.start()
        locals_.append(cp)

    @pl.when(y != c)
    def _():
        for i, arr in enumerate((x_in, cot)):
            out = (x_ext, cot_ext)[i]
            for j, (who, part) in enumerate((({"y": 1 - y}, c), ({"y": 1 - y, "c": 1 - c}, 1 - c))):
                src = arr.at[pl.ds(pl.multiple_of(part * EXT_ROWS, EXT_ROWS), EXT_ROWS)]
                send(src, out, e_s.at[i, j], e_r.at[i], who).start()

    def spread(m, g, src):
        t = groups[g]
        for dz in range(1, nz):
            go(send(src, block(m, t, z, x), z_s.at[m, g, dz], z_r.at[m, g, dz], {"z": lax.rem(z + dz, nz)}))
        go(send(src, block(m, t, z, x), x_s.at[m, g, 0], x_r.at[m, g, 0], {"x": 1 - x}))
        go(send(src, block(m, t, z, x), c_s.at[m, g, 0, 0], c_r.at[m, g, 0, 0], {"c": 1 - c}))

    def arrived(m, g, dz, xx, sem):
        zz = lax.rem(z + nz - dz, nz)
        ref = block(m, groups[g], zz, xx)
        send(ref, ref, sem, sem, {"c": 1 - c}).wait_recv()
        return ref

    for m in range(3):
        spread(m, 0, mats[m].at[y])
    copy.wait()
    n1 = send(n_all.at[me], n_all.at[me], n_s.at[0], n_r.at[0], {"c": 1 - c})
    go(n1)
    n1.wait_recv()
    base = pl.multiple_of(me - c, 2)
    n2 = send(n_all.at[pl.ds(base, 2)], n_all.at[pl.ds(base, 2)], n_s.at[1], n_r.at[1], {"y": 1 - y})
    go(n2)
    n2.wait_recv()
    base = pl.multiple_of((z * 2 + x) * 4, 4)
    n3 = send(n_all.at[pl.ds(base, 4)], n_all.at[pl.ds(base, 4)], n_s.at[2], n_r.at[2], {"x": 1 - x})
    go(n3)
    n3.wait_recv()
    base = pl.multiple_of(z * 8, 8)
    for dz in range(1, nz):
        go(send(n_all.at[pl.ds(base, 8)], n_all.at[pl.ds(base, 8)], n_s.at[2 + dz], n_r.at[2 + dz], {"z": lax.rem(z + dz, nz)}))
    for m in range(3):
        ref = block(m, groups[1], z, x)
        send(ref, ref, y_r.at[m], y_r.at[m], {"y": 1 - y}).wait_recv()
        spread(m, 1, ref)
    for m in range(3):
        for g in range(2):
            for dz in range(1, nz):
                ref = arrived(m, g, dz, x, z_r.at[m, g, dz])
                go(send(ref, ref, x_s.at[m, g, dz], x_r.at[m, g, dz], {"x": 1 - x}))
                go(send(ref, ref, c_s.at[m, g, dz, 0], c_r.at[m, g, dz, 0], {"c": 1 - c}))
        for g in range(2):
            for dz in range(nz):
                ref = arrived(m, g, dz, 1 - x, x_r.at[m, g, dz])
                go(send(ref, ref, c_s.at[m, g, dz, 1], c_r.at[m, g, dz, 1], {"c": 1 - c}))
    for m in range(3):
        for g in range(2):
            for dz in range(nz):
                zz = lax.rem(z + nz - dz, nz)
                for q, xx in enumerate((x, 1 - x)):
                    ref = block(m, (1 - 2 * c) + groups[g], zz, xx)
                    send(ref, ref, c_r.at[m, g, dz, q], c_r.at[m, g, dz, q], {"c": 1 - c}).wait_recv()
    for dz in range(1, nz):
        zz = lax.rem(z + nz - dz, nz)
        ref = n_all.at[pl.ds(pl.multiple_of(zz * 8, 8), 8)]
        send(ref, ref, n_r.at[2 + dz], n_r.at[2 + dz], {"x": 1 - x}).wait_recv()
    for i, out in enumerate((x_ext, cot_ext)):
        send(out, out, e_r.at[i], e_r.at[i], {"y": 1 - y}).wait_recv()
    for cp in locals_:
        cp.wait()
    for cp in sent:
        cp.wait_send()

    @pl.when(y != c)
    def _():
        for i in range(2):
            for j in range(2):
                src = x_in.at[pl.ds(0, EXT_ROWS)]
                send(src, src, e_s.at[i, j], e_r.at[i], {"y": 1 - y}).wait_send()


def gather_all(nz, x_in, cot, qo, up, dn, norms):
    rows = qo.shape[1]
    sem = pltpu.SemaphoreType.DMA
    return pl.pallas_call(
        partial(gather_kernel, nz, rows),
        out_shape=(
            jax.ShapeDtypeStruct((3, GROUPS, D, D), BF),
            jax.ShapeDtypeStruct((EXT_ROWS, D), BF),
            jax.ShapeDtypeStruct((EXT_ROWS, D), BF),
            jax.ShapeDtypeStruct((nz * 8, 8, 128), F32),
        ),
        in_specs=[ANY] * 6,
        out_specs=(ANY,) * 4,
        scratch_shapes=[
            sem((3,)), sem((3,)),
            sem((3, 2, nz)), sem((3, 2, nz)),
            sem((3, 2, nz)), sem((3, 2, nz)),
            sem((3, 2, nz, 2)), sem((3, 2, nz, 2)),
            sem((2, 2)), sem((2,)),
            sem((nz + 2,)), sem((nz + 2,)),
            sem((4,)),
        ],
        compiler_params=pltpu.CompilerParams(collective_id=0, has_side_effects=True),
        name="gather_weights",
    )(x_in, cot, qo, up, dn, norms)


def scatter_kernel(nz, rows, grads, ngrad, y_ext, g_ext, own_out, oth_out, n_out, y_back, g_back,
                   own, r_c, r_x, r_z, half, nbuf, n_c, n_x, n_z, nsum,
                   c_s, c_r, x_s, x_r, z_s, z_r, y_s, y_r, e_s, e_r, n_s, n_r, l_s):
    z, x, y, c = place()

    def send(src, dst, s_sem, r_sem, who):
        return pltpu.make_async_remote_copy(
            src_ref=src, dst_ref=dst, send_sem=s_sem, recv_sem=r_sem, device_id=who, device_id_type=MESH
        )

    def part(zz, xx):
        return pl.ds(pl.multiple_of((zz * 2 + xx) * rows, rows), rows)

    meet(nz, z, x, y, c)
    sent = []

    def go(copy):
        copy.start()
        sent.append(copy)

    order = [(m, g) for m in (2, 1, 0) for g in range(2)]
    loads = {}
    for m, g in order:
        go(send(grads.at[m, 2 * g + 1 - c], r_c.at[m, g], c_s.at[m, g], c_r.at[m, g], {"c": 1 - c}))
        loads[m, g] = pltpu.make_async_copy(grads.at[m, 2 * g + c], own.at[m, g], l_s.at[m, g])
        loads[m, g].start()

    for i, (src, dst) in enumerate(((y_ext, y_back), (g_ext, g_back))):
        dst = dst.at[pl.ds(pl.multiple_of(c * EXT_ROWS, EXT_ROWS), EXT_ROWS)]

        @pl.when(c == y)
        def _():
            send(src, dst, e_s.at[i], e_r.at[i, c], {"y": 1 - y}).start()

        @pl.when(c != y)
        def _():
            send(src, dst, e_s.at[i], e_r.at[i, c], {"y": 1 - y, "c": 1 - c}).start()

    nbuf[...] = ngrad[...]
    a = send(nbuf, n_c, n_s.at[0], n_r.at[0], {"c": 1 - c})
    go(a)
    a.wait_recv()
    nsum[0] = nbuf[...] + n_c[...]
    b = send(nsum.at[0], n_x, n_s.at[1], n_r.at[1], {"x": 1 - x})
    go(b)
    b.wait_recv()
    nsum[1] = nsum[0] + n_x[...]
    for dz in range(1, nz):
        go(send(nsum.at[1], n_z.at[dz], n_s.at[1 + dz], n_r.at[1 + dz], {"z": lax.rem(z + dz, nz)}))

    for m, g in order:
        loads[m, g].wait()
        send(r_c.at[m, g], r_c.at[m, g], c_r.at[m, g], c_r.at[m, g], {"c": 1 - c}).wait_recv()

        def add(zz, _):
            for xx in (1 - x, x):
                p = part(zz, xx)
                own[m, g, p] = (own[m, g, p].astype(F32) + r_c[m, g, p].astype(F32)).astype(BF)
            return 0

        lax.fori_loop(0, nz, add, 0)
        for zz in range(nz):
            go(send(own.at[m, g, part(zz, 1 - x)], r_x.at[m, g, zz], x_s.at[m, g, zz], x_r.at[m, g, zz], {"x": 1 - x}))
    for m, g in order:
        for dz in range(1, nz + 1):
            zz = lax.rem(z + dz, nz)
            send(r_x.at[m, g, zz], r_x.at[m, g, zz], x_r.at[m, g, zz], x_r.at[m, g, zz], {"x": 1 - x}).wait_recv()
            p = part(zz, x)
            own[m, g, p] = (own[m, g, p].astype(F32) + r_x[m, g, zz].astype(F32)).astype(BF)
            if dz < nz:
                go(send(own.at[m, g, p], r_z.at[m, g, dz], z_s.at[m, g, dz], z_r.at[m, g, dz], {"z": zz}))
    total = nsum[1]
    for dz in range(1, nz):
        send(n_z.at[dz], n_z.at[dz], n_r.at[1 + dz], n_r.at[1 + dz], {"x": 1 - x}).wait_recv()
        total = total + n_z[dz]
    n_out[y] = total
    nd = send(n_out.at[y], n_out.at[y], n_s.at[nz + 1], n_r.at[nz + 1], {"y": 1 - y})
    go(nd)
    for m, g in order:
        p = part(z, x)
        total = own[m, g, p].astype(F32)
        for dz in range(1, nz):
            send(r_z.at[m, g, dz], r_z.at[m, g, dz], z_r.at[m, g, dz], z_r.at[m, g, dz], {"x": 1 - x}).wait_recv()
            total = total + r_z[m, g, dz].astype(F32)

        @pl.when(y == g)
        def _():
            own_out[m] = total

        @pl.when(y != g)
        def _():
            half[m] = total.astype(BF)
            send(half.at[m], oth_out.at[m], y_s.at[m], y_r.at[m], {"y": 1 - y}).start()
    for m in range(3):
        send(half.at[m], oth_out.at[m], y_s.at[m], y_r.at[m], {"y": 1 - y}).wait()
    nd.wait_recv()

    @pl.when(y != c)
    def _():
        for i, dst in enumerate((y_back, g_back)):
            for j in range(2):
                ref = dst.at[pl.ds(j * EXT_ROWS, EXT_ROWS)]
                send(ref, ref, e_s.at[i], e_r.at[i, j], {"y": 1 - y}).wait_recv()

    for i in range(2):
        send(y_ext, y_ext, e_s.at[i], e_s.at[i], {"y": 1 - y}).wait_send()
    for cp in sent:
        cp.wait_send()


def scatter_all(nz, rows, grads, ngrad, y_ext, g_ext):
    sem = pltpu.SemaphoreType.DMA
    V = pl.BlockSpec(memory_space=pltpu.VMEM)
    return pl.pallas_call(
        partial(scatter_kernel, nz, rows),
        out_shape=(
            jax.ShapeDtypeStruct((3, rows, D), F32),
            jax.ShapeDtypeStruct((3, rows, D), BF),
            jax.ShapeDtypeStruct((2, 8, D), F32),
            jax.ShapeDtypeStruct((OWN_ROWS, D), BF),
            jax.ShapeDtypeStruct((OWN_ROWS, D), BF),
        ),
        in_specs=[ANY, V, ANY, ANY],
        out_specs=(V, ANY, V, ANY, ANY),
        scratch_shapes=[
            pltpu.VMEM((3, 2, D, D), BF),
            pltpu.VMEM((3, 2, D, D), BF),
            pltpu.VMEM((3, 2, nz, rows, D), BF),
            pltpu.VMEM((3, 2, nz, rows, D), BF),
            pltpu.VMEM((3, rows, D), BF),
            pltpu.VMEM((8, D), F32),
            pltpu.VMEM((8, D), F32),
            pltpu.VMEM((8, D), F32),
            pltpu.VMEM((nz, 8, D), F32),
            pltpu.VMEM((2, 8, D), F32),
            sem((3, 2)), sem((3, 2)),
            sem((3, 2, nz)), sem((3, 2, nz)),
            sem((3, 2, nz)), sem((3, 2, nz)),
            sem((3,)), sem((3,)),
            sem((2,)), sem((2, 2)),
            sem((nz + 2,)), sem((nz + 2,)),
            sem((3, 2)),
        ],
        compiler_params=pltpu.CompilerParams(
            collective_id=1, has_side_effects=True, vmem_limit_bytes=48 * 1024 * 1024
        ),
        name="scatter_grads",
    )(grads, ngrad, y_ext, g_ext)


CHUNK = 320
N_CHUNK = ROWS // CHUNK
WIDE = 3 * LENGTH
GW = 256


def dot_nn(a, b):
    return lax.dot_general(a, b, (((1,), (0,)), ((), ())), preferred_element_type=F32)


def dot_nt(a, b):
    return lax.dot_general(a, b, (((1,), (1,)), ((), ())), preferred_element_type=F32)


def dot_tn(a, b):
    return lax.dot_general(a, b, (((0,), (0,)), ((), ())), preferred_element_type=F32)


def lanes(shape):
    return lax.broadcasted_iota(jnp.int32, shape, len(shape) - 1)


def head_mask(h, shape):
    lane = lanes(shape)
    return jnp.logical_and(lane >= h * HEAD_DIM, lane < (h + 1) * HEAD_DIM)


def stack_heads(rows):
    zero = jnp.zeros_like(rows)
    return jnp.concatenate([jnp.where(head_mask(h, rows.shape), rows, zero) for h in range(3)], 0)


def merge_heads(stack):
    out = jnp.zeros((LENGTH, GW), stack.dtype)
    for h in range(3):
        out = jnp.where(head_mask(h, out.shape), stack[h * LENGTH : (h + 1) * LENGTH], out)
    return out


def chunk_rows(i, size=CHUNK):
    return pl.ds(pl.multiple_of(i * size, size), size)


def loop(count, body):
    def step(i, carry):
        body(i)
        return carry

    lax.fori_loop(0, count, step, 0)


def project(t, x, w, proj):
    def rows(i):
        r = chunk_rows(i)
        proj[t, r] = dot_nn(x[r], w[0, t]).astype(BF)

    loop(N_CHUNK, rows)


def out_columns(t, w, wo):
    low = lanes((D, 128)) < HEAD_DIM
    tiles = [w[0, t, :, GW * i + 128 : GW * i + 256].astype(F32) for i in range(3)]
    wo[t, :, :128] = jnp.where(low, pltpu.roll(tiles[0], 64, 1), tiles[1]).astype(BF)
    wo[t, :, 128:] = jnp.where(low, pltpu.roll(tiles[2], 64, 1), 0.0).astype(BF)


def attend(t, s, lens, proj, probs, hout):
    r = chunk_rows(s, LENGTH)
    query = stack_heads(proj[t, r, :GW] * jnp.asarray(0.125, BF))
    scores = dot_nt(proj[t, r, GW : 2 * GW], query)
    valid = lax.broadcasted_iota(jnp.int32, (LENGTH, 1), 0) < lens[s]
    scores = jnp.where(valid, scores, NEG)
    expo = jnp.exp(scores - jnp.max(scores, 0, keepdims=True))
    low = (expo * (1.0 / jnp.sum(expo, 0, keepdims=True))).astype(BF)
    probs[t, s, :, :WIDE] = low
    hout[t, r] = merge_heads(dot_tn(low, proj[t, r, 2 * GW :])).astype(BF)


def norm_rows(values):
    center = values - jnp.mean(values, -1, keepdims=True)
    factor = lax.rsqrt(jnp.mean(center * center, -1, keepdims=True) + EPS)
    return center * factor, factor


def norm_back(scaled, normed, factor):
    return factor * (
        scaled
        - jnp.mean(scaled, -1, keepdims=True)
        - normed * jnp.mean(scaled * normed, -1, keepdims=True)
    )


def first_norm(i, x, hout, wo, prm, mid, n1, s1, mid_low):
    r = chunk_rows(i)
    attn = dot_nt(hout[0, r], wo[0])
    for t in range(1, GROUPS):
        attn += dot_nt(hout[t, r], wo[t])
    normed, factor = norm_rows(x[r].astype(F32) + attn)
    n1[r] = normed
    s1[r] = jnp.broadcast_to(factor, (CHUNK, 128))
    value = normed * prm[0:1] + prm[2:3]
    mid[r] = value
    mid_low[r] = value.astype(BF)


def feed_up(t, i, mid_low, w, act, slope):
    r = chunk_rows(i)
    up = dot_nn(mid_low[r], w[1, t])
    cdf = 0.5 * (1.0 + lax.erf(up * 0.7071067811865476))
    act[t, r] = (up * cdf).astype(BF)
    slope[t, r] = (cdf + up * (0.3989422804014327 * jnp.exp(-0.5 * up * up))).astype(BF)


def second_norm(i, act, w, prm, mid, cot, mine, y_rows, d_ffn, ngrad):
    r = chunk_rows(i)
    ffn = dot_nt(act[0, r], w[2, 0])
    for t in range(1, GROUPS):
        ffn += dot_nt(act[t, r], w[2, t])
    normed, factor = norm_rows(ffn + mid[r])
    y_rows[r] = (normed * prm[1:2] + prm[3:4]).astype(BF)
    first = lax.broadcasted_iota(jnp.int32, (CHUNK, 1), 0) < LENGTH
    grad = cot[r].astype(F32) * jnp.where(first, mine[2 * i], mine[2 * i + 1])
    ngrad[1:2] += jnp.sum(grad * normed, 0, keepdims=True)
    ngrad[3:4] += jnp.sum(grad, 0, keepdims=True)
    back = norm_back(grad * prm[1:2], normed, factor)
    mid[r] = back
    d_ffn[r] = back.astype(BF)


def back_up(t, i, d_ffn, w, slope):
    r = chunk_rows(i)
    slope[t, r] = (dot_nn(d_ffn[r], w[2, t]) * slope[t, r].astype(F32)).astype(BF)


def back_first_norm(i, d_up, w, prm, mid, n1, s1, d_attn, ngrad):
    r = chunk_rows(i)
    grad = mid[r]
    for t in range(GROUPS):
        grad += dot_nt(d_up[t, r], w[1, t])
    ngrad[0:1] += jnp.sum(grad * n1[r], 0, keepdims=True)
    ngrad[2:3] += jnp.sum(grad, 0, keepdims=True)
    back = norm_back(grad * prm[0:1], n1[r], s1[r, 0:1])
    mid[r] = back
    d_attn[r] = back.astype(BF)


def back_heads(t, i, d_attn, wo, d_heads):
    r = chunk_rows(i)
    d_heads[t, r, :GW] = dot_nn(d_attn[r], wo[t]).astype(BF)


def back_attend(t, s, proj, probs, d_heads):
    r = chunk_rows(s, LENGTH)
    grad = stack_heads(d_heads[t, r, :GW])
    low = probs[t, s, :, :WIDE]
    p = low.astype(F32)
    d_probs = dot_nt(proj[t, r, 2 * GW :], grad)
    d_scores = (p * (d_probs - jnp.sum(d_probs * p, 0, keepdims=True))).astype(BF)
    query = stack_heads(proj[t, r, :GW] * jnp.asarray(0.125, BF))
    key = proj[t, r, GW : 2 * GW]
    d_query = merge_heads(dot_tn(d_scores, key)) * 0.125
    d_key = dot_nn(d_scores, query)
    d_value = dot_nn(low, grad)
    proj[t, r, :GW] = d_query.astype(BF)
    proj[t, r, GW : 2 * GW] = d_key.astype(BF)
    proj[t, r, 2 * GW :] = d_value.astype(BF)


def grad_qkv_out(t, x, d_proj, d_attn, hout, store):
    low = lanes((D, 128)) < HEAD_DIM
    outs = dot_tn(d_attn[...], hout[t])
    places = (pltpu.roll(outs[:, :128], 64, 1), outs[:, :128], pltpu.roll(outs[:, 128:], 64, 1))
    for i in range(3):
        part = dot_tn(x[...], d_proj[t, :, GW * i : GW * (i + 1)])
        store(GW * i, part[:, :128])
        store(GW * i + 128, jnp.where(low, part[:, 128:], places[i]))


def back_input(i, d_proj, w, mid, out):
    r = chunk_rows(i)
    grad = mid[r]
    for t in range(GROUPS):
        grad += dot_nt(d_proj[t, r], w[0, t])
    out(r, grad)


def layer_kernel(x_hbm, cot_hbm, lens, mine, prm, w_hbm, y_rows, g_rows, grads, ngrad,
                 w, x, cot, proj, probs, hout, wo, mid, n1, s1, mid_low, act, slope, d_ffn, slot, l_s, g_s):
    loads = [pltpu.make_async_copy(x_hbm, x, l_s.at[3]), pltpu.make_async_copy(cot_hbm, cot, l_s.at[4])]
    loads += [pltpu.make_async_copy(w_hbm.at[m], w.at[m], l_s.at[m]) for m in range(3)]
    for cp in loads:
        cp.start()
    ngrad[...] = jnp.zeros_like(ngrad)
    loads[0].wait()
    loads[2].wait()

    def one(t):
        project(t, x, w, proj)
        out_columns(t, w, wo)

    loop(GROUPS, one)
    loop(GROUPS * SLOTS, lambda i: attend(i // SLOTS, i % SLOTS, lens, proj, probs, hout))
    loop(N_CHUNK, lambda i: first_norm(i, x, hout, wo, prm, mid, n1, s1, mid_low))
    loads[3].wait()
    loop(GROUPS * N_CHUNK, lambda i: feed_up(i // N_CHUNK, i % N_CHUNK, mid_low, w, act, slope))
    loads[4].wait()
    loads[1].wait()
    loop(N_CHUNK, lambda i: second_norm(i, act, w, prm, mid, cot, mine, y_rows, d_ffn, ngrad))

    def put(m, t, j):
        return pltpu.make_async_copy(slot.at[j], grads.at[m, t], g_s.at[j])

    def grad_loop(m, a, b):
        def body(t):
            j = t % 2

            @pl.when(t >= 2)
            def _():
                put(m, t, j).wait()

            slot[j] = dot_tn(a[...], b[t]).astype(BF)
            put(m, t, j).start()

        loop(GROUPS, body)
        for j in range(2):
            put(m, 0, j).wait()

    grad_loop(2, d_ffn, act)
    loop(GROUPS * N_CHUNK, lambda i: back_up(i // N_CHUNK, i % N_CHUNK, d_ffn, w, slope))
    grad_loop(1, mid_low, slope)
    loop(N_CHUNK, lambda i: back_first_norm(i, slope, w, prm, mid, n1, s1, d_ffn, ngrad))
    loop(GROUPS * N_CHUNK, lambda i: back_heads(i // N_CHUNK, i % N_CHUNK, d_ffn, wo, act))
    loop(GROUPS * SLOTS, lambda i: back_attend(i // SLOTS, i % SLOTS, proj, probs, act))

    def last(t):
        j = t % 2

        @pl.when(t >= 2)
        def _():
            put(0, t, j).wait()

        def store(col, value):
            slot[j, :, pl.ds(col, 128)] = value.astype(BF)

        grad_qkv_out(t, x, proj, d_ffn, hout, store)
        put(0, t, j).start()

    loop(GROUPS, last)
    for j in range(2):
        put(0, 0, j).wait()

    def write(r, grad):
        g_rows[r] = grad

    loop(N_CHUNK, lambda i: back_input(i, proj, w, mid, write))


def run_layer(x, cot, lens, mine, prm, w):
    V = pl.BlockSpec(memory_space=pltpu.VMEM)
    S = pl.BlockSpec(memory_space=pltpu.SMEM)
    sem = pltpu.SemaphoreType.DMA
    return pl.pallas_call(
        layer_kernel,
        out_shape=(
            jax.ShapeDtypeStruct((ROWS, D), BF),
            jax.ShapeDtypeStruct((ROWS, D), F32),
            jax.ShapeDtypeStruct((3, GROUPS, D, D), BF),
            jax.ShapeDtypeStruct((8, D), F32),
        ),
        in_specs=[ANY, ANY, S, S, V, ANY],
        out_specs=(V, V, ANY, V),
        scratch_shapes=[
            pltpu.VMEM((3, GROUPS, D, D), BF),
            pltpu.VMEM((ROWS, D), BF),
            pltpu.VMEM((ROWS, D), BF),
            pltpu.VMEM((GROUPS, ROWS, D), BF),
            pltpu.VMEM((GROUPS, SLOTS, LENGTH, 512), BF),
            pltpu.VMEM((GROUPS, ROWS, GW), BF),
            pltpu.VMEM((GROUPS, D, GW), BF),
            pltpu.VMEM((ROWS, D), F32),
            pltpu.VMEM((ROWS, D), F32),
            pltpu.VMEM((ROWS, 128), F32),
            pltpu.VMEM((ROWS, D), BF),
            pltpu.VMEM((GROUPS, ROWS, D), BF),
            pltpu.VMEM((GROUPS, ROWS, D), BF),
            pltpu.VMEM((ROWS, D), BF),
            pltpu.VMEM((2, D, D), BF),
            sem((5,)),
            sem((2,)),
        ],
        compiler_params=pltpu.CompilerParams(vmem_limit_bytes=67043328),
        name="layer",
    )(x, cot, lens, mine, prm, w)


def split_local(nz, x_in, tags, lengths, w_qkv, w_out, w_up, w_down, norm_gain, norm_bias, cotangent):
    z, x, y, c = place()
    rows = w_up.shape[1]
    cols = norm_gain.shape[2]
    own = 2 * y + c
    qo = []
    for i in range(3):
        qo += [w_qkv[:, :, i], w_out[:, :, HEAD_DIM * i : HEAD_DIM * (i + 1)]]
    qo = jnp.concatenate(qo, -1)
    norms = jnp.concatenate([norm_gain.reshape(4, cols), norm_bias.reshape(4, cols)], 0)
    norms = jnp.pad(norms, ((0, 0), (0, 128 - cols)))
    w, x_ext, cot_ext, n_all = gather_all(nz, x_in, cotangent, qo, w_up, w_down, norms)
    params = n_all[:, :, :cols].transpose(1, 0, 2).reshape(2, 2, 2, D)
    params = lax.dynamic_index_in_dim(params, y, 1, keepdims=False).reshape(4, D)

    def slots(values):
        mine = lax.dynamic_slice_in_dim(values, own * OWN, OWN)
        lent = lax.dynamic_slice_in_dim(values, (2 - y) * OWN + c * EXTRA, EXTRA)
        return jnp.concatenate([mine, lent])

    kinds = slots(tags)
    lens = slots(lengths)
    mine = jnp.repeat(kinds == y, LENGTH)[:, None]
    rows_x = jnp.concatenate([x_in, x_ext])
    rows_cot = jnp.concatenate([cotangent, cot_ext])
    y_rows, g_rows, grads, ngrad = run_layer(
        rows_x, rows_cot, lens, (kinds == y).astype(F32), params, w
    )
    own_g, oth_g, n_sum, y_back, g_back = scatter_all(
        nz, rows, grads, ngrad, y_rows[OWN_ROWS:], g_rows[OWN_ROWS:].astype(BF)
    )
    y_out = jnp.where(mine[:OWN_ROWS], y_rows[:OWN_ROWS], y_back)
    x_grad = jnp.where(mine[:OWN_ROWS], g_rows[:OWN_ROWS], g_back.astype(F32))
    oth_g = oth_g.astype(F32)
    both = jnp.stack([jnp.where(y == 0, own_g, oth_g), jnp.where(y == 0, oth_g, own_g)])
    packed = both[:, 0].reshape(2, rows, 3, GW)
    g_out = packed[..., GW - HEAD_DIM :].reshape(w_out.shape)
    me = ((z * 2 + x) * 2 + y) * 2 + c
    n_mine = lax.dynamic_slice_in_dim(n_sum, me * cols, cols, 2)
    return (
        y_out,
        x_grad,
        packed[..., : GW - HEAD_DIM],
        g_out,
        both[:, 1],
        both[:, 2],
        n_mine[:, :2],
        n_mine[:, 2:4],
    )


def typed_map(operand, stacked, chain_kinds, pattern):

    def single(element):
        weight = lax.dynamic_index_in_dim(stacked, element[1], 0, keepdims=False)
        return jnp.einsum(pattern, element[0], weight, preferred_element_type=jnp.float32)

    return lax.map(single, (operand, chain_kinds))


def typed_grads(running, operand, partner, chain_kinds, pattern):

    def single(carry, element):
        product_term = jnp.einsum(
            pattern, element[0], element[1], preferred_element_type=jnp.float32
        )
        previous = lax.dynamic_index_in_dim(carry, element[2], 0, keepdims=False)
        return (
            lax.dynamic_update_index_in_dim(carry, previous + product_term, element[2], 0),
            None,
        )

    return lax.scan(single, running, (operand, partner, chain_kinds))[0]


def row_terms(operand, stacked, chain_kinds, pattern, row_count):
    result = typed_map(operand, stacked, chain_kinds, pattern)
    return result.reshape(row_count, result.shape[-1])


def old_norm_forward(values, gain_rows, shift_rows):
    center = values - jnp.mean(values, -1, keepdims=True)
    factor = lax.rsqrt(jnp.mean(center * center, -1, keepdims=True) + EPS)
    normed = center * factor
    return (normed * gain_rows + shift_rows, normed, factor)


def old_norm_backward(grad_out, normed, factor, gain_rows):
    scaled = grad_out * gain_rows
    mean_plain = jnp.mean(scaled, -1, keepdims=True)
    mean_normed = jnp.mean(scaled * normed, -1, keepdims=True)
    return factor * (scaled - mean_plain - normed * mean_normed)


def type_sums(onehot, values):
    return jnp.dot(onehot.T, values, precision=HIGH, preferred_element_type=jnp.float32)


def general_local(x_in, tags, lengths, w_qkv, w_out, w_up, w_down, norm_gain, norm_bias, cotangent):
    tp_count = lax.axis_size("tensor")
    tp_index = lax.axis_index("tensor")
    local_rows = CHAINS_PART * LENGTH
    batch_chains = tp_count * CHAINS_PART
    head_cols = w_qkv.shape[3]
    local_heads = head_cols // HEAD_DIM
    tag_grid = tags.reshape(tp_count, MICRO, CHAINS_PART)
    len_grid = lengths.reshape(tp_count, MICRO, CHAINS_PART)
    own_tags = lax.dynamic_index_in_dim(tag_grid, tp_index, 0, keepdims=False)
    gains, shifts = (
        lax.all_gather(norm_gain, ("dp", "tensor"), axis=2, tiled=True),
        lax.all_gather(norm_bias, ("dp", "tensor"), axis=2, tiled=True),
    )
    grad_full = (
        jnp.zeros((2, D, 3, head_cols), jnp.float32),
        jnp.zeros((2, D, head_cols), jnp.float32),
        jnp.zeros((2, D, w_up.shape[2]), jnp.float32),
        jnp.zeros((2, D, w_down.shape[2]), jnp.float32),
    )
    shards = (
        jnp.zeros(w_qkv.shape, jnp.float32),
        jnp.zeros(w_out.shape, jnp.float32),
        jnp.zeros(w_up.shape, jnp.float32),
        jnp.zeros(w_down.shape, jnp.float32),
    )
    gain_acc = jnp.zeros((2, 2, D), jnp.float32)
    shift_acc = jnp.zeros((2, 2, D), jnp.float32)
    outputs = []
    input_grads = []
    for micro_index in range(MICRO):
        held = (
            lax.all_gather(w_qkv, "dp", axis=1, tiled=True),
            lax.all_gather(w_out, "dp", axis=1, tiled=True),
            lax.all_gather(w_up, "dp", axis=1, tiled=True),
            lax.all_gather(w_down, "dp", axis=1, tiled=True),
        )
        qkv_w, out_w, up_w, down_w = held
        chain_kinds = tag_grid[:, micro_index].reshape(batch_chains)
        chain_lens = len_grid[:, micro_index].reshape(batch_chains)
        own_rows = x_in[micro_index * local_rows : (micro_index + 1) * local_rows]
        kinds_rows = jnp.repeat(own_tags[micro_index], LENGTH)
        heavy_rows = (kinds_rows == 0)[:, None]
        onehot = (kinds_rows[:, None] == jnp.arange(2)[None, :]).astype(jnp.float32)
        gain_mid = jnp.where(heavy_rows, gains[0, 0], gains[1, 0])
        shift_mid = jnp.where(heavy_rows, shifts[0, 0], shifts[1, 0])
        gain_end = jnp.where(heavy_rows, gains[0, 1], gains[1, 1])
        shift_end = jnp.where(heavy_rows, shifts[0, 1], shifts[1, 1])
        gathered = lax.all_gather(own_rows, "tensor", axis=0, tiled=True).reshape(
            batch_chains, LENGTH, D
        )
        projected = typed_map(gathered, qkv_w, chain_kinds, "ld,dkh->lkh").astype(jnp.bfloat16)
        query = projected[:, :, 0].reshape(batch_chains, LENGTH, local_heads, HEAD_DIM)
        keys_low = projected[:, :, 1].reshape(batch_chains, LENGTH, local_heads, HEAD_DIM)
        values_low = projected[:, :, 2].reshape(batch_chains, LENGTH, local_heads, HEAD_DIM)
        valid = (
            lax.broadcasted_iota(jnp.int32, (batch_chains, 1, 1, LENGTH), 3)
            < chain_lens[:, None, None, None]
        )
        scores = (
            jnp.einsum("cqhe,ckhe->chqk", query, keys_low, preferred_element_type=jnp.float32)
            * 0.125
        )
        scores = jnp.where(valid, scores, NEG)
        highest = jnp.max(scores, -1, keepdims=True)
        expo = jnp.exp(scores - highest)
        totals = jnp.sum(expo, -1, keepdims=True)
        probs = expo / totals
        log_total = highest + jnp.log(totals)
        heads_low = jnp.einsum(
            "chqk,ckhe->cqhe",
            probs.astype(jnp.bfloat16),
            values_low,
            preferred_element_type=jnp.float32,
        ).astype(jnp.bfloat16)
        heads_low = heads_low.reshape(batch_chains, LENGTH, head_cols)
        attn_sum = lax.psum_scatter(
            row_terms(
                heads_low, out_w, chain_kinds, "lh,dh->ld", lax.axis_size("tensor") * local_rows
            ).astype(jnp.bfloat16),
            "tensor",
            scatter_dimension=0,
            tiled=True,
        ).astype(jnp.float32)
        mid, normed_mid, factor_mid = old_norm_forward(
            own_rows.astype(jnp.float32) + attn_sum, gain_mid, shift_mid
        )
        mid_all = lax.all_gather(mid.astype(jnp.bfloat16), "tensor", axis=0, tiled=True).reshape(
            batch_chains, LENGTH, D
        )
        up_value = typed_map(mid_all, up_w, chain_kinds, "ld,df->lf")
        act_low = jax.nn.gelu(up_value, approximate=False).astype(jnp.bfloat16)
        ffn_sum = lax.psum_scatter(
            row_terms(
                act_low, down_w, chain_kinds, "lf,df->ld", lax.axis_size("tensor") * local_rows
            ).astype(jnp.bfloat16),
            "tensor",
            scatter_dimension=0,
            tiled=True,
        ).astype(jnp.float32)
        final, normed_end, factor_end = old_norm_forward(ffn_sum + mid, gain_end, shift_end)
        outputs.append(final.astype(jnp.bfloat16))
        base = grad_full
        grad_final = cotangent[micro_index * local_rows : (micro_index + 1) * local_rows].astype(
            jnp.float32
        )
        gain_acc = gain_acc.at[:, 1].add(type_sums(onehot, grad_final * normed_end))
        shift_acc = shift_acc.at[:, 1].add(type_sums(onehot, grad_final))
        grad_resid2 = old_norm_backward(grad_final, normed_end, factor_end, gain_end)
        grad_ffn = lax.all_gather(
            grad_resid2.astype(jnp.bfloat16), "tensor", axis=0, tiled=True
        ).reshape(batch_chains, LENGTH, D)
        grad_act = typed_map(grad_ffn, down_w, chain_kinds, "ld,df->lf")
        unused_value, gelu_back = jax.vjp(partial(jax.nn.gelu, approximate=False), up_value)
        grad_up = gelu_back(grad_act)[0].astype(jnp.bfloat16)
        down_acc = typed_grads(base[3], grad_ffn, act_low, chain_kinds, "ld,lf->df")
        up_acc = typed_grads(base[2], mid_all, grad_up, chain_kinds, "ld,lf->df")
        grad_mid = grad_resid2 + lax.psum_scatter(
            row_terms(
                grad_up, up_w, chain_kinds, "lf,df->ld", lax.axis_size("tensor") * local_rows
            ).astype(jnp.bfloat16),
            "tensor",
            scatter_dimension=0,
            tiled=True,
        ).astype(jnp.float32)
        gain_acc = gain_acc.at[:, 0].add(type_sums(onehot, grad_mid * normed_mid))
        shift_acc = shift_acc.at[:, 0].add(type_sums(onehot, grad_mid))
        grad_resid1 = old_norm_backward(grad_mid, normed_mid, factor_mid, gain_mid)
        grad_attn = lax.all_gather(
            grad_resid1.astype(jnp.bfloat16), "tensor", axis=0, tiled=True
        ).reshape(batch_chains, LENGTH, D)
        grad_heads = typed_map(grad_attn, out_w, chain_kinds, "ld,dh->lh").astype(jnp.bfloat16)
        out_acc = typed_grads(base[1], grad_attn, heads_low, chain_kinds, "ld,lh->dh")
        grad_heads = grad_heads.reshape(batch_chains, LENGTH, local_heads, HEAD_DIM)
        again = (
            jnp.einsum("cqhe,ckhe->chqk", query, keys_low, preferred_element_type=jnp.float32)
            * 0.125
        )
        probs_again = jnp.exp(jnp.where(valid, again, NEG) - log_total)
        grad_probs = jnp.einsum(
            "cqhe,ckhe->chqk", grad_heads, values_low, preferred_element_type=jnp.float32
        )
        inner = jnp.sum(grad_probs * probs_again, -1, keepdims=True)
        grad_scores = (probs_again * (grad_probs - inner)).astype(jnp.bfloat16)
        grad_query = (
            jnp.einsum("chqk,ckhe->cqhe", grad_scores, keys_low, preferred_element_type=jnp.float32)
            * 0.125
        ).astype(jnp.bfloat16)
        grad_keys = (
            jnp.einsum("chqk,cqhe->ckhe", grad_scores, query, preferred_element_type=jnp.float32)
            * 0.125
        ).astype(jnp.bfloat16)
        grad_values = jnp.einsum(
            "chqk,cqhe->ckhe",
            probs_again.astype(jnp.bfloat16),
            grad_heads,
            preferred_element_type=jnp.float32,
        ).astype(jnp.bfloat16)
        grad_proj = jnp.stack([grad_query, grad_keys, grad_values], 2).reshape(
            batch_chains, LENGTH, 3, head_cols
        )
        qkv_acc = typed_grads(base[0], gathered, grad_proj, chain_kinds, "ld,lkh->dkh")
        grad_input = grad_resid1 + lax.psum_scatter(
            row_terms(
                grad_proj, qkv_w, chain_kinds, "lkh,dkh->ld", lax.axis_size("tensor") * local_rows
            ).astype(jnp.bfloat16),
            "tensor",
            scatter_dimension=0,
            tiled=True,
        ).astype(jnp.float32)
        input_grads.append(grad_input)
        updated = (qkv_acc, out_acc, up_acc, down_acc)
        grad_full = updated
    shards = (
        lax.psum_scatter(grad_full[0], "dp", scatter_dimension=1, tiled=True),
        lax.psum_scatter(grad_full[1], "dp", scatter_dimension=1, tiled=True),
        lax.psum_scatter(grad_full[2], "dp", scatter_dimension=1, tiled=True),
        lax.psum_scatter(grad_full[3], "dp", scatter_dimension=1, tiled=True),
    )
    gain_grad, shift_grad = (
        lax.psum_scatter(gain_acc, ("dp", "tensor"), scatter_dimension=2, tiled=True),
        lax.psum_scatter(shift_acc, ("dp", "tensor"), scatter_dimension=2, tiled=True),
    )
    return (
        jnp.concatenate(outputs, 0),
        jnp.concatenate(input_grads, 0),
        shards[0],
        shards[1],
        shards[2],
        shards[3],
        gain_grad,
        shift_grad,
    )


def solution(mesh):
    placed = (
        P(("dp", "tensor"), None),
        P("dp"),
        P("dp"),
        P(None, "dp", None, "tensor"),
        P(None, "dp", "tensor"),
        P(None, "dp", "tensor"),
        P(None, "dp", "tensor"),
        P(None, None, ("dp", "tensor")),
        P(None, None, ("dp", "tensor")),
        P(("dp", "tensor"), None),
    )
    results = (
        P(("dp", "tensor"), None),
        P(("dp", "tensor"), None),
        P(None, "dp", None, "tensor"),
        P(None, "dp", "tensor"),
        P(None, "dp", "tensor"),
        P(None, "dp", "tensor"),
        P(None, None, ("dp", "tensor")),
        P(None, None, ("dp", "tensor")),
    )
    n_dp, n_tensor = mesh.shape["dp"], mesh.shape["tensor"]
    if n_tensor != GROUPS or n_dp % 2 or D % (16 * n_dp):
        return jax.shard_map(
            general_local, mesh=mesh, in_specs=placed, out_specs=results, check_vma=False
        )
    fine = Mesh(mesh.devices.reshape(n_dp // 2, 2, 2, 2), AXES)
    names = {"dp": ("z", "x"), "tensor": ("y", "c")}

    def refine(spec):
        parts = []
        for entry in spec:
            entry = (entry,) if isinstance(entry, str) else entry
            parts.append(entry and sum((names[a] for a in entry), ()))
        return P(*parts)

    return jax.shard_map(
        partial(split_local, n_dp // 2),
        mesh=fine,
        in_specs=tuple(refine(s) for s in placed),
        out_specs=tuple(refine(s) for s in results),
        check_vma=False,
    )
```

```python
from functools import partial

import jax
import jax.numpy as jnp
from jax import lax
from jax.experimental import pallas as pl
from jax.experimental.pallas import tpu as pltpu
from jax.sharding import Mesh
from jax.sharding import PartitionSpec as P

D = 768
HEADS = 12
HEAD_DIM = 64
MICRO = 4
CHAINS_PART = 1
LENGTH = 160
GROUPS = 4
OWN = 4
EXTRA = 2
SLOTS = OWN + EXTRA
EXT_ROWS = EXTRA * LENGTH
OWN_ROWS = OWN * LENGTH
ROWS = SLOTS * LENGTH

EPS = 1e-12
NEG = -1e30
HIGH = lax.Precision.HIGHEST
BF = jnp.bfloat16
F32 = jnp.float32
MESH = pl.DeviceIdType.MESH
ANY = pl.BlockSpec(memory_space=pl.ANY)
AXES = ("z", "x", "y", "c")


def place():
    return tuple(lax.axis_index(a) for a in AXES)


def meet(nz, z, x, y, c):
    barrier = pltpu.get_barrier_semaphore()
    friends = [{"c": 1 - c}, {"y": 1 - y}, {"y": 1 - y, "c": 1 - c}, {"x": 1 - x}]
    friends += [{"z": lax.rem(z + dz, nz)} for dz in range(1, nz)]
    for friend in friends:
        pl.semaphore_signal(barrier, inc=1, device_id=friend, device_id_type=MESH)
    pl.semaphore_wait(barrier, len(friends))


CHUNK = 320
SUB = 80
N_CHUNK = ROWS // CHUNK
WIDE = 3 * LENGTH
GW = 256
PAIR = 3


def dot_nn(a, b):
    return lax.dot_general(a, b, (((1,), (0,)), ((), ())), preferred_element_type=F32)


def dot_nt(a, b):
    return lax.dot_general(a, b, (((1,), (1,)), ((), ())), preferred_element_type=F32)


def dot_tn(a, b):
    return lax.dot_general(a, b, (((0,), (0,)), ((), ())), preferred_element_type=F32)


def lanes(shape):
    return lax.broadcasted_iota(jnp.int32, shape, len(shape) - 1)


def head_mask(h, shape):
    lane = lanes(shape)
    return jnp.logical_and(lane >= h * HEAD_DIM, lane < (h + 1) * HEAD_DIM)


def stack_heads(rows):
    zero = jnp.zeros_like(rows)
    return jnp.concatenate([jnp.where(head_mask(h, rows.shape), rows, zero) for h in range(3)], 0)


def merge_heads(stack):
    out = jnp.zeros((LENGTH, GW), stack.dtype)
    for h in range(3):
        out = jnp.where(head_mask(h, out.shape), stack[h * LENGTH : (h + 1) * LENGTH], out)
    return out


def chunk_rows(i, size=CHUNK):
    return pl.ds(pl.multiple_of(i * size, size), size)


def loop(count, body):
    def step(i, carry):
        body(i)
        return carry

    lax.fori_loop(0, count, step, 0)


def out_columns(t, w, wo):
    low = lanes((D, 128)) < HEAD_DIM
    tiles = [w[0, t, :, GW * i + 128 : GW * i + 256].astype(F32) for i in range(3)]
    wo[t, :, :128] = jnp.where(low, pltpu.roll(tiles[0], 64, 1), tiles[1]).astype(BF)
    wo[t, :, 128:] = jnp.where(low, pltpu.roll(tiles[2], 64, 1), 0.0).astype(BF)


def attend(t, chains, lens, proj, probs, hout):
    rows = [chunk_rows(s, LENGTH) for s in chains]
    parts = [(proj[t, r, :GW], proj[t, r, GW : 2 * GW], proj[t, r, 2 * GW :]) for r in rows]
    lows, outs = [], []
    for s, (query, key, value) in zip(chains, parts):
        scores = dot_nt(key, stack_heads(query * jnp.asarray(0.125, BF)))
        valid = lax.broadcasted_iota(jnp.int32, (LENGTH, 1), 0) < lens(s)
        scores = jnp.where(valid, scores, NEG)
        expo = jnp.exp(scores - jnp.max(scores, 0, keepdims=True))
        lows.append((expo * (1.0 / jnp.sum(expo, 0, keepdims=True))).astype(BF))
        outs.append(merge_heads(dot_tn(lows[-1], value)).astype(BF))
    for s, r, low, out in zip(chains, rows, lows, outs):
        probs[t, s, :, :WIDE] = low
        hout[t, r] = out


def norm_rows(values):
    center = values - jnp.mean(values, -1, keepdims=True)
    factor = lax.rsqrt(jnp.mean(center * center, -1, keepdims=True) + EPS)
    return center * factor, factor


def norm_back(scaled, normed, factor):
    return factor * (
        scaled
        - jnp.mean(scaled, -1, keepdims=True)
        - normed * jnp.mean(scaled * normed, -1, keepdims=True)
    )


def pieces(i, body):
    def step(k):
        body(pl.ds(pl.multiple_of(i * CHUNK + k * SUB, SUB), SUB), k)

    loop(CHUNK // SUB, step)


def first_norm(i, x, hout, wo, prm, mid, n1, s1, mid_low):
    r = chunk_rows(i)
    attn = dot_nt(hout[0, r], wo[0])
    for t in range(1, GROUPS):
        attn += dot_nt(hout[t, r], wo[t])
    mid[r] = attn

    def piece(p, k):
        normed, factor = norm_rows(x[p].astype(F32) + mid[p])
        n1[p] = normed.astype(BF)
        s1[p] = jnp.broadcast_to(factor, (SUB, 128))
        value = normed * prm[0:1] + prm[2:3]
        mid[p] = value
        mid_low[p] = value.astype(BF)

    pieces(i, piece)


def feed_up(t, i, mid_low, w, act, slope):
    r = chunk_rows(i)
    for k in range(0, D, GW):
        up = dot_nn(mid_low[r], w[1, t, :, k : k + GW])
        cdf = 0.5 * (1.0 + lax.erf(up * 0.7071067811865476))
        act[t, r, k : k + GW] = (up * cdf).astype(BF)
        bell = 0.3989422804014327 * jnp.exp(-0.5 * up * up)
        slope[t, r, k : k + GW] = (cdf + up * bell).astype(BF)


def second_norm(i, act, w, prm, mid, cot, mine, y_rows, d_ffn, ngrad):
    r = chunk_rows(i)
    ffn = dot_nt(act[0, r], w[2, 0])
    for t in range(1, GROUPS):
        ffn += dot_nt(act[t, r], w[2, t])
    mid[r] += ffn

    def piece(p, k):
        normed, factor = norm_rows(mid[p])
        y_rows[pl.ds(pl.multiple_of(k * SUB, SUB), SUB)] = (normed * prm[1:2] + prm[3:4]).astype(BF)
        grad = cot[p].astype(F32) * jnp.where(k < LENGTH // SUB, mine(2 * i), mine(2 * i + 1))
        ngrad[1:2] += jnp.sum(grad * normed, 0, keepdims=True)
        ngrad[3:4] += jnp.sum(grad, 0, keepdims=True)
        back = norm_back(grad * prm[1:2], normed, factor)
        mid[p] = back
        d_ffn[p] = back.astype(BF)

    pieces(i, piece)


def back_up(t, i, d_ffn, w, slope):
    r = chunk_rows(i)
    slope[t, r] = (dot_nn(d_ffn[r], w[2, t]) * slope[t, r].astype(F32)).astype(BF)


def back_first_norm(i, d_up, w, prm, mid, n1, s1, d_attn, ngrad):
    r = chunk_rows(i)
    grad = dot_nt(d_up[0, r], w[1, 0])
    for t in range(1, GROUPS):
        grad += dot_nt(d_up[t, r], w[1, t])
    mid[r] += grad

    def piece(p, k):
        grad = mid[p]
        normed = n1[p].astype(F32)
        ngrad[0:1] += jnp.sum(grad * normed, 0, keepdims=True)
        ngrad[2:3] += jnp.sum(grad, 0, keepdims=True)
        back = norm_back(grad * prm[0:1], normed, s1[p, 0:1])
        mid[p] = back
        d_attn[p] = back.astype(BF)

    pieces(i, piece)


def back_heads(t, i, d_attn, wo, d_heads):
    r = chunk_rows(i)
    d_heads[t, r, :GW] = dot_nn(d_attn[r], wo[t]).astype(BF)


def back_attend(t, chains, proj, probs, d_heads):
    rows = [chunk_rows(s, LENGTH) for s in chains]
    parts = [
        (proj[t, r, :GW], proj[t, r, GW : 2 * GW], proj[t, r, 2 * GW :], d_heads[t, r, :GW], probs[t, s, :, :WIDE])
        for s, r in zip(chains, rows)
    ]
    results = []
    for query, key, value, grad, low in parts:
        grad = stack_heads(grad)
        p = low.astype(F32)
        d_probs = dot_nt(value, grad)
        d_scores = (p * (d_probs - jnp.sum(d_probs * p, 0, keepdims=True))).astype(BF)
        d_query = merge_heads(dot_tn(d_scores, key)) * 0.125
        d_key = dot_nn(d_scores, stack_heads(query * jnp.asarray(0.125, BF)))
        results.append((d_query.astype(BF), d_key.astype(BF), dot_nn(low, grad).astype(BF)))
    for r, (d_query, d_key, d_value) in zip(rows, results):
        proj[t, r, :GW] = d_query
        proj[t, r, GW : 2 * GW] = d_key
        proj[t, r, 2 * GW :] = d_value


def grad_qkv_out(t, x, d_proj, d_attn, hout, store):
    low = lanes((D, 128)) < HEAD_DIM
    outs = dot_tn(d_attn[...], hout[t])
    places = (pltpu.roll(outs[:, :128], 64, 1), outs[:, :128], pltpu.roll(outs[:, 128:], 64, 1))
    for i in range(3):
        part = dot_tn(x[...], d_proj[t, :, GW * i : GW * (i + 1)])
        store(GW * i, part[:, :128])
        store(GW * i + 128, jnp.where(low, part[:, 128:], places[i]))


def back_input(i, d_proj, w, mid, out):
    r = chunk_rows(i)
    grad = mid[r]
    for t in range(GROUPS):
        grad += dot_nt(d_proj[t, r], w[0, t])
    out(r, grad)


def remote(src, dst, s_sem, r_sem, who):
    return pltpu.make_async_remote_copy(
        src_ref=src, dst_ref=dst, send_sem=s_sem, recv_sem=r_sem, device_id=who, device_id_type=MESH
    )


def arrived(ref, sem):
    remote(ref, ref, sem, sem, {"c": 1 - lax.axis_index("c")}).wait_recv()


def has_left(ref, sem):
    remote(ref, ref, sem, sem, {"c": 1 - lax.axis_index("c")}).wait_send()


def step_kernel(nz, rows,
                tags, lens, x_in, cot, qo, up, dn, gain, bias,
                y_own, g_own, own_out, oth_out, n_out, y_back, g_back, r_c,
                w, x, proj, probs, hout, wo, mid, n1, s1, mid_low, act, slope, d_ffn, gown, r_x,
                n_all, prm, ngrad, n_c, n_x, n_z,
                load_s, io_s, stage_s,
                ys_s, ys_r, zs_s, zs_r, xs_s, xs_r, cs_s, cs_r, ex_s, ex_r, na_s, na_r,
                c_s, c_r, x_s, x_r, z_s, z_r, y_s, y_r, e_s, e_r, ng_s, ng_r, free_s):
    z, xc, y, c = place()
    core, across, other_x = {"c": 1 - c}, {"y": 1 - y}, {"x": 1 - xc}
    diagonal = {"y": 1 - y, "c": 1 - c}
    mats = (qo, up, dn)
    lender = y != c
    home = (2 * y + c) * OWN
    away = (2 - y) * OWN + c * EXTRA

    def z_of(dz):
        return lax.rem(z + dz, nz)

    def chain(s):
        return jnp.where(s < OWN, home + s, away + s - OWN)

    def length_of(s):
        return lens[chain(s)]

    def mine(s):
        return jnp.where(tags[chain(s)] == y, 1.0, 0.0)

    def part(zz, xx):
        return pl.ds(pl.multiple_of((zz * 2 + xx) * rows, rows), rows)

    def group(g):
        return 2 * lax.rem(y + g, 2) + c

    def block(m, g, zz, xx):
        return w.at[m, group(g), part(zz, xx)]

    loads = [pltpu.make_async_copy(mats[m].at[y], block(m, 0, z, xc), load_s.at[m]) for m in range(3)]
    loads += [
        pltpu.make_async_copy(x_in, x.at[pl.ds(0, OWN_ROWS)], load_s.at[3]),
        pltpu.make_async_copy(cot, d_ffn.at[pl.ds(0, OWN_ROWS)], load_s.at[4]),
    ]
    for cp in loads:
        cp.start()
    me = ((z * 2 + xc) * 2 + y) * 2 + c
    cols = gain.shape[2]
    n_all[me] = jnp.zeros((8, 128), F32)
    for i in range(2):
        n_all[me, 2 * i : 2 * i + 2, :cols] = gain[i]
        n_all[me, 4 + 2 * i : 6 + 2 * i, :cols] = bias[i]
    ngrad[...] = jnp.zeros_like(ngrad)
    meet(nz, z, xc, y, c)

    def lend(arr, out, i, act_on):
        @pl.when(lender)
        def _():
            for j, (who, p) in enumerate(((across, c), (diagonal, 1 - c))):
                src = arr.at[pl.ds(pl.multiple_of(p * EXT_ROWS, EXT_ROWS), EXT_ROWS)]
                act_on(remote(src, out.at[pl.ds(OWN_ROWS, EXT_ROWS)], ex_s.at[i, j], ex_r.at[i], who))

    for m in range(3):
        remote(mats[m].at[1 - y], w.at[m, group(0), part(z, xc)], ys_s.at[m], ys_r.at[m], across).start()
    lend(x_in, x, 0, lambda cp: cp.start())
    lend(cot, d_ffn, 1, lambda cp: cp.start())

    def spread_z(m, g):
        ref = block(m, g, z, xc)
        for dz in range(1, nz):
            remote(ref, ref, zs_s.at[m, g, dz], zs_r.at[m, g, dz], {"z": z_of(dz)}).start()

    def spread_xc(m, g):
        ref = block(m, g, z, xc)
        remote(ref, ref, xs_s.at[m, g, 0], xs_r.at[m, g, 0], other_x).start()
        remote(ref, ref, cs_s.at[m, g, 0, 0], cs_r.at[m, g, 0, 0], core).start()

    def z_event(m, g, dz):
        ref = block(m, g, lax.rem(z + nz - dz, nz), xc)
        arrived(ref, zs_r.at[m, g, dz])
        remote(ref, ref, xs_s.at[m, g, dz], xs_r.at[m, g, dz], other_x).start()
        remote(ref, ref, cs_s.at[m, g, dz, 0], cs_r.at[m, g, dz, 0], core).start()

    def x_event(m, g, dz):
        ref = block(m, g, lax.rem(z + nz - dz, nz), 1 - xc)
        arrived(ref, xs_r.at[m, g, dz])
        remote(ref, ref, cs_s.at[m, g, dz, 1], cs_r.at[m, g, dz, 1], core).start()

    per_g = 2 * nz - 1
    n_events = 2 * per_g

    def gather_event(m, e):
        g = e // per_g
        r = e % per_g

        @pl.when(jnp.logical_and(r < nz - 1, e < n_events))
        def _():
            z_event(m, g, r + 1)

        @pl.when(jnp.logical_and(r >= nz - 1, e < n_events))
        def _():
            x_event(m, g, r - (nz - 1))

    def gathered(m):
        def body(i):
            q = i % 2
            dz = (i // 2) % nz
            g = i // (2 * nz)
            t = 2 * lax.rem(y + g, 2) + 1 - c
            ref = w.at[m, t, part(lax.rem(z + nz - dz, nz), lax.rem(xc + q, 2))]
            arrived(ref, cs_r.at[m, g, dz, q])

        loop(4 * nz, body)

    def norm_hop(i, act_on):
        if i == 0:
            act_on(remote(n_all.at[me], n_all.at[me], na_s.at[0], na_r.at[0], core))
        elif i == 1:
            ref = n_all.at[pl.ds(me - c, 2)]
            act_on(remote(ref, ref, na_s.at[1], na_r.at[1], across))
        elif i == 2:
            ref = n_all.at[pl.ds(me - c - 2 * y, 4)]
            act_on(remote(ref, ref, na_s.at[2], na_r.at[2], other_x))
        else:
            ref = n_all.at[pl.ds(8 * z, 8)]
            for dz in range(1, nz):
                act_on(remote(ref, ref, na_s.at[2 + dz], na_r.at[2 + dz], {"z": z_of(dz)}))

    def start(cp):
        cp.start()

    def recv(cp):
        cp.wait_recv()

    for m in range(3):
        loads[m].wait()
    norm_hop(0, start)
    spread_z(0, 0)
    spread_xc(0, 0)
    for m in range(3):
        arrived(block(m, 1, z, xc), ys_r.at[m])
        spread_z(m, 1)
        if m == 0:
            spread_xc(0, 1)
            norm_hop(0, recv)
            norm_hop(1, start)
        if m < 2:
            spread_z(m + 1, 0)
    norm_hop(1, recv)
    norm_hop(2, start)
    loop(per_g, lambda e: gather_event(0, e))
    norm_hop(2, recv)
    norm_hop(3, start)
    loop(per_g, lambda e: gather_event(0, per_g + e))
    for g in range(2):
        spread_xc(1, g)
    gathered(0)
    loads[3].wait()
    arrived(x.at[pl.ds(OWN_ROWS, EXT_ROWS)], ex_r.at[0])

    def projection(i):
        t, k = i // N_CHUNK, i % N_CHUNK
        r = chunk_rows(k)
        proj[t, r] = dot_nn(x[r], w[0, t]).astype(BF)

        @pl.when(k == N_CHUNK - 1)
        def _():
            out_columns(t, w, wo)
            gather_event(1, t)

    loop(GROUPS * N_CHUNK, projection)
    norm_hop(3, recv)
    lane = lanes((2, D))
    gains, shifts = jnp.zeros((2, D), F32), jnp.zeros((2, D), F32)
    for d in range(8 * nz):
        inside = jnp.logical_and(lane >= d * cols, lane < (d + 1) * cols)
        for name in range(2):
            piece = n_all[d, pl.ds(4 * name + 2 * y, 2), :]
            piece = jnp.concatenate([piece, jnp.zeros((2, D - 128), F32)], 1)
            piece = jnp.where(inside, pltpu.roll(piece, d * cols, 1) if d else piece, 0.0)
            if name == 0:
                gains += piece
            else:
                shifts += piece
    prm[0:2] = gains
    prm[2:4] = shifts
    per = SLOTS // PAIR

    def attention(i):
        attend(i // per, [(i % per) * PAIR + k for k in range(PAIR)], length_of, proj, probs, hout)
        gather_event(1, GROUPS + i)

    loop(GROUPS * per, attention)

    def norm_one(i):
        first_norm(i, x, hout, wo, prm, mid, n1, s1, mid_low)
        gather_event(1, GROUPS + GROUPS * per + i)

    loop(N_CHUNK, norm_one)
    done = GROUPS + GROUPS * per + N_CHUNK
    if done < n_events:
        loop(n_events - done, lambda e: gather_event(1, done + e))
    for g in range(2):
        spread_xc(2, g)
    gathered(1)

    def feed(i):
        feed_up(i // N_CHUNK, i % N_CHUNK, mid_low, w, act, slope)
        gather_event(2, i)

    loop(GROUPS * N_CHUNK, feed)
    done = GROUPS * N_CHUNK
    if done < n_events:
        loop(n_events - done, lambda e: gather_event(2, done + e))
    gathered(2)
    loads[4].wait()
    arrived(d_ffn.at[pl.ds(OWN_ROWS, EXT_ROWS)], ex_r.at[1])

    def y_stage(i):
        return gown.at[1, i // 2, pl.ds((i % 2) * CHUNK, CHUNK)]

    def give_back(src, dst, i, act_on):
        dst = dst.at[pl.ds(pl.multiple_of(c * EXT_ROWS, EXT_ROWS), EXT_ROWS)]

        @pl.when(c == y)
        def _():
            act_on(remote(src, dst, e_s.at[i], e_r.at[i, c], across))

        @pl.when(c != y)
        def _():
            act_on(remote(src, dst, e_s.at[i], e_r.at[i, c], diagonal))

    def y_copy(i):
        return pltpu.make_async_copy(y_stage(i), y_own.at[pl.ds(i * CHUNK, CHUNK)], io_s.at[i])

    for i in range(N_CHUNK):
        second_norm(i, act, w, prm, mid, d_ffn, mine, y_stage(i), d_ffn, ngrad)
    for i in range(2):
        y_copy(i).start()
    give_back(y_stage(2), y_back, 0, start)

    def spare(m, g):
        return gown.at[0, g] if m else act.at[2 + g, pl.ds(0, D)]

    def r_z(m, g, dz):
        return w.at[2, m, pl.ds(pl.multiple_of((g * nz + dz) * rows, rows), rows)]

    def core_send(m, g):
        return remote(spare(m, g), r_c.at[m, g], c_s.at[m, g], c_r.at[m, g], core)

    def fetch(m, g):
        return pltpu.make_async_copy(r_c.at[m, g], act.at[g, pl.ds(0, D)], stage_s.at[g])

    def core_fetch(m, g):
        arrived(r_c.at[m, g], c_r.at[m, g])
        fetch(m, g).start()

    def core_add(m, g):
        fetch(m, g).wait()

        def body(i):
            dz = i // 2 + 1
            zz = z_of(dz)
            xx = lax.rem(xc + 1 + i, 2)
            p = part(zz, xx)
            gown[m, g, p] = (gown[m, g, p].astype(F32) + act[g, p].astype(F32)).astype(BF)

        loop(2 * nz, body)
        for dz in range(1, nz + 1):
            zz = z_of(dz)
            remote(gown.at[m, g, part(zz, 1 - xc)], r_x.at[m, g, zz], x_s.at[m, g, zz], x_r.at[m, g, zz], other_x).start()

    def sum_event(q):
        m = 2 - q // (2 * nz)
        g = (q // nz) % 2
        dz = q % nz + 1
        zz = z_of(dz)
        arrived(r_x.at[m, g, zz], x_r.at[m, g, zz])
        p = part(zz, xc)
        gown[m, g, p] = (gown[m, g, p].astype(F32) + r_x[m, g, zz].astype(F32)).astype(BF)

        @pl.when(dz < nz)
        def _():
            remote(gown.at[m, g, p], r_z(m, g, dz), z_s.at[m, g, dz], z_r.at[m, g, dz], {"z": zz}).start()

    def own_copy(m):
        return pltpu.make_async_copy(mid.at[pl.ds(OWN_ROWS + m * rows, rows)], own_out.at[m], io_s.at[3 + m])

    def last_send(m):
        return remote(mid_low.at[pl.ds(EXT_ROWS + m * rows, rows)], oth_out.at[m], y_s.at[m], y_r.at[m], across)

    def finish(m, g):
        total = gown[m, g, part(z, xc)].astype(F32)
        for dz in range(1, nz):
            arrived(r_z(m, g, dz), z_r.at[m, g, dz])
            total += r_z(m, g, dz)[...].astype(F32)

        @pl.when(y == g)
        def _():
            mid[OWN_ROWS + m * rows : OWN_ROWS + (m + 1) * rows] = total
            own_copy(m).start()

        @pl.when(y != g)
        def _():
            mid_low[EXT_ROWS + m * rows : EXT_ROWS + (m + 1) * rows] = total.astype(BF)
            last_send(m).start()

    def products(a, b, t, dst):
        for k in range(0, D, GW):
            dst[:, k : k + GW] = dot_tn(a[...], b[t, :, k : k + GW]).astype(BF)

    def slope_grads(m, a, b):
        for g in range(2):
            products(a, b, 2 * g + 1 - c, spare(m, g))
            core_send(m, g).start()
        for g in range(2):
            products(a, b, 2 * g + c, gown.at[m, g])

    slope_grads(2, d_ffn, act)

    def gather_sent(i):
        m, g = i // 2, i % 2
        ref = w.at[0, 0, pl.ds(0, rows)]
        for dz in range(nz):
            if dz:
                has_left(ref, zs_s.at[m, g, dz])
            has_left(ref, xs_s.at[m, g, dz])
            for q in range(2):
                has_left(ref, cs_s.at[m, g, dz, q])

    def up_back(i):
        back_up(i // N_CHUNK, i % N_CHUNK, d_ffn, w, slope)

    loop(N_CHUNK, up_back)
    for g in range(2):
        core_fetch(2, g)
    loop(N_CHUNK, lambda i: up_back(N_CHUNK + i))
    for g in range(2):
        core_add(2, g)
        core_send(2, g).wait_send()
    loop(2 * N_CHUNK, lambda i: up_back(2 * N_CHUNK + i))
    loop(6, gather_sent)
    for dz in range(1, nz):
        pl.semaphore_signal(free_s, inc=1, device_id={"z": z_of(dz)}, device_id_type=MESH)
    for i in range(2):
        y_copy(i).wait()
    has_left(y_stage(2), e_s.at[0])
    slope_grads(1, mid_low, slope)
    for g in range(2):
        core_fetch(1, g)
    pl.semaphore_wait(free_s, nz - 1)
    sum_event(0)
    sum_event(1)
    back_first_norm(0, slope, w, prm, mid, n1, s1, d_ffn, ngrad)
    for g in range(2):
        core_add(1, g)
        core_send(1, g).wait_send()
    sum_event(2)
    back_first_norm(1, slope, w, prm, mid, n1, s1, d_ffn, ngrad)
    sum_event(3)
    back_first_norm(2, slope, w, prm, mid, n1, s1, d_ffn, ngrad)

    def send_norms(i, act_on):
        if i == 0:
            act_on(remote(ngrad, n_c, ng_s.at[0], ng_r.at[0], core))
        elif i == 1:
            act_on(remote(n_c, n_x, ng_s.at[1], ng_r.at[1], other_x))
        elif i == 2:
            for dz in range(1, nz):
                act_on(remote(n_x, n_z.at[dz], ng_s.at[1 + dz], ng_r.at[1 + dz], {"z": z_of(dz)}))
        else:
            act_on(remote(n_out.at[y], n_out.at[y], ng_s.at[nz + 1], ng_r.at[nz + 1], across))

    send_norms(0, start)
    loop(GROUPS * N_CHUNK, lambda i: back_heads(i // N_CHUNK, i % N_CHUNK, d_ffn, wo, slope))
    sum_event(4)
    send_norms(0, recv)
    send_norms(0, lambda cp: cp.wait_send())
    n_c[...] += ngrad[...]
    send_norms(1, start)

    def attention_back(i):
        back_attend(i // per, [(i % per) * PAIR + k for k in range(PAIR)], proj, probs, slope)

        @pl.when(i % 2 == 1)
        def _():
            sum_event(5 + i // 2)

    loop(GROUPS * per, attention_back)
    send_norms(1, recv)
    send_norms(1, lambda cp: cp.wait_send())
    n_x[...] += n_c[...]
    send_norms(2, start)
    seen = 5 + GROUPS * per // 2

    def qkv_grads(t, dst):
        def store(col, value):
            dst[:, col : col + 128] = value.astype(BF)

        grad_qkv_out(t, x, proj, d_ffn, hout, store)

    for g in range(2):
        qkv_grads(2 * g + 1 - c, spare(0, g))
        core_send(0, g).start()
        sum_event(seen + g)
    seen += 2
    for g in range(2):
        qkv_grads(2 * g + c, gown.at[0, g])
    for g in range(2):
        core_fetch(0, g)
        core_add(0, g)
    total = n_x[...]
    for dz in range(1, nz):
        arrived(n_z.at[dz], ng_r.at[1 + dz])
        total += n_z[dz]
    n_out[y] = total
    send_norms(3, start)

    def g_stage(r, grad):
        mid_low[:EXT_ROWS] = grad.astype(BF)

    def g_keep(r, grad):
        mid[r] = grad

    back_input(2, proj, w, mid, g_stage)
    give_back(mid_low.at[pl.ds(0, EXT_ROWS)], g_back, 1, start)
    sum_event(seen)
    back_input(0, proj, w, mid, g_keep)
    sum_event(seen + 1)
    back_input(1, proj, w, mid, g_keep)
    g_copy = pltpu.make_async_copy(mid.at[pl.ds(0, OWN_ROWS)], g_own, io_s.at[2])
    g_copy.start()
    seen += 2
    total_events = 6 * nz
    after = 4 * nz
    if seen < after:
        loop(after - seen, lambda q: sum_event(seen + q))
        seen = after
    for g in range(2):
        finish(2, g)
    loop(nz, lambda q: sum_event(after + q))
    for g in range(2):
        finish(1, g)
    loop(nz, lambda q: sum_event(after + nz + q))
    for g in range(2):
        finish(0, g)

    def sums_sent(i):
        m, g = i // 2, i % 2
        for dz in range(nz):
            if dz:
                has_left(r_x.at[0, 0, 0], z_s.at[m, g, dz])
            has_left(r_x.at[0, 0, 0], x_s.at[m, g, dz])

    loop(6, sums_sent)
    for g in range(2):
        core_send(0, g).wait_send()
    for m in range(3):
        has_left(mats[m].at[0], ys_s.at[m])
        own_copy(m).wait()
        last_send(m).wait()
    lend(x_in, x, 0, lambda cp: cp.wait_send())
    lend(cot, d_ffn, 1, lambda cp: cp.wait_send())
    for i in range(4):
        norm_hop(i, lambda cp: cp.wait_send())
    send_norms(2, lambda cp: cp.wait_send())
    send_norms(3, lambda cp: cp.wait())
    g_copy.wait()
    has_left(mid_low.at[pl.ds(0, EXT_ROWS)], e_s.at[1])

    @pl.when(lender)
    def _():
        for i, dst in enumerate((y_back, g_back)):
            for j in range(2):
                arrived(dst.at[pl.ds(j * EXT_ROWS, EXT_ROWS)], e_r.at[i, j])


def run_step(nz, tags, lens, x_in, cot, qo, up, dn, gain, bias):
    rows = up.shape[1]
    V = pl.BlockSpec(memory_space=pltpu.VMEM)
    S = pl.BlockSpec(memory_space=pltpu.SMEM)
    sem = pltpu.SemaphoreType.DMA
    out = jax.ShapeDtypeStruct
    return pl.pallas_call(
        partial(step_kernel, nz, rows),
        out_shape=(
            out((OWN_ROWS, D), BF),
            out((OWN_ROWS, D), F32),
            out((3, rows, D), F32),
            out((3, rows, D), BF),
            out((2, 8, D), F32),
            out((OWN_ROWS, D), BF),
            out((OWN_ROWS, D), BF),
            out((3, 2, D, D), BF),
        ),
        in_specs=[S, S, ANY, ANY, ANY, ANY, ANY, V, V],
        out_specs=(ANY, ANY, ANY, ANY, V, ANY, ANY, ANY),
        scratch_shapes=[
            pltpu.VMEM((3, GROUPS, D, D), BF),
            pltpu.VMEM((ROWS, D), BF),
            pltpu.VMEM((GROUPS, ROWS, D), BF),
            pltpu.VMEM((GROUPS, SLOTS, LENGTH, 512), BF),
            pltpu.VMEM((GROUPS, ROWS, GW), BF),
            pltpu.VMEM((GROUPS, D, GW), BF),
            pltpu.VMEM((ROWS, D), F32),
            pltpu.VMEM((ROWS, D), BF),
            pltpu.VMEM((ROWS, 128), F32),
            pltpu.VMEM((ROWS, D), BF),
            pltpu.VMEM((GROUPS, ROWS, D), BF),
            pltpu.VMEM((GROUPS, ROWS, D), BF),
            pltpu.VMEM((ROWS, D), BF),
            pltpu.VMEM((3, 2, D, D), BF),
            pltpu.VMEM((3, 2, nz, rows, D), BF),
            pltpu.VMEM((8 * nz, 8, 128), F32),
            pltpu.VMEM((8, D), F32),
            pltpu.VMEM((8, D), F32),
            pltpu.VMEM((8, D), F32),
            pltpu.VMEM((8, D), F32),
            pltpu.VMEM((nz, 8, D), F32),
            sem((5,)), sem((6,)), sem((2,)),
            sem((3,)), sem((3,)),
            sem((3, 2, nz)), sem((3, 2, nz)),
            sem((3, 2, nz)), sem((3, 2, nz)),
            sem((3, 2, nz, 2)), sem((3, 2, nz, 2)),
            sem((2, 2)), sem((2,)),
            sem((nz + 2,)), sem((nz + 2,)),
            sem((3, 2)), sem((3, 2)),
            sem((3, 2, nz)), sem((3, 2, nz)),
            sem((3, 2, nz)), sem((3, 2, nz)),
            sem((3,)), sem((3,)),
            sem((2,)), sem((2, 2)),
            sem((nz + 2,)), sem((nz + 2,)),
            pltpu.SemaphoreType.REGULAR,
        ],
        compiler_params=pltpu.CompilerParams(
            collective_id=0, has_side_effects=True, vmem_limit_bytes=67043328
        ),
        name="layer_step",
    )(tags, lens, x_in, cot, qo, up, dn, gain, bias)


def split_local(nz, x_in, tags, lengths, w_qkv, w_out, w_up, w_down, norm_gain, norm_bias, cotangent):
    z, x, y, c = place()
    rows = w_up.shape[1]
    cols = norm_gain.shape[2]
    qo = []
    for i in range(3):
        qo += [w_qkv[:, :, i], w_out[:, :, HEAD_DIM * i : HEAD_DIM * (i + 1)]]
    qo = jnp.concatenate(qo, -1)
    y_own, g_own, own_g, oth_g, n_sum, y_back, g_back, _ = run_step(
        nz, tags, lengths, x_in, cotangent, qo, w_up, w_down, norm_gain, norm_bias
    )
    kinds = lax.dynamic_slice_in_dim(tags, (2 * y + c) * OWN, OWN)
    mine = jnp.repeat(kinds == y, LENGTH)[:, None]
    y_out = jnp.where(mine, y_own, y_back)
    x_grad = jnp.where(mine, g_own, g_back.astype(F32))
    oth_g = oth_g.astype(F32)
    both = jnp.stack([jnp.where(y == 0, own_g, oth_g), jnp.where(y == 0, oth_g, own_g)])
    packed = both[:, 0].reshape(2, rows, 3, GW)
    me = ((z * 2 + x) * 2 + y) * 2 + c
    n_mine = lax.dynamic_slice_in_dim(n_sum, me * cols, cols, 2)
    return (
        y_out,
        x_grad,
        packed[..., : GW - HEAD_DIM],
        packed[..., GW - HEAD_DIM :].reshape(w_out.shape),
        both[:, 1],
        both[:, 2],
        n_mine[:, :2],
        n_mine[:, 2:4],
    )


def typed_map(operand, stacked, chain_kinds, pattern):

    def single(element):
        weight = lax.dynamic_index_in_dim(stacked, element[1], 0, keepdims=False)
        return jnp.einsum(pattern, element[0], weight, preferred_element_type=jnp.float32)

    return lax.map(single, (operand, chain_kinds))


def typed_grads(running, operand, partner, chain_kinds, pattern):

    def single(carry, element):
        product_term = jnp.einsum(
            pattern, element[0], element[1], preferred_element_type=jnp.float32
        )
        previous = lax.dynamic_index_in_dim(carry, element[2], 0, keepdims=False)
        return (
            lax.dynamic_update_index_in_dim(carry, previous + product_term, element[2], 0),
            None,
        )

    return lax.scan(single, running, (operand, partner, chain_kinds))[0]


def row_terms(operand, stacked, chain_kinds, pattern, row_count):
    result = typed_map(operand, stacked, chain_kinds, pattern)
    return result.reshape(row_count, result.shape[-1])


def old_norm_forward(values, gain_rows, shift_rows):
    center = values - jnp.mean(values, -1, keepdims=True)
    factor = lax.rsqrt(jnp.mean(center * center, -1, keepdims=True) + EPS)
    normed = center * factor
    return (normed * gain_rows + shift_rows, normed, factor)


def old_norm_backward(grad_out, normed, factor, gain_rows):
    scaled = grad_out * gain_rows
    mean_plain = jnp.mean(scaled, -1, keepdims=True)
    mean_normed = jnp.mean(scaled * normed, -1, keepdims=True)
    return factor * (scaled - mean_plain - normed * mean_normed)


def type_sums(onehot, values):
    return jnp.dot(onehot.T, values, precision=HIGH, preferred_element_type=jnp.float32)


def general_local(x_in, tags, lengths, w_qkv, w_out, w_up, w_down, norm_gain, norm_bias, cotangent):
    tp_count = lax.axis_size("tensor")
    tp_index = lax.axis_index("tensor")
    local_rows = CHAINS_PART * LENGTH
    batch_chains = tp_count * CHAINS_PART
    head_cols = w_qkv.shape[3]
    local_heads = head_cols // HEAD_DIM
    tag_grid = tags.reshape(tp_count, MICRO, CHAINS_PART)
    len_grid = lengths.reshape(tp_count, MICRO, CHAINS_PART)
    own_tags = lax.dynamic_index_in_dim(tag_grid, tp_index, 0, keepdims=False)
    gains, shifts = (
        lax.all_gather(norm_gain, ("dp", "tensor"), axis=2, tiled=True),
        lax.all_gather(norm_bias, ("dp", "tensor"), axis=2, tiled=True),
    )
    grad_full = (
        jnp.zeros((2, D, 3, head_cols), jnp.float32),
        jnp.zeros((2, D, head_cols), jnp.float32),
        jnp.zeros((2, D, w_up.shape[2]), jnp.float32),
        jnp.zeros((2, D, w_down.shape[2]), jnp.float32),
    )
    shards = (
        jnp.zeros(w_qkv.shape, jnp.float32),
        jnp.zeros(w_out.shape, jnp.float32),
        jnp.zeros(w_up.shape, jnp.float32),
        jnp.zeros(w_down.shape, jnp.float32),
    )
    gain_acc = jnp.zeros((2, 2, D), jnp.float32)
    shift_acc = jnp.zeros((2, 2, D), jnp.float32)
    outputs = []
    input_grads = []
    for micro_index in range(MICRO):
        held = (
            lax.all_gather(w_qkv, "dp", axis=1, tiled=True),
            lax.all_gather(w_out, "dp", axis=1, tiled=True),
            lax.all_gather(w_up, "dp", axis=1, tiled=True),
            lax.all_gather(w_down, "dp", axis=1, tiled=True),
        )
        qkv_w, out_w, up_w, down_w = held
        chain_kinds = tag_grid[:, micro_index].reshape(batch_chains)
        chain_lens = len_grid[:, micro_index].reshape(batch_chains)
        own_rows = x_in[micro_index * local_rows : (micro_index + 1) * local_rows]
        kinds_rows = jnp.repeat(own_tags[micro_index], LENGTH)
        heavy_rows = (kinds_rows == 0)[:, None]
        onehot = (kinds_rows[:, None] == jnp.arange(2)[None, :]).astype(jnp.float32)
        gain_mid = jnp.where(heavy_rows, gains[0, 0], gains[1, 0])
        shift_mid = jnp.where(heavy_rows, shifts[0, 0], shifts[1, 0])
        gain_end = jnp.where(heavy_rows, gains[0, 1], gains[1, 1])
        shift_end = jnp.where(heavy_rows, shifts[0, 1], shifts[1, 1])
        gathered = lax.all_gather(own_rows, "tensor", axis=0, tiled=True).reshape(
            batch_chains, LENGTH, D
        )
        projected = typed_map(gathered, qkv_w, chain_kinds, "ld,dkh->lkh").astype(jnp.bfloat16)
        query = projected[:, :, 0].reshape(batch_chains, LENGTH, local_heads, HEAD_DIM)
        keys_low = projected[:, :, 1].reshape(batch_chains, LENGTH, local_heads, HEAD_DIM)
        values_low = projected[:, :, 2].reshape(batch_chains, LENGTH, local_heads, HEAD_DIM)
        valid = (
            lax.broadcasted_iota(jnp.int32, (batch_chains, 1, 1, LENGTH), 3)
            < chain_lens[:, None, None, None]
        )
        scores = (
            jnp.einsum("cqhe,ckhe->chqk", query, keys_low, preferred_element_type=jnp.float32)
            * 0.125
        )
        scores = jnp.where(valid, scores, NEG)
        highest = jnp.max(scores, -1, keepdims=True)
        expo = jnp.exp(scores - highest)
        totals = jnp.sum(expo, -1, keepdims=True)
        probs = expo / totals
        log_total = highest + jnp.log(totals)
        heads_low = jnp.einsum(
            "chqk,ckhe->cqhe",
            probs.astype(jnp.bfloat16),
            values_low,
            preferred_element_type=jnp.float32,
        ).astype(jnp.bfloat16)
        heads_low = heads_low.reshape(batch_chains, LENGTH, head_cols)
        attn_sum = lax.psum_scatter(
            row_terms(
                heads_low, out_w, chain_kinds, "lh,dh->ld", lax.axis_size("tensor") * local_rows
            ).astype(jnp.bfloat16),
            "tensor",
            scatter_dimension=0,
            tiled=True,
        ).astype(jnp.float32)
        mid, normed_mid, factor_mid = old_norm_forward(
            own_rows.astype(jnp.float32) + attn_sum, gain_mid, shift_mid
        )
        mid_all = lax.all_gather(mid.astype(jnp.bfloat16), "tensor", axis=0, tiled=True).reshape(
            batch_chains, LENGTH, D
        )
        up_value = typed_map(mid_all, up_w, chain_kinds, "ld,df->lf")
        act_low = jax.nn.gelu(up_value, approximate=False).astype(jnp.bfloat16)
        ffn_sum = lax.psum_scatter(
            row_terms(
                act_low, down_w, chain_kinds, "lf,df->ld", lax.axis_size("tensor") * local_rows
            ).astype(jnp.bfloat16),
            "tensor",
            scatter_dimension=0,
            tiled=True,
        ).astype(jnp.float32)
        final, normed_end, factor_end = old_norm_forward(ffn_sum + mid, gain_end, shift_end)
        outputs.append(final.astype(jnp.bfloat16))
        base = grad_full
        grad_final = cotangent[micro_index * local_rows : (micro_index + 1) * local_rows].astype(
            jnp.float32
        )
        gain_acc = gain_acc.at[:, 1].add(type_sums(onehot, grad_final * normed_end))
        shift_acc = shift_acc.at[:, 1].add(type_sums(onehot, grad_final))
        grad_resid2 = old_norm_backward(grad_final, normed_end, factor_end, gain_end)
        grad_ffn = lax.all_gather(
            grad_resid2.astype(jnp.bfloat16), "tensor", axis=0, tiled=True
        ).reshape(batch_chains, LENGTH, D)
        grad_act = typed_map(grad_ffn, down_w, chain_kinds, "ld,df->lf")
        unused_value, gelu_back = jax.vjp(partial(jax.nn.gelu, approximate=False), up_value)
        grad_up = gelu_back(grad_act)[0].astype(jnp.bfloat16)
        down_acc = typed_grads(base[3], grad_ffn, act_low, chain_kinds, "ld,lf->df")
        up_acc = typed_grads(base[2], mid_all, grad_up, chain_kinds, "ld,lf->df")
        grad_mid = grad_resid2 + lax.psum_scatter(
            row_terms(
                grad_up, up_w, chain_kinds, "lf,df->ld", lax.axis_size("tensor") * local_rows
            ).astype(jnp.bfloat16),
            "tensor",
            scatter_dimension=0,
            tiled=True,
        ).astype(jnp.float32)
        gain_acc = gain_acc.at[:, 0].add(type_sums(onehot, grad_mid * normed_mid))
        shift_acc = shift_acc.at[:, 0].add(type_sums(onehot, grad_mid))
        grad_resid1 = old_norm_backward(grad_mid, normed_mid, factor_mid, gain_mid)
        grad_attn = lax.all_gather(
            grad_resid1.astype(jnp.bfloat16), "tensor", axis=0, tiled=True
        ).reshape(batch_chains, LENGTH, D)
        grad_heads = typed_map(grad_attn, out_w, chain_kinds, "ld,dh->lh").astype(jnp.bfloat16)
        out_acc = typed_grads(base[1], grad_attn, heads_low, chain_kinds, "ld,lh->dh")
        grad_heads = grad_heads.reshape(batch_chains, LENGTH, local_heads, HEAD_DIM)
        again = (
            jnp.einsum("cqhe,ckhe->chqk", query, keys_low, preferred_element_type=jnp.float32)
            * 0.125
        )
        probs_again = jnp.exp(jnp.where(valid, again, NEG) - log_total)
        grad_probs = jnp.einsum(
            "cqhe,ckhe->chqk", grad_heads, values_low, preferred_element_type=jnp.float32
        )
        inner = jnp.sum(grad_probs * probs_again, -1, keepdims=True)
        grad_scores = (probs_again * (grad_probs - inner)).astype(jnp.bfloat16)
        grad_query = (
            jnp.einsum("chqk,ckhe->cqhe", grad_scores, keys_low, preferred_element_type=jnp.float32)
            * 0.125
        ).astype(jnp.bfloat16)
        grad_keys = (
            jnp.einsum("chqk,cqhe->ckhe", grad_scores, query, preferred_element_type=jnp.float32)
            * 0.125
        ).astype(jnp.bfloat16)
        grad_values = jnp.einsum(
            "chqk,cqhe->ckhe",
            probs_again.astype(jnp.bfloat16),
            grad_heads,
            preferred_element_type=jnp.float32,
        ).astype(jnp.bfloat16)
        grad_proj = jnp.stack([grad_query, grad_keys, grad_values], 2).reshape(
            batch_chains, LENGTH, 3, head_cols
        )
        qkv_acc = typed_grads(base[0], gathered, grad_proj, chain_kinds, "ld,lkh->dkh")
        grad_input = grad_resid1 + lax.psum_scatter(
            row_terms(
                grad_proj, qkv_w, chain_kinds, "lkh,dkh->ld", lax.axis_size("tensor") * local_rows
            ).astype(jnp.bfloat16),
            "tensor",
            scatter_dimension=0,
            tiled=True,
        ).astype(jnp.float32)
        input_grads.append(grad_input)
        updated = (qkv_acc, out_acc, up_acc, down_acc)
        grad_full = updated
    shards = (
        lax.psum_scatter(grad_full[0], "dp", scatter_dimension=1, tiled=True),
        lax.psum_scatter(grad_full[1], "dp", scatter_dimension=1, tiled=True),
        lax.psum_scatter(grad_full[2], "dp", scatter_dimension=1, tiled=True),
        lax.psum_scatter(grad_full[3], "dp", scatter_dimension=1, tiled=True),
    )
    gain_grad, shift_grad = (
        lax.psum_scatter(gain_acc, ("dp", "tensor"), scatter_dimension=2, tiled=True),
        lax.psum_scatter(shift_acc, ("dp", "tensor"), scatter_dimension=2, tiled=True),
    )
    return (
        jnp.concatenate(outputs, 0),
        jnp.concatenate(input_grads, 0),
        shards[0],
        shards[1],
        shards[2],
        shards[3],
        gain_grad,
        shift_grad,
    )


def solution(mesh):
    placed = (
        P(("dp", "tensor"), None),
        P("dp"),
        P("dp"),
        P(None, "dp", None, "tensor"),
        P(None, "dp", "tensor"),
        P(None, "dp", "tensor"),
        P(None, "dp", "tensor"),
        P(None, None, ("dp", "tensor")),
        P(None, None, ("dp", "tensor")),
        P(("dp", "tensor"), None),
    )
    results = (
        P(("dp", "tensor"), None),
        P(("dp", "tensor"), None),
        P(None, "dp", None, "tensor"),
        P(None, "dp", "tensor"),
        P(None, "dp", "tensor"),
        P(None, "dp", "tensor"),
        P(None, None, ("dp", "tensor")),
        P(None, None, ("dp", "tensor")),
    )
    n_dp, n_tensor = mesh.shape["dp"], mesh.shape["tensor"]
    if n_tensor != GROUPS or n_dp % 2 or D % (16 * n_dp):
        return jax.shard_map(
            general_local, mesh=mesh, in_specs=placed, out_specs=results, check_vma=False
        )
    fine = Mesh(mesh.devices.reshape(n_dp // 2, 2, 2, 2), AXES)
    names = {"dp": ("z", "x"), "tensor": ("y", "c")}

    def refine(spec):
        parts = []
        for entry in spec:
            entry = (entry,) if isinstance(entry, str) else entry
            parts.append(entry and sum((names[a] for a in entry), ()))
        return P(*parts)

    return jax.shard_map(
        partial(split_local, n_dp // 2),
        mesh=fine,
        in_specs=tuple(refine(s) for s in placed),
        out_specs=tuple(refine(s) for s in results),
        check_vma=False,
    )
```

```python
from functools import partial

import jax
import jax.numpy as jnp
from jax import lax
from jax.experimental import pallas as pl
from jax.experimental.pallas import tpu as pltpu
from jax.sharding import Mesh
from jax.sharding import PartitionSpec as P

D = 768
HEADS = 12
HEAD_DIM = 64
MICRO = 4
CHAINS_PART = 1
LENGTH = 160
GROUPS = 4
OWN = 4
EXTRA = 2
SLOTS = OWN + EXTRA
EXT_ROWS = EXTRA * LENGTH
OWN_ROWS = OWN * LENGTH
ROWS = SLOTS * LENGTH

EPS = 1e-12
NEG = -1e30
HIGH = lax.Precision.HIGHEST
BF = jnp.bfloat16
F32 = jnp.float32
MESH = pl.DeviceIdType.MESH
ANY = pl.BlockSpec(memory_space=pl.ANY)
AXES = ("z", "x", "y", "c")


def place():
    return tuple(lax.axis_index(a) for a in AXES)


def meet(nz, z, x, y, c):
    barrier = pltpu.get_barrier_semaphore()
    friends = [{"c": 1 - c}, {"y": 1 - y}, {"y": 1 - y, "c": 1 - c}, {"x": 1 - x}]
    friends += [{"z": lax.rem(z + dz, nz)} for dz in range(1, nz)]
    for friend in friends:
        pl.semaphore_signal(barrier, inc=1, device_id=friend, device_id_type=MESH)
    pl.semaphore_wait(barrier, len(friends))


CHUNK = 320
SUB = 80
N_CHUNK = ROWS // CHUNK
WIDE = 3 * LENGTH
GW = 256
PAIR = 3


def dot_nn(a, b):
    return lax.dot_general(a, b, (((1,), (0,)), ((), ())), preferred_element_type=F32)


def dot_nt(a, b):
    return lax.dot_general(a, b, (((1,), (1,)), ((), ())), preferred_element_type=F32)


def dot_tn(a, b):
    return lax.dot_general(a, b, (((0,), (0,)), ((), ())), preferred_element_type=F32)


def lanes(shape):
    return lax.broadcasted_iota(jnp.int32, shape, len(shape) - 1)


def head_mask(h, shape):
    lane = lanes(shape)
    return jnp.logical_and(lane >= h * HEAD_DIM, lane < (h + 1) * HEAD_DIM)


def stack_heads(rows):
    zero = jnp.zeros_like(rows)
    return jnp.concatenate([jnp.where(head_mask(h, rows.shape), rows, zero) for h in range(3)], 0)


def merge_heads(stack):
    out = jnp.zeros((LENGTH, GW), stack.dtype)
    for h in range(3):
        out = jnp.where(head_mask(h, out.shape), stack[h * LENGTH : (h + 1) * LENGTH], out)
    return out


def chunk_rows(i, size=CHUNK):
    return pl.ds(pl.multiple_of(i * size, size), size)


def loop(count, body):
    def step(i, carry):
        body(i)
        return carry

    lax.fori_loop(0, count, step, 0)


def weave(count, unit, extra):
    def body(i):
        unit(i)
        for k, step in extra.items():
            pl.when(i == k)(step)

    loop(count, body)


def out_columns(t, w, wo):
    low = lanes((D, 128)) < HEAD_DIM
    tiles = [w[0, t, :, GW * i + 128 : GW * i + 256].astype(F32) for i in range(3)]
    wo[t, :, :128] = jnp.where(low, pltpu.roll(tiles[0], 64, 1), tiles[1]).astype(BF)
    wo[t, :, 128:] = jnp.where(low, pltpu.roll(tiles[2], 64, 1), 0.0).astype(BF)


def attend(t, chains, lens, proj, probs, hout):
    rows = [chunk_rows(s, LENGTH) for s in chains]
    parts = [(proj[t, r, :GW], proj[t, r, GW : 2 * GW], proj[t, r, 2 * GW :]) for r in rows]
    lows, outs = [], []
    for s, (query, key, value) in zip(chains, parts):
        scores = dot_nt(key, stack_heads(query * jnp.asarray(0.125, BF)))
        valid = lax.broadcasted_iota(jnp.int32, (LENGTH, 1), 0) < lens(s)
        scores = jnp.where(valid, scores, NEG)
        expo = jnp.exp(scores - jnp.max(scores, 0, keepdims=True))
        lows.append((expo * (1.0 / jnp.sum(expo, 0, keepdims=True))).astype(BF))
        outs.append(merge_heads(dot_tn(lows[-1], value)).astype(BF))
    for s, r, low, out in zip(chains, rows, lows, outs):
        probs[t, s, :, :WIDE] = low
        hout[t, r] = out


def norm_rows(values):
    center = values - jnp.mean(values, -1, keepdims=True)
    factor = lax.rsqrt(jnp.mean(center * center, -1, keepdims=True) + EPS)
    return center * factor, factor


def norm_back(scaled, normed, factor):
    return factor * (
        scaled
        - jnp.mean(scaled, -1, keepdims=True)
        - normed * jnp.mean(scaled * normed, -1, keepdims=True)
    )


def pieces(i, body):
    def step(k):
        body(pl.ds(pl.multiple_of(i * CHUNK + k * SUB, SUB), SUB), k)

    loop(CHUNK // SUB, step)


def first_norm(i, x, hout, wo, prm, mid, n1, s1, mid_low):
    r = chunk_rows(i)
    attn = dot_nt(hout[0, r], wo[0])
    for t in range(1, GROUPS):
        attn += dot_nt(hout[t, r], wo[t])
    mid[r] = attn

    def piece(p, k):
        normed, factor = norm_rows(x[p].astype(F32) + mid[p])
        n1[p] = normed.astype(BF)
        s1[p] = jnp.broadcast_to(factor, (SUB, 128))
        value = normed * prm[0:1] + prm[2:3]
        mid[p] = value
        mid_low[p] = value.astype(BF)

    pieces(i, piece)


def feed_up(t, i, mid_low, w, act, slope):
    r = chunk_rows(i)
    for k in range(0, D, GW):
        up = dot_nn(mid_low[r], w[1, t, :, k : k + GW])
        cdf = 0.5 * (1.0 + lax.erf(up * 0.7071067811865476))
        act[t, r, k : k + GW] = (up * cdf).astype(BF)
        bell = 0.3989422804014327 * jnp.exp(-0.5 * up * up)
        slope[t, r, k : k + GW] = (cdf + up * bell).astype(BF)


def second_norm(i, act, w, prm, mid, cot, mine, y_rows, d_ffn, ngrad):
    r = chunk_rows(i)
    ffn = dot_nt(act[0, r], w[2, 0])
    for t in range(1, GROUPS):
        ffn += dot_nt(act[t, r], w[2, t])
    mid[r] += ffn

    def piece(p, k):
        normed, factor = norm_rows(mid[p])
        y_rows[pl.ds(pl.multiple_of(k * SUB, SUB), SUB)] = (normed * prm[1:2] + prm[3:4]).astype(BF)
        grad = cot[p].astype(F32) * jnp.where(k < LENGTH // SUB, mine(2 * i), mine(2 * i + 1))
        ngrad[1:2] += jnp.sum(grad * normed, 0, keepdims=True)
        ngrad[3:4] += jnp.sum(grad, 0, keepdims=True)
        back = norm_back(grad * prm[1:2], normed, factor)
        mid[p] = back
        d_ffn[p] = back.astype(BF)

    pieces(i, piece)


def back_up(t, i, d_ffn, w, slope):
    r = chunk_rows(i)
    slope[t, r] = (dot_nn(d_ffn[r], w[2, t]) * slope[t, r].astype(F32)).astype(BF)


def back_first_norm(i, d_up, w, prm, mid, n1, s1, d_attn, ngrad):
    r = chunk_rows(i)
    grad = dot_nt(d_up[0, r], w[1, 0])
    for t in range(1, GROUPS):
        grad += dot_nt(d_up[t, r], w[1, t])
    mid[r] += grad

    def piece(p, k):
        grad = mid[p]
        normed = n1[p].astype(F32)
        ngrad[0:1] += jnp.sum(grad * normed, 0, keepdims=True)
        ngrad[2:3] += jnp.sum(grad, 0, keepdims=True)
        back = norm_back(grad * prm[0:1], normed, s1[p, 0:1])
        mid[p] = back
        d_attn[p] = back.astype(BF)

    pieces(i, piece)


def back_heads(t, i, d_attn, wo, d_heads):
    r = chunk_rows(i)
    d_heads[t, r, :GW] = dot_nn(d_attn[r], wo[t]).astype(BF)


def back_attend(t, chains, proj, probs, d_heads):
    rows = [chunk_rows(s, LENGTH) for s in chains]
    parts = [
        (proj[t, r, :GW], proj[t, r, GW : 2 * GW], proj[t, r, 2 * GW :], d_heads[t, r, :GW], probs[t, s, :, :WIDE])
        for s, r in zip(chains, rows)
    ]
    results = []
    for query, key, value, grad, low in parts:
        grad = stack_heads(grad)
        p = low.astype(F32)
        d_probs = dot_nt(value, grad)
        d_scores = (p * (d_probs - jnp.sum(d_probs * p, 0, keepdims=True))).astype(BF)
        d_query = merge_heads(dot_tn(d_scores, key)) * 0.125
        d_key = dot_nn(d_scores, stack_heads(query * jnp.asarray(0.125, BF)))
        results.append((d_query.astype(BF), d_key.astype(BF), dot_nn(low, grad).astype(BF)))
    for r, (d_query, d_key, d_value) in zip(rows, results):
        proj[t, r, :GW] = d_query
        proj[t, r, GW : 2 * GW] = d_key
        proj[t, r, 2 * GW :] = d_value


def grad_qkv_out(t, x, d_proj, d_attn, hout, store):
    low = lanes((D, 128)) < HEAD_DIM
    outs = dot_tn(d_attn[...], hout[t])
    places = (pltpu.roll(outs[:, :128], 64, 1), outs[:, :128], pltpu.roll(outs[:, 128:], 64, 1))
    for i in range(3):
        part = dot_tn(x[...], d_proj[t, :, GW * i : GW * (i + 1)])
        store(GW * i, part[:, :128])
        store(GW * i + 128, jnp.where(low, part[:, 128:], places[i]))


def back_input(i, d_proj, w, mid, out):
    r = chunk_rows(i)
    grad = mid[r]
    for t in range(GROUPS):
        grad += dot_nt(d_proj[t, r], w[0, t])
    out(r, grad)


def remote(src, dst, s_sem, r_sem, who):
    return pltpu.make_async_remote_copy(
        src_ref=src, dst_ref=dst, send_sem=s_sem, recv_sem=r_sem, device_id=who, device_id_type=MESH
    )


def arrived(ref, sem):
    remote(ref, ref, sem, sem, {"c": 1 - lax.axis_index("c")}).wait_recv()


def has_left(ref, sem):
    remote(ref, ref, sem, sem, {"c": 1 - lax.axis_index("c")}).wait_send()


def step_kernel(nz, rows,
                tags, lens, x_in, cot, qo, up, dn, gain, bias,
                y_own, g_own, own_out, oth_out, n_out, y_back, g_back, r_c,
                w, x, proj, probs, hout, wo, mid, n1, s1, mid_low, act, slope, d_ffn, gown, r_x,
                n_all, prm, ngrad, n_c, n_x, n_z,
                load_s, io_s, stage_s,
                ys_s, ys_r, zs_s, zs_r, xs_s, xs_r, cs_s, cs_r, ex_s, ex_r, na_s, na_r,
                c_s, c_r, x_s, x_r, z_s, z_r, y_s, y_r, e_s, e_r, ng_s, ng_r, free_s):
    z, xc, y, c = place()
    core, across, other_x = {"c": 1 - c}, {"y": 1 - y}, {"x": 1 - xc}
    diagonal = {"y": 1 - y, "c": 1 - c}
    mats = (qo, up, dn)
    lender = y != c
    home = (2 * y + c) * OWN
    away = (2 - y) * OWN + c * EXTRA

    def z_of(dz):
        return lax.rem(z + dz, nz)

    def chain(s):
        return jnp.where(s < OWN, home + s, away + s - OWN)

    def length_of(s):
        return lens[chain(s)]

    def mine(s):
        return jnp.where(tags[chain(s)] == y, 1.0, 0.0)

    def part(zz, xx):
        return pl.ds(pl.multiple_of((zz * 2 + xx) * rows, rows), rows)

    def group(g):
        return 2 * lax.rem(y + g, 2) + c

    def block(m, g, zz, xx):
        return w.at[m, group(g), part(zz, xx)]

    loads = [pltpu.make_async_copy(mats[m].at[y], block(m, 0, z, xc), load_s.at[m]) for m in range(3)]
    loads += [
        pltpu.make_async_copy(x_in, x.at[pl.ds(0, OWN_ROWS)], load_s.at[3]),
        pltpu.make_async_copy(cot, d_ffn.at[pl.ds(0, OWN_ROWS)], load_s.at[4]),
    ]
    for cp in loads:
        cp.start()
    me = ((z * 2 + xc) * 2 + y) * 2 + c
    cols = gain.shape[2]
    n_all[me] = jnp.zeros((8, 128), F32)
    for i in range(2):
        n_all[me, 2 * i : 2 * i + 2, :cols] = gain[i]
        n_all[me, 4 + 2 * i : 6 + 2 * i, :cols] = bias[i]
    ngrad[...] = jnp.zeros_like(ngrad)
    meet(nz, z, xc, y, c)

    def lend(arr, out, i, act_on):
        @pl.when(lender)
        def _():
            for j, (who, p) in enumerate(((across, c), (diagonal, 1 - c))):
                src = arr.at[pl.ds(pl.multiple_of(p * EXT_ROWS, EXT_ROWS), EXT_ROWS)]
                act_on(remote(src, out.at[pl.ds(OWN_ROWS, EXT_ROWS)], ex_s.at[i, j], ex_r.at[i], who))

    for m in range(3):
        remote(mats[m].at[1 - y], w.at[m, group(0), part(z, xc)], ys_s.at[m], ys_r.at[m], across).start()
    lend(x_in, x, 0, lambda cp: cp.start())
    lend(cot, d_ffn, 1, lambda cp: cp.start())

    def inside(zz):
        return jnp.logical_and(zz >= 0, zz < nz)

    def start(cp):
        cp.start()

    def recv(cp):
        cp.wait_recv()

    def hop(m, g, d, j, ref, act_on):
        to = z + 1 - 2 * d

        @pl.when(jnp.logical_and(inside(to), j < nz))
        def _():
            act_on(remote(ref, ref, zs_s.at[m, g, d, j], zs_r.at[m, g, d, j], {"z": to}))

    def x_copy(m, g, zz):
        ref = block(m, g, zz, xc)
        return remote(ref, ref, xs_s.at[m, g, zz], xs_r.at[m, g, zz], other_x)

    def c_copy(m, g, zz, xx):
        ref = block(m, g, zz, xx)
        return remote(ref, ref, cs_s.at[m, g, zz, xx], cs_r.at[m, g, zz, xx], core)

    def own_z(m):
        def body(g):
            @pl.when(g == 1)
            def _():
                arrived(block(m, 1, z, xc), ys_r.at[m])

            for d in range(2):
                hop(m, g, d, 1, block(m, g, z, xc), start)

        loop(2, body)

    def own_xc(m):
        def body(g):
            x_copy(m, g, z).start()
            c_copy(m, g, z, xc).start()

        loop(2, body)

    def z_event(m, j):
        def body(q):
            g, d = q // 2, q % 2
            zz = z - j + 2 * j * d

            @pl.when(inside(zz))
            def _():
                ref = block(m, g, zz, xc)
                arrived(ref, zs_r.at[m, g, d, j])
                hop(m, g, d, j + 1, ref, start)
                x_copy(m, g, zz).start()
                c_copy(m, g, zz, xc).start()

        loop(4, body)

    def x_event(m, j):
        def body(q):
            g, d = q // 2, q % 2
            zz = z - j + 2 * j * d

            @pl.when(jnp.logical_and(inside(zz), j + 1 > d))
            def _():
                arrived(block(m, g, zz, 1 - xc), xs_r.at[m, g, zz])
                c_copy(m, g, zz, 1 - xc).start()

        loop(4, body)

    def gathered(m):
        def body(i):
            t = 2 * lax.rem(y + i // (2 * nz), 2) + 1 - c
            zz, xx = (i // 2) % nz, i % 2
            arrived(w.at[m, t, part(zz, xx)], cs_r.at[m, i // (2 * nz), zz, xx])

        loop(4 * nz, body)

    def gather_sent(i):
        m, g = i // 2, i % 2
        ref = w.at[0, 0, pl.ds(0, rows)]
        for j in range(1, nz):
            for d in range(2):
                @pl.when(inside(z - (1 - 2 * d) * (j - 1)))
                def _():
                    hop(m, g, d, j, ref, lambda cp: cp.wait_send())
        for zz in range(nz):
            has_left(ref, xs_s.at[m, g, zz])
            for xx in range(2):
                has_left(ref, cs_s.at[m, g, zz, xx])

    def norm_hop(i, act_on):
        if i == 0:
            act_on(remote(n_all.at[me], n_all.at[me], na_s.at[0], na_r.at[0], core))
        elif i == 1:
            ref = n_all.at[pl.ds(me - c, 2)]
            act_on(remote(ref, ref, na_s.at[1], na_r.at[1], across))
        elif i == 2:
            ref = n_all.at[pl.ds(me - c - 2 * y, 4)]
            act_on(remote(ref, ref, na_s.at[2], na_r.at[2], other_x))
        else:
            ref = n_all.at[pl.ds(8 * z, 8)]
            for dz in range(1, nz):
                act_on(remote(ref, ref, na_s.at[2 + dz], na_r.at[2 + dz], {"z": z_of(dz)}))

    for m in range(3):
        loads[m].wait()
    norm_hop(0, start)
    own_z(0)
    own_xc(0)
    z_event(0, 1)
    norm_hop(0, recv)
    norm_hop(1, start)
    for j in range(2, nz):
        z_event(0, j)
        if j == 2:
            own_z(1)
    if nz < 3:
        own_z(1)
    norm_hop(1, recv)
    norm_hop(2, start)
    own_xc(1)
    x_event(0, 0)
    x_event(0, 1)
    for j in range(1, nz - 1):
        z_event(1, j)
        x_event(0, j + 1)
    own_z(2)
    norm_hop(2, recv)
    norm_hop(3, start)
    gathered(0)
    loads[3].wait()
    arrived(x.at[pl.ds(OWN_ROWS, EXT_ROWS)], ex_r.at[0])

    def projection(i):
        t, k = i // N_CHUNK, i % N_CHUNK
        r = chunk_rows(k)
        proj[t, r] = dot_nn(x[r], w[0, t]).astype(BF)

        @pl.when(k == N_CHUNK - 1)
        def _():
            out_columns(t, w, wo)

    def more_own():
        z_event(1, nz - 1)
        own_xc(2)

    weave(
        GROUPS * N_CHUNK,
        projection,
        {0: more_own, 8: lambda: x_event(1, 0), 11: lambda: z_event(2, 1)},
    )
    norm_hop(3, recv)
    lane = lanes((2, D))
    gains, shifts = jnp.zeros((2, D), F32), jnp.zeros((2, D), F32)
    for d in range(8 * nz):
        within = jnp.logical_and(lane >= d * cols, lane < (d + 1) * cols)
        for name in range(2):
            piece = n_all[d, pl.ds(4 * name + 2 * y, 2), :]
            piece = jnp.concatenate([piece, jnp.zeros((2, D - 128), F32)], 1)
            piece = jnp.where(within, pltpu.roll(piece, d * cols, 1) if d else piece, 0.0)
            if name == 0:
                gains += piece
            else:
                shifts += piece
    prm[0:2] = gains
    prm[2:4] = shifts
    per = SLOTS // PAIR

    def attention(i):
        attend(i // per, [(i % per) * PAIR + k for k in range(PAIR)], length_of, proj, probs, hout)

    weave(
        GROUPS * per,
        attention,
        {2: lambda: x_event(1, 1), 3: lambda: z_event(2, 2), 7: lambda: x_event(1, 2)},
    )
    loop(N_CHUNK, lambda i: first_norm(i, x, hout, wo, prm, mid, n1, s1, mid_low))
    for j in range(3, nz):
        z_event(2, j)
        x_event(1, j)
    gathered(1)
    weave(
        GROUPS * N_CHUNK,
        lambda i: feed_up(i // N_CHUNK, i % N_CHUNK, mid_low, w, act, slope),
        {2: lambda: x_event(2, 0), 7: lambda: x_event(2, 1)},
    )
    for j in range(2, nz):
        x_event(2, j)
    gathered(2)
    loads[4].wait()
    arrived(d_ffn.at[pl.ds(OWN_ROWS, EXT_ROWS)], ex_r.at[1])

    def y_stage(i):
        return gown.at[1, i // 2, pl.ds(pl.multiple_of((i % 2) * CHUNK, CHUNK), CHUNK)]

    def give_back(src, dst, i, act_on):
        dst = dst.at[pl.ds(pl.multiple_of(c * EXT_ROWS, EXT_ROWS), EXT_ROWS)]

        @pl.when(c == y)
        def _():
            act_on(remote(src, dst, e_s.at[i], e_r.at[i, c], across))

        @pl.when(c != y)
        def _():
            act_on(remote(src, dst, e_s.at[i], e_r.at[i, c], diagonal))

    def y_copy(i):
        return pltpu.make_async_copy(y_stage(i), y_own.at[pl.ds(i * CHUNK, CHUNK)], io_s.at[i])

    loop(
        N_CHUNK,
        lambda i: second_norm(i, act, w, prm, mid, d_ffn, mine, y_stage(i), d_ffn, ngrad),
    )
    for i in range(2):
        y_copy(i).start()
    give_back(y_stage(2), y_back, 0, start)

    def spare(m, g):
        return gown.at[0, g] if m else act.at[2 + g, pl.ds(0, D)]

    def r_z(m, g, dz):
        return w.at[2, m, pl.ds(pl.multiple_of((g * nz + dz) * rows, rows), rows)]

    def core_send(m, g):
        return remote(spare(m, g), r_c.at[m, g], c_s.at[m, g], c_r.at[m, g], core)

    def fetch(m, g):
        return pltpu.make_async_copy(r_c.at[m, g], act.at[g, pl.ds(0, D)], stage_s.at[g])

    def core_fetch(m, g):
        arrived(r_c.at[m, g], c_r.at[m, g])
        fetch(m, g).start()

    def core_add(m, g):
        fetch(m, g).wait()

        def body(i):
            dz = i // 2 + 1
            zz = z_of(dz)
            xx = lax.rem(xc + 1 + i, 2)
            p = part(zz, xx)
            gown[m, g, p] = (gown[m, g, p].astype(F32) + act[g, p].astype(F32)).astype(BF)

        loop(2 * nz, body)
        for dz in range(1, nz + 1):
            zz = z_of(dz)
            remote(gown.at[m, g, part(zz, 1 - xc)], r_x.at[m, g, zz], x_s.at[m, g, zz], x_r.at[m, g, zz], other_x).start()

    def sum_event(q):
        m = 2 - q // (2 * nz)
        g = (q // nz) % 2
        dz = q % nz + 1
        zz = z_of(dz)
        arrived(r_x.at[m, g, zz], x_r.at[m, g, zz])
        p = part(zz, xc)
        gown[m, g, p] = (gown[m, g, p].astype(F32) + r_x[m, g, zz].astype(F32)).astype(BF)

        @pl.when(dz < nz)
        def _():
            remote(gown.at[m, g, p], r_z(m, g, dz), z_s.at[m, g, dz], z_r.at[m, g, dz], {"z": zz}).start()

    def own_copy(m):
        return pltpu.make_async_copy(mid.at[pl.ds(OWN_ROWS + m * rows, rows)], own_out.at[m], io_s.at[3 + m])

    def last_send(m):
        return remote(mid_low.at[pl.ds(EXT_ROWS + m * rows, rows)], oth_out.at[m], y_s.at[m], y_r.at[m], across)

    def finish(m, g):
        total = gown[m, g, part(z, xc)].astype(F32)
        for dz in range(1, nz):
            arrived(r_z(m, g, dz), z_r.at[m, g, dz])
            total += r_z(m, g, dz)[...].astype(F32)

        @pl.when(y == g)
        def _():
            mid[OWN_ROWS + m * rows : OWN_ROWS + (m + 1) * rows] = total
            own_copy(m).start()

        @pl.when(y != g)
        def _():
            mid_low[EXT_ROWS + m * rows : EXT_ROWS + (m + 1) * rows] = total.astype(BF)
            last_send(m).start()

    def slope_grads(m, a, b):
        def body(q):
            g = q % 2
            t = 2 * g + jnp.where(q < 2, 1 - c, c)
            dst = gown.at[jnp.where(q < 2, 0, m), g]
            for k in range(0, D, GW):
                dst[:, k : k + GW] = dot_tn(a[...], b[t, :, k : k + GW]).astype(BF)

            @pl.when(q < 2)
            def _():
                core_send(m, g).start()

        loop(4, body)

    slope_grads(2, d_ffn, act)

    def up_back(i):
        back_up(i // N_CHUNK, i % N_CHUNK, d_ffn, w, slope)

    def fetch_two(m):
        for g in range(2):
            core_fetch(m, g)

    def add_two(m):
        for g in range(2):
            core_add(m, g)

    def gather_over():
        loop(6, gather_sent)

    weave(
        GROUPS * N_CHUNK,
        up_back,
        {1: lambda: fetch_two(2), 3: lambda: add_two(2), 4: gather_over},
    )
    for dz in range(1, nz):
        pl.semaphore_signal(free_s, inc=1, device_id={"z": z_of(dz)}, device_id_type=MESH)
    for g in range(2):
        core_send(2, g).wait_send()
    for i in range(2):
        y_copy(i).wait()
    has_left(y_stage(2), e_s.at[0])
    slope_grads(1, mid_low, slope)
    fetch_two(1)
    pl.semaphore_wait(free_s, nz - 1)
    loop(2, sum_event)
    weave(
        N_CHUNK,
        lambda i: back_first_norm(i, slope, w, prm, mid, n1, s1, d_ffn, ngrad),
        {0: lambda: add_two(1), 1: lambda: sum_event(2)},
    )
    for g in range(2):
        core_send(1, g).wait_send()
    sum_event(3)

    def send_norms(i, act_on):
        if i == 0:
            act_on(remote(ngrad, n_c, ng_s.at[0], ng_r.at[0], core))
        elif i == 1:
            act_on(remote(n_c, n_x, ng_s.at[1], ng_r.at[1], other_x))
        elif i == 2:
            for dz in range(1, nz):
                act_on(remote(n_x, n_z.at[dz], ng_s.at[1 + dz], ng_r.at[1 + dz], {"z": z_of(dz)}))
        else:
            act_on(remote(n_out.at[y], n_out.at[y], ng_s.at[nz + 1], ng_r.at[nz + 1], across))

    send_norms(0, start)
    loop(GROUPS * N_CHUNK, lambda i: back_heads(i // N_CHUNK, i % N_CHUNK, d_ffn, wo, slope))
    sum_event(4)
    send_norms(0, recv)
    send_norms(0, lambda cp: cp.wait_send())
    n_c[...] += ngrad[...]
    send_norms(1, start)

    def attention_back(i):
        back_attend(i // per, [(i % per) * PAIR + k for k in range(PAIR)], proj, probs, slope)

        @pl.when(i % 2 == 1)
        def _():
            sum_event(5 + i // 2)

    loop(GROUPS * per, attention_back)
    send_norms(1, recv)
    send_norms(1, lambda cp: cp.wait_send())
    n_x[...] += n_c[...]
    send_norms(2, start)
    seen = 5 + GROUPS * per // 2

    def qkv_grads(q):
        g = q % 2

        def store(col, value):
            value = value.astype(BF)

            @pl.when(q < 2)
            def _():
                spare(0, g)[:, col : col + 128] = value

            @pl.when(q >= 2)
            def _():
                gown[0, g, :, col : col + 128] = value

        grad_qkv_out(2 * g + jnp.where(q < 2, 1 - c, c), x, proj, d_ffn, hout, store)

        @pl.when(q < 2)
        def _():
            core_send(0, g).start()

        sum_event(seen + q)

    loop(4, qkv_grads)
    seen += 4
    fetch_two(0)
    add_two(0)
    total = n_x[...]
    for dz in range(1, nz):
        arrived(n_z.at[dz], ng_r.at[1 + dz])
        total += n_z[dz]
    n_out[y] = total
    send_norms(3, start)

    def inputs_back(i):
        k = lax.rem(i + N_CHUNK - 1, N_CHUNK)

        def keep(r, grad):
            mid[r] = grad

            @pl.when(i == 0)
            def _():
                mid_low[:EXT_ROWS] = grad.astype(BF)

        back_input(k, proj, w, mid, keep)

        @pl.when(i == 0)
        def _():
            give_back(mid_low.at[pl.ds(0, EXT_ROWS)], g_back, 1, start)

        sum_event(seen + i)

    loop(N_CHUNK, inputs_back)
    seen += N_CHUNK
    g_copy = pltpu.make_async_copy(mid.at[pl.ds(0, OWN_ROWS)], g_own, io_s.at[2])
    g_copy.start()
    total_events = 6 * nz
    after = 4 * nz
    if seen < after:
        loop(after - seen, lambda q: sum_event(seen + q))
        seen = after
    for g in range(2):
        finish(2, g)
    loop(nz, lambda q: sum_event(after + q))
    for g in range(2):
        finish(1, g)
    loop(nz, lambda q: sum_event(after + nz + q))
    for g in range(2):
        finish(0, g)

    def sums_sent(i):
        m, g = i // 2, i % 2
        for dz in range(nz):
            if dz:
                has_left(r_x.at[0, 0, 0], z_s.at[m, g, dz])
            has_left(r_x.at[0, 0, 0], x_s.at[m, g, dz])

    loop(6, sums_sent)
    for g in range(2):
        core_send(0, g).wait_send()
    for m in range(3):
        has_left(mats[m].at[0], ys_s.at[m])
        own_copy(m).wait()
        last_send(m).wait()
    lend(x_in, x, 0, lambda cp: cp.wait_send())
    lend(cot, d_ffn, 1, lambda cp: cp.wait_send())
    for i in range(4):
        norm_hop(i, lambda cp: cp.wait_send())
    send_norms(2, lambda cp: cp.wait_send())
    send_norms(3, lambda cp: cp.wait())
    g_copy.wait()
    has_left(mid_low.at[pl.ds(0, EXT_ROWS)], e_s.at[1])

    @pl.when(lender)
    def _():
        for i, dst in enumerate((y_back, g_back)):
            for j in range(2):
                arrived(dst.at[pl.ds(j * EXT_ROWS, EXT_ROWS)], e_r.at[i, j])


def run_step(nz, tags, lens, x_in, cot, qo, up, dn, gain, bias):
    rows = up.shape[1]
    V = pl.BlockSpec(memory_space=pltpu.VMEM)
    S = pl.BlockSpec(memory_space=pltpu.SMEM)
    sem = pltpu.SemaphoreType.DMA
    out = jax.ShapeDtypeStruct
    return pl.pallas_call(
        partial(step_kernel, nz, rows),
        out_shape=(
            out((OWN_ROWS, D), BF),
            out((OWN_ROWS, D), F32),
            out((3, rows, D), F32),
            out((3, rows, D), BF),
            out((2, 8, D), F32),
            out((OWN_ROWS, D), BF),
            out((OWN_ROWS, D), BF),
            out((3, 2, D, D), BF),
        ),
        in_specs=[S, S, ANY, ANY, ANY, ANY, ANY, V, V],
        out_specs=(ANY, ANY, ANY, ANY, V, ANY, ANY, ANY),
        scratch_shapes=[
            pltpu.VMEM((3, GROUPS, D, D), BF),
            pltpu.VMEM((ROWS, D), BF),
            pltpu.VMEM((GROUPS, ROWS, D), BF),
            pltpu.VMEM((GROUPS, SLOTS, LENGTH, 512), BF),
            pltpu.VMEM((GROUPS, ROWS, GW), BF),
            pltpu.VMEM((GROUPS, D, GW), BF),
            pltpu.VMEM((ROWS, D), F32),
            pltpu.VMEM((ROWS, D), BF),
            pltpu.VMEM((ROWS, 128), F32),
            pltpu.VMEM((ROWS, D), BF),
            pltpu.VMEM((GROUPS, ROWS, D), BF),
            pltpu.VMEM((GROUPS, ROWS, D), BF),
            pltpu.VMEM((ROWS, D), BF),
            pltpu.VMEM((3, 2, D, D), BF),
            pltpu.VMEM((3, 2, nz, rows, D), BF),
            pltpu.VMEM((8 * nz, 8, 128), F32),
            pltpu.VMEM((8, D), F32),
            pltpu.VMEM((8, D), F32),
            pltpu.VMEM((8, D), F32),
            pltpu.VMEM((8, D), F32),
            pltpu.VMEM((nz, 8, D), F32),
            sem((5,)), sem((6,)), sem((2,)),
            sem((3,)), sem((3,)),
            sem((3, 2, 2, nz)), sem((3, 2, 2, nz)),
            sem((3, 2, nz)), sem((3, 2, nz)),
            sem((3, 2, nz, 2)), sem((3, 2, nz, 2)),
            sem((2, 2)), sem((2,)),
            sem((nz + 2,)), sem((nz + 2,)),
            sem((3, 2)), sem((3, 2)),
            sem((3, 2, nz)), sem((3, 2, nz)),
            sem((3, 2, nz)), sem((3, 2, nz)),
            sem((3,)), sem((3,)),
            sem((2,)), sem((2, 2)),
            sem((nz + 2,)), sem((nz + 2,)),
            pltpu.SemaphoreType.REGULAR,
        ],
        compiler_params=pltpu.CompilerParams(
            collective_id=0, has_side_effects=True, vmem_limit_bytes=67043328
        ),
        name="layer_step",
    )(tags, lens, x_in, cot, qo, up, dn, gain, bias)


def split_local(nz, x_in, tags, lengths, w_qkv, w_out, w_up, w_down, norm_gain, norm_bias, cotangent):
    z, x, y, c = place()
    rows = w_up.shape[1]
    cols = norm_gain.shape[2]
    qo = []
    for i in range(3):
        qo += [w_qkv[:, :, i], w_out[:, :, HEAD_DIM * i : HEAD_DIM * (i + 1)]]
    qo = jnp.concatenate(qo, -1)
    y_own, g_own, own_g, oth_g, n_sum, y_back, g_back, _ = run_step(
        nz, tags, lengths, x_in, cotangent, qo, w_up, w_down, norm_gain, norm_bias
    )
    kinds = lax.dynamic_slice_in_dim(tags, (2 * y + c) * OWN, OWN)
    mine = jnp.repeat(kinds == y, LENGTH)[:, None]
    y_out = jnp.where(mine, y_own, y_back)
    x_grad = jnp.where(mine, g_own, g_back.astype(F32))
    oth_g = oth_g.astype(F32)
    both = jnp.stack([jnp.where(y == 0, own_g, oth_g), jnp.where(y == 0, oth_g, own_g)])
    packed = both[:, 0].reshape(2, rows, 3, GW)
    me = ((z * 2 + x) * 2 + y) * 2 + c
    n_mine = lax.dynamic_slice_in_dim(n_sum, me * cols, cols, 2)
    return (
        y_out,
        x_grad,
        packed[..., : GW - HEAD_DIM],
        packed[..., GW - HEAD_DIM :].reshape(w_out.shape),
        both[:, 1],
        both[:, 2],
        n_mine[:, :2],
        n_mine[:, 2:4],
    )


def typed_map(operand, stacked, chain_kinds, pattern):

    def single(element):
        weight = lax.dynamic_index_in_dim(stacked, element[1], 0, keepdims=False)
        return jnp.einsum(pattern, element[0], weight, preferred_element_type=jnp.float32)

    return lax.map(single, (operand, chain_kinds))


def typed_grads(running, operand, partner, chain_kinds, pattern):

    def single(carry, element):
        product_term = jnp.einsum(
            pattern, element[0], element[1], preferred_element_type=jnp.float32
        )
        previous = lax.dynamic_index_in_dim(carry, element[2], 0, keepdims=False)
        return (
            lax.dynamic_update_index_in_dim(carry, previous + product_term, element[2], 0),
            None,
        )

    return lax.scan(single, running, (operand, partner, chain_kinds))[0]


def row_terms(operand, stacked, chain_kinds, pattern, row_count):
    result = typed_map(operand, stacked, chain_kinds, pattern)
    return result.reshape(row_count, result.shape[-1])


def old_norm_forward(values, gain_rows, shift_rows):
    center = values - jnp.mean(values, -1, keepdims=True)
    factor = lax.rsqrt(jnp.mean(center * center, -1, keepdims=True) + EPS)
    normed = center * factor
    return (normed * gain_rows + shift_rows, normed, factor)


def old_norm_backward(grad_out, normed, factor, gain_rows):
    scaled = grad_out * gain_rows
    mean_plain = jnp.mean(scaled, -1, keepdims=True)
    mean_normed = jnp.mean(scaled * normed, -1, keepdims=True)
    return factor * (scaled - mean_plain - normed * mean_normed)


def type_sums(onehot, values):
    return jnp.dot(onehot.T, values, precision=HIGH, preferred_element_type=jnp.float32)


def general_local(x_in, tags, lengths, w_qkv, w_out, w_up, w_down, norm_gain, norm_bias, cotangent):
    tp_count = lax.axis_size("tensor")
    tp_index = lax.axis_index("tensor")
    local_rows = CHAINS_PART * LENGTH
    batch_chains = tp_count * CHAINS_PART
    head_cols = w_qkv.shape[3]
    local_heads = head_cols // HEAD_DIM
    tag_grid = tags.reshape(tp_count, MICRO, CHAINS_PART)
    len_grid = lengths.reshape(tp_count, MICRO, CHAINS_PART)
    own_tags = lax.dynamic_index_in_dim(tag_grid, tp_index, 0, keepdims=False)
    gains, shifts = (
        lax.all_gather(norm_gain, ("dp", "tensor"), axis=2, tiled=True),
        lax.all_gather(norm_bias, ("dp", "tensor"), axis=2, tiled=True),
    )
    grad_full = (
        jnp.zeros((2, D, 3, head_cols), jnp.float32),
        jnp.zeros((2, D, head_cols), jnp.float32),
        jnp.zeros((2, D, w_up.shape[2]), jnp.float32),
        jnp.zeros((2, D, w_down.shape[2]), jnp.float32),
    )
    shards = (
        jnp.zeros(w_qkv.shape, jnp.float32),
        jnp.zeros(w_out.shape, jnp.float32),
        jnp.zeros(w_up.shape, jnp.float32),
        jnp.zeros(w_down.shape, jnp.float32),
    )
    gain_acc = jnp.zeros((2, 2, D), jnp.float32)
    shift_acc = jnp.zeros((2, 2, D), jnp.float32)
    outputs = []
    input_grads = []
    for micro_index in range(MICRO):
        held = (
            lax.all_gather(w_qkv, "dp", axis=1, tiled=True),
            lax.all_gather(w_out, "dp", axis=1, tiled=True),
            lax.all_gather(w_up, "dp", axis=1, tiled=True),
            lax.all_gather(w_down, "dp", axis=1, tiled=True),
        )
        qkv_w, out_w, up_w, down_w = held
        chain_kinds = tag_grid[:, micro_index].reshape(batch_chains)
        chain_lens = len_grid[:, micro_index].reshape(batch_chains)
        own_rows = x_in[micro_index * local_rows : (micro_index + 1) * local_rows]
        kinds_rows = jnp.repeat(own_tags[micro_index], LENGTH)
        heavy_rows = (kinds_rows == 0)[:, None]
        onehot = (kinds_rows[:, None] == jnp.arange(2)[None, :]).astype(jnp.float32)
        gain_mid = jnp.where(heavy_rows, gains[0, 0], gains[1, 0])
        shift_mid = jnp.where(heavy_rows, shifts[0, 0], shifts[1, 0])
        gain_end = jnp.where(heavy_rows, gains[0, 1], gains[1, 1])
        shift_end = jnp.where(heavy_rows, shifts[0, 1], shifts[1, 1])
        gathered = lax.all_gather(own_rows, "tensor", axis=0, tiled=True).reshape(
            batch_chains, LENGTH, D
        )
        projected = typed_map(gathered, qkv_w, chain_kinds, "ld,dkh->lkh").astype(jnp.bfloat16)
        query = projected[:, :, 0].reshape(batch_chains, LENGTH, local_heads, HEAD_DIM)
        keys_low = projected[:, :, 1].reshape(batch_chains, LENGTH, local_heads, HEAD_DIM)
        values_low = projected[:, :, 2].reshape(batch_chains, LENGTH, local_heads, HEAD_DIM)
        valid = (
            lax.broadcasted_iota(jnp.int32, (batch_chains, 1, 1, LENGTH), 3)
            < chain_lens[:, None, None, None]
        )
        scores = (
            jnp.einsum("cqhe,ckhe->chqk", query, keys_low, preferred_element_type=jnp.float32)
            * 0.125
        )
        scores = jnp.where(valid, scores, NEG)
        highest = jnp.max(scores, -1, keepdims=True)
        expo = jnp.exp(scores - highest)
        totals = jnp.sum(expo, -1, keepdims=True)
        probs = expo / totals
        log_total = highest + jnp.log(totals)
        heads_low = jnp.einsum(
            "chqk,ckhe->cqhe",
            probs.astype(jnp.bfloat16),
            values_low,
            preferred_element_type=jnp.float32,
        ).astype(jnp.bfloat16)
        heads_low = heads_low.reshape(batch_chains, LENGTH, head_cols)
        attn_sum = lax.psum_scatter(
            row_terms(
                heads_low, out_w, chain_kinds, "lh,dh->ld", lax.axis_size("tensor") * local_rows
            ).astype(jnp.bfloat16),
            "tensor",
            scatter_dimension=0,
            tiled=True,
        ).astype(jnp.float32)
        mid, normed_mid, factor_mid = old_norm_forward(
            own_rows.astype(jnp.float32) + attn_sum, gain_mid, shift_mid
        )
        mid_all = lax.all_gather(mid.astype(jnp.bfloat16), "tensor", axis=0, tiled=True).reshape(
            batch_chains, LENGTH, D
        )
        up_value = typed_map(mid_all, up_w, chain_kinds, "ld,df->lf")
        act_low = jax.nn.gelu(up_value, approximate=False).astype(jnp.bfloat16)
        ffn_sum = lax.psum_scatter(
            row_terms(
                act_low, down_w, chain_kinds, "lf,df->ld", lax.axis_size("tensor") * local_rows
            ).astype(jnp.bfloat16),
            "tensor",
            scatter_dimension=0,
            tiled=True,
        ).astype(jnp.float32)
        final, normed_end, factor_end = old_norm_forward(ffn_sum + mid, gain_end, shift_end)
        outputs.append(final.astype(jnp.bfloat16))
        base = grad_full
        grad_final = cotangent[micro_index * local_rows : (micro_index + 1) * local_rows].astype(
            jnp.float32
        )
        gain_acc = gain_acc.at[:, 1].add(type_sums(onehot, grad_final * normed_end))
        shift_acc = shift_acc.at[:, 1].add(type_sums(onehot, grad_final))
        grad_resid2 = old_norm_backward(grad_final, normed_end, factor_end, gain_end)
        grad_ffn = lax.all_gather(
            grad_resid2.astype(jnp.bfloat16), "tensor", axis=0, tiled=True
        ).reshape(batch_chains, LENGTH, D)
        grad_act = typed_map(grad_ffn, down_w, chain_kinds, "ld,df->lf")
        unused_value, gelu_back = jax.vjp(partial(jax.nn.gelu, approximate=False), up_value)
        grad_up = gelu_back(grad_act)[0].astype(jnp.bfloat16)
        down_acc = typed_grads(base[3], grad_ffn, act_low, chain_kinds, "ld,lf->df")
        up_acc = typed_grads(base[2], mid_all, grad_up, chain_kinds, "ld,lf->df")
        grad_mid = grad_resid2 + lax.psum_scatter(
            row_terms(
                grad_up, up_w, chain_kinds, "lf,df->ld", lax.axis_size("tensor") * local_rows
            ).astype(jnp.bfloat16),
            "tensor",
            scatter_dimension=0,
            tiled=True,
        ).astype(jnp.float32)
        gain_acc = gain_acc.at[:, 0].add(type_sums(onehot, grad_mid * normed_mid))
        shift_acc = shift_acc.at[:, 0].add(type_sums(onehot, grad_mid))
        grad_resid1 = old_norm_backward(grad_mid, normed_mid, factor_mid, gain_mid)
        grad_attn = lax.all_gather(
            grad_resid1.astype(jnp.bfloat16), "tensor", axis=0, tiled=True
        ).reshape(batch_chains, LENGTH, D)
        grad_heads = typed_map(grad_attn, out_w, chain_kinds, "ld,dh->lh").astype(jnp.bfloat16)
        out_acc = typed_grads(base[1], grad_attn, heads_low, chain_kinds, "ld,lh->dh")
        grad_heads = grad_heads.reshape(batch_chains, LENGTH, local_heads, HEAD_DIM)
        again = (
            jnp.einsum("cqhe,ckhe->chqk", query, keys_low, preferred_element_type=jnp.float32)
            * 0.125
        )
        probs_again = jnp.exp(jnp.where(valid, again, NEG) - log_total)
        grad_probs = jnp.einsum(
            "cqhe,ckhe->chqk", grad_heads, values_low, preferred_element_type=jnp.float32
        )
        inner = jnp.sum(grad_probs * probs_again, -1, keepdims=True)
        grad_scores = (probs_again * (grad_probs - inner)).astype(jnp.bfloat16)
        grad_query = (
            jnp.einsum("chqk,ckhe->cqhe", grad_scores, keys_low, preferred_element_type=jnp.float32)
            * 0.125
        ).astype(jnp.bfloat16)
        grad_keys = (
            jnp.einsum("chqk,cqhe->ckhe", grad_scores, query, preferred_element_type=jnp.float32)
            * 0.125
        ).astype(jnp.bfloat16)
        grad_values = jnp.einsum(
            "chqk,cqhe->ckhe",
            probs_again.astype(jnp.bfloat16),
            grad_heads,
            preferred_element_type=jnp.float32,
        ).astype(jnp.bfloat16)
        grad_proj = jnp.stack([grad_query, grad_keys, grad_values], 2).reshape(
            batch_chains, LENGTH, 3, head_cols
        )
        qkv_acc = typed_grads(base[0], gathered, grad_proj, chain_kinds, "ld,lkh->dkh")
        grad_input = grad_resid1 + lax.psum_scatter(
            row_terms(
                grad_proj, qkv_w, chain_kinds, "lkh,dkh->ld", lax.axis_size("tensor") * local_rows
            ).astype(jnp.bfloat16),
            "tensor",
            scatter_dimension=0,
            tiled=True,
        ).astype(jnp.float32)
        input_grads.append(grad_input)
        updated = (qkv_acc, out_acc, up_acc, down_acc)
        grad_full = updated
    shards = (
        lax.psum_scatter(grad_full[0], "dp", scatter_dimension=1, tiled=True),
        lax.psum_scatter(grad_full[1], "dp", scatter_dimension=1, tiled=True),
        lax.psum_scatter(grad_full[2], "dp", scatter_dimension=1, tiled=True),
        lax.psum_scatter(grad_full[3], "dp", scatter_dimension=1, tiled=True),
    )
    gain_grad, shift_grad = (
        lax.psum_scatter(gain_acc, ("dp", "tensor"), scatter_dimension=2, tiled=True),
        lax.psum_scatter(shift_acc, ("dp", "tensor"), scatter_dimension=2, tiled=True),
    )
    return (
        jnp.concatenate(outputs, 0),
        jnp.concatenate(input_grads, 0),
        shards[0],
        shards[1],
        shards[2],
        shards[3],
        gain_grad,
        shift_grad,
    )


def solution(mesh):
    placed = (
        P(("dp", "tensor"), None),
        P("dp"),
        P("dp"),
        P(None, "dp", None, "tensor"),
        P(None, "dp", "tensor"),
        P(None, "dp", "tensor"),
        P(None, "dp", "tensor"),
        P(None, None, ("dp", "tensor")),
        P(None, None, ("dp", "tensor")),
        P(("dp", "tensor"), None),
    )
    results = (
        P(("dp", "tensor"), None),
        P(("dp", "tensor"), None),
        P(None, "dp", None, "tensor"),
        P(None, "dp", "tensor"),
        P(None, "dp", "tensor"),
        P(None, "dp", "tensor"),
        P(None, None, ("dp", "tensor")),
        P(None, None, ("dp", "tensor")),
    )
    n_dp, n_tensor = mesh.shape["dp"], mesh.shape["tensor"]
    if n_tensor != GROUPS or n_dp not in (8, 16):
        return jax.shard_map(
            general_local, mesh=mesh, in_specs=placed, out_specs=results, check_vma=False
        )
    fine = Mesh(mesh.devices.reshape(n_dp // 2, 2, 2, 2), AXES)
    names = {"dp": ("z", "x"), "tensor": ("y", "c")}

    def refine(spec):
        parts = []
        for entry in spec:
            entry = (entry,) if isinstance(entry, str) else entry
            parts.append(entry and sum((names[a] for a in entry), ()))
        return P(*parts)

    return jax.shard_map(
        partial(split_local, n_dp // 2),
        mesh=fine,
        in_specs=tuple(refine(s) for s in placed),
        out_specs=tuple(refine(s) for s in results),
        check_vma=False,
    )
```

```python
from functools import partial

import jax
import jax.numpy as jnp
from jax import lax
from jax.experimental import pallas as pl
from jax.experimental.pallas import tpu as pltpu
from jax.sharding import Mesh
from jax.sharding import PartitionSpec as P

D = 768
HEADS = 12
HEAD_DIM = 64
MICRO = 4
CHAINS_PART = 1
LENGTH = 160
GROUPS = 4
OWN = 4
EXTRA = 2
SLOTS = OWN + EXTRA
EXT_ROWS = EXTRA * LENGTH
OWN_ROWS = OWN * LENGTH
ROWS = SLOTS * LENGTH

EPS = 1e-12
NEG = -1e30
HIGH = lax.Precision.HIGHEST
BF = jnp.bfloat16
F32 = jnp.float32
MESH = pl.DeviceIdType.MESH
ANY = pl.BlockSpec(memory_space=pl.ANY)
AXES = ("z", "x", "y", "c")


def place():
    return tuple(lax.axis_index(a) for a in AXES)


def meet(nz, z, x, y, c):
    barrier = pltpu.get_barrier_semaphore()
    friends = [{"c": 1 - c}, {"y": 1 - y}, {"y": 1 - y, "c": 1 - c}, {"x": 1 - x}]
    friends += [{"z": lax.rem(z + dz, nz)} for dz in range(1, nz)]
    for friend in friends:
        pl.semaphore_signal(barrier, inc=1, device_id=friend, device_id_type=MESH)
    pl.semaphore_wait(barrier, len(friends))


CHUNK = 320
SUB = 80
N_CHUNK = ROWS // CHUNK
WIDE = 3 * LENGTH
GW = 256
PAIR = 3


def dot_nn(a, b):
    return lax.dot_general(a, b, (((1,), (0,)), ((), ())), preferred_element_type=F32)


def dot_nt(a, b):
    return lax.dot_general(a, b, (((1,), (1,)), ((), ())), preferred_element_type=F32)


def dot_tn(a, b):
    return lax.dot_general(a, b, (((0,), (0,)), ((), ())), preferred_element_type=F32)


def lanes(shape):
    return lax.broadcasted_iota(jnp.int32, shape, len(shape) - 1)


def head_mask(h, shape):
    lane = lanes(shape)
    return jnp.logical_and(lane >= h * HEAD_DIM, lane < (h + 1) * HEAD_DIM)


def stack_heads(rows):
    zero = jnp.zeros_like(rows)
    return jnp.concatenate([jnp.where(head_mask(h, rows.shape), rows, zero) for h in range(3)], 0)


def merge_heads(stack):
    out = jnp.zeros((LENGTH, GW), stack.dtype)
    for h in range(3):
        out = jnp.where(head_mask(h, out.shape), stack[h * LENGTH : (h + 1) * LENGTH], out)
    return out


def chunk_rows(i, size=CHUNK):
    return pl.ds(pl.multiple_of(i * size, size), size)


def loop(count, body):
    def step(i, carry):
        body(i)
        return carry

    lax.fori_loop(0, count, step, 0)


def weave(count, unit, extra):
    def body(i):
        unit(i)
        for k, step in extra.items():
            pl.when(i == k)(step)

    loop(count, body)


def out_columns(t, w, wo):
    low = lanes((D, 128)) < HEAD_DIM
    tiles = [w[0, t, :, GW * i + 128 : GW * i + 256].astype(F32) for i in range(3)]
    wo[t, :, :128] = jnp.where(low, pltpu.roll(tiles[0], 64, 1), tiles[1]).astype(BF)
    wo[t, :, 128:] = jnp.where(low, pltpu.roll(tiles[2], 64, 1), 0.0).astype(BF)


def attend(t, chains, lens, proj, probs, hout):
    rows = [chunk_rows(s, LENGTH) for s in chains]
    parts = [(proj[t, r, :GW], proj[t, r, GW : 2 * GW], proj[t, r, 2 * GW :]) for r in rows]
    lows, outs = [], []
    for s, (query, key, value) in zip(chains, parts):
        scores = dot_nt(key, stack_heads(query * jnp.asarray(0.125, BF)))
        valid = lax.broadcasted_iota(jnp.int32, (LENGTH, 1), 0) < lens(s)
        scores = jnp.where(valid, scores, NEG)
        expo = jnp.exp(scores - jnp.max(scores, 0, keepdims=True))
        lows.append((expo * (1.0 / jnp.sum(expo, 0, keepdims=True))).astype(BF))
        outs.append(merge_heads(dot_tn(lows[-1], value)).astype(BF))
    for s, r, low, out in zip(chains, rows, lows, outs):
        probs[t, s, :, :WIDE] = low
        hout[t, r] = out


def norm_rows(values):
    center = values - jnp.mean(values, -1, keepdims=True)
    factor = lax.rsqrt(jnp.mean(center * center, -1, keepdims=True) + EPS)
    return center * factor, factor


def norm_back(scaled, normed, factor):
    return factor * (
        scaled
        - jnp.mean(scaled, -1, keepdims=True)
        - normed * jnp.mean(scaled * normed, -1, keepdims=True)
    )


def pieces(i, body):
    def step(k):
        body(pl.ds(pl.multiple_of(i * CHUNK + k * SUB, SUB), SUB), k)

    loop(CHUNK // SUB, step)


def first_norm(i, x, hout, wo, prm, mid, n1, s1, mid_low):
    r = chunk_rows(i)
    attn = dot_nt(hout[0, r], wo[0])
    for t in range(1, GROUPS):
        attn += dot_nt(hout[t, r], wo[t])
    mid[r] = attn

    def piece(p, k):
        normed, factor = norm_rows(x[p].astype(F32) + mid[p])
        n1[p] = normed.astype(BF)
        s1[p] = jnp.broadcast_to(factor, (SUB, 128))
        value = normed * prm[0:1] + prm[2:3]
        mid[p] = value
        mid_low[p] = value.astype(BF)

    pieces(i, piece)


def feed_up(t, i, mid_low, w, act, slope):
    r = chunk_rows(i)
    for k in range(0, D, GW):
        up = dot_nn(mid_low[r], w[1, t, :, k : k + GW])
        cdf = 0.5 * (1.0 + lax.erf(up * 0.7071067811865476))
        act[t, r, k : k + GW] = (up * cdf).astype(BF)
        bell = 0.3989422804014327 * jnp.exp(-0.5 * up * up)
        slope[t, r, k : k + GW] = (cdf + up * bell).astype(BF)


def feed_down(i, t, act, w, mid):
    r = chunk_rows(i)
    mid[r] += dot_nt(act[t, r], w[2, t]) + dot_nt(act[t + 1, r], w[2, t + 1])


def second_norm(i, t, act, w, prm, mid, cot, mine, y_rows, d_ffn, ngrad):
    feed_down(i, t, act, w, mid)

    def piece(p, k):
        normed, factor = norm_rows(mid[p])
        y_rows[pl.ds(pl.multiple_of(k * SUB, SUB), SUB)] = (normed * prm[1:2] + prm[3:4]).astype(BF)
        grad = cot[p].astype(F32) * jnp.where(k < LENGTH // SUB, mine(2 * i), mine(2 * i + 1))
        ngrad[1:2] += jnp.sum(grad * normed, 0, keepdims=True)
        ngrad[3:4] += jnp.sum(grad, 0, keepdims=True)
        back = norm_back(grad * prm[1:2], normed, factor)
        mid[p] = back
        d_ffn[p] = back.astype(BF)

    pieces(i, piece)


def back_up(t, i, d_ffn, w, slope):
    r = chunk_rows(i)
    slope[t, r] = (dot_nn(d_ffn[r], w[2, t]) * slope[t, r].astype(F32)).astype(BF)


def back_first_norm(i, d_up, w, prm, mid, n1, s1, d_attn, ngrad):
    r = chunk_rows(i)
    grad = dot_nt(d_up[0, r], w[1, 0])
    for t in range(1, GROUPS):
        grad += dot_nt(d_up[t, r], w[1, t])
    mid[r] += grad

    def piece(p, k):
        grad = mid[p]
        normed = n1[p].astype(F32)
        ngrad[0:1] += jnp.sum(grad * normed, 0, keepdims=True)
        ngrad[2:3] += jnp.sum(grad, 0, keepdims=True)
        back = norm_back(grad * prm[0:1], normed, s1[p, 0:1])
        mid[p] = back
        d_attn[p] = back.astype(BF)

    pieces(i, piece)


def back_heads(t, i, d_attn, wo, d_heads):
    r = chunk_rows(i)
    d_heads[t, r, :GW] = dot_nn(d_attn[r], wo[t]).astype(BF)


def back_attend(t, chains, proj, probs, d_heads):
    rows = [chunk_rows(s, LENGTH) for s in chains]
    parts = [
        (proj[t, r, :GW], proj[t, r, GW : 2 * GW], proj[t, r, 2 * GW :], d_heads[t, r, :GW], probs[t, s, :, :WIDE])
        for s, r in zip(chains, rows)
    ]
    results = []
    for query, key, value, grad, low in parts:
        grad = stack_heads(grad)
        p = low.astype(F32)
        d_probs = dot_nt(value, grad)
        d_scores = (p * (d_probs - jnp.sum(d_probs * p, 0, keepdims=True))).astype(BF)
        d_query = merge_heads(dot_tn(d_scores, key)) * 0.125
        d_key = dot_nn(d_scores, stack_heads(query * jnp.asarray(0.125, BF)))
        results.append((d_query.astype(BF), d_key.astype(BF), dot_nn(low, grad).astype(BF)))
    for r, (d_query, d_key, d_value) in zip(rows, results):
        proj[t, r, :GW] = d_query
        proj[t, r, GW : 2 * GW] = d_key
        proj[t, r, 2 * GW :] = d_value


def grad_qkv_out(t, x, d_proj, d_attn, hout, store):
    low = lanes((D, 128)) < HEAD_DIM
    outs = dot_tn(d_attn[...], hout[t])
    places = (pltpu.roll(outs[:, :128], 64, 1), outs[:, :128], pltpu.roll(outs[:, 128:], 64, 1))
    for i in range(3):
        part = dot_tn(x[...], d_proj[t, :, GW * i : GW * (i + 1)])
        store(GW * i, part[:, :128])
        store(GW * i + 128, jnp.where(low, part[:, 128:], places[i]))


def back_input(i, d_proj, w, mid, out):
    r = chunk_rows(i)
    grad = mid[r]
    for t in range(GROUPS):
        grad += dot_nt(d_proj[t, r], w[0, t])
    out(r, grad)


def remote(src, dst, s_sem, r_sem, who):
    return pltpu.make_async_remote_copy(
        src_ref=src, dst_ref=dst, send_sem=s_sem, recv_sem=r_sem, device_id=who, device_id_type=MESH
    )


def arrived(ref, sem):
    remote(ref, ref, sem, sem, {"c": 1 - lax.axis_index("c")}).wait_recv()


def has_left(ref, sem):
    remote(ref, ref, sem, sem, {"c": 1 - lax.axis_index("c")}).wait_send()


def step_kernel(nz, rows,
                tags, lens, x_in, cot, qo, up, dn, gain, bias,
                y_own, g_own, own_out, oth_out, n_out, y_back, g_back, r_c,
                w, x, proj, probs, hout, wo, mid, n1, s1, mid_low, act, slope, d_ffn, gown, r_x, r_z,
                n_all, prm, ngrad, n_c, n_x, n_z,
                load_s, io_s, stage_s,
                ys_s, ys_r, zs_s, zs_r, xs_s, xs_r, cs_s, cs_r, ex_s, ex_r, na_s, na_r,
                c_s, c_r, x_s, x_r, z_s, z_r, y_s, y_r, e_s, e_r, ng_s, ng_r):
    z, xc, y, c = place()
    core, across, other_x = {"c": 1 - c}, {"y": 1 - y}, {"x": 1 - xc}
    diagonal = {"y": 1 - y, "c": 1 - c}
    mats = (qo, up, dn)
    lender = y != c
    home = (2 * y + c) * OWN
    away = (2 - y) * OWN + c * EXTRA

    def z_of(dz):
        return lax.rem(z + dz, nz)

    def chain(s):
        return jnp.where(s < OWN, home + s, away + s - OWN)

    def length_of(s):
        return lens[chain(s)]

    def mine(s):
        return jnp.where(tags[chain(s)] == y, 1.0, 0.0)

    def part(zz, xx):
        return pl.ds(pl.multiple_of((zz * 2 + xx) * rows, rows), rows)

    def group(g):
        return 2 * lax.rem(y + g, 2) + c

    def block(m, g, zz, xx):
        return w.at[m, group(g), part(zz, xx)]

    loads = [pltpu.make_async_copy(mats[m].at[y], block(m, 0, z, xc), load_s.at[m]) for m in range(3)]
    loads += [
        pltpu.make_async_copy(x_in, x.at[pl.ds(0, OWN_ROWS)], load_s.at[3]),
        pltpu.make_async_copy(cot, d_ffn.at[pl.ds(0, OWN_ROWS)], load_s.at[4]),
    ]
    for cp in loads:
        cp.start()
    me = ((z * 2 + xc) * 2 + y) * 2 + c
    cols = gain.shape[2]
    n_all[me] = jnp.zeros((8, 128), F32)
    for i in range(2):
        n_all[me, 2 * i : 2 * i + 2, :cols] = gain[i]
        n_all[me, 4 + 2 * i : 6 + 2 * i, :cols] = bias[i]
    ngrad[...] = jnp.zeros_like(ngrad)
    meet(nz, z, xc, y, c)

    def lend(arr, out, i, act_on):
        @pl.when(lender)
        def _():
            for j, (who, p) in enumerate(((across, c), (diagonal, 1 - c))):
                src = arr.at[pl.ds(pl.multiple_of(p * EXT_ROWS, EXT_ROWS), EXT_ROWS)]
                act_on(remote(src, out.at[pl.ds(OWN_ROWS, EXT_ROWS)], ex_s.at[i, j], ex_r.at[i], who))

    for m in range(3):
        remote(mats[m].at[1 - y], w.at[m, group(0), part(z, xc)], ys_s.at[m], ys_r.at[m], across).start()
    lend(x_in, x, 0, lambda cp: cp.start())
    lend(cot, d_ffn, 1, lambda cp: cp.start())

    def inside(zz):
        return jnp.logical_and(zz >= 0, zz < nz)

    def start(cp):
        cp.start()

    def recv(cp):
        cp.wait_recv()

    def hop(m, g, d, j, ref, act_on):
        to = z + 1 - 2 * d

        @pl.when(jnp.logical_and(inside(to), j < nz))
        def _():
            act_on(remote(ref, ref, zs_s.at[m, g, d, j], zs_r.at[m, g, d, j], {"z": to}))

    def x_copy(m, g, zz):
        ref = block(m, g, zz, xc)
        return remote(ref, ref, xs_s.at[m, g, zz], xs_r.at[m, g, zz], other_x)

    def c_copy(m, g, zz, xx):
        ref = block(m, g, zz, xx)
        return remote(ref, ref, cs_s.at[m, g, zz, xx], cs_r.at[m, g, zz, xx], core)

    def own_z(m):
        def body(g):
            @pl.when(g == 1)
            def _():
                arrived(block(m, 1, z, xc), ys_r.at[m])

            for d in range(2):
                hop(m, g, d, 1, block(m, g, z, xc), start)

        loop(2, body)

    def own_xc(m, g):
        x_copy(m, g, z).start()
        c_copy(m, g, z, xc).start()

    def z_event(m, j, first=0, last=2):
        def body(q):
            g, d = first + q // 2, q % 2
            zz = z - j + 2 * j * d

            @pl.when(inside(zz))
            def _():
                ref = block(m, g, zz, xc)
                arrived(ref, zs_r.at[m, g, d, j])
                hop(m, g, d, j + 1, ref, start)
                x_copy(m, g, zz).start()
                c_copy(m, g, zz, xc).start()

        loop(2 * (last - first), body)

    def x_event(m, j, first=0, last=2):
        def body(q):
            g, d = first + q // 2, q % 2
            zz = z - j + 2 * j * d

            @pl.when(jnp.logical_and(inside(zz), j + 1 > d))
            def _():
                arrived(block(m, g, zz, 1 - xc), xs_r.at[m, g, zz])
                c_copy(m, g, zz, 1 - xc).start()

        loop(2 * (last - first), body)

    def gathered(m, first=0, last=2):
        def body(i):
            g = first + i // (2 * nz)
            t = 2 * lax.rem(y + g, 2) + 1 - c
            zz, xx = (i // 2) % nz, i % 2
            arrived(w.at[m, t, part(zz, xx)], cs_r.at[m, g, zz, xx])

        loop(2 * nz * (last - first), body)

    def gather_sent(i):
        m, g = i // 2, i % 2
        ref = w.at[0, 0, pl.ds(0, rows)]
        for j in range(1, nz):
            for d in range(2):
                @pl.when(inside(z - (1 - 2 * d) * (j - 1)))
                def _():
                    hop(m, g, d, j, ref, lambda cp: cp.wait_send())
        for zz in range(nz):
            has_left(ref, xs_s.at[m, g, zz])
            for xx in range(2):
                has_left(ref, cs_s.at[m, g, zz, xx])

    def norm_hop(i, act_on):
        if i == 0:
            act_on(remote(n_all.at[me], n_all.at[me], na_s.at[0], na_r.at[0], core))
        elif i == 1:
            ref = n_all.at[pl.ds(me - c, 2)]
            act_on(remote(ref, ref, na_s.at[1], na_r.at[1], across))
        elif i == 2:
            ref = n_all.at[pl.ds(me - c - 2 * y, 4)]
            act_on(remote(ref, ref, na_s.at[2], na_r.at[2], other_x))
        else:
            ref = n_all.at[pl.ds(8 * z, 8)]
            for dz in range(1, nz):
                act_on(remote(ref, ref, na_s.at[2 + dz], na_r.at[2 + dz], {"z": z_of(dz)}))

    for m in range(3):
        loads[m].wait()
    norm_hop(0, start)
    own_z(0)
    for g in range(2):
        own_xc(0, g)
    z_event(0, 1)
    norm_hop(0, recv)
    norm_hop(1, start)
    for j in range(2, nz):
        z_event(0, j)
        if j == 2:
            own_z(1)
    if nz < 3:
        own_z(1)
    norm_hop(1, recv)
    norm_hop(2, start)
    for g in range(2):
        own_xc(1, g)
    x_event(0, 0)
    x_event(0, 1)
    for j in range(1, nz - 1):
        z_event(1, j)
        x_event(0, j + 1)
    own_z(2)
    norm_hop(2, recv)
    norm_hop(3, start)
    gathered(0)
    loads[3].wait()
    arrived(x.at[pl.ds(OWN_ROWS, EXT_ROWS)], ex_r.at[0])

    def projection(i):
        t, k = i // N_CHUNK, i % N_CHUNK
        r = chunk_rows(k)
        proj[t, r] = dot_nn(x[r], w[0, t]).astype(BF)

        @pl.when(k == N_CHUNK - 1)
        def _():
            out_columns(t, w, wo)

    def more_own():
        z_event(1, nz - 1)
        own_xc(2, 0)

    weave(
        GROUPS * N_CHUNK,
        projection,
        {0: more_own, 8: lambda: x_event(1, 0), 11: lambda: z_event(2, 1, 0, 1)},
    )
    per = SLOTS // PAIR

    def attention(i):
        attend(i // per, [(i % per) * PAIR + k for k in range(PAIR)], length_of, proj, probs, hout)

    weave(
        GROUPS * per,
        attention,
        {2: lambda: x_event(1, 1), 3: lambda: z_event(2, 2, 0, 1), 7: lambda: x_event(1, 2)},
    )
    norm_hop(3, recv)
    lane = lanes((2, D))
    gains, shifts = jnp.zeros((2, D), F32), jnp.zeros((2, D), F32)
    for d in range(8 * nz):
        within = jnp.logical_and(lane >= d * cols, lane < (d + 1) * cols)
        for name in range(2):
            piece = n_all[d, pl.ds(4 * name + 2 * y, 2), :]
            piece = jnp.concatenate([piece, jnp.zeros((2, D - 128), F32)], 1)
            piece = jnp.where(within, pltpu.roll(piece, d * cols, 1) if d else piece, 0.0)
            if name == 0:
                gains += piece
            else:
                shifts += piece
    prm[0:2] = gains
    prm[2:4] = shifts
    loop(N_CHUNK, lambda i: first_norm(i, x, hout, wo, prm, mid, n1, s1, mid_low))
    for j in range(3, nz):
        z_event(2, j, 0, 1)
        x_event(1, j)
    own_xc(2, 1)
    gathered(1)
    weave(
        GROUPS * N_CHUNK,
        lambda i: feed_up(i // N_CHUNK, i % N_CHUNK, mid_low, w, act, slope),
        {
            0: lambda: z_event(2, 1, 1, 2),
            2: lambda: x_event(2, 0, 0, 1),
            4: lambda: z_event(2, 2, 1, 2),
            7: lambda: x_event(2, 1, 0, 1),
        },
    )
    for j in range(2, nz):
        if j > 2:
            z_event(2, j, 1, 2)
        x_event(2, j, 0, 1)
    gathered(2, 0, 1)
    first_two = 2 * y
    last_two = 2 - first_two
    weave(
        N_CHUNK,
        lambda i: feed_down(i, first_two, act, w, mid),
        {0: lambda: x_event(2, 0, 1, 2), 2: lambda: x_event(2, 1, 1, 2)},
    )
    for j in range(2, nz):
        x_event(2, j, 1, 2)
    gathered(2, 1, 2)
    loads[4].wait()
    arrived(d_ffn.at[pl.ds(OWN_ROWS, EXT_ROWS)], ex_r.at[1])

    def y_stage(i):
        return gown.at[1, i // 2, pl.ds(pl.multiple_of((i % 2) * CHUNK, CHUNK), CHUNK)]

    def give_back(src, dst, i, act_on):
        dst = dst.at[pl.ds(pl.multiple_of(c * EXT_ROWS, EXT_ROWS), EXT_ROWS)]

        @pl.when(c == y)
        def _():
            act_on(remote(src, dst, e_s.at[i], e_r.at[i, c], across))

        @pl.when(c != y)
        def _():
            act_on(remote(src, dst, e_s.at[i], e_r.at[i, c], diagonal))

    def y_copy(i):
        return pltpu.make_async_copy(y_stage(i), y_own.at[pl.ds(i * CHUNK, CHUNK)], io_s.at[i])

    loop(
        N_CHUNK,
        lambda i: second_norm(
            i, last_two, act, w, prm, mid, d_ffn, mine, y_stage(i), d_ffn, ngrad
        ),
    )
    for i in range(2):
        y_copy(i).start()
    give_back(y_stage(2), y_back, 0, start)

    def spare(m, g):
        return gown.at[0, g] if m else act.at[2 * g + c, pl.ds(0, D)]

    def core_send(m, g):
        return remote(spare(m, g), r_c.at[m, g], c_s.at[m, g], c_r.at[m, g], core)

    def fetch(m, g):
        return pltpu.make_async_copy(r_c.at[m, g], act.at[2 * g + 1 - c, pl.ds(0, D)], stage_s.at[g])

    def core_fetch(m, g):
        arrived(r_c.at[m, g], c_r.at[m, g])
        fetch(m, g).start()

    def core_add(m, g):
        fetch(m, g).wait()

        def body(i):
            dz = i // 2 + 1
            zz = z_of(dz)
            xx = lax.rem(xc + 1 + i, 2)
            p = part(zz, xx)
            gown[m, g, p] = (gown[m, g, p].astype(F32) + act[2 * g + 1 - c, p].astype(F32)).astype(BF)

        loop(2 * nz, body)
        for dz in range(1, nz + 1):
            zz = z_of(dz)
            remote(gown.at[m, g, part(zz, 1 - xc)], r_x.at[m, g, zz], x_s.at[m, g, zz], x_r.at[m, g, zz], other_x).start()

    def sum_event(q):
        m = 2 - q // (2 * nz)
        g = (q // nz) % 2
        dz = q % nz + 1
        zz = z_of(dz)
        arrived(r_x.at[m, g, zz], x_r.at[m, g, zz])
        p = part(zz, xc)
        gown[m, g, p] = (gown[m, g, p].astype(F32) + r_x[m, g, zz].astype(F32)).astype(BF)

        @pl.when(dz < nz)
        def _():
            remote(gown.at[m, g, p], r_z.at[m, g, dz], z_s.at[m, g, dz], z_r.at[m, g, dz], {"z": zz}).start()

    def own_copy(m):
        return pltpu.make_async_copy(mid.at[pl.ds(OWN_ROWS + m * rows, rows)], own_out.at[m], io_s.at[3 + m])

    def last_send(m):
        return remote(mid_low.at[pl.ds(EXT_ROWS + m * rows, rows)], oth_out.at[m], y_s.at[m], y_r.at[m], across)

    def finish(m, g):
        total = gown[m, g, part(z, xc)].astype(F32)
        for dz in range(1, nz):
            arrived(r_z.at[m, g, dz], z_r.at[m, g, dz])
            total += r_z[m, g, dz].astype(F32)

        @pl.when(y == g)
        def _():
            mid[OWN_ROWS + m * rows : OWN_ROWS + (m + 1) * rows] = total
            own_copy(m).start()

        @pl.when(y != g)
        def _():
            mid_low[EXT_ROWS + m * rows : EXT_ROWS + (m + 1) * rows] = total.astype(BF)
            last_send(m).start()

    def slope_grads(m, a, b, extra):
        def unit(q):
            g = q % 2
            t = 2 * g + jnp.where(q < 2, 1 - c, c)
            dst = gown.at[jnp.where(q < 2, 0, m), g]
            for k in range(0, D, GW):
                dst[:, k : k + GW] = dot_tn(a[...], b[t, :, k : k + GW]).astype(BF)

            @pl.when(q < 2)
            def _():
                core_send(m, g).start()

        weave(4, unit, extra)

    def then(*steps):
        def run():
            for f, *args in steps:
                f(*args)

        return run

    def core_over(m):
        for g in range(2):
            core_send(m, g).wait_send()

    slope_grads(
        2,
        d_ffn,
        act,
        {
            1: then((core_fetch, 2, 0)),
            2: then((core_fetch, 2, 1), (core_add, 2, 0)),
            3: then((core_add, 2, 1), (core_over, 2)),
        },
    )

    def up_back(i):
        back_up(i // N_CHUNK, i % N_CHUNK, d_ffn, w, slope)

    weave(GROUPS * N_CHUNK, up_back, {7: then((sum_event, 0)), 11: then((sum_event, 1))})
    for i in range(2):
        y_copy(i).wait()
    has_left(y_stage(2), e_s.at[0])
    slope_grads(1, mid_low, slope, {1: then((sum_event, 2)), 3: then((sum_event, 3))})
    for g in range(2):
        core_fetch(1, g)
    weave(
        N_CHUNK,
        lambda i: back_first_norm(i, slope, w, prm, mid, n1, s1, d_ffn, ngrad),
        {
            0: then((core_add, 1, 0), (core_add, 1, 1), (core_over, 1)),
            1: then((sum_event, 4)),
            2: then((sum_event, 5)),
        },
    )

    def send_norms(i, act_on):
        if i == 0:
            act_on(remote(ngrad, n_c, ng_s.at[0], ng_r.at[0], core))
        elif i == 1:
            act_on(remote(n_c, n_x, ng_s.at[1], ng_r.at[1], other_x))
        elif i == 2:
            for dz in range(1, nz):
                act_on(remote(n_x, n_z.at[dz], ng_s.at[1 + dz], ng_r.at[1 + dz], {"z": z_of(dz)}))
        else:
            act_on(remote(n_out.at[y], n_out.at[y], ng_s.at[nz + 1], ng_r.at[nz + 1], across))

    send_norms(0, start)
    loop(GROUPS * N_CHUNK, lambda i: back_heads(i // N_CHUNK, i % N_CHUNK, d_ffn, wo, slope))
    sum_event(6)
    send_norms(0, recv)
    send_norms(0, lambda cp: cp.wait_send())
    n_c[...] += ngrad[...]
    send_norms(1, start)

    def attention_back(i):
        back_attend(i // per, [(i % per) * PAIR + k for k in range(PAIR)], proj, probs, slope)

        @pl.when(i % 2 == 1)
        def _():
            sum_event(7 + i // 2)

    loop(GROUPS * per, attention_back)
    seen = 7 + GROUPS * per // 2

    def qkv_grads(q):
        g = q % 2

        def store(col, value):
            value = value.astype(BF)

            @pl.when(q < 2)
            def _():
                spare(0, g)[:, col : col + 128] = value

            @pl.when(q >= 2)
            def _():
                gown[0, g, :, col : col + 128] = value

        grad_qkv_out(2 * g + jnp.where(q < 2, 1 - c, c), x, proj, d_ffn, hout, store)

        @pl.when(q < 2)
        def _():
            core_send(0, g).start()

    weave(
        4,
        qkv_grads,
        {
            1: then((sum_event, seen)),
            2: then((core_fetch, 0, 0), (core_fetch, 0, 1), (sum_event, seen + 1)),
            3: then((core_add, 0, 0), (core_add, 0, 1), (sum_event, seen + 2)),
        },
    )
    seen += 3
    def inputs_back(i):
        k = lax.rem(i + N_CHUNK - 1, N_CHUNK)

        def keep(r, grad):
            mid[r] = grad

            @pl.when(i == 0)
            def _():
                mid_low[:EXT_ROWS] = grad.astype(BF)

        back_input(k, proj, w, mid, keep)

        @pl.when(i == 0)
        def _():
            give_back(mid_low.at[pl.ds(0, EXT_ROWS)], g_back, 1, start)

    weave(N_CHUNK, inputs_back, {1: then((sum_event, seen)), 2: then((sum_event, seen + 1))})
    seen += 2
    g_copy = pltpu.make_async_copy(mid.at[pl.ds(0, OWN_ROWS)], g_own, io_s.at[2])
    g_copy.start()
    total_events = 6 * nz
    after = 4 * nz
    if seen < after:
        loop(after - seen, lambda q: sum_event(seen + q))
        seen = after
    for g in range(2):
        finish(2, g)
    loop(nz, lambda q: sum_event(after + q))
    send_norms(1, recv)
    send_norms(1, lambda cp: cp.wait_send())
    n_x[...] += n_c[...]
    send_norms(2, start)
    for g in range(2):
        finish(1, g)
    loop(nz, lambda q: sum_event(after + nz + q))
    total = n_x[...]
    for dz in range(1, nz):
        arrived(n_z.at[dz], ng_r.at[1 + dz])
        total += n_z[dz]
    n_out[y] = total
    send_norms(3, start)
    for g in range(2):
        finish(0, g)

    def sums_sent(i):
        m, g = i // 2, i % 2
        for dz in range(nz):
            if dz:
                has_left(r_x.at[0, 0, 0], z_s.at[m, g, dz])
            has_left(r_x.at[0, 0, 0], x_s.at[m, g, dz])

    loop(6, sums_sent)
    loop(6, gather_sent)
    for g in range(2):
        core_send(0, g).wait_send()
    for m in range(3):
        has_left(mats[m].at[0], ys_s.at[m])
        own_copy(m).wait()
        last_send(m).wait()
    lend(x_in, x, 0, lambda cp: cp.wait_send())
    lend(cot, d_ffn, 1, lambda cp: cp.wait_send())
    for i in range(4):
        norm_hop(i, lambda cp: cp.wait_send())
    send_norms(2, lambda cp: cp.wait_send())
    send_norms(3, lambda cp: cp.wait())
    g_copy.wait()
    has_left(mid_low.at[pl.ds(0, EXT_ROWS)], e_s.at[1])

    @pl.when(lender)
    def _():
        for i, dst in enumerate((y_back, g_back)):
            for j in range(2):
                arrived(dst.at[pl.ds(j * EXT_ROWS, EXT_ROWS)], e_r.at[i, j])


def run_step(nz, tags, lens, x_in, cot, qo, up, dn, gain, bias):
    rows = up.shape[1]
    V = pl.BlockSpec(memory_space=pltpu.VMEM)
    S = pl.BlockSpec(memory_space=pltpu.SMEM)
    sem = pltpu.SemaphoreType.DMA
    out = jax.ShapeDtypeStruct
    return pl.pallas_call(
        partial(step_kernel, nz, rows),
        out_shape=(
            out((OWN_ROWS, D), BF),
            out((OWN_ROWS, D), F32),
            out((3, rows, D), F32),
            out((3, rows, D), BF),
            out((2, 8, D), F32),
            out((OWN_ROWS, D), BF),
            out((OWN_ROWS, D), BF),
            out((3, 2, D, D), BF),
        ),
        in_specs=[S, S, ANY, ANY, ANY, ANY, ANY, V, V],
        out_specs=(ANY, ANY, ANY, ANY, V, ANY, ANY, ANY),
        scratch_shapes=[
            pltpu.VMEM((3, GROUPS, D, D), BF),
            pltpu.VMEM((ROWS, D), BF),
            pltpu.VMEM((GROUPS, ROWS, D), BF),
            pltpu.VMEM((GROUPS, SLOTS, LENGTH, 512), BF),
            pltpu.VMEM((GROUPS, ROWS, GW), BF),
            pltpu.VMEM((GROUPS, D, GW), BF),
            pltpu.VMEM((ROWS, D), F32),
            pltpu.VMEM((ROWS, D), BF),
            pltpu.VMEM((ROWS, 128), F32),
            pltpu.VMEM((ROWS, D), BF),
            pltpu.VMEM((GROUPS, ROWS, D), BF),
            pltpu.VMEM((GROUPS, ROWS, D), BF),
            pltpu.VMEM((ROWS, D), BF),
            pltpu.VMEM((3, 2, D, D), BF),
            pltpu.VMEM((3, 2, nz, rows, D), BF),
            pltpu.VMEM((3, 2, nz, rows, D), BF),
            pltpu.VMEM((8 * nz, 8, 128), F32),
            pltpu.VMEM((8, D), F32),
            pltpu.VMEM((8, D), F32),
            pltpu.VMEM((8, D), F32),
            pltpu.VMEM((8, D), F32),
            pltpu.VMEM((nz, 8, D), F32),
            sem((5,)), sem((6,)), sem((2,)),
            sem((3,)), sem((3,)),
            sem((3, 2, 2, nz)), sem((3, 2, 2, nz)),
            sem((3, 2, nz)), sem((3, 2, nz)),
            sem((3, 2, nz, 2)), sem((3, 2, nz, 2)),
            sem((2, 2)), sem((2,)),
            sem((nz + 2,)), sem((nz + 2,)),
            sem((3, 2)), sem((3, 2)),
            sem((3, 2, nz)), sem((3, 2, nz)),
            sem((3, 2, nz)), sem((3, 2, nz)),
            sem((3,)), sem((3,)),
            sem((2,)), sem((2, 2)),
            sem((nz + 2,)), sem((nz + 2,)),
        ],
        compiler_params=pltpu.CompilerParams(
            collective_id=0, has_side_effects=True, vmem_limit_bytes=67043328
        ),
        name="layer_step",
    )(tags, lens, x_in, cot, qo, up, dn, gain, bias)


def split_local(nz, x_in, tags, lengths, w_qkv, w_out, w_up, w_down, norm_gain, norm_bias, cotangent):
    z, x, y, c = place()
    rows = w_up.shape[1]
    cols = norm_gain.shape[2]
    qo = []
    for i in range(3):
        qo += [w_qkv[:, :, i], w_out[:, :, HEAD_DIM * i : HEAD_DIM * (i + 1)]]
    qo = jnp.concatenate(qo, -1)
    y_own, g_own, own_g, oth_g, n_sum, y_back, g_back, _ = run_step(
        nz, tags, lengths, x_in, cotangent, qo, w_up, w_down, norm_gain, norm_bias
    )
    kinds = lax.dynamic_slice_in_dim(tags, (2 * y + c) * OWN, OWN)
    mine = jnp.repeat(kinds == y, LENGTH)[:, None]
    y_out = jnp.where(mine, y_own, y_back)
    x_grad = jnp.where(mine, g_own, g_back.astype(F32))
    oth_g = oth_g.astype(F32)
    both = jnp.stack([jnp.where(y == 0, own_g, oth_g), jnp.where(y == 0, oth_g, own_g)])
    packed = both[:, 0].reshape(2, rows, 3, GW)
    me = ((z * 2 + x) * 2 + y) * 2 + c
    n_mine = lax.dynamic_slice_in_dim(n_sum, me * cols, cols, 2)
    return (
        y_out,
        x_grad,
        packed[..., : GW - HEAD_DIM],
        packed[..., GW - HEAD_DIM :].reshape(w_out.shape),
        both[:, 1],
        both[:, 2],
        n_mine[:, :2],
        n_mine[:, 2:4],
    )


def typed_map(operand, stacked, chain_kinds, pattern):

    def single(element):
        weight = lax.dynamic_index_in_dim(stacked, element[1], 0, keepdims=False)
        return jnp.einsum(pattern, element[0], weight, preferred_element_type=jnp.float32)

    return lax.map(single, (operand, chain_kinds))


def typed_grads(running, operand, partner, chain_kinds, pattern):

    def single(carry, element):
        product_term = jnp.einsum(
            pattern, element[0], element[1], preferred_element_type=jnp.float32
        )
        previous = lax.dynamic_index_in_dim(carry, element[2], 0, keepdims=False)
        return (
            lax.dynamic_update_index_in_dim(carry, previous + product_term, element[2], 0),
            None,
        )

    return lax.scan(single, running, (operand, partner, chain_kinds))[0]


def row_terms(operand, stacked, chain_kinds, pattern, row_count):
    result = typed_map(operand, stacked, chain_kinds, pattern)
    return result.reshape(row_count, result.shape[-1])


def old_norm_forward(values, gain_rows, shift_rows):
    center = values - jnp.mean(values, -1, keepdims=True)
    factor = lax.rsqrt(jnp.mean(center * center, -1, keepdims=True) + EPS)
    normed = center * factor
    return (normed * gain_rows + shift_rows, normed, factor)


def old_norm_backward(grad_out, normed, factor, gain_rows):
    scaled = grad_out * gain_rows
    mean_plain = jnp.mean(scaled, -1, keepdims=True)
    mean_normed = jnp.mean(scaled * normed, -1, keepdims=True)
    return factor * (scaled - mean_plain - normed * mean_normed)


def type_sums(onehot, values):
    return jnp.dot(onehot.T, values, precision=HIGH, preferred_element_type=jnp.float32)


def general_local(x_in, tags, lengths, w_qkv, w_out, w_up, w_down, norm_gain, norm_bias, cotangent):
    tp_count = lax.axis_size("tensor")
    tp_index = lax.axis_index("tensor")
    local_rows = CHAINS_PART * LENGTH
    batch_chains = tp_count * CHAINS_PART
    head_cols = w_qkv.shape[3]
    local_heads = head_cols // HEAD_DIM
    tag_grid = tags.reshape(tp_count, MICRO, CHAINS_PART)
    len_grid = lengths.reshape(tp_count, MICRO, CHAINS_PART)
    own_tags = lax.dynamic_index_in_dim(tag_grid, tp_index, 0, keepdims=False)
    gains, shifts = (
        lax.all_gather(norm_gain, ("dp", "tensor"), axis=2, tiled=True),
        lax.all_gather(norm_bias, ("dp", "tensor"), axis=2, tiled=True),
    )
    grad_full = (
        jnp.zeros((2, D, 3, head_cols), jnp.float32),
        jnp.zeros((2, D, head_cols), jnp.float32),
        jnp.zeros((2, D, w_up.shape[2]), jnp.float32),
        jnp.zeros((2, D, w_down.shape[2]), jnp.float32),
    )
    shards = (
        jnp.zeros(w_qkv.shape, jnp.float32),
        jnp.zeros(w_out.shape, jnp.float32),
        jnp.zeros(w_up.shape, jnp.float32),
        jnp.zeros(w_down.shape, jnp.float32),
    )
    gain_acc = jnp.zeros((2, 2, D), jnp.float32)
    shift_acc = jnp.zeros((2, 2, D), jnp.float32)
    outputs = []
    input_grads = []
    for micro_index in range(MICRO):
        held = (
            lax.all_gather(w_qkv, "dp", axis=1, tiled=True),
            lax.all_gather(w_out, "dp", axis=1, tiled=True),
            lax.all_gather(w_up, "dp", axis=1, tiled=True),
            lax.all_gather(w_down, "dp", axis=1, tiled=True),
        )
        qkv_w, out_w, up_w, down_w = held
        chain_kinds = tag_grid[:, micro_index].reshape(batch_chains)
        chain_lens = len_grid[:, micro_index].reshape(batch_chains)
        own_rows = x_in[micro_index * local_rows : (micro_index + 1) * local_rows]
        kinds_rows = jnp.repeat(own_tags[micro_index], LENGTH)
        heavy_rows = (kinds_rows == 0)[:, None]
        onehot = (kinds_rows[:, None] == jnp.arange(2)[None, :]).astype(jnp.float32)
        gain_mid = jnp.where(heavy_rows, gains[0, 0], gains[1, 0])
        shift_mid = jnp.where(heavy_rows, shifts[0, 0], shifts[1, 0])
        gain_end = jnp.where(heavy_rows, gains[0, 1], gains[1, 1])
        shift_end = jnp.where(heavy_rows, shifts[0, 1], shifts[1, 1])
        gathered = lax.all_gather(own_rows, "tensor", axis=0, tiled=True).reshape(
            batch_chains, LENGTH, D
        )
        projected = typed_map(gathered, qkv_w, chain_kinds, "ld,dkh->lkh").astype(jnp.bfloat16)
        query = projected[:, :, 0].reshape(batch_chains, LENGTH, local_heads, HEAD_DIM)
        keys_low = projected[:, :, 1].reshape(batch_chains, LENGTH, local_heads, HEAD_DIM)
        values_low = projected[:, :, 2].reshape(batch_chains, LENGTH, local_heads, HEAD_DIM)
        valid = (
            lax.broadcasted_iota(jnp.int32, (batch_chains, 1, 1, LENGTH), 3)
            < chain_lens[:, None, None, None]
        )
        scores = (
            jnp.einsum("cqhe,ckhe->chqk", query, keys_low, preferred_element_type=jnp.float32)
            * 0.125
        )
        scores = jnp.where(valid, scores, NEG)
        highest = jnp.max(scores, -1, keepdims=True)
        expo = jnp.exp(scores - highest)
        totals = jnp.sum(expo, -1, keepdims=True)
        probs = expo / totals
        log_total = highest + jnp.log(totals)
        heads_low = jnp.einsum(
            "chqk,ckhe->cqhe",
            probs.astype(jnp.bfloat16),
            values_low,
            preferred_element_type=jnp.float32,
        ).astype(jnp.bfloat16)
        heads_low = heads_low.reshape(batch_chains, LENGTH, head_cols)
        attn_sum = lax.psum_scatter(
            row_terms(
                heads_low, out_w, chain_kinds, "lh,dh->ld", lax.axis_size("tensor") * local_rows
            ).astype(jnp.bfloat16),
            "tensor",
            scatter_dimension=0,
            tiled=True,
        ).astype(jnp.float32)
        mid, normed_mid, factor_mid = old_norm_forward(
            own_rows.astype(jnp.float32) + attn_sum, gain_mid, shift_mid
        )
        mid_all = lax.all_gather(mid.astype(jnp.bfloat16), "tensor", axis=0, tiled=True).reshape(
            batch_chains, LENGTH, D
        )
        up_value = typed_map(mid_all, up_w, chain_kinds, "ld,df->lf")
        act_low = jax.nn.gelu(up_value, approximate=False).astype(jnp.bfloat16)
        ffn_sum = lax.psum_scatter(
            row_terms(
                act_low, down_w, chain_kinds, "lf,df->ld", lax.axis_size("tensor") * local_rows
            ).astype(jnp.bfloat16),
            "tensor",
            scatter_dimension=0,
            tiled=True,
        ).astype(jnp.float32)
        final, normed_end, factor_end = old_norm_forward(ffn_sum + mid, gain_end, shift_end)
        outputs.append(final.astype(jnp.bfloat16))
        base = grad_full
        grad_final = cotangent[micro_index * local_rows : (micro_index + 1) * local_rows].astype(
            jnp.float32
        )
        gain_acc = gain_acc.at[:, 1].add(type_sums(onehot, grad_final * normed_end))
        shift_acc = shift_acc.at[:, 1].add(type_sums(onehot, grad_final))
        grad_resid2 = old_norm_backward(grad_final, normed_end, factor_end, gain_end)
        grad_ffn = lax.all_gather(
            grad_resid2.astype(jnp.bfloat16), "tensor", axis=0, tiled=True
        ).reshape(batch_chains, LENGTH, D)
        grad_act = typed_map(grad_ffn, down_w, chain_kinds, "ld,df->lf")
        unused_value, gelu_back = jax.vjp(partial(jax.nn.gelu, approximate=False), up_value)
        grad_up = gelu_back(grad_act)[0].astype(jnp.bfloat16)
        down_acc = typed_grads(base[3], grad_ffn, act_low, chain_kinds, "ld,lf->df")
        up_acc = typed_grads(base[2], mid_all, grad_up, chain_kinds, "ld,lf->df")
        grad_mid = grad_resid2 + lax.psum_scatter(
            row_terms(
                grad_up, up_w, chain_kinds, "lf,df->ld", lax.axis_size("tensor") * local_rows
            ).astype(jnp.bfloat16),
            "tensor",
            scatter_dimension=0,
            tiled=True,
        ).astype(jnp.float32)
        gain_acc = gain_acc.at[:, 0].add(type_sums(onehot, grad_mid * normed_mid))
        shift_acc = shift_acc.at[:, 0].add(type_sums(onehot, grad_mid))
        grad_resid1 = old_norm_backward(grad_mid, normed_mid, factor_mid, gain_mid)
        grad_attn = lax.all_gather(
            grad_resid1.astype(jnp.bfloat16), "tensor", axis=0, tiled=True
        ).reshape(batch_chains, LENGTH, D)
        grad_heads = typed_map(grad_attn, out_w, chain_kinds, "ld,dh->lh").astype(jnp.bfloat16)
        out_acc = typed_grads(base[1], grad_attn, heads_low, chain_kinds, "ld,lh->dh")
        grad_heads = grad_heads.reshape(batch_chains, LENGTH, local_heads, HEAD_DIM)
        again = (
            jnp.einsum("cqhe,ckhe->chqk", query, keys_low, preferred_element_type=jnp.float32)
            * 0.125
        )
        probs_again = jnp.exp(jnp.where(valid, again, NEG) - log_total)
        grad_probs = jnp.einsum(
            "cqhe,ckhe->chqk", grad_heads, values_low, preferred_element_type=jnp.float32
        )
        inner = jnp.sum(grad_probs * probs_again, -1, keepdims=True)
        grad_scores = (probs_again * (grad_probs - inner)).astype(jnp.bfloat16)
        grad_query = (
            jnp.einsum("chqk,ckhe->cqhe", grad_scores, keys_low, preferred_element_type=jnp.float32)
            * 0.125
        ).astype(jnp.bfloat16)
        grad_keys = (
            jnp.einsum("chqk,cqhe->ckhe", grad_scores, query, preferred_element_type=jnp.float32)
            * 0.125
        ).astype(jnp.bfloat16)
        grad_values = jnp.einsum(
            "chqk,cqhe->ckhe",
            probs_again.astype(jnp.bfloat16),
            grad_heads,
            preferred_element_type=jnp.float32,
        ).astype(jnp.bfloat16)
        grad_proj = jnp.stack([grad_query, grad_keys, grad_values], 2).reshape(
            batch_chains, LENGTH, 3, head_cols
        )
        qkv_acc = typed_grads(base[0], gathered, grad_proj, chain_kinds, "ld,lkh->dkh")
        grad_input = grad_resid1 + lax.psum_scatter(
            row_terms(
                grad_proj, qkv_w, chain_kinds, "lkh,dkh->ld", lax.axis_size("tensor") * local_rows
            ).astype(jnp.bfloat16),
            "tensor",
            scatter_dimension=0,
            tiled=True,
        ).astype(jnp.float32)
        input_grads.append(grad_input)
        updated = (qkv_acc, out_acc, up_acc, down_acc)
        grad_full = updated
    shards = (
        lax.psum_scatter(grad_full[0], "dp", scatter_dimension=1, tiled=True),
        lax.psum_scatter(grad_full[1], "dp", scatter_dimension=1, tiled=True),
        lax.psum_scatter(grad_full[2], "dp", scatter_dimension=1, tiled=True),
        lax.psum_scatter(grad_full[3], "dp", scatter_dimension=1, tiled=True),
    )
    gain_grad, shift_grad = (
        lax.psum_scatter(gain_acc, ("dp", "tensor"), scatter_dimension=2, tiled=True),
        lax.psum_scatter(shift_acc, ("dp", "tensor"), scatter_dimension=2, tiled=True),
    )
    return (
        jnp.concatenate(outputs, 0),
        jnp.concatenate(input_grads, 0),
        shards[0],
        shards[1],
        shards[2],
        shards[3],
        gain_grad,
        shift_grad,
    )


def solution(mesh):
    placed = (
        P(("dp", "tensor"), None),
        P("dp"),
        P("dp"),
        P(None, "dp", None, "tensor"),
        P(None, "dp", "tensor"),
        P(None, "dp", "tensor"),
        P(None, "dp", "tensor"),
        P(None, None, ("dp", "tensor")),
        P(None, None, ("dp", "tensor")),
        P(("dp", "tensor"), None),
    )
    results = (
        P(("dp", "tensor"), None),
        P(("dp", "tensor"), None),
        P(None, "dp", None, "tensor"),
        P(None, "dp", "tensor"),
        P(None, "dp", "tensor"),
        P(None, "dp", "tensor"),
        P(None, None, ("dp", "tensor")),
        P(None, None, ("dp", "tensor")),
    )
    n_dp, n_tensor = mesh.shape["dp"], mesh.shape["tensor"]
    if n_tensor != GROUPS or n_dp not in (8, 16):
        return jax.shard_map(
            general_local, mesh=mesh, in_specs=placed, out_specs=results, check_vma=False
        )
    fine = Mesh(mesh.devices.reshape(n_dp // 2, 2, 2, 2), AXES)
    names = {"dp": ("z", "x"), "tensor": ("y", "c")}

    def refine(spec):
        parts = []
        for entry in spec:
            entry = (entry,) if isinstance(entry, str) else entry
            parts.append(entry and sum((names[a] for a in entry), ()))
        return P(*parts)

    return jax.shard_map(
        partial(split_local, n_dp // 2),
        mesh=fine,
        in_specs=tuple(refine(s) for s in placed),
        out_specs=tuple(refine(s) for s in results),
        check_vma=False,
    )
```

```python
from functools import partial

import jax
import jax.numpy as jnp
from jax import lax
from jax.experimental import pallas as pl
from jax.experimental.pallas import tpu as pltpu
from jax.sharding import Mesh
from jax.sharding import PartitionSpec as P

D = 768
HEADS = 12
HEAD_DIM = 64
MICRO = 4
CHAINS_PART = 1
LENGTH = 160
GROUPS = 4
OWN = 4
EXTRA = 2
SLOTS = OWN + EXTRA
EXT_ROWS = EXTRA * LENGTH
OWN_ROWS = OWN * LENGTH
ROWS = SLOTS * LENGTH

EPS = 1e-12
NEG = -1e30
HIGH = lax.Precision.HIGHEST
BF = jnp.bfloat16
F32 = jnp.float32
MESH = pl.DeviceIdType.MESH
ANY = pl.BlockSpec(memory_space=pl.ANY)
AXES = ("z", "x", "y", "c")


def place():
    return tuple(lax.axis_index(a) for a in AXES)


def meet(nz, z, x, y, c):
    barrier = pltpu.get_barrier_semaphore()
    friends = [{"c": 1 - c}, {"y": 1 - y}, {"y": 1 - y, "c": 1 - c}, {"x": 1 - x}]
    friends += [{"z": lax.rem(z + dz, nz)} for dz in range(1, nz)]
    for friend in friends:
        pl.semaphore_signal(barrier, inc=1, device_id=friend, device_id_type=MESH)
    pl.semaphore_wait(barrier, len(friends))


CHUNK = 320
SUB = 80
N_CHUNK = ROWS // CHUNK
WIDE = 3 * LENGTH
GW = 256
PAIR = 3


def dot_nn(a, b):
    return lax.dot_general(a, b, (((1,), (0,)), ((), ())), preferred_element_type=F32)


def dot_nt(a, b):
    return lax.dot_general(a, b, (((1,), (1,)), ((), ())), preferred_element_type=F32)


def dot_tn(a, b):
    return lax.dot_general(a, b, (((0,), (0,)), ((), ())), preferred_element_type=F32)


def lanes(shape):
    return lax.broadcasted_iota(jnp.int32, shape, len(shape) - 1)


def head_mask(h, shape):
    lane = lanes(shape)
    return jnp.logical_and(lane >= h * HEAD_DIM, lane < (h + 1) * HEAD_DIM)


def stack_heads(rows):
    zero = jnp.zeros_like(rows)
    return jnp.concatenate([jnp.where(head_mask(h, rows.shape), rows, zero) for h in range(3)], 0)


def merge_heads(stack):
    out = jnp.zeros((LENGTH, GW), stack.dtype)
    for h in range(3):
        out = jnp.where(head_mask(h, out.shape), stack[h * LENGTH : (h + 1) * LENGTH], out)
    return out


def chunk_rows(i, size=CHUNK):
    return pl.ds(pl.multiple_of(i * size, size), size)


def loop(count, body):
    def step(i, carry):
        body(i)
        return carry

    lax.fori_loop(0, count, step, 0)


def weave(count, unit, extra):
    def body(i):
        unit(i)
        for k, step in extra.items():
            pl.when(i == k)(step)

    loop(count, body)


def out_columns(t, w, wo):
    low = lanes((D, 128)) < HEAD_DIM
    tiles = [w[0, t, :, GW * i + 128 : GW * i + 256].astype(F32) for i in range(3)]
    wo[t, :, :128] = jnp.where(low, pltpu.roll(tiles[0], 64, 1), tiles[1]).astype(BF)
    wo[t, :, 128:] = jnp.where(low, pltpu.roll(tiles[2], 64, 1), 0.0).astype(BF)


def attend(t, chains, lens, proj, probs, hout):
    rows = [chunk_rows(s, LENGTH) for s in chains]
    parts = [(proj[t, r, :GW], proj[t, r, GW : 2 * GW], proj[t, r, 2 * GW :]) for r in rows]
    lows, outs = [], []
    for s, (query, key, value) in zip(chains, parts):
        scores = dot_nt(key, stack_heads(query * jnp.asarray(0.125, BF)))
        valid = lax.broadcasted_iota(jnp.int32, (LENGTH, 1), 0) < lens(s)
        scores = jnp.where(valid, scores, NEG)
        expo = jnp.exp(scores - jnp.max(scores, 0, keepdims=True))
        lows.append((expo * (1.0 / jnp.sum(expo, 0, keepdims=True))).astype(BF))
        outs.append(merge_heads(dot_tn(lows[-1], value)).astype(BF))
    for s, r, low, out in zip(chains, rows, lows, outs):
        probs[t, s, :, :WIDE] = low
        hout[t, r] = out


def norm_rows(values):
    center = values - jnp.mean(values, -1, keepdims=True)
    factor = lax.rsqrt(jnp.mean(center * center, -1, keepdims=True) + EPS)
    return center * factor, factor


def norm_back(scaled, normed, factor):
    return factor * (
        scaled
        - jnp.mean(scaled, -1, keepdims=True)
        - normed * jnp.mean(scaled * normed, -1, keepdims=True)
    )


def pieces(i, body):
    def step(k):
        body(pl.ds(pl.multiple_of(i * CHUNK + k * SUB, SUB), SUB), k)

    loop(CHUNK // SUB, step)


def first_norm(i, x, hout, wo, prm, mid, n1, s1, mid_low):
    r = chunk_rows(i)
    attn = dot_nt(hout[0, r], wo[0])
    for t in range(1, GROUPS):
        attn += dot_nt(hout[t, r], wo[t])
    mid[r] = attn

    def piece(p, k):
        normed, factor = norm_rows(x[p].astype(F32) + mid[p])
        n1[p] = normed.astype(BF)
        s1[p] = jnp.broadcast_to(factor, (SUB, 128))
        value = normed * prm[0:1] + prm[2:3]
        mid[p] = value
        mid_low[p] = value.astype(BF)

    pieces(i, piece)


def feed_up(t, i, mid_low, w, act, slope):
    r = chunk_rows(i)
    for k in range(0, D, GW):
        up = dot_nn(mid_low[r], w[1, t, :, k : k + GW])
        cdf = 0.5 * (1.0 + lax.erf(up * 0.7071067811865476))
        act[t, r, k : k + GW] = (up * cdf).astype(BF)
        bell = 0.3989422804014327 * jnp.exp(-0.5 * up * up)
        slope[t, r, k : k + GW] = (cdf + up * bell).astype(BF)


def feed_down(i, t, act, w, mid):
    r = chunk_rows(i)
    mid[r] += dot_nt(act[t, r], w[2, t]) + dot_nt(act[t + 1, r], w[2, t + 1])


def second_norm(i, t, act, w, prm, mid, cot, mine, y_rows, d_ffn, ngrad):
    feed_down(i, t, act, w, mid)

    def piece(p, k):
        normed, factor = norm_rows(mid[p])
        y_rows[pl.ds(pl.multiple_of(k * SUB, SUB), SUB)] = (normed * prm[1:2] + prm[3:4]).astype(BF)
        grad = cot[p].astype(F32) * jnp.where(k < LENGTH // SUB, mine(2 * i), mine(2 * i + 1))
        ngrad[1:2] += jnp.sum(grad * normed, 0, keepdims=True)
        ngrad[3:4] += jnp.sum(grad, 0, keepdims=True)
        back = norm_back(grad * prm[1:2], normed, factor)
        mid[p] = back
        d_ffn[p] = back.astype(BF)

    pieces(i, piece)


def back_up(t, i, d_ffn, w, slope):
    r = chunk_rows(i)
    slope[t, r] = (dot_nn(d_ffn[r], w[2, t]) * slope[t, r].astype(F32)).astype(BF)


def back_first_norm(i, d_up, w, prm, mid, n1, s1, d_attn, ngrad):
    r = chunk_rows(i)
    grad = dot_nt(d_up[0, r], w[1, 0])
    for t in range(1, GROUPS):
        grad += dot_nt(d_up[t, r], w[1, t])
    mid[r] += grad

    def piece(p, k):
        grad = mid[p]
        normed = n1[p].astype(F32)
        ngrad[0:1] += jnp.sum(grad * normed, 0, keepdims=True)
        ngrad[2:3] += jnp.sum(grad, 0, keepdims=True)
        back = norm_back(grad * prm[0:1], normed, s1[p, 0:1])
        mid[p] = back
        d_attn[p] = back.astype(BF)

    pieces(i, piece)


def back_heads(t, d_attn, wo, d_heads):
    d_heads[t, :, :GW] = dot_nn(d_attn[...], wo[t]).astype(BF)


def back_attend(t, chains, proj, probs, d_heads):
    rows = [chunk_rows(s, LENGTH) for s in chains]
    parts = [
        (proj[t, r, :GW], proj[t, r, GW : 2 * GW], proj[t, r, 2 * GW :], d_heads[t, r, :GW], probs[t, s, :, :WIDE])
        for s, r in zip(chains, rows)
    ]
    results = []
    for query, key, value, grad, low in parts:
        grad = stack_heads(grad)
        p = low.astype(F32)
        d_probs = dot_nt(value, grad)
        d_scores = (p * (d_probs - jnp.sum(d_probs * p, 0, keepdims=True))).astype(BF)
        d_query = merge_heads(dot_tn(d_scores, key)) * 0.125
        d_key = dot_nn(d_scores, stack_heads(query * jnp.asarray(0.125, BF)))
        results.append((d_query.astype(BF), d_key.astype(BF), dot_nn(low, grad).astype(BF)))
    for r, (d_query, d_key, d_value) in zip(rows, results):
        proj[t, r, :GW] = d_query
        proj[t, r, GW : 2 * GW] = d_key
        proj[t, r, 2 * GW :] = d_value


def grad_qkv_out(t, x, d_proj, d_attn, hout, store):
    low = lanes((D, 128)) < HEAD_DIM
    outs = dot_tn(d_attn[...], hout[t])
    places = (pltpu.roll(outs[:, :128], 64, 1), outs[:, :128], pltpu.roll(outs[:, 128:], 64, 1))
    for i in range(3):
        part = dot_tn(x[...], d_proj[t, :, GW * i : GW * (i + 1)])
        store(GW * i, part[:, :128])
        store(GW * i + 128, jnp.where(low, part[:, 128:], places[i]))


def back_input(i, d_proj, w, mid, out):
    r = chunk_rows(i)
    grad = mid[r]
    for t in range(GROUPS):
        grad += dot_nt(d_proj[t, r], w[0, t])
    out(r, grad)


def remote(src, dst, s_sem, r_sem, who):
    return pltpu.make_async_remote_copy(
        src_ref=src, dst_ref=dst, send_sem=s_sem, recv_sem=r_sem, device_id=who, device_id_type=MESH
    )


def arrived(ref, sem):
    remote(ref, ref, sem, sem, {"c": 1 - lax.axis_index("c")}).wait_recv()


def has_left(ref, sem):
    remote(ref, ref, sem, sem, {"c": 1 - lax.axis_index("c")}).wait_send()


def step_kernel(nz, rows,
                tags, lens, x_in, cot, qo, up, dn, gain, bias,
                y_out, g_out, qo_out, up_out, dn_out, n_out, y_back, g_back, r_c,
                w, x, proj, probs, hout, wo, mid, n1, s1, mid_low, act, slope, d_ffn, gown, r_x, r_z, oth,
                n_all, prm, ngrad, n_c, n_x, n_z,
                load_s, io_s, stage_s, out_s,
                ys_s, ys_r, zs_s, zs_r, xs_s, xs_r, cs_s, cs_r, ex_s, ex_r, na_s, na_r,
                c_s, c_r, x_s, x_r, z_s, z_r, y_s, y_r, e_s, e_r, ng_s, ng_r):
    z, xc, y, c = place()
    core, across, other_x = {"c": 1 - c}, {"y": 1 - y}, {"x": 1 - xc}
    diagonal = {"y": 1 - y, "c": 1 - c}
    mats = (qo, up, dn)
    lender = y != c
    home = (2 * y + c) * OWN
    away = (2 - y) * OWN + c * EXTRA

    def z_of(dz):
        return lax.rem(z + dz, nz)

    def chain(s):
        return jnp.where(s < OWN, home + s, away + s - OWN)

    def length_of(s):
        return lens[chain(s)]

    def mine(s):
        return jnp.where(tags[chain(s)] == y, 1.0, 0.0)

    def part(zz, xx):
        return pl.ds(pl.multiple_of((zz * 2 + xx) * rows, rows), rows)

    def group(g):
        return 2 * lax.rem(y + g, 2) + c

    def block(m, g, zz, xx):
        return w.at[m, group(g), part(zz, xx)]

    loads = [pltpu.make_async_copy(mats[m].at[y], block(m, 0, z, xc), load_s.at[m]) for m in range(3)]
    loads += [
        pltpu.make_async_copy(x_in, x.at[pl.ds(0, OWN_ROWS)], load_s.at[3]),
        pltpu.make_async_copy(cot, d_ffn.at[pl.ds(0, OWN_ROWS)], load_s.at[4]),
    ]
    for cp in loads:
        cp.start()
    me = ((z * 2 + xc) * 2 + y) * 2 + c
    cols = gain.shape[2]
    n_all[me] = jnp.zeros((8, 128), F32)
    for i in range(2):
        n_all[me, 2 * i : 2 * i + 2, :cols] = gain[i]
        n_all[me, 4 + 2 * i : 6 + 2 * i, :cols] = bias[i]
    ngrad[...] = jnp.zeros_like(ngrad)
    meet(nz, z, xc, y, c)

    def lend(arr, out, i, act_on):
        @pl.when(lender)
        def _():
            for j, (who, p) in enumerate(((across, c), (diagonal, 1 - c))):
                src = arr.at[pl.ds(pl.multiple_of(p * EXT_ROWS, EXT_ROWS), EXT_ROWS)]
                act_on(remote(src, out.at[pl.ds(OWN_ROWS, EXT_ROWS)], ex_s.at[i, j], ex_r.at[i], who))

    for m in range(3):
        remote(mats[m].at[1 - y], w.at[m, group(0), part(z, xc)], ys_s.at[m], ys_r.at[m], across).start()
    lend(x_in, x, 0, lambda cp: cp.start())
    lend(cot, d_ffn, 1, lambda cp: cp.start())

    def inside(zz):
        return jnp.logical_and(zz >= 0, zz < nz)

    def start(cp):
        cp.start()

    def recv(cp):
        cp.wait_recv()

    def hop(m, g, d, j, ref, act_on):
        to = z + 1 - 2 * d

        @pl.when(jnp.logical_and(inside(to), j < nz))
        def _():
            act_on(remote(ref, ref, zs_s.at[m, g, d, j], zs_r.at[m, g, d, j], {"z": to}))

    def x_copy(m, g, zz):
        ref = block(m, g, zz, xc)
        return remote(ref, ref, xs_s.at[m, g, zz], xs_r.at[m, g, zz], other_x)

    def c_copy(m, g, zz, xx):
        ref = block(m, g, zz, xx)
        return remote(ref, ref, cs_s.at[m, g, zz, xx], cs_r.at[m, g, zz, xx], core)

    def own_z(m):
        def body(g):
            @pl.when(g == 1)
            def _():
                arrived(block(m, 1, z, xc), ys_r.at[m])

            for d in range(2):
                hop(m, g, d, 1, block(m, g, z, xc), start)

        loop(2, body)

    def own_xc(m, g):
        x_copy(m, g, z).start()
        c_copy(m, g, z, xc).start()

    def z_event(m, j, first=0, last=2):
        def body(q):
            g, d = first + q // 2, q % 2
            zz = z - j + 2 * j * d

            @pl.when(inside(zz))
            def _():
                ref = block(m, g, zz, xc)
                arrived(ref, zs_r.at[m, g, d, j])
                hop(m, g, d, j + 1, ref, start)
                x_copy(m, g, zz).start()
                c_copy(m, g, zz, xc).start()

        loop(2 * (last - first), body)

    def x_event(m, j, first=0, last=2):
        def body(q):
            g, d = first + q // 2, q % 2
            zz = z - j + 2 * j * d

            @pl.when(jnp.logical_and(inside(zz), j + 1 > d))
            def _():
                arrived(block(m, g, zz, 1 - xc), xs_r.at[m, g, zz])
                c_copy(m, g, zz, 1 - xc).start()

        loop(2 * (last - first), body)

    def gathered(m, first=0, last=2):
        def body(i):
            g = first + i // (2 * nz)
            t = 2 * lax.rem(y + g, 2) + 1 - c
            zz, xx = (i // 2) % nz, i % 2
            arrived(w.at[m, t, part(zz, xx)], cs_r.at[m, g, zz, xx])

        loop(2 * nz * (last - first), body)

    def gather_sent(i):
        m, g = i // 2, i % 2
        ref = w.at[0, 0, pl.ds(0, rows)]
        for j in range(1, nz):
            for d in range(2):
                @pl.when(inside(z - (1 - 2 * d) * (j - 1)))
                def _():
                    hop(m, g, d, j, ref, lambda cp: cp.wait_send())
        for zz in range(nz):
            has_left(ref, xs_s.at[m, g, zz])
            for xx in range(2):
                has_left(ref, cs_s.at[m, g, zz, xx])

    def norm_hop(i, act_on):
        if i == 0:
            act_on(remote(n_all.at[me], n_all.at[me], na_s.at[0], na_r.at[0], core))
        elif i == 1:
            ref = n_all.at[pl.ds(me - c, 2)]
            act_on(remote(ref, ref, na_s.at[1], na_r.at[1], across))
        elif i == 2:
            ref = n_all.at[pl.ds(me - c - 2 * y, 4)]
            act_on(remote(ref, ref, na_s.at[2], na_r.at[2], other_x))
        else:
            ref = n_all.at[pl.ds(8 * z, 8)]
            for dz in range(1, nz):
                act_on(remote(ref, ref, na_s.at[2 + dz], na_r.at[2 + dz], {"z": z_of(dz)}))

    for m in range(3):
        loads[m].wait()
    norm_hop(0, start)
    own_z(0)
    for g in range(2):
        own_xc(0, g)
    z_event(0, 1)
    norm_hop(0, recv)
    norm_hop(1, start)
    for j in range(2, nz):
        z_event(0, j)
        if j == 2:
            own_z(1)
    if nz < 3:
        own_z(1)
    norm_hop(1, recv)
    norm_hop(2, start)
    for g in range(2):
        own_xc(1, g)
    x_event(0, 0)
    x_event(0, 1)
    for j in range(1, nz - 1):
        z_event(1, j)
        x_event(0, j + 1)
    own_z(2)
    norm_hop(2, recv)
    norm_hop(3, start)
    gathered(0)
    loads[3].wait()
    arrived(x.at[pl.ds(OWN_ROWS, EXT_ROWS)], ex_r.at[0])

    def projection(i):
        t, k = i // N_CHUNK, i % N_CHUNK
        r = chunk_rows(k)
        proj[t, r] = dot_nn(x[r], w[0, t]).astype(BF)

        @pl.when(k == N_CHUNK - 1)
        def _():
            out_columns(t, w, wo)

    def more_own():
        z_event(1, nz - 1)
        own_xc(2, 0)

    weave(
        GROUPS * N_CHUNK,
        projection,
        {0: more_own, 8: lambda: x_event(1, 0), 11: lambda: z_event(2, 1, 0, 1)},
    )
    per = SLOTS // PAIR

    def attention(i):
        attend(i // per, [(i % per) * PAIR + k for k in range(PAIR)], length_of, proj, probs, hout)

    weave(
        GROUPS * per,
        attention,
        {2: lambda: x_event(1, 1), 3: lambda: z_event(2, 2, 0, 1), 7: lambda: x_event(1, 2)},
    )
    norm_hop(3, recv)
    lane = lanes((2, D))
    gains, shifts = jnp.zeros((2, D), F32), jnp.zeros((2, D), F32)
    for d in range(8 * nz):
        within = jnp.logical_and(lane >= d * cols, lane < (d + 1) * cols)
        for name in range(2):
            piece = n_all[d, pl.ds(4 * name + 2 * y, 2), :]
            piece = jnp.concatenate([piece, jnp.zeros((2, D - 128), F32)], 1)
            piece = jnp.where(within, pltpu.roll(piece, d * cols, 1) if d else piece, 0.0)
            if name == 0:
                gains += piece
            else:
                shifts += piece
    prm[0:2] = gains
    prm[2:4] = shifts
    loop(N_CHUNK, lambda i: first_norm(i, x, hout, wo, prm, mid, n1, s1, mid_low))
    for j in range(3, nz):
        z_event(2, j, 0, 1)
        x_event(1, j)
    own_xc(2, 1)
    gathered(1)
    weave(
        GROUPS * N_CHUNK,
        lambda i: feed_up(i // N_CHUNK, i % N_CHUNK, mid_low, w, act, slope),
        {
            0: lambda: z_event(2, 1, 1, 2),
            2: lambda: x_event(2, 0, 0, 1),
            4: lambda: z_event(2, 2, 1, 2),
            7: lambda: x_event(2, 1, 0, 1),
        },
    )
    for j in range(2, nz):
        if j > 2:
            z_event(2, j, 1, 2)
        x_event(2, j, 0, 1)
    gathered(2, 0, 1)
    first_two = 2 * y
    last_two = 2 - first_two
    weave(
        N_CHUNK,
        lambda i: feed_down(i, first_two, act, w, mid),
        {0: lambda: x_event(2, 0, 1, 2), 2: lambda: x_event(2, 1, 1, 2)},
    )
    for j in range(2, nz):
        x_event(2, j, 1, 2)
    gathered(2, 1, 2)
    loads[4].wait()
    arrived(d_ffn.at[pl.ds(OWN_ROWS, EXT_ROWS)], ex_r.at[1])

    def y_stage(i):
        return gown.at[1, i // 2, pl.ds(pl.multiple_of((i % 2) * CHUNK, CHUNK), CHUNK)]

    def give_back(src, dst, i, act_on):
        dst = dst.at[pl.ds(pl.multiple_of(c * EXT_ROWS, EXT_ROWS), EXT_ROWS)]

        @pl.when(c == y)
        def _():
            act_on(remote(src, dst, e_s.at[i], e_r.at[i, c], across))

        @pl.when(c != y)
        def _():
            act_on(remote(src, dst, e_s.at[i], e_r.at[i, c], diagonal))

    def y_copy(i):
        return pltpu.make_async_copy(y_stage(i), y_out.at[pl.ds(i * CHUNK, CHUNK)], io_s.at[i])

    loop(
        N_CHUNK,
        lambda i: second_norm(
            i, last_two, act, w, prm, mid, d_ffn, mine, y_stage(i), d_ffn, ngrad
        ),
    )
    for i in range(2):
        y_copy(i).start()
    give_back(y_stage(2), y_back, 0, start)

    def spare(m, g):
        return gown.at[0, g] if m else act.at[2 * g + c, pl.ds(0, D)]

    def core_send(m, g):
        return remote(spare(m, g), r_c.at[m, g], c_s.at[m, g], c_r.at[m, g], core)

    def fetch(m, g):
        return pltpu.make_async_copy(r_c.at[m, g], act.at[2 * g + 1 - c, pl.ds(0, D)], stage_s.at[g])

    def core_fetch(m, g):
        arrived(r_c.at[m, g], c_r.at[m, g])
        fetch(m, g).start()

    middle = jnp.logical_and(z > 0, z < nz - 1)

    def target(k):
        down = jnp.where(nz - 1 - k > z, nz - 1 - k, nz - 2 - k)
        up = jnp.where(k < z, k, k + 1)
        return jnp.where(k == nz - 1, z, jnp.where(z < nz // 2, down, up))

    def core_add(m, g):
        fetch(m, g).wait()

        def body(i):
            p = part(target(i // 2), lax.rem(xc + 1 + i, 2))
            gown[m, g, p] = (gown[m, g, p].astype(F32) + act[2 * g + 1 - c, p].astype(F32)).astype(BF)

        loop(2 * nz, body)

        def over(k):
            zz = target(k)
            remote(gown.at[m, g, part(zz, 1 - xc)], r_x.at[m, g, zz], x_s.at[m, g, zz], x_r.at[m, g, zz], other_x).start()

        loop(nz, over)

    def sum_event(q):
        m = 2 - q // (2 * nz)
        g = (q // nz) % 2
        k = q % nz
        zz = target(k)
        arrived(r_x.at[m, g, zz], x_r.at[m, g, zz])
        p = part(zz, xc)
        gown[m, g, p] = (gown[m, g, p].astype(F32) + r_x[m, g, zz].astype(F32)).astype(BF)

        joins = jnp.logical_and(k == 0, jnp.logical_not(middle))
        waits = jnp.logical_and(k == 0, middle)
        beside = jnp.where(z == 0, 1, nz - 2)
        to = jnp.where(joins, beside, zz)
        slot = jnp.where(joins, beside, z)

        @pl.when(jnp.logical_and(k < nz - 1, jnp.logical_not(waits)))
        def _():
            remote(gown.at[m, g, p], r_z.at[m, g, slot], z_s.at[m, g, zz], z_r.at[m, g, slot], {"z": to}).start()

        @pl.when(jnp.logical_and(k == jnp.where(m == 0, 1, nz - 2), middle))
        def _():
            far = target(0)
            f = part(far, xc)
            arrived(r_z.at[m, g, z], z_r.at[m, g, z])
            gown[m, g, f] = (gown[m, g, f].astype(F32) + r_z[m, g, z].astype(F32)).astype(BF)
            remote(gown.at[m, g, f], r_z.at[m, g, z], z_s.at[m, g, far], z_r.at[m, g, z], {"z": far}).start()

    outs = (qo_out, up_out, dn_out)

    def out_stage(m, other):
        return mid.at[pl.ds(m * rows + (0 if other else OWN_ROWS), rows)]

    def out_copy(m, other):
        return pltpu.make_async_copy(out_stage(m, other), outs[m].at[1 - y if other else y], out_s.at[m, other])

    def last_send(m):
        return remote(mid_low.at[pl.ds(EXT_ROWS + m * rows, rows)], oth.at[m], y_s.at[m], y_r.at[m], across)

    def finish(m, g):
        total = gown[m, g, part(z, xc)].astype(F32)
        for dz in range(1, nz):
            source = z_of(dz)
            direct = jnp.abs(source - z) < nz - 1

            @pl.when(direct)
            def _():
                arrived(r_z.at[m, g, source], z_r.at[m, g, source])

            total += jnp.where(direct, r_z[m, g, source].astype(F32), 0.0)

        @pl.when(y == g)
        def _():
            out_stage(m, 0)[...] = total
            out_copy(m, 0).start()

        @pl.when(y != g)
        def _():
            mid_low[EXT_ROWS + m * rows : EXT_ROWS + (m + 1) * rows] = total.astype(BF)
            last_send(m).start()

    def slope_grads(m, a, b, extra):
        def unit(q):
            g = q % 2
            t = 2 * g + jnp.where(q < 2, 1 - c, c)
            dst = gown.at[jnp.where(q < 2, 0, m), g]
            for k in range(0, D, GW):
                dst[:, k : k + GW] = dot_tn(a[...], b[t, :, k : k + GW]).astype(BF)

            @pl.when(q < 2)
            def _():
                core_send(m, g).start()

        weave(4, unit, extra)

    def then(*steps):
        def run():
            for f, *args in steps:
                f(*args)

        return run

    def core_over(m):
        for g in range(2):
            core_send(m, g).wait_send()

    slope_grads(
        2,
        d_ffn,
        act,
        {
            1: then((core_fetch, 2, 0)),
            2: then((core_fetch, 2, 1), (core_add, 2, 0)),
            3: then((core_add, 2, 1), (core_over, 2)),
        },
    )

    def up_back(i):
        back_up(i // N_CHUNK, i % N_CHUNK, d_ffn, w, slope)

    weave(GROUPS * N_CHUNK, up_back, {7: then((sum_event, 0)), 11: then((sum_event, 1))})
    for i in range(2):
        y_copy(i).wait()
    has_left(y_stage(2), e_s.at[0])
    slope_grads(1, mid_low, slope, {1: then((sum_event, 2)), 3: then((sum_event, 3))})
    for g in range(2):
        core_fetch(1, g)
    weave(
        N_CHUNK,
        lambda i: back_first_norm(i, slope, w, prm, mid, n1, s1, d_ffn, ngrad),
        {
            0: then((core_add, 1, 0), (core_add, 1, 1), (core_over, 1)),
            1: then((sum_event, 4)),
            2: then((sum_event, 5)),
        },
    )

    def send_norms(i, act_on):
        if i == 0:
            act_on(remote(ngrad, n_c, ng_s.at[0], ng_r.at[0], core))
        elif i == 1:
            act_on(remote(n_c, n_x, ng_s.at[1], ng_r.at[1], other_x))
        elif i == 2:
            for dz in range(1, nz):
                act_on(remote(n_x, n_z.at[dz], ng_s.at[1 + dz], ng_r.at[1 + dz], {"z": z_of(dz)}))
        else:
            act_on(remote(n_out.at[y], n_out.at[y], ng_s.at[nz + 1], ng_r.at[nz + 1], across))

    send_norms(0, start)
    loop(GROUPS, lambda t: back_heads(t, d_ffn, wo, slope))
    sum_event(6)
    send_norms(0, recv)
    send_norms(0, lambda cp: cp.wait_send())
    n_c[...] += ngrad[...]
    send_norms(1, start)

    def attention_back(i):
        back_attend(i // per, [(i % per) * PAIR + k for k in range(PAIR)], proj, probs, slope)

        @pl.when(i % 2 == 1)
        def _():
            sum_event(7 + i // 2)

    loop(GROUPS * per, attention_back)
    seen = 7 + GROUPS * per // 2

    def qkv_grads(q):
        g, own = q // 2, q % 2

        def store(col, value):
            value = value.astype(BF)

            @pl.when(own == 0)
            def _():
                spare(0, g)[:, col : col + 128] = value

            @pl.when(own == 1)
            def _():
                gown[0, g, :, col : col + 128] = value

        grad_qkv_out(2 * g + jnp.where(own == 0, 1 - c, c), x, proj, d_ffn, hout, store)

        @pl.when(own == 0)
        def _():
            core_send(0, g).start()

    weave(
        4,
        qkv_grads,
        {
            0: then((sum_event, seen)),
            1: then((core_fetch, 0, 0), (sum_event, seen + 1)),
            2: then((core_add, 0, 0), (sum_event, seen + 2)),
            3: then((core_fetch, 0, 1), (core_add, 0, 1)),
        },
    )
    seen += 3

    def inputs_back(i):
        k = lax.rem(i + N_CHUNK - 1, N_CHUNK)

        def keep(r, grad):
            mid[r] = grad

            @pl.when(i == 0)
            def _():
                mid_low[:EXT_ROWS] = grad.astype(BF)

        back_input(k, proj, w, mid, keep)

        @pl.when(i == 0)
        def _():
            give_back(mid_low.at[pl.ds(0, EXT_ROWS)], g_back, 1, start)

    weave(N_CHUNK, inputs_back, {1: then((sum_event, seen)), 2: then((sum_event, seen + 1))})
    seen += 2
    after = 4 * nz
    if seen < after:
        loop(after - seen, lambda q: sum_event(seen + q))
    for g in range(2):
        finish(2, g)
    loop(2, lambda q: sum_event(after + q))

    trips = [
        pltpu.make_async_copy(g_back, proj.at[0, pl.ds(0, OWN_ROWS)], io_s.at[0]),
        pltpu.make_async_copy(y_out, proj.at[1, pl.ds(0, OWN_ROWS)], io_s.at[1]),
        pltpu.make_async_copy(y_back, proj.at[2, pl.ds(0, OWN_ROWS)], io_s.at[2]),
    ]
    y_again = pltpu.make_async_copy(proj.at[1, pl.ds(0, OWN_ROWS)], y_out, io_s.at[1])
    g_copy = pltpu.make_async_copy(mid.at[pl.ds(0, OWN_ROWS)], g_out, io_s.at[3])

    @pl.when(lender)
    def _():
        for i, dst in enumerate((y_back, g_back)):
            for j in range(2):
                arrived(dst.at[pl.ds(j * EXT_ROWS, EXT_ROWS)], e_r.at[i, j])
        for cp in trips:
            cp.start()
        for cp in trips:
            cp.wait()

        def merge(s):
            r = chunk_rows(s, LENGTH)
            keep = jnp.zeros((LENGTH, D), F32) + mine(s) > 0.5
            mid[r] = jnp.where(keep, mid[r], proj[0, r].astype(F32))
            proj[1, r] = jnp.where(keep, proj[1, r].astype(F32), proj[2, r].astype(F32)).astype(BF)

        loop(OWN, merge)
        y_again.start()

    g_copy.start()
    loop(nz - 2, lambda q: sum_event(after + 2 + q))
    send_norms(1, recv)
    send_norms(1, lambda cp: cp.wait_send())
    n_x[...] += n_c[...]
    send_norms(2, start)
    for g in range(2):
        finish(1, g)
    loop(nz - 1, lambda q: sum_event(after + nz + q))
    total = n_x[...]
    for dz in range(1, nz):
        arrived(n_z.at[dz], ng_r.at[1 + dz])
        total += n_z[dz]
    n_out[y] = total
    send_norms(3, start)
    finish(0, 0)
    sum_event(after + 2 * nz - 1)
    finish(0, 1)
    g_copy.wait()
    for m in (2, 1, 0):
        arrived(oth.at[m], y_r.at[m])
        out_stage(m, 1)[...] = oth[m].astype(F32)
        out_copy(m, 1).start()

    def sums_sent(i):
        m, g = i // 2, i % 2
        for zz in range(nz):
            @pl.when(z != zz)
            def _():
                has_left(r_x.at[0, 0, 0], z_s.at[m, g, zz])

            has_left(r_x.at[0, 0, 0], x_s.at[m, g, zz])

    loop(6, sums_sent)
    loop(6, gather_sent)
    for g in range(2):
        core_send(0, g).wait_send()
    for m in range(3):
        has_left(mats[m].at[0], ys_s.at[m])
        for other in range(2):
            out_copy(m, other).wait()
        last_send(m).wait_send()
    lend(x_in, x, 0, lambda cp: cp.wait_send())
    lend(cot, d_ffn, 1, lambda cp: cp.wait_send())
    for i in range(4):
        norm_hop(i, lambda cp: cp.wait_send())
    send_norms(2, lambda cp: cp.wait_send())
    send_norms(3, lambda cp: cp.wait())
    has_left(mid_low.at[pl.ds(0, EXT_ROWS)], e_s.at[1])

    @pl.when(lender)
    def _():
        y_again.wait()


def run_step(nz, tags, lens, x_in, cot, qo, up, dn, gain, bias):
    rows = up.shape[1]
    V = pl.BlockSpec(memory_space=pltpu.VMEM)
    S = pl.BlockSpec(memory_space=pltpu.SMEM)
    sem = pltpu.SemaphoreType.DMA
    out = jax.ShapeDtypeStruct
    return pl.pallas_call(
        partial(step_kernel, nz, rows),
        out_shape=(
            out((OWN_ROWS, D), BF),
            out((OWN_ROWS, D), F32),
            out((2, rows, D), F32),
            out((2, rows, D), F32),
            out((2, rows, D), F32),
            out((2, 8, D), F32),
            out((OWN_ROWS, D), BF),
            out((OWN_ROWS, D), BF),
            out((3, 2, D, D), BF),
        ),
        in_specs=[S, S, ANY, ANY, ANY, ANY, ANY, V, V],
        out_specs=(ANY, ANY, ANY, ANY, ANY, V, ANY, ANY, ANY),
        scratch_shapes=[
            pltpu.VMEM((3, GROUPS, D, D), BF),
            pltpu.VMEM((ROWS, D), BF),
            pltpu.VMEM((GROUPS, ROWS, D), BF),
            pltpu.VMEM((GROUPS, SLOTS, LENGTH, 512), BF),
            pltpu.VMEM((GROUPS, ROWS, GW), BF),
            pltpu.VMEM((GROUPS, D, GW), BF),
            pltpu.VMEM((ROWS, D), F32),
            pltpu.VMEM((ROWS, D), BF),
            pltpu.VMEM((ROWS, 128), F32),
            pltpu.VMEM((ROWS, D), BF),
            pltpu.VMEM((GROUPS, ROWS, D), BF),
            pltpu.VMEM((GROUPS, ROWS, D), BF),
            pltpu.VMEM((ROWS, D), BF),
            pltpu.VMEM((3, 2, D, D), BF),
            pltpu.VMEM((3, 2, nz, rows, D), BF),
            pltpu.VMEM((3, 2, nz, rows, D), BF),
            pltpu.VMEM((3, rows, D), BF),
            pltpu.VMEM((8 * nz, 8, 128), F32),
            pltpu.VMEM((8, D), F32),
            pltpu.VMEM((8, D), F32),
            pltpu.VMEM((8, D), F32),
            pltpu.VMEM((8, D), F32),
            pltpu.VMEM((nz, 8, D), F32),
            sem((5,)), sem((4,)), sem((2,)), sem((3, 2)),
            sem((3,)), sem((3,)),
            sem((3, 2, 2, nz)), sem((3, 2, 2, nz)),
            sem((3, 2, nz)), sem((3, 2, nz)),
            sem((3, 2, nz, 2)), sem((3, 2, nz, 2)),
            sem((2, 2)), sem((2,)),
            sem((nz + 2,)), sem((nz + 2,)),
            sem((3, 2)), sem((3, 2)),
            sem((3, 2, nz)), sem((3, 2, nz)),
            sem((3, 2, nz)), sem((3, 2, nz)),
            sem((3,)), sem((3,)),
            sem((2,)), sem((2, 2)),
            sem((nz + 2,)), sem((nz + 2,)),
        ],
        compiler_params=pltpu.CompilerParams(
            collective_id=0, has_side_effects=True, vmem_limit_bytes=67043328
        ),
        name="layer_step",
    )(tags, lens, x_in, cot, qo, up, dn, gain, bias)


def split_local(nz, x_in, tags, lengths, w_qkv, w_out, w_up, w_down, norm_gain, norm_bias, cotangent):
    z, x, y, c = place()
    rows = w_up.shape[1]
    cols = norm_gain.shape[2]
    qo = []
    for i in range(3):
        qo += [w_qkv[:, :, i], w_out[:, :, HEAD_DIM * i : HEAD_DIM * (i + 1)]]
    qo = jnp.concatenate(qo, -1)
    y_out, x_grad, qo_grad, up_grad, down_grad, n_sum, _, _, _ = run_step(
        nz, tags, lengths, x_in, cotangent, qo, w_up, w_down, norm_gain, norm_bias
    )
    packed = qo_grad.reshape(2, rows, 3, GW)
    me = ((z * 2 + x) * 2 + y) * 2 + c
    n_mine = lax.dynamic_slice_in_dim(n_sum, me * cols, cols, 2)
    return (
        y_out,
        x_grad,
        packed[..., : GW - HEAD_DIM],
        packed[..., GW - HEAD_DIM :].reshape(w_out.shape),
        up_grad,
        down_grad,
        n_mine[:, :2],
        n_mine[:, 2:4],
    )


def typed_map(operand, stacked, chain_kinds, pattern):

    def single(element):
        weight = lax.dynamic_index_in_dim(stacked, element[1], 0, keepdims=False)
        return jnp.einsum(pattern, element[0], weight, preferred_element_type=jnp.float32)

    return lax.map(single, (operand, chain_kinds))


def typed_grads(running, operand, partner, chain_kinds, pattern):

    def single(carry, element):
        product_term = jnp.einsum(
            pattern, element[0], element[1], preferred_element_type=jnp.float32
        )
        previous = lax.dynamic_index_in_dim(carry, element[2], 0, keepdims=False)
        return (
            lax.dynamic_update_index_in_dim(carry, previous + product_term, element[2], 0),
            None,
        )

    return lax.scan(single, running, (operand, partner, chain_kinds))[0]


def row_terms(operand, stacked, chain_kinds, pattern, row_count):
    result = typed_map(operand, stacked, chain_kinds, pattern)
    return result.reshape(row_count, result.shape[-1])


def old_norm_forward(values, gain_rows, shift_rows):
    center = values - jnp.mean(values, -1, keepdims=True)
    factor = lax.rsqrt(jnp.mean(center * center, -1, keepdims=True) + EPS)
    normed = center * factor
    return (normed * gain_rows + shift_rows, normed, factor)


def old_norm_backward(grad_out, normed, factor, gain_rows):
    scaled = grad_out * gain_rows
    mean_plain = jnp.mean(scaled, -1, keepdims=True)
    mean_normed = jnp.mean(scaled * normed, -1, keepdims=True)
    return factor * (scaled - mean_plain - normed * mean_normed)


def type_sums(onehot, values):
    return jnp.dot(onehot.T, values, precision=HIGH, preferred_element_type=jnp.float32)


def general_local(x_in, tags, lengths, w_qkv, w_out, w_up, w_down, norm_gain, norm_bias, cotangent):
    tp_count = lax.axis_size("tensor")
    tp_index = lax.axis_index("tensor")
    local_rows = CHAINS_PART * LENGTH
    batch_chains = tp_count * CHAINS_PART
    head_cols = w_qkv.shape[3]
    local_heads = head_cols // HEAD_DIM
    tag_grid = tags.reshape(tp_count, MICRO, CHAINS_PART)
    len_grid = lengths.reshape(tp_count, MICRO, CHAINS_PART)
    own_tags = lax.dynamic_index_in_dim(tag_grid, tp_index, 0, keepdims=False)
    gains, shifts = (
        lax.all_gather(norm_gain, ("dp", "tensor"), axis=2, tiled=True),
        lax.all_gather(norm_bias, ("dp", "tensor"), axis=2, tiled=True),
    )
    grad_full = (
        jnp.zeros((2, D, 3, head_cols), jnp.float32),
        jnp.zeros((2, D, head_cols), jnp.float32),
        jnp.zeros((2, D, w_up.shape[2]), jnp.float32),
        jnp.zeros((2, D, w_down.shape[2]), jnp.float32),
    )
    shards = (
        jnp.zeros(w_qkv.shape, jnp.float32),
        jnp.zeros(w_out.shape, jnp.float32),
        jnp.zeros(w_up.shape, jnp.float32),
        jnp.zeros(w_down.shape, jnp.float32),
    )
    gain_acc = jnp.zeros((2, 2, D), jnp.float32)
    shift_acc = jnp.zeros((2, 2, D), jnp.float32)
    outputs = []
    input_grads = []
    for micro_index in range(MICRO):
        held = (
            lax.all_gather(w_qkv, "dp", axis=1, tiled=True),
            lax.all_gather(w_out, "dp", axis=1, tiled=True),
            lax.all_gather(w_up, "dp", axis=1, tiled=True),
            lax.all_gather(w_down, "dp", axis=1, tiled=True),
        )
        qkv_w, out_w, up_w, down_w = held
        chain_kinds = tag_grid[:, micro_index].reshape(batch_chains)
        chain_lens = len_grid[:, micro_index].reshape(batch_chains)
        own_rows = x_in[micro_index * local_rows : (micro_index + 1) * local_rows]
        kinds_rows = jnp.repeat(own_tags[micro_index], LENGTH)
        heavy_rows = (kinds_rows == 0)[:, None]
        onehot = (kinds_rows[:, None] == jnp.arange(2)[None, :]).astype(jnp.float32)
        gain_mid = jnp.where(heavy_rows, gains[0, 0], gains[1, 0])
        shift_mid = jnp.where(heavy_rows, shifts[0, 0], shifts[1, 0])
        gain_end = jnp.where(heavy_rows, gains[0, 1], gains[1, 1])
        shift_end = jnp.where(heavy_rows, shifts[0, 1], shifts[1, 1])
        gathered = lax.all_gather(own_rows, "tensor", axis=0, tiled=True).reshape(
            batch_chains, LENGTH, D
        )
        projected = typed_map(gathered, qkv_w, chain_kinds, "ld,dkh->lkh").astype(jnp.bfloat16)
        query = projected[:, :, 0].reshape(batch_chains, LENGTH, local_heads, HEAD_DIM)
        keys_low = projected[:, :, 1].reshape(batch_chains, LENGTH, local_heads, HEAD_DIM)
        values_low = projected[:, :, 2].reshape(batch_chains, LENGTH, local_heads, HEAD_DIM)
        valid = (
            lax.broadcasted_iota(jnp.int32, (batch_chains, 1, 1, LENGTH), 3)
            < chain_lens[:, None, None, None]
        )
        scores = (
            jnp.einsum("cqhe,ckhe->chqk", query, keys_low, preferred_element_type=jnp.float32)
            * 0.125
        )
        scores = jnp.where(valid, scores, NEG)
        highest = jnp.max(scores, -1, keepdims=True)
        expo = jnp.exp(scores - highest)
        totals = jnp.sum(expo, -1, keepdims=True)
        probs = expo / totals
        log_total = highest + jnp.log(totals)
        heads_low = jnp.einsum(
            "chqk,ckhe->cqhe",
            probs.astype(jnp.bfloat16),
            values_low,
            preferred_element_type=jnp.float32,
        ).astype(jnp.bfloat16)
        heads_low = heads_low.reshape(batch_chains, LENGTH, head_cols)
        attn_sum = lax.psum_scatter(
            row_terms(
                heads_low, out_w, chain_kinds, "lh,dh->ld", lax.axis_size("tensor") * local_rows
            ).astype(jnp.bfloat16),
            "tensor",
            scatter_dimension=0,
            tiled=True,
        ).astype(jnp.float32)
        mid, normed_mid, factor_mid = old_norm_forward(
            own_rows.astype(jnp.float32) + attn_sum, gain_mid, shift_mid
        )
        mid_all = lax.all_gather(mid.astype(jnp.bfloat16), "tensor", axis=0, tiled=True).reshape(
            batch_chains, LENGTH, D
        )
        up_value = typed_map(mid_all, up_w, chain_kinds, "ld,df->lf")
        act_low = jax.nn.gelu(up_value, approximate=False).astype(jnp.bfloat16)
        ffn_sum = lax.psum_scatter(
            row_terms(
                act_low, down_w, chain_kinds, "lf,df->ld", lax.axis_size("tensor") * local_rows
            ).astype(jnp.bfloat16),
            "tensor",
            scatter_dimension=0,
            tiled=True,
        ).astype(jnp.float32)
        final, normed_end, factor_end = old_norm_forward(ffn_sum + mid, gain_end, shift_end)
        outputs.append(final.astype(jnp.bfloat16))
        base = grad_full
        grad_final = cotangent[micro_index * local_rows : (micro_index + 1) * local_rows].astype(
            jnp.float32
        )
        gain_acc = gain_acc.at[:, 1].add(type_sums(onehot, grad_final * normed_end))
        shift_acc = shift_acc.at[:, 1].add(type_sums(onehot, grad_final))
        grad_resid2 = old_norm_backward(grad_final, normed_end, factor_end, gain_end)
        grad_ffn = lax.all_gather(
            grad_resid2.astype(jnp.bfloat16), "tensor", axis=0, tiled=True
        ).reshape(batch_chains, LENGTH, D)
        grad_act = typed_map(grad_ffn, down_w, chain_kinds, "ld,df->lf")
        unused_value, gelu_back = jax.vjp(partial(jax.nn.gelu, approximate=False), up_value)
        grad_up = gelu_back(grad_act)[0].astype(jnp.bfloat16)
        down_acc = typed_grads(base[3], grad_ffn, act_low, chain_kinds, "ld,lf->df")
        up_acc = typed_grads(base[2], mid_all, grad_up, chain_kinds, "ld,lf->df")
        grad_mid = grad_resid2 + lax.psum_scatter(
            row_terms(
                grad_up, up_w, chain_kinds, "lf,df->ld", lax.axis_size("tensor") * local_rows
            ).astype(jnp.bfloat16),
            "tensor",
            scatter_dimension=0,
            tiled=True,
        ).astype(jnp.float32)
        gain_acc = gain_acc.at[:, 0].add(type_sums(onehot, grad_mid * normed_mid))
        shift_acc = shift_acc.at[:, 0].add(type_sums(onehot, grad_mid))
        grad_resid1 = old_norm_backward(grad_mid, normed_mid, factor_mid, gain_mid)
        grad_attn = lax.all_gather(
            grad_resid1.astype(jnp.bfloat16), "tensor", axis=0, tiled=True
        ).reshape(batch_chains, LENGTH, D)
        grad_heads = typed_map(grad_attn, out_w, chain_kinds, "ld,dh->lh").astype(jnp.bfloat16)
        out_acc = typed_grads(base[1], grad_attn, heads_low, chain_kinds, "ld,lh->dh")
        grad_heads = grad_heads.reshape(batch_chains, LENGTH, local_heads, HEAD_DIM)
        again = (
            jnp.einsum("cqhe,ckhe->chqk", query, keys_low, preferred_element_type=jnp.float32)
            * 0.125
        )
        probs_again = jnp.exp(jnp.where(valid, again, NEG) - log_total)
        grad_probs = jnp.einsum(
            "cqhe,ckhe->chqk", grad_heads, values_low, preferred_element_type=jnp.float32
        )
        inner = jnp.sum(grad_probs * probs_again, -1, keepdims=True)
        grad_scores = (probs_again * (grad_probs - inner)).astype(jnp.bfloat16)
        grad_query = (
            jnp.einsum("chqk,ckhe->cqhe", grad_scores, keys_low, preferred_element_type=jnp.float32)
            * 0.125
        ).astype(jnp.bfloat16)
        grad_keys = (
            jnp.einsum("chqk,cqhe->ckhe", grad_scores, query, preferred_element_type=jnp.float32)
            * 0.125
        ).astype(jnp.bfloat16)
        grad_values = jnp.einsum(
            "chqk,cqhe->ckhe",
            probs_again.astype(jnp.bfloat16),
            grad_heads,
            preferred_element_type=jnp.float32,
        ).astype(jnp.bfloat16)
        grad_proj = jnp.stack([grad_query, grad_keys, grad_values], 2).reshape(
            batch_chains, LENGTH, 3, head_cols
        )
        qkv_acc = typed_grads(base[0], gathered, grad_proj, chain_kinds, "ld,lkh->dkh")
        grad_input = grad_resid1 + lax.psum_scatter(
            row_terms(
                grad_proj, qkv_w, chain_kinds, "lkh,dkh->ld", lax.axis_size("tensor") * local_rows
            ).astype(jnp.bfloat16),
            "tensor",
            scatter_dimension=0,
            tiled=True,
        ).astype(jnp.float32)
        input_grads.append(grad_input)
        updated = (qkv_acc, out_acc, up_acc, down_acc)
        grad_full = updated
    shards = (
        lax.psum_scatter(grad_full[0], "dp", scatter_dimension=1, tiled=True),
        lax.psum_scatter(grad_full[1], "dp", scatter_dimension=1, tiled=True),
        lax.psum_scatter(grad_full[2], "dp", scatter_dimension=1, tiled=True),
        lax.psum_scatter(grad_full[3], "dp", scatter_dimension=1, tiled=True),
    )
    gain_grad, shift_grad = (
        lax.psum_scatter(gain_acc, ("dp", "tensor"), scatter_dimension=2, tiled=True),
        lax.psum_scatter(shift_acc, ("dp", "tensor"), scatter_dimension=2, tiled=True),
    )
    return (
        jnp.concatenate(outputs, 0),
        jnp.concatenate(input_grads, 0),
        shards[0],
        shards[1],
        shards[2],
        shards[3],
        gain_grad,
        shift_grad,
    )


def solution(mesh):
    placed = (
        P(("dp", "tensor"), None),
        P("dp"),
        P("dp"),
        P(None, "dp", None, "tensor"),
        P(None, "dp", "tensor"),
        P(None, "dp", "tensor"),
        P(None, "dp", "tensor"),
        P(None, None, ("dp", "tensor")),
        P(None, None, ("dp", "tensor")),
        P(("dp", "tensor"), None),
    )
    results = (
        P(("dp", "tensor"), None),
        P(("dp", "tensor"), None),
        P(None, "dp", None, "tensor"),
        P(None, "dp", "tensor"),
        P(None, "dp", "tensor"),
        P(None, "dp", "tensor"),
        P(None, None, ("dp", "tensor")),
        P(None, None, ("dp", "tensor")),
    )
    n_dp, n_tensor = mesh.shape["dp"], mesh.shape["tensor"]
    if n_tensor != GROUPS or n_dp != 8:
        return jax.shard_map(
            general_local, mesh=mesh, in_specs=placed, out_specs=results, check_vma=False
        )
    fine = Mesh(mesh.devices.reshape(n_dp // 2, 2, 2, 2), AXES)
    names = {"dp": ("z", "x"), "tensor": ("y", "c")}

    def refine(spec):
        parts = []
        for entry in spec:
            entry = (entry,) if isinstance(entry, str) else entry
            parts.append(entry and sum((names[a] for a in entry), ()))
        return P(*parts)

    return jax.shard_map(
        partial(split_local, n_dp // 2),
        mesh=fine,
        in_specs=tuple(refine(s) for s in placed),
        out_specs=tuple(refine(s) for s in results),
        check_vma=False,
    )
```

```python
from functools import partial

import jax
import jax.numpy as jnp
from jax import lax
from jax.experimental import pallas as pl
from jax.experimental.pallas import tpu as pltpu
from jax.sharding import Mesh
from jax.sharding import PartitionSpec as P

D = 768
HEADS = 12
HEAD_DIM = 64
MICRO = 4
CHAINS_PART = 1
LENGTH = 160
GROUPS = 4
OWN = 4
EXTRA = 2
SLOTS = OWN + EXTRA
EXT_ROWS = EXTRA * LENGTH
OWN_ROWS = OWN * LENGTH
ROWS = SLOTS * LENGTH

EPS = 1e-12
NEG = -1e30
HIGH = lax.Precision.HIGHEST
BF = jnp.bfloat16
F32 = jnp.float32
MESH = pl.DeviceIdType.MESH
ANY = pl.BlockSpec(memory_space=pl.ANY)
AXES = ("z", "x", "y", "c")


def place():
    return tuple(lax.axis_index(a) for a in AXES)


def meet(nz, z, x, y, c):
    barrier = pltpu.get_barrier_semaphore()
    friends = [{"c": 1 - c}, {"y": 1 - y}, {"y": 1 - y, "c": 1 - c}, {"x": 1 - x}]
    friends += [{"z": lax.rem(z + dz, nz)} for dz in range(1, nz)]
    for friend in friends:
        pl.semaphore_signal(barrier, inc=1, device_id=friend, device_id_type=MESH)
    pl.semaphore_wait(barrier, len(friends))


CHUNK = 320
SUB = 80
N_CHUNK = ROWS // CHUNK
WIDE = 3 * LENGTH
GW = 256
PAIR = 3


def dot_nn(a, b):
    return lax.dot_general(a, b, (((1,), (0,)), ((), ())), preferred_element_type=F32)


def dot_nt(a, b):
    return lax.dot_general(a, b, (((1,), (1,)), ((), ())), preferred_element_type=F32)


def dot_tn(a, b):
    return lax.dot_general(a, b, (((0,), (0,)), ((), ())), preferred_element_type=F32)


def lanes(shape):
    return lax.broadcasted_iota(jnp.int32, shape, len(shape) - 1)


def head_mask(h, shape):
    lane = lanes(shape)
    return jnp.logical_and(lane >= h * HEAD_DIM, lane < (h + 1) * HEAD_DIM)


def stack_heads(rows):
    zero = jnp.zeros_like(rows)
    return jnp.concatenate([jnp.where(head_mask(h, rows.shape), rows, zero) for h in range(3)], 0)


def merge_heads(stack):
    out = jnp.zeros((LENGTH, GW), stack.dtype)
    for h in range(3):
        out = jnp.where(head_mask(h, out.shape), stack[h * LENGTH : (h + 1) * LENGTH], out)
    return out


def chunk_rows(i, size=CHUNK):
    return pl.ds(pl.multiple_of(i * size, size), size)


def loop(count, body):
    def step(i, carry):
        body(i)
        return carry

    lax.fori_loop(0, count, step, 0)


def weave(count, unit, extra):
    def body(i):
        unit(i)
        for k, step in extra.items():
            pl.when(i == k)(step)

    loop(count, body)


def out_columns(t, w, wo):
    low = lanes((D, 128)) < HEAD_DIM
    tiles = [w[0, t, :, GW * i + 128 : GW * i + 256].astype(F32) for i in range(3)]
    wo[t, :, :128] = jnp.where(low, pltpu.roll(tiles[0], 64, 1), tiles[1]).astype(BF)
    wo[t, :, 128:] = jnp.where(low, pltpu.roll(tiles[2], 64, 1), 0.0).astype(BF)


def attend(t, chains, lens, proj, probs, hout):
    rows = [chunk_rows(s, LENGTH) for s in chains]
    parts = [(proj[t, r, :GW], proj[t, r, GW : 2 * GW], proj[t, r, 2 * GW :]) for r in rows]
    lows, outs = [], []
    for s, (query, key, value) in zip(chains, parts):
        scores = dot_nt(key, stack_heads(query * jnp.asarray(0.125, BF)))
        valid = lax.broadcasted_iota(jnp.int32, (LENGTH, 1), 0) < lens(s)
        scores = jnp.where(valid, scores, NEG)
        expo = jnp.exp(scores - jnp.max(scores, 0, keepdims=True))
        lows.append((expo * (1.0 / jnp.sum(expo, 0, keepdims=True))).astype(BF))
        outs.append(merge_heads(dot_tn(lows[-1], value)).astype(BF))
    for s, r, low, out in zip(chains, rows, lows, outs):
        probs[t, s, :, :WIDE] = low
        hout[t, r] = out


def norm_rows(values):
    center = values - jnp.mean(values, -1, keepdims=True)
    factor = lax.rsqrt(jnp.mean(center * center, -1, keepdims=True) + EPS)
    return center * factor, factor


def norm_back(scaled, normed, factor):
    return factor * (
        scaled
        - jnp.mean(scaled, -1, keepdims=True)
        - normed * jnp.mean(scaled * normed, -1, keepdims=True)
    )


def pieces(i, body):
    def step(k):
        body(pl.ds(pl.multiple_of(i * CHUNK + k * SUB, SUB), SUB), k)

    loop(CHUNK // SUB, step)


def first_norm(i, x, hout, wo, prm, mid, n1, s1, mid_low):
    r = chunk_rows(i)
    attn = dot_nt(hout[0, r], wo[0])
    for t in range(1, GROUPS):
        attn += dot_nt(hout[t, r], wo[t])
    mid[r] = attn

    def piece(p, k):
        normed, factor = norm_rows(x[p].astype(F32) + mid[p])
        n1[p] = normed.astype(BF)
        s1[p] = jnp.broadcast_to(factor, (SUB, 128))
        value = normed * prm[0:1] + prm[2:3]
        mid[p] = value
        mid_low[p] = value.astype(BF)

    pieces(i, piece)


def feed_up(t, i, mid_low, w, act, slope):
    r = chunk_rows(i)
    for k in range(0, D, GW):
        up = dot_nn(mid_low[r], w[1, t, :, k : k + GW])
        cdf = 0.5 * (1.0 + lax.erf(up * 0.7071067811865476))
        act[t, r, k : k + GW] = (up * cdf).astype(BF)
        bell = 0.3989422804014327 * jnp.exp(-0.5 * up * up)
        slope[t, r, k : k + GW] = (cdf + up * bell).astype(BF)


def feed_down(i, t, act, w, mid):
    r = chunk_rows(i)
    mid[r] += dot_nt(act[t, r], w[2, t]) + dot_nt(act[t + 1, r], w[2, t + 1])


def second_norm(i, t, act, w, prm, mid, cot, mine, y_rows, d_ffn, ngrad):
    feed_down(i, t, act, w, mid)

    def piece(p, k):
        normed, factor = norm_rows(mid[p])
        y_rows[pl.ds(pl.multiple_of(k * SUB, SUB), SUB)] = (normed * prm[1:2] + prm[3:4]).astype(BF)
        grad = cot[p].astype(F32) * jnp.where(k < LENGTH // SUB, mine(2 * i), mine(2 * i + 1))
        ngrad[1:2] += jnp.sum(grad * normed, 0, keepdims=True)
        ngrad[3:4] += jnp.sum(grad, 0, keepdims=True)
        back = norm_back(grad * prm[1:2], normed, factor)
        mid[p] = back
        d_ffn[p] = back.astype(BF)

    pieces(i, piece)


def back_up(t, i, d_ffn, w, slope):
    r = chunk_rows(i)
    slope[t, r] = (dot_nn(d_ffn[r], w[2, t]) * slope[t, r].astype(F32)).astype(BF)


def back_first_norm(i, d_up, w, prm, mid, n1, s1, d_attn, ngrad):
    r = chunk_rows(i)
    grad = dot_nt(d_up[0, r], w[1, 0])
    for t in range(1, GROUPS):
        grad += dot_nt(d_up[t, r], w[1, t])
    mid[r] += grad

    def piece(p, k):
        grad = mid[p]
        normed = n1[p].astype(F32)
        ngrad[0:1] += jnp.sum(grad * normed, 0, keepdims=True)
        ngrad[2:3] += jnp.sum(grad, 0, keepdims=True)
        back = norm_back(grad * prm[0:1], normed, s1[p, 0:1])
        mid[p] = back
        d_attn[p] = back.astype(BF)

    pieces(i, piece)


def back_heads(t, d_attn, wo, d_heads):
    d_heads[t, :, :GW] = dot_nn(d_attn[...], wo[t]).astype(BF)


def back_attend(t, chains, proj, probs, d_heads):
    rows = [chunk_rows(s, LENGTH) for s in chains]
    parts = [
        (proj[t, r, :GW], proj[t, r, GW : 2 * GW], proj[t, r, 2 * GW :], d_heads[t, r, :GW], probs[t, s, :, :WIDE])
        for s, r in zip(chains, rows)
    ]
    results = []
    for query, key, value, grad, low in parts:
        grad = stack_heads(grad)
        p = low.astype(F32)
        d_probs = dot_nt(value, grad)
        d_scores = (p * (d_probs - jnp.sum(d_probs * p, 0, keepdims=True))).astype(BF)
        d_query = merge_heads(dot_tn(d_scores, key)) * 0.125
        d_key = dot_nn(d_scores, stack_heads(query * jnp.asarray(0.125, BF)))
        results.append((d_query.astype(BF), d_key.astype(BF), dot_nn(low, grad).astype(BF)))
    for r, (d_query, d_key, d_value) in zip(rows, results):
        proj[t, r, :GW] = d_query
        proj[t, r, GW : 2 * GW] = d_key
        proj[t, r, 2 * GW :] = d_value


def grad_qkv_out(t, x, d_proj, d_attn, hout, store):
    low = lanes((D, 128)) < HEAD_DIM
    outs = dot_tn(d_attn[...], hout[t])
    places = (pltpu.roll(outs[:, :128], 64, 1), outs[:, :128], pltpu.roll(outs[:, 128:], 64, 1))
    for i in range(3):
        part = dot_tn(x[...], d_proj[t, :, GW * i : GW * (i + 1)])
        store(GW * i, part[:, :128])
        store(GW * i + 128, jnp.where(low, part[:, 128:], places[i]))


def back_input(i, d_proj, w, mid, out):
    r = chunk_rows(i)
    grad = mid[r]
    for t in range(GROUPS):
        grad += dot_nt(d_proj[t, r], w[0, t])
    out(r, grad)


def remote(src, dst, s_sem, r_sem, who):
    return pltpu.make_async_remote_copy(
        src_ref=src, dst_ref=dst, send_sem=s_sem, recv_sem=r_sem, device_id=who, device_id_type=MESH
    )


def arrived(ref, sem):
    remote(ref, ref, sem, sem, {"c": 1 - lax.axis_index("c")}).wait_recv()


def has_left(ref, sem):
    remote(ref, ref, sem, sem, {"c": 1 - lax.axis_index("c")}).wait_send()


def step_kernel(nz, rows,
                tags, lens, x_in, cot, qkv, wout, up, dn, gain, bias,
                y_out, g_out, qo_out, up_out, dn_out, n_out, y_back, g_back, r_c,
                w, x, proj, probs, hout, wo, mid, n1, s1, mid_low, act, slope, d_ffn, gown, r_x, r_z, oth, v_qkv, v_out, far,
                n_all, prm, ngrad, n_c, n_x, n_z,
                load_s, io_s, stage_s, out_s,
                ys_s, ys_r, zs_s, zs_r, xs_s, xs_r, cs_s, cs_r, ex_s, ex_r, na_s, na_r,
                c_s, c_r, x_s, x_r, z_s, z_r, y_s, y_r, e_s, e_r, ng_s, ng_r):
    z, xc, y, c = place()
    core, across, other_x = {"c": 1 - c}, {"y": 1 - y}, {"x": 1 - xc}
    diagonal = {"y": 1 - y, "c": 1 - c}
    mats = (None, up, dn)
    lender = y != c
    home = (2 * y + c) * OWN
    away = (2 - y) * OWN + c * EXTRA

    def z_of(dz):
        return lax.rem(z + dz, nz)

    def chain(s):
        return jnp.where(s < OWN, home + s, away + s - OWN)

    def length_of(s):
        return lens[chain(s)]

    def mine(s):
        return jnp.where(tags[chain(s)] == y, 1.0, 0.0)

    def part(zz, xx):
        return pl.ds(pl.multiple_of((zz * 2 + xx) * rows, rows), rows)

    def group(g):
        return 2 * lax.rem(y + g, 2) + c

    def block(m, g, zz, xx):
        return w.at[m, group(g), part(zz, xx)]

    loads = [pltpu.make_async_copy(mats[m].at[y], block(m, 0, z, xc), load_s.at[m]) for m in range(1, 3)]
    loads += [
        pltpu.make_async_copy(x_in, x.at[pl.ds(0, OWN_ROWS)], load_s.at[3]),
        pltpu.make_async_copy(cot, d_ffn.at[pl.ds(0, OWN_ROWS)], load_s.at[4]),
        pltpu.make_async_copy(qkv, v_qkv, load_s.at[0]),
        pltpu.make_async_copy(wout, v_out, load_s.at[5]),
    ]
    for cp in loads:
        cp.start()
    me = ((z * 2 + xc) * 2 + y) * 2 + c
    cols = gain.shape[2]
    n_all[me] = jnp.zeros((8, 128), F32)
    for i in range(2):
        n_all[me, 2 * i : 2 * i + 2, :cols] = gain[i]
        n_all[me, 4 + 2 * i : 6 + 2 * i, :cols] = bias[i]
    ngrad[...] = jnp.zeros_like(ngrad)
    for cp in loads[4:]:
        cp.wait()

    def packed(k):
        tail = v_out[k]
        cols = []
        for i in range(3):
            cols += [v_qkv[k, i], tail[:, HEAD_DIM * i : HEAD_DIM * (i + 1)]]
        return jnp.concatenate(cols, 1)

    w[0, group(0), part(z, xc)] = packed(y)
    far[...] = packed(1 - y)
    meet(nz, z, xc, y, c)

    def given(m):
        return mats[m].at[1 - y] if m else far

    def lend(arr, out, i, act_on):
        @pl.when(lender)
        def _():
            for j, (who, p) in enumerate(((across, c), (diagonal, 1 - c))):
                src = arr.at[pl.ds(pl.multiple_of(p * EXT_ROWS, EXT_ROWS), EXT_ROWS)]
                act_on(remote(src, out.at[pl.ds(OWN_ROWS, EXT_ROWS)], ex_s.at[i, j], ex_r.at[i], who))

    for m in range(3):
        remote(given(m), w.at[m, group(0), part(z, xc)], ys_s.at[m], ys_r.at[m], across).start()
    lend(x_in, x, 0, lambda cp: cp.start())
    lend(cot, d_ffn, 1, lambda cp: cp.start())

    def inside(zz):
        return jnp.logical_and(zz >= 0, zz < nz)

    def start(cp):
        cp.start()

    def recv(cp):
        cp.wait_recv()

    def hop(m, g, d, j, ref, act_on):
        to = z + 1 - 2 * d

        @pl.when(jnp.logical_and(inside(to), j < nz))
        def _():
            act_on(remote(ref, ref, zs_s.at[m, g, d, j], zs_r.at[m, g, d, j], {"z": to}))

    def x_copy(m, g, zz):
        ref = block(m, g, zz, xc)
        return remote(ref, ref, xs_s.at[m, g, zz], xs_r.at[m, g, zz], other_x)

    def c_copy(m, g, zz, xx):
        ref = block(m, g, zz, xx)
        return remote(ref, ref, cs_s.at[m, g, zz, xx], cs_r.at[m, g, zz, xx], core)

    def own_z(m):
        def body(g):
            @pl.when(g == 1)
            def _():
                arrived(block(m, 1, z, xc), ys_r.at[m])

            for d in range(2):
                hop(m, g, d, 1, block(m, g, z, xc), start)

        loop(2, body)

    def own_xc(m, g):
        x_copy(m, g, z).start()
        c_copy(m, g, z, xc).start()

    def z_event(m, j, first=0, last=2):
        def body(q):
            g, d = first + q // 2, q % 2
            zz = z - j + 2 * j * d

            @pl.when(inside(zz))
            def _():
                ref = block(m, g, zz, xc)
                arrived(ref, zs_r.at[m, g, d, j])
                hop(m, g, d, j + 1, ref, start)
                x_copy(m, g, zz).start()
                c_copy(m, g, zz, xc).start()

        loop(2 * (last - first), body)

    def x_event(m, j, first=0, last=2):
        def body(q):
            g, d = first + q // 2, q % 2
            zz = z - j + 2 * j * d

            @pl.when(jnp.logical_and(inside(zz), j + 1 > d))
            def _():
                arrived(block(m, g, zz, 1 - xc), xs_r.at[m, g, zz])
                c_copy(m, g, zz, 1 - xc).start()

        loop(2 * (last - first), body)

    def gathered(m, first=0, last=2):
        def body(i):
            g = first + i // (2 * nz)
            t = 2 * lax.rem(y + g, 2) + 1 - c
            zz, xx = (i // 2) % nz, i % 2
            arrived(w.at[m, t, part(zz, xx)], cs_r.at[m, g, zz, xx])

        loop(2 * nz * (last - first), body)

    def gather_sent(i):
        m, g = i // 2, i % 2
        ref = w.at[0, 0, pl.ds(0, rows)]
        for j in range(1, nz):
            for d in range(2):
                @pl.when(inside(z - (1 - 2 * d) * (j - 1)))
                def _():
                    hop(m, g, d, j, ref, lambda cp: cp.wait_send())
        for zz in range(nz):
            has_left(ref, xs_s.at[m, g, zz])
            for xx in range(2):
                has_left(ref, cs_s.at[m, g, zz, xx])

    def norm_hop(i, act_on):
        if i == 0:
            act_on(remote(n_all.at[me], n_all.at[me], na_s.at[0], na_r.at[0], core))
        elif i == 1:
            ref = n_all.at[pl.ds(me - c, 2)]
            act_on(remote(ref, ref, na_s.at[1], na_r.at[1], across))
        elif i == 2:
            ref = n_all.at[pl.ds(me - c - 2 * y, 4)]
            act_on(remote(ref, ref, na_s.at[2], na_r.at[2], other_x))
        else:
            ref = n_all.at[pl.ds(8 * z, 8)]
            for dz in range(1, nz):
                act_on(remote(ref, ref, na_s.at[2 + dz], na_r.at[2 + dz], {"z": z_of(dz)}))

    for cp in loads[:2]:
        cp.wait()
    norm_hop(0, start)
    own_z(0)
    for g in range(2):
        own_xc(0, g)
    z_event(0, 1)
    norm_hop(0, recv)
    norm_hop(1, start)
    for j in range(2, nz):
        z_event(0, j)
        if j == 2:
            own_z(1)
    if nz < 3:
        own_z(1)
    norm_hop(1, recv)
    norm_hop(2, start)
    for g in range(2):
        own_xc(1, g)
    x_event(0, 0)
    x_event(0, 1)
    for j in range(1, nz - 1):
        z_event(1, j)
        x_event(0, j + 1)
    own_z(2)
    norm_hop(2, recv)
    norm_hop(3, start)
    gathered(0)
    loads[2].wait()
    arrived(x.at[pl.ds(OWN_ROWS, EXT_ROWS)], ex_r.at[0])

    def projection(i):
        t, k = i // N_CHUNK, i % N_CHUNK
        r = chunk_rows(k)
        proj[t, r] = dot_nn(x[r], w[0, t]).astype(BF)

        @pl.when(k == N_CHUNK - 1)
        def _():
            out_columns(t, w, wo)

    def more_own():
        z_event(1, nz - 1)
        own_xc(2, 0)

    weave(
        GROUPS * N_CHUNK,
        projection,
        {0: more_own, 8: lambda: x_event(1, 0), 11: lambda: z_event(2, 1, 0, 1)},
    )
    per = SLOTS // PAIR

    def attention(i):
        attend(i // per, [(i % per) * PAIR + k for k in range(PAIR)], length_of, proj, probs, hout)

    weave(
        GROUPS * per,
        attention,
        {2: lambda: x_event(1, 1), 3: lambda: z_event(2, 2, 0, 1), 7: lambda: x_event(1, 2)},
    )
    norm_hop(3, recv)
    lane = lanes((2, D))
    gains, shifts = jnp.zeros((2, D), F32), jnp.zeros((2, D), F32)
    for d in range(8 * nz):
        within = jnp.logical_and(lane >= d * cols, lane < (d + 1) * cols)
        for name in range(2):
            piece = n_all[d, pl.ds(4 * name + 2 * y, 2), :]
            piece = jnp.concatenate([piece, jnp.zeros((2, D - 128), F32)], 1)
            piece = jnp.where(within, pltpu.roll(piece, d * cols, 1) if d else piece, 0.0)
            if name == 0:
                gains += piece
            else:
                shifts += piece
    prm[0:2] = gains
    prm[2:4] = shifts
    loop(N_CHUNK, lambda i: first_norm(i, x, hout, wo, prm, mid, n1, s1, mid_low))
    for j in range(3, nz):
        z_event(2, j, 0, 1)
        x_event(1, j)
    own_xc(2, 1)
    gathered(1)
    weave(
        GROUPS * N_CHUNK,
        lambda i: feed_up(i // N_CHUNK, i % N_CHUNK, mid_low, w, act, slope),
        {
            0: lambda: z_event(2, 1, 1, 2),
            2: lambda: x_event(2, 0, 0, 1),
            4: lambda: z_event(2, 2, 1, 2),
            7: lambda: x_event(2, 1, 0, 1),
        },
    )
    for j in range(2, nz):
        if j > 2:
            z_event(2, j, 1, 2)
        x_event(2, j, 0, 1)
    gathered(2, 0, 1)
    first_two = 2 * y
    last_two = 2 - first_two
    weave(
        N_CHUNK,
        lambda i: feed_down(i, first_two, act, w, mid),
        {0: lambda: x_event(2, 0, 1, 2), 2: lambda: x_event(2, 1, 1, 2)},
    )
    for j in range(2, nz):
        x_event(2, j, 1, 2)
    gathered(2, 1, 2)
    loads[3].wait()
    arrived(d_ffn.at[pl.ds(OWN_ROWS, EXT_ROWS)], ex_r.at[1])

    def y_stage(i):
        return gown.at[1, i // 2, pl.ds(pl.multiple_of((i % 2) * CHUNK, CHUNK), CHUNK)]

    def give_back(src, dst, i, act_on):
        dst = dst.at[pl.ds(pl.multiple_of(c * EXT_ROWS, EXT_ROWS), EXT_ROWS)]

        @pl.when(c == y)
        def _():
            act_on(remote(src, dst, e_s.at[i], e_r.at[i, c], across))

        @pl.when(c != y)
        def _():
            act_on(remote(src, dst, e_s.at[i], e_r.at[i, c], diagonal))

    def y_copy(i):
        return pltpu.make_async_copy(y_stage(i), y_out.at[pl.ds(i * CHUNK, CHUNK)], io_s.at[i])

    loop(
        N_CHUNK,
        lambda i: second_norm(
            i, last_two, act, w, prm, mid, d_ffn, mine, y_stage(i), d_ffn, ngrad
        ),
    )
    for i in range(2):
        y_copy(i).start()
    give_back(y_stage(2), y_back, 0, start)

    def spare(m, g):
        return gown.at[0, g] if m else act.at[2 * g + c, pl.ds(0, D)]

    def core_send(m, g):
        return remote(spare(m, g), r_c.at[m, g], c_s.at[m, g], c_r.at[m, g], core)

    def fetch(m, g):
        return pltpu.make_async_copy(r_c.at[m, g], act.at[2 * g + 1 - c, pl.ds(0, D)], stage_s.at[g])

    def core_fetch(m, g):
        arrived(r_c.at[m, g], c_r.at[m, g])
        fetch(m, g).start()

    middle = jnp.logical_and(z > 0, z < nz - 1)

    def target(k):
        down = jnp.where(nz - 1 - k > z, nz - 1 - k, nz - 2 - k)
        up = jnp.where(k < z, k, k + 1)
        return jnp.where(k == nz - 1, z, jnp.where(z < nz // 2, down, up))

    def core_add(m, g):
        fetch(m, g).wait()

        def body(i):
            p = part(target(i // 2), lax.rem(xc + 1 + i, 2))
            gown[m, g, p] = (gown[m, g, p].astype(F32) + act[2 * g + 1 - c, p].astype(F32)).astype(BF)

        loop(2 * nz, body)

        def over(k):
            zz = target(k)
            remote(gown.at[m, g, part(zz, 1 - xc)], r_x.at[m, g, zz], x_s.at[m, g, zz], x_r.at[m, g, zz], other_x).start()

        loop(nz, over)

    def sum_event(q):
        m = 2 - q // (2 * nz)
        g = (q // nz) % 2
        k = q % nz
        zz = target(k)
        arrived(r_x.at[m, g, zz], x_r.at[m, g, zz])
        p = part(zz, xc)
        gown[m, g, p] = (gown[m, g, p].astype(F32) + r_x[m, g, zz].astype(F32)).astype(BF)

        joins = jnp.logical_and(k == 0, jnp.logical_not(middle))
        waits = jnp.logical_and(k == 0, middle)
        beside = jnp.where(z == 0, 1, nz - 2)
        to = jnp.where(joins, beside, zz)
        slot = jnp.where(joins, beside, z)

        @pl.when(jnp.logical_and(k < nz - 1, jnp.logical_not(waits)))
        def _():
            remote(gown.at[m, g, p], r_z.at[m, g, slot], z_s.at[m, g, zz], z_r.at[m, g, slot], {"z": to}).start()

        @pl.when(jnp.logical_and(k == jnp.where(m == 0, 1, nz - 2), middle))
        def _():
            far = target(0)
            f = part(far, xc)
            arrived(r_z.at[m, g, z], z_r.at[m, g, z])
            gown[m, g, f] = (gown[m, g, f].astype(F32) + r_z[m, g, z].astype(F32)).astype(BF)
            remote(gown.at[m, g, f], r_z.at[m, g, z], z_s.at[m, g, far], z_r.at[m, g, z], {"z": far}).start()

    outs = (qo_out, up_out, dn_out)

    def out_stage(m, other):
        return mid.at[pl.ds(m * rows + (0 if other else OWN_ROWS), rows)]

    def out_copy(m, other):
        return pltpu.make_async_copy(out_stage(m, other), outs[m].at[1 - y if other else y], out_s.at[m, other])

    def last_send(m):
        return remote(mid_low.at[pl.ds(EXT_ROWS + m * rows, rows)], oth.at[m], y_s.at[m], y_r.at[m], across)

    def finish(m, g):
        total = gown[m, g, part(z, xc)].astype(F32)
        for dz in range(1, nz):
            source = z_of(dz)
            direct = jnp.abs(source - z) < nz - 1

            @pl.when(direct)
            def _():
                arrived(r_z.at[m, g, source], z_r.at[m, g, source])

            total += jnp.where(direct, r_z[m, g, source].astype(F32), 0.0)

        @pl.when(y == g)
        def _():
            out_stage(m, 0)[...] = total
            out_copy(m, 0).start()

        @pl.when(y != g)
        def _():
            mid_low[EXT_ROWS + m * rows : EXT_ROWS + (m + 1) * rows] = total.astype(BF)
            last_send(m).start()

    def slope_grads(m, a, b, extra):
        def unit(q):
            g = q % 2
            t = 2 * g + jnp.where(q < 2, 1 - c, c)
            dst = gown.at[jnp.where(q < 2, 0, m), g]
            for k in range(0, D, GW):
                dst[:, k : k + GW] = dot_tn(a[...], b[t, :, k : k + GW]).astype(BF)

            @pl.when(q < 2)
            def _():
                core_send(m, g).start()

        weave(4, unit, extra)

    def then(*steps):
        def run():
            for f, *args in steps:
                f(*args)

        return run

    def core_over(m):
        for g in range(2):
            core_send(m, g).wait_send()

    slope_grads(
        2,
        d_ffn,
        act,
        {
            1: then((core_fetch, 2, 0)),
            2: then((core_fetch, 2, 1), (core_add, 2, 0)),
            3: then((core_add, 2, 1), (core_over, 2)),
        },
    )

    def up_back(i):
        back_up(i // N_CHUNK, i % N_CHUNK, d_ffn, w, slope)

    weave(GROUPS * N_CHUNK, up_back, {7: then((sum_event, 0)), 11: then((sum_event, 1))})
    for i in range(2):
        y_copy(i).wait()
    has_left(y_stage(2), e_s.at[0])
    slope_grads(1, mid_low, slope, {1: then((sum_event, 2)), 3: then((sum_event, 3))})
    for g in range(2):
        core_fetch(1, g)
    weave(
        N_CHUNK,
        lambda i: back_first_norm(i, slope, w, prm, mid, n1, s1, d_ffn, ngrad),
        {
            0: then((core_add, 1, 0), (core_add, 1, 1), (core_over, 1)),
            1: then((sum_event, 4)),
            2: then((sum_event, 5)),
        },
    )

    def send_norms(i, act_on):
        if i == 0:
            act_on(remote(ngrad, n_c, ng_s.at[0], ng_r.at[0], core))
        elif i == 1:
            act_on(remote(n_c, n_x, ng_s.at[1], ng_r.at[1], other_x))
        elif i == 2:
            for dz in range(1, nz):
                act_on(remote(n_x, n_z.at[dz], ng_s.at[1 + dz], ng_r.at[1 + dz], {"z": z_of(dz)}))
        else:
            act_on(remote(n_out.at[y], n_out.at[y], ng_s.at[nz + 1], ng_r.at[nz + 1], across))

    send_norms(0, start)
    loop(GROUPS, lambda t: back_heads(t, d_ffn, wo, slope))
    sum_event(6)
    send_norms(0, recv)
    send_norms(0, lambda cp: cp.wait_send())
    n_c[...] += ngrad[...]
    send_norms(1, start)

    def attention_back(i):
        back_attend(i // per, [(i % per) * PAIR + k for k in range(PAIR)], proj, probs, slope)

        @pl.when(i % 2 == 1)
        def _():
            sum_event(7 + i // 2)

    loop(GROUPS * per, attention_back)
    seen = 7 + GROUPS * per // 2

    def qkv_grads(q):
        g, own = q // 2, q % 2

        def store(col, value):
            value = value.astype(BF)

            @pl.when(own == 0)
            def _():
                spare(0, g)[:, col : col + 128] = value

            @pl.when(own == 1)
            def _():
                gown[0, g, :, col : col + 128] = value

        grad_qkv_out(2 * g + jnp.where(own == 0, 1 - c, c), x, proj, d_ffn, hout, store)

        @pl.when(own == 0)
        def _():
            core_send(0, g).start()

    weave(
        4,
        qkv_grads,
        {
            0: then((sum_event, seen)),
            1: then((core_fetch, 0, 0), (sum_event, seen + 1)),
            2: then((core_add, 0, 0), (sum_event, seen + 2)),
            3: then((core_fetch, 0, 1), (core_add, 0, 1)),
        },
    )
    seen += 3

    def inputs_back(i):
        k = lax.rem(i + N_CHUNK - 1, N_CHUNK)

        def keep(r, grad):
            mid[r] = grad

            @pl.when(i == 0)
            def _():
                mid_low[:EXT_ROWS] = grad.astype(BF)

        back_input(k, proj, w, mid, keep)

        @pl.when(i == 0)
        def _():
            give_back(mid_low.at[pl.ds(0, EXT_ROWS)], g_back, 1, start)

    weave(N_CHUNK, inputs_back, {1: then((sum_event, seen)), 2: then((sum_event, seen + 1))})
    seen += 2
    after = 4 * nz
    if seen < after:
        loop(after - seen, lambda q: sum_event(seen + q))
    for g in range(2):
        finish(2, g)
    loop(2, lambda q: sum_event(after + q))

    trips = [
        pltpu.make_async_copy(g_back, proj.at[0, pl.ds(0, OWN_ROWS)], io_s.at[0]),
        pltpu.make_async_copy(y_out, proj.at[1, pl.ds(0, OWN_ROWS)], io_s.at[1]),
        pltpu.make_async_copy(y_back, proj.at[2, pl.ds(0, OWN_ROWS)], io_s.at[2]),
    ]
    y_again = pltpu.make_async_copy(proj.at[1, pl.ds(0, OWN_ROWS)], y_out, io_s.at[1])
    g_copy = pltpu.make_async_copy(mid.at[pl.ds(0, OWN_ROWS)], g_out, io_s.at[3])

    @pl.when(lender)
    def _():
        for i, dst in enumerate((y_back, g_back)):
            for j in range(2):
                arrived(dst.at[pl.ds(j * EXT_ROWS, EXT_ROWS)], e_r.at[i, j])
        for cp in trips:
            cp.start()
        for cp in trips:
            cp.wait()

        def merge(s):
            r = chunk_rows(s, LENGTH)
            keep = jnp.zeros((LENGTH, D), F32) + mine(s) > 0.5
            mid[r] = jnp.where(keep, mid[r], proj[0, r].astype(F32))
            proj[1, r] = jnp.where(keep, proj[1, r].astype(F32), proj[2, r].astype(F32)).astype(BF)

        loop(OWN, merge)
        y_again.start()

    g_copy.start()
    loop(nz - 2, lambda q: sum_event(after + 2 + q))
    send_norms(1, recv)
    send_norms(1, lambda cp: cp.wait_send())
    n_x[...] += n_c[...]
    send_norms(2, start)
    for g in range(2):
        finish(1, g)
    loop(nz - 1, lambda q: sum_event(after + nz + q))
    total = n_x[...]
    for dz in range(1, nz):
        arrived(n_z.at[dz], ng_r.at[1 + dz])
        total += n_z[dz]
    n_out[y] = total
    send_norms(3, start)
    finish(0, 0)
    sum_event(after + 2 * nz - 1)
    finish(0, 1)
    g_copy.wait()
    for m in (2, 1, 0):
        arrived(oth.at[m], y_r.at[m])
        out_stage(m, 1)[...] = oth[m].astype(F32)
        out_copy(m, 1).start()

    def sums_sent(i):
        m, g = i // 2, i % 2
        for zz in range(nz):
            @pl.when(z != zz)
            def _():
                has_left(r_x.at[0, 0, 0], z_s.at[m, g, zz])

            has_left(r_x.at[0, 0, 0], x_s.at[m, g, zz])

    loop(6, sums_sent)
    loop(6, gather_sent)
    for g in range(2):
        core_send(0, g).wait_send()
    for m in range(3):
        has_left(given(m), ys_s.at[m])
        for other in range(2):
            out_copy(m, other).wait()
        last_send(m).wait_send()
    lend(x_in, x, 0, lambda cp: cp.wait_send())
    lend(cot, d_ffn, 1, lambda cp: cp.wait_send())
    for i in range(4):
        norm_hop(i, lambda cp: cp.wait_send())
    send_norms(2, lambda cp: cp.wait_send())
    send_norms(3, lambda cp: cp.wait())
    has_left(mid_low.at[pl.ds(0, EXT_ROWS)], e_s.at[1])

    @pl.when(lender)
    def _():
        y_again.wait()


def run_step(nz, tags, lens, x_in, cot, qkv, wout, up, dn, gain, bias):
    rows = up.shape[1]
    V = pl.BlockSpec(memory_space=pltpu.VMEM)
    S = pl.BlockSpec(memory_space=pltpu.SMEM)
    sem = pltpu.SemaphoreType.DMA
    out = jax.ShapeDtypeStruct
    return pl.pallas_call(
        partial(step_kernel, nz, rows),
        out_shape=(
            out((OWN_ROWS, D), BF),
            out((OWN_ROWS, D), F32),
            out((2, rows, D), F32),
            out((2, rows, D), F32),
            out((2, rows, D), F32),
            out((2, 8, D), F32),
            out((OWN_ROWS, D), BF),
            out((OWN_ROWS, D), BF),
            out((3, 2, D, D), BF),
        ),
        in_specs=[S, S] + [ANY] * 6 + [V, V],
        out_specs=(ANY, ANY, ANY, ANY, ANY, V, ANY, ANY, ANY),
        scratch_shapes=[
            pltpu.VMEM((3, GROUPS, D, D), BF),
            pltpu.VMEM((ROWS, D), BF),
            pltpu.VMEM((GROUPS, ROWS, D), BF),
            pltpu.VMEM((GROUPS, SLOTS, LENGTH, 512), BF),
            pltpu.VMEM((GROUPS, ROWS, GW), BF),
            pltpu.VMEM((GROUPS, D, GW), BF),
            pltpu.VMEM((ROWS, D), F32),
            pltpu.VMEM((ROWS, D), BF),
            pltpu.VMEM((ROWS, 128), F32),
            pltpu.VMEM((ROWS, D), BF),
            pltpu.VMEM((GROUPS, ROWS, D), BF),
            pltpu.VMEM((GROUPS, ROWS, D), BF),
            pltpu.VMEM((ROWS, D), BF),
            pltpu.VMEM((3, 2, D, D), BF),
            pltpu.VMEM((3, 2, nz, rows, D), BF),
            pltpu.VMEM((3, 2, nz, rows, D), BF),
            pltpu.VMEM((3, rows, D), BF),
            pltpu.VMEM(qkv.shape, BF),
            pltpu.VMEM(wout.shape, BF),
            pltpu.VMEM((rows, D), BF),
            pltpu.VMEM((8 * nz, 8, 128), F32),
            pltpu.VMEM((8, D), F32),
            pltpu.VMEM((8, D), F32),
            pltpu.VMEM((8, D), F32),
            pltpu.VMEM((8, D), F32),
            pltpu.VMEM((nz, 8, D), F32),
            sem((6,)), sem((4,)), sem((2,)), sem((3, 2)),
            sem((3,)), sem((3,)),
            sem((3, 2, 2, nz)), sem((3, 2, 2, nz)),
            sem((3, 2, nz)), sem((3, 2, nz)),
            sem((3, 2, nz, 2)), sem((3, 2, nz, 2)),
            sem((2, 2)), sem((2,)),
            sem((nz + 2,)), sem((nz + 2,)),
            sem((3, 2)), sem((3, 2)),
            sem((3, 2, nz)), sem((3, 2, nz)),
            sem((3, 2, nz)), sem((3, 2, nz)),
            sem((3,)), sem((3,)),
            sem((2,)), sem((2, 2)),
            sem((nz + 2,)), sem((nz + 2,)),
        ],
        compiler_params=pltpu.CompilerParams(
            collective_id=0, has_side_effects=True, vmem_limit_bytes=67043328
        ),
        name="layer_step",
    )(tags, lens, x_in, cot, qkv, wout, up, dn, gain, bias)


def deliver_kernel(cols, y_in, g_in, qo, up_in, dn_in, sums,
                   y_out, g_out, qkv_out, wout_out, up_out, dn_out, gain_out, bias_out,
                   v_y, v_g, v_qo, v_up, v_dn, v_qkv, v_out, in_s, out_s):
    through = [(up_in, v_up, up_out), (dn_in, v_dn, dn_out)]
    for k in range(OWN):
        r = pl.ds(k * LENGTH, LENGTH)
        through.append((g_in.at[r], v_g.at[r], g_out.at[r]))
    for k in range(2):
        r = pl.ds(k * CHUNK, CHUNK)
        through.append((y_in.at[r], v_y.at[r], y_out.at[r]))
    n = len(through)
    first = pltpu.make_async_copy(qo, v_qo, in_s.at[n])
    first.start()
    loads, stores = [], []
    for i, (src, via, dst) in enumerate(through):
        loads.append(pltpu.make_async_copy(src, via, in_s.at[i]))
        stores.append(pltpu.make_async_copy(via, dst, out_s.at[i]))
        loads[-1].start()
    z, x, y, c = place()
    me = ((z * 2 + x) * 2 + y) * 2 + c
    for k in range(2):
        turned = pltpu.roll(sums[k], lax.rem(D - me * cols, D), 1)
        gain_out[k] = turned[0:2, :cols]
        bias_out[k] = turned[2:4, :cols]
    first.wait()
    for k in range(2):
        tail = []
        for i in range(3):
            v_qkv[k, i] = v_qo[k, :, GW * i : GW * i + GW - HEAD_DIM]
            tail.append(v_qo[k, :, GW * (i + 1) - HEAD_DIM : GW * (i + 1)])
        v_out[k] = jnp.concatenate(tail, 1)
    stores.append(pltpu.make_async_copy(v_qkv, qkv_out, out_s.at[n]))
    stores.append(pltpu.make_async_copy(v_out, wout_out, out_s.at[n + 1]))
    for i in range(n):
        loads[i].wait()
        stores[i].start()
    for cp in stores[n:]:
        cp.start()
    for cp in stores:
        cp.wait()


def deliver(cols, y_in, g_in, qo, up_in, dn_in, sums):
    rows = qo.shape[1]
    V = pl.BlockSpec(memory_space=pltpu.VMEM)
    sem = pltpu.SemaphoreType.DMA
    out = jax.ShapeDtypeStruct
    width = GW - HEAD_DIM
    shapes = [((2, 3, rows, width), F32), ((2, rows, width), F32)]
    whole = [(y_in.shape, BF), (g_in.shape, F32), (qo.shape, F32), (qo.shape, F32), (qo.shape, F32)]
    return pl.pallas_call(
        partial(deliver_kernel, cols),
        out_shape=tuple(
            out(*p) for p in whole[:2] + shapes + whole[3:] + [((2, 2, cols), F32)] * 2
        ),
        in_specs=[ANY] * 5 + [V],
        out_specs=(ANY,) * 6 + (V, V),
        scratch_shapes=[pltpu.VMEM(*p) for p in whole + shapes] + [sem((9,)), sem((10,))],
        name="deliver",
    )(y_in, g_in, qo, up_in, dn_in, sums)


def split_local(nz, x_in, tags, lengths, w_qkv, w_out, w_up, w_down, norm_gain, norm_bias, cotangent):
    cols = norm_gain.shape[2]
    y_out, x_grad, qo_grad, up_grad, down_grad, n_sum, _, _, _ = run_step(
        nz, tags, lengths, x_in, cotangent, w_qkv.transpose(0, 2, 1, 3), w_out, w_up, w_down, norm_gain, norm_bias
    )
    y_out, x_grad, qkv, out, up, down, gain, bias = deliver(
        cols, y_out, x_grad, qo_grad, up_grad, down_grad, n_sum
    )
    return y_out, x_grad, qkv.transpose(0, 2, 1, 3), out, up, down, gain, bias


def typed_map(operand, stacked, chain_kinds, pattern):

    def single(element):
        weight = lax.dynamic_index_in_dim(stacked, element[1], 0, keepdims=False)
        return jnp.einsum(pattern, element[0], weight, preferred_element_type=jnp.float32)

    return lax.map(single, (operand, chain_kinds))


def typed_grads(running, operand, partner, chain_kinds, pattern):

    def single(carry, element):
        product_term = jnp.einsum(
            pattern, element[0], element[1], preferred_element_type=jnp.float32
        )
        previous = lax.dynamic_index_in_dim(carry, element[2], 0, keepdims=False)
        return (
            lax.dynamic_update_index_in_dim(carry, previous + product_term, element[2], 0),
            None,
        )

    return lax.scan(single, running, (operand, partner, chain_kinds))[0]


def row_terms(operand, stacked, chain_kinds, pattern, row_count):
    result = typed_map(operand, stacked, chain_kinds, pattern)
    return result.reshape(row_count, result.shape[-1])


def old_norm_forward(values, gain_rows, shift_rows):
    center = values - jnp.mean(values, -1, keepdims=True)
    factor = lax.rsqrt(jnp.mean(center * center, -1, keepdims=True) + EPS)
    normed = center * factor
    return (normed * gain_rows + shift_rows, normed, factor)


def old_norm_backward(grad_out, normed, factor, gain_rows):
    scaled = grad_out * gain_rows
    mean_plain = jnp.mean(scaled, -1, keepdims=True)
    mean_normed = jnp.mean(scaled * normed, -1, keepdims=True)
    return factor * (scaled - mean_plain - normed * mean_normed)


def type_sums(onehot, values):
    return jnp.dot(onehot.T, values, precision=HIGH, preferred_element_type=jnp.float32)


def general_local(x_in, tags, lengths, w_qkv, w_out, w_up, w_down, norm_gain, norm_bias, cotangent):
    tp_count = lax.axis_size("tensor")
    tp_index = lax.axis_index("tensor")
    local_rows = CHAINS_PART * LENGTH
    batch_chains = tp_count * CHAINS_PART
    head_cols = w_qkv.shape[3]
    local_heads = head_cols // HEAD_DIM
    tag_grid = tags.reshape(tp_count, MICRO, CHAINS_PART)
    len_grid = lengths.reshape(tp_count, MICRO, CHAINS_PART)
    own_tags = lax.dynamic_index_in_dim(tag_grid, tp_index, 0, keepdims=False)
    gains, shifts = (
        lax.all_gather(norm_gain, ("dp", "tensor"), axis=2, tiled=True),
        lax.all_gather(norm_bias, ("dp", "tensor"), axis=2, tiled=True),
    )
    grad_full = (
        jnp.zeros((2, D, 3, head_cols), jnp.float32),
        jnp.zeros((2, D, head_cols), jnp.float32),
        jnp.zeros((2, D, w_up.shape[2]), jnp.float32),
        jnp.zeros((2, D, w_down.shape[2]), jnp.float32),
    )
    shards = (
        jnp.zeros(w_qkv.shape, jnp.float32),
        jnp.zeros(w_out.shape, jnp.float32),
        jnp.zeros(w_up.shape, jnp.float32),
        jnp.zeros(w_down.shape, jnp.float32),
    )
    gain_acc = jnp.zeros((2, 2, D), jnp.float32)
    shift_acc = jnp.zeros((2, 2, D), jnp.float32)
    outputs = []
    input_grads = []
    for micro_index in range(MICRO):
        held = (
            lax.all_gather(w_qkv, "dp", axis=1, tiled=True),
            lax.all_gather(w_out, "dp", axis=1, tiled=True),
            lax.all_gather(w_up, "dp", axis=1, tiled=True),
            lax.all_gather(w_down, "dp", axis=1, tiled=True),
        )
        qkv_w, out_w, up_w, down_w = held
        chain_kinds = tag_grid[:, micro_index].reshape(batch_chains)
        chain_lens = len_grid[:, micro_index].reshape(batch_chains)
        own_rows = x_in[micro_index * local_rows : (micro_index + 1) * local_rows]
        kinds_rows = jnp.repeat(own_tags[micro_index], LENGTH)
        heavy_rows = (kinds_rows == 0)[:, None]
        onehot = (kinds_rows[:, None] == jnp.arange(2)[None, :]).astype(jnp.float32)
        gain_mid = jnp.where(heavy_rows, gains[0, 0], gains[1, 0])
        shift_mid = jnp.where(heavy_rows, shifts[0, 0], shifts[1, 0])
        gain_end = jnp.where(heavy_rows, gains[0, 1], gains[1, 1])
        shift_end = jnp.where(heavy_rows, shifts[0, 1], shifts[1, 1])
        gathered = lax.all_gather(own_rows, "tensor", axis=0, tiled=True).reshape(
            batch_chains, LENGTH, D
        )
        projected = typed_map(gathered, qkv_w, chain_kinds, "ld,dkh->lkh").astype(jnp.bfloat16)
        query = projected[:, :, 0].reshape(batch_chains, LENGTH, local_heads, HEAD_DIM)
        keys_low = projected[:, :, 1].reshape(batch_chains, LENGTH, local_heads, HEAD_DIM)
        values_low = projected[:, :, 2].reshape(batch_chains, LENGTH, local_heads, HEAD_DIM)
        valid = (
            lax.broadcasted_iota(jnp.int32, (batch_chains, 1, 1, LENGTH), 3)
            < chain_lens[:, None, None, None]
        )
        scores = (
            jnp.einsum("cqhe,ckhe->chqk", query, keys_low, preferred_element_type=jnp.float32)
            * 0.125
        )
        scores = jnp.where(valid, scores, NEG)
        highest = jnp.max(scores, -1, keepdims=True)
        expo = jnp.exp(scores - highest)
        totals = jnp.sum(expo, -1, keepdims=True)
        probs = expo / totals
        log_total = highest + jnp.log(totals)
        heads_low = jnp.einsum(
            "chqk,ckhe->cqhe",
            probs.astype(jnp.bfloat16),
            values_low,
            preferred_element_type=jnp.float32,
        ).astype(jnp.bfloat16)
        heads_low = heads_low.reshape(batch_chains, LENGTH, head_cols)
        attn_sum = lax.psum_scatter(
            row_terms(
                heads_low, out_w, chain_kinds, "lh,dh->ld", lax.axis_size("tensor") * local_rows
            ).astype(jnp.bfloat16),
            "tensor",
            scatter_dimension=0,
            tiled=True,
        ).astype(jnp.float32)
        mid, normed_mid, factor_mid = old_norm_forward(
            own_rows.astype(jnp.float32) + attn_sum, gain_mid, shift_mid
        )
        mid_all = lax.all_gather(mid.astype(jnp.bfloat16), "tensor", axis=0, tiled=True).reshape(
            batch_chains, LENGTH, D
        )
        up_value = typed_map(mid_all, up_w, chain_kinds, "ld,df->lf")
        act_low = jax.nn.gelu(up_value, approximate=False).astype(jnp.bfloat16)
        ffn_sum = lax.psum_scatter(
            row_terms(
                act_low, down_w, chain_kinds, "lf,df->ld", lax.axis_size("tensor") * local_rows
            ).astype(jnp.bfloat16),
            "tensor",
            scatter_dimension=0,
            tiled=True,
        ).astype(jnp.float32)
        final, normed_end, factor_end = old_norm_forward(ffn_sum + mid, gain_end, shift_end)
        outputs.append(final.astype(jnp.bfloat16))
        base = grad_full
        grad_final = cotangent[micro_index * local_rows : (micro_index + 1) * local_rows].astype(
            jnp.float32
        )
        gain_acc = gain_acc.at[:, 1].add(type_sums(onehot, grad_final * normed_end))
        shift_acc = shift_acc.at[:, 1].add(type_sums(onehot, grad_final))
        grad_resid2 = old_norm_backward(grad_final, normed_end, factor_end, gain_end)
        grad_ffn = lax.all_gather(
            grad_resid2.astype(jnp.bfloat16), "tensor", axis=0, tiled=True
        ).reshape(batch_chains, LENGTH, D)
        grad_act = typed_map(grad_ffn, down_w, chain_kinds, "ld,df->lf")
        unused_value, gelu_back = jax.vjp(partial(jax.nn.gelu, approximate=False), up_value)
        grad_up = gelu_back(grad_act)[0].astype(jnp.bfloat16)
        down_acc = typed_grads(base[3], grad_ffn, act_low, chain_kinds, "ld,lf->df")
        up_acc = typed_grads(base[2], mid_all, grad_up, chain_kinds, "ld,lf->df")
        grad_mid = grad_resid2 + lax.psum_scatter(
            row_terms(
                grad_up, up_w, chain_kinds, "lf,df->ld", lax.axis_size("tensor") * local_rows
            ).astype(jnp.bfloat16),
            "tensor",
            scatter_dimension=0,
            tiled=True,
        ).astype(jnp.float32)
        gain_acc = gain_acc.at[:, 0].add(type_sums(onehot, grad_mid * normed_mid))
        shift_acc = shift_acc.at[:, 0].add(type_sums(onehot, grad_mid))
        grad_resid1 = old_norm_backward(grad_mid, normed_mid, factor_mid, gain_mid)
        grad_attn = lax.all_gather(
            grad_resid1.astype(jnp.bfloat16), "tensor", axis=0, tiled=True
        ).reshape(batch_chains, LENGTH, D)
        grad_heads = typed_map(grad_attn, out_w, chain_kinds, "ld,dh->lh").astype(jnp.bfloat16)
        out_acc = typed_grads(base[1], grad_attn, heads_low, chain_kinds, "ld,lh->dh")
        grad_heads = grad_heads.reshape(batch_chains, LENGTH, local_heads, HEAD_DIM)
        again = (
            jnp.einsum("cqhe,ckhe->chqk", query, keys_low, preferred_element_type=jnp.float32)
            * 0.125
        )
        probs_again = jnp.exp(jnp.where(valid, again, NEG) - log_total)
        grad_probs = jnp.einsum(
            "cqhe,ckhe->chqk", grad_heads, values_low, preferred_element_type=jnp.float32
        )
        inner = jnp.sum(grad_probs * probs_again, -1, keepdims=True)
        grad_scores = (probs_again * (grad_probs - inner)).astype(jnp.bfloat16)
        grad_query = (
            jnp.einsum("chqk,ckhe->cqhe", grad_scores, keys_low, preferred_element_type=jnp.float32)
            * 0.125
        ).astype(jnp.bfloat16)
        grad_keys = (
            jnp.einsum("chqk,cqhe->ckhe", grad_scores, query, preferred_element_type=jnp.float32)
            * 0.125
        ).astype(jnp.bfloat16)
        grad_values = jnp.einsum(
            "chqk,cqhe->ckhe",
            probs_again.astype(jnp.bfloat16),
            grad_heads,
            preferred_element_type=jnp.float32,
        ).astype(jnp.bfloat16)
        grad_proj = jnp.stack([grad_query, grad_keys, grad_values], 2).reshape(
            batch_chains, LENGTH, 3, head_cols
        )
        qkv_acc = typed_grads(base[0], gathered, grad_proj, chain_kinds, "ld,lkh->dkh")
        grad_input = grad_resid1 + lax.psum_scatter(
            row_terms(
                grad_proj, qkv_w, chain_kinds, "lkh,dkh->ld", lax.axis_size("tensor") * local_rows
            ).astype(jnp.bfloat16),
            "tensor",
            scatter_dimension=0,
            tiled=True,
        ).astype(jnp.float32)
        input_grads.append(grad_input)
        updated = (qkv_acc, out_acc, up_acc, down_acc)
        grad_full = updated
    shards = (
        lax.psum_scatter(grad_full[0], "dp", scatter_dimension=1, tiled=True),
        lax.psum_scatter(grad_full[1], "dp", scatter_dimension=1, tiled=True),
        lax.psum_scatter(grad_full[2], "dp", scatter_dimension=1, tiled=True),
        lax.psum_scatter(grad_full[3], "dp", scatter_dimension=1, tiled=True),
    )
    gain_grad, shift_grad = (
        lax.psum_scatter(gain_acc, ("dp", "tensor"), scatter_dimension=2, tiled=True),
        lax.psum_scatter(shift_acc, ("dp", "tensor"), scatter_dimension=2, tiled=True),
    )
    return (
        jnp.concatenate(outputs, 0),
        jnp.concatenate(input_grads, 0),
        shards[0],
        shards[1],
        shards[2],
        shards[3],
        gain_grad,
        shift_grad,
    )


def solution(mesh):
    placed = (
        P(("dp", "tensor"), None),
        P("dp"),
        P("dp"),
        P(None, "dp", None, "tensor"),
        P(None, "dp", "tensor"),
        P(None, "dp", "tensor"),
        P(None, "dp", "tensor"),
        P(None, None, ("dp", "tensor")),
        P(None, None, ("dp", "tensor")),
        P(("dp", "tensor"), None),
    )
    results = (
        P(("dp", "tensor"), None),
        P(("dp", "tensor"), None),
        P(None, "dp", None, "tensor"),
        P(None, "dp", "tensor"),
        P(None, "dp", "tensor"),
        P(None, "dp", "tensor"),
        P(None, None, ("dp", "tensor")),
        P(None, None, ("dp", "tensor")),
    )
    n_dp, n_tensor = mesh.shape["dp"], mesh.shape["tensor"]
    if n_tensor != GROUPS or n_dp != 8:
        return jax.shard_map(
            general_local, mesh=mesh, in_specs=placed, out_specs=results, check_vma=False
        )
    fine = Mesh(mesh.devices.reshape(n_dp // 2, 2, 2, 2), AXES)
    names = {"dp": ("z", "x"), "tensor": ("y", "c")}

    def refine(spec):
        parts = []
        for entry in spec:
            entry = (entry,) if isinstance(entry, str) else entry
            parts.append(entry and sum((names[a] for a in entry), ()))
        return P(*parts)

    return jax.shard_map(
        partial(split_local, n_dp // 2),
        mesh=fine,
        in_specs=tuple(refine(s) for s in placed),
        out_specs=tuple(refine(s) for s in results),
        check_vma=False,
    )
```

```python
from functools import partial

import jax
import jax.numpy as jnp
from jax import lax
from jax.experimental import pallas as pl
from jax.experimental.pallas import tpu as pltpu
from jax.sharding import Mesh
from jax.sharding import PartitionSpec as P

D = 768
HEADS = 12
HEAD_DIM = 64
MICRO = 4
CHAINS_PART = 1
LENGTH = 160
GROUPS = 4
OWN = 4
EXTRA = 2
SLOTS = OWN + EXTRA
EXT_ROWS = EXTRA * LENGTH
OWN_ROWS = OWN * LENGTH
ROWS = SLOTS * LENGTH

EPS = 1e-12
NEG = -1e30
HIGH = lax.Precision.HIGHEST
BF = jnp.bfloat16
F32 = jnp.float32
MESH = pl.DeviceIdType.MESH
ANY = pl.BlockSpec(memory_space=pl.ANY)
AXES = ("z", "x", "y", "c")


def place():
    return tuple(lax.axis_index(a) for a in AXES)


def meet(nz, z, x, y, c):
    barrier = pltpu.get_barrier_semaphore()
    friends = [{"c": 1 - c}, {"y": 1 - y}, {"y": 1 - y, "c": 1 - c}, {"x": 1 - x}]
    friends += [{"z": lax.rem(z + dz, nz)} for dz in range(1, nz)]
    for friend in friends:
        pl.semaphore_signal(barrier, inc=1, device_id=friend, device_id_type=MESH)
    pl.semaphore_wait(barrier, len(friends))


CHUNK = 320
SUB = 80
N_CHUNK = ROWS // CHUNK
WIDE = 3 * LENGTH
GW = 256
PAIR = 3


def dot_nn(a, b):
    return lax.dot_general(a, b, (((1,), (0,)), ((), ())), preferred_element_type=F32)


def dot_nt(a, b):
    return lax.dot_general(a, b, (((1,), (1,)), ((), ())), preferred_element_type=F32)


def dot_tn(a, b):
    return lax.dot_general(a, b, (((0,), (0,)), ((), ())), preferred_element_type=F32)


def lanes(shape):
    return lax.broadcasted_iota(jnp.int32, shape, len(shape) - 1)


def head_mask(h, shape):
    lane = lanes(shape)
    return jnp.logical_and(lane >= h * HEAD_DIM, lane < (h + 1) * HEAD_DIM)


def stack_heads(rows):
    zero = jnp.zeros_like(rows)
    return jnp.concatenate([jnp.where(head_mask(h, rows.shape), rows, zero) for h in range(3)], 0)


def merge_heads(stack):
    out = jnp.zeros((LENGTH, GW), stack.dtype)
    for h in range(3):
        out = jnp.where(head_mask(h, out.shape), stack[h * LENGTH : (h + 1) * LENGTH], out)
    return out


def chunk_rows(i, size=CHUNK):
    return pl.ds(pl.multiple_of(i * size, size), size)


def loop(count, body):
    def step(i, carry):
        body(i)
        return carry

    lax.fori_loop(0, count, step, 0)


def weave(count, unit, extra):
    def body(i):
        unit(i)
        for k, step in extra.items():
            pl.when(i == k)(step)

    loop(count, body)


def out_columns(t, w, wo):
    low = lanes((D, 128)) < HEAD_DIM
    tiles = [w[0, t, :, GW * i + 128 : GW * i + 256].astype(F32) for i in range(3)]
    wo[t, :, :128] = jnp.where(low, pltpu.roll(tiles[0], 64, 1), tiles[1]).astype(BF)
    wo[t, :, 128:] = jnp.where(low, pltpu.roll(tiles[2], 64, 1), 0.0).astype(BF)


def attend(t, chains, lens, proj, probs, hout):
    rows = [chunk_rows(s, LENGTH) for s in chains]
    parts = [(proj[t, r, :GW], proj[t, r, GW : 2 * GW], proj[t, r, 2 * GW :]) for r in rows]
    lows, outs = [], []
    for s, (query, key, value) in zip(chains, parts):
        scores = dot_nt(key, stack_heads(query * jnp.asarray(0.125, BF)))
        valid = lax.broadcasted_iota(jnp.int32, (LENGTH, 1), 0) < lens(s)
        scores = jnp.where(valid, scores, NEG)
        expo = jnp.exp(scores - jnp.max(scores, 0, keepdims=True))
        lows.append((expo * (1.0 / jnp.sum(expo, 0, keepdims=True))).astype(BF))
        outs.append(merge_heads(dot_tn(lows[-1], value)).astype(BF))
    for s, r, low, out in zip(chains, rows, lows, outs):
        probs[t, s, :, :WIDE] = low
        hout[t, r] = out


def norm_rows(values):
    center = values - jnp.mean(values, -1, keepdims=True)
    factor = lax.rsqrt(jnp.mean(center * center, -1, keepdims=True) + EPS)
    return center * factor, factor


def norm_back(scaled, normed, factor):
    return factor * (
        scaled
        - jnp.mean(scaled, -1, keepdims=True)
        - normed * jnp.mean(scaled * normed, -1, keepdims=True)
    )


def pieces(i, body):
    def step(k):
        body(pl.ds(pl.multiple_of(i * CHUNK + k * SUB, SUB), SUB), k)

    loop(CHUNK // SUB, step)


def first_norm(i, x, hout, wo, prm, mid, n1, s1, mid_low):
    r = chunk_rows(i)
    attn = dot_nt(hout[0, r], wo[0])
    for t in range(1, GROUPS):
        attn += dot_nt(hout[t, r], wo[t])
    mid[r] = attn

    def piece(p, k):
        normed, factor = norm_rows(x[p].astype(F32) + mid[p])
        n1[p] = normed.astype(BF)
        s1[p] = jnp.broadcast_to(factor, (SUB, 128))
        value = normed * prm[0:1] + prm[2:3]
        mid[p] = value
        mid_low[p] = value.astype(BF)

    pieces(i, piece)


def feed_up(t, i, mid_low, w, act, slope):
    r = chunk_rows(i)
    for k in range(0, D, GW):
        up = dot_nn(mid_low[r], w[1, t, :, k : k + GW])
        cdf = 0.5 * (1.0 + lax.erf(up * 0.7071067811865476))
        act[t, r, k : k + GW] = (up * cdf).astype(BF)
        bell = 0.3989422804014327 * jnp.exp(-0.5 * up * up)
        slope[t, r, k : k + GW] = (cdf + up * bell).astype(BF)


def feed_down(i, t, act, w, mid):
    r = chunk_rows(i)
    mid[r] += dot_nt(act[t, r], w[2, t]) + dot_nt(act[t + 1, r], w[2, t + 1])


def second_norm(i, t, act, w, prm, mid, cot, mine, y_rows, d_ffn, ngrad):
    feed_down(i, t, act, w, mid)

    def piece(p, k):
        normed, factor = norm_rows(mid[p])
        y_rows[pl.ds(pl.multiple_of(k * SUB, SUB), SUB)] = (normed * prm[1:2] + prm[3:4]).astype(BF)
        grad = cot[p].astype(F32) * jnp.where(k < LENGTH // SUB, mine(2 * i), mine(2 * i + 1))
        ngrad[1:2] += jnp.sum(grad * normed, 0, keepdims=True)
        ngrad[3:4] += jnp.sum(grad, 0, keepdims=True)
        back = norm_back(grad * prm[1:2], normed, factor)
        mid[p] = back
        d_ffn[p] = back.astype(BF)

    pieces(i, piece)


def back_up(t, i, d_ffn, w, slope):
    r = chunk_rows(i)
    slope[t, r] = (dot_nn(d_ffn[r], w[2, t]) * slope[t, r].astype(F32)).astype(BF)


def back_first_norm(i, d_up, w, prm, mid, n1, s1, d_attn, ngrad):
    r = chunk_rows(i)
    grad = dot_nt(d_up[0, r], w[1, 0])
    for t in range(1, GROUPS):
        grad += dot_nt(d_up[t, r], w[1, t])
    mid[r] += grad

    def piece(p, k):
        grad = mid[p]
        normed = n1[p].astype(F32)
        ngrad[0:1] += jnp.sum(grad * normed, 0, keepdims=True)
        ngrad[2:3] += jnp.sum(grad, 0, keepdims=True)
        back = norm_back(grad * prm[0:1], normed, s1[p, 0:1])
        mid[p] = back
        d_attn[p] = back.astype(BF)

    pieces(i, piece)


def back_heads(t, d_attn, wo, d_heads):
    d_heads[t, :, :GW] = dot_nn(d_attn[...], wo[t]).astype(BF)


def back_attend(t, chains, proj, probs, d_heads):
    rows = [chunk_rows(s, LENGTH) for s in chains]
    parts = [
        (proj[t, r, :GW], proj[t, r, GW : 2 * GW], proj[t, r, 2 * GW :], d_heads[t, r, :GW], probs[t, s, :, :WIDE])
        for s, r in zip(chains, rows)
    ]
    results = []
    for query, key, value, grad, low in parts:
        grad = stack_heads(grad)
        p = low.astype(F32)
        d_probs = dot_nt(value, grad)
        d_scores = (p * (d_probs - jnp.sum(d_probs * p, 0, keepdims=True))).astype(BF)
        d_query = merge_heads(dot_tn(d_scores, key)) * 0.125
        d_key = dot_nn(d_scores, stack_heads(query * jnp.asarray(0.125, BF)))
        results.append((d_query.astype(BF), d_key.astype(BF), dot_nn(low, grad).astype(BF)))
    for r, (d_query, d_key, d_value) in zip(rows, results):
        proj[t, r, :GW] = d_query
        proj[t, r, GW : 2 * GW] = d_key
        proj[t, r, 2 * GW :] = d_value


def grad_qkv_out(t, x, d_proj, d_attn, hout, store):
    low = lanes((D, 128)) < HEAD_DIM
    outs = dot_tn(d_attn[...], hout[t])
    places = (pltpu.roll(outs[:, :128], 64, 1), outs[:, :128], pltpu.roll(outs[:, 128:], 64, 1))
    for i in range(3):
        part = dot_tn(x[...], d_proj[t, :, GW * i : GW * (i + 1)])
        store(GW * i, part[:, :128])
        store(GW * i + 128, jnp.where(low, part[:, 128:], places[i]))


def back_input(i, d_proj, w, mid, out):
    r = chunk_rows(i)
    grad = mid[r]
    for t in range(GROUPS):
        grad += dot_nt(d_proj[t, r], w[0, t])
    out(r, grad)


MIXED = (2, 1)
GATHER_FIRST = (
    ('X', 0, 0), ('L', 0, 0), ('y', 0), ('X', 0, 1), ('L', 0, 1),
    ('z', 0, 0, 1), ('z', 0, 1, 1), ('z', 0, 0, 2), ('x', 0, 0, 0), ('z', 0, 1, 2),
    ('z', 0, 0, 3), ('y', 1), ('L', 1, 1), ('x', 0, 1, 1), ('z', 0, 1, 3),
    ('x', 0, 1, 0), ('y', 2), ('X', 2, 1), ('L', 1, 0), ('X', 1, 0),
    ('x', 0, 0, 2), ('X', 1, 1), ('z', 1, 1, 1), ('x', 0, 0, 3), ('L', 2, 0),
    ('x', 0, 0, 1), ('x', 0, 1, 2), ('x', 0, 1, 3), ('z', 1, 0, 1),
)
GATHER_QKV = {
    6: (('z', 1, 1, 2),),
    11: (('z', 1, 0, 2),),
}
GATHER_ATTEND = {
    2: (('x', 2, 1, 0),),
    3: (('x', 1, 1, 1), ('x', 1, 0, 0), ('z', 1, 0, 3),),
    4: (('L', 2, 1), ('z', 1, 1, 3), ('x', 1, 1, 0),),
    5: (('z', 2, 0, 1), ('X', 2, 0),),
}
GATHER_NORM = {
    0: (('z', 2, 1, 1),),
    1: (('x', 1, 0, 3), ('x', 1, 0, 1), ('x', 1, 1, 2), ('x', 1, 0, 2), ('x', 1, 1, 3),),
    2: (('z', 2, 0, 2),),
}
GATHER_UP = {
    3: (('z', 2, 1, 2),),
    5: (('z', 2, 0, 3),),
    8: (('x', 2, 0, 1),),
    10: (('x', 2, 0, 0), ('x', 2, 0, 2), ('x', 2, 0, 3),),
    11: (('z', 2, 1, 3),),
}


def remote(src, dst, s_sem, r_sem, who):
    return pltpu.make_async_remote_copy(
        src_ref=src, dst_ref=dst, send_sem=s_sem, recv_sem=r_sem, device_id=who, device_id_type=MESH
    )


def arrived(ref, sem):
    remote(ref, ref, sem, sem, {"c": 1 - lax.axis_index("c")}).wait_recv()


def has_left(ref, sem):
    remote(ref, ref, sem, sem, {"c": 1 - lax.axis_index("c")}).wait_send()


def step_kernel(nz, rows,
                tags, lens, x_in, cot, qkv, wout, up, dn, gain, bias,
                y_out, g_out, qo_out, up_out, dn_out, n_out, y_back, g_back, r_c,
                w, x, proj, probs, hout, wo, mid, n1, s1, mid_low, act, slope, d_ffn, gown, r_x, r_z, oth, v_qkv, v_out, far,
                n_all, prm, ngrad, n_c, n_x, n_z,
                load_s, io_s, stage_s, out_s,
                ys_s, ys_r, zs_s, zs_r, zm_s, zm_r, xs_s, xs_r, cs_s, cs_r, ex_s, ex_r, na_s, na_r,
                c_s, c_r, x_s, x_r, z_s, z_r, y_s, y_r, e_s, e_r, ng_s, ng_r):
    z, xc, y, c = place()
    core, across, other_x = {"c": 1 - c}, {"y": 1 - y}, {"x": 1 - xc}
    diagonal = {"y": 1 - y, "c": 1 - c}
    mats = (None, up, dn)
    lender = y != c
    home = (2 * y + c) * OWN
    away = (2 - y) * OWN + c * EXTRA

    def z_of(dz):
        return lax.rem(z + dz, nz)

    def chain(s):
        return jnp.where(s < OWN, home + s, away + s - OWN)

    def length_of(s):
        return lens[chain(s)]

    def mine(s):
        return jnp.where(tags[chain(s)] == y, 1.0, 0.0)

    def part(zz, xx):
        return pl.ds(pl.multiple_of((zz * 2 + xx) * rows, rows), rows)

    def group(g):
        return 2 * lax.rem(y + g, 2) + c

    def block(m, g, zz, xx):
        return w.at[m, group(g), part(zz, xx)]

    loads = [pltpu.make_async_copy(mats[m].at[y], block(m, 0, z, xc), load_s.at[m]) for m in range(1, 3)]
    loads += [
        pltpu.make_async_copy(x_in, x.at[pl.ds(0, OWN_ROWS)], load_s.at[3]),
        pltpu.make_async_copy(cot, d_ffn.at[pl.ds(0, OWN_ROWS)], load_s.at[4]),
        pltpu.make_async_copy(qkv, v_qkv, load_s.at[0]),
        pltpu.make_async_copy(wout, v_out, load_s.at[5]),
    ]
    for cp in loads:
        cp.start()
    me = ((z * 2 + xc) * 2 + y) * 2 + c
    cols = gain.shape[2]
    n_all[me] = jnp.zeros((8, 128), F32)
    for i in range(2):
        n_all[me, 2 * i : 2 * i + 2, :cols] = gain[i]
        n_all[me, 4 + 2 * i : 6 + 2 * i, :cols] = bias[i]
    ngrad[...] = jnp.zeros_like(ngrad)
    for cp in loads[4:]:
        cp.wait()

    def packed(k):
        tail = v_out[k]
        cols = []
        for i in range(3):
            cols += [v_qkv[k, i], tail[:, HEAD_DIM * i : HEAD_DIM * (i + 1)]]
        return jnp.concatenate(cols, 1)

    w[0, group(0), part(z, xc)] = packed(y)
    far[...] = packed(1 - y)
    meet(nz, z, xc, y, c)

    def given(m):
        return mats[m].at[1 - y] if m else far

    def lend(arr, out, i, act_on):
        @pl.when(lender)
        def _():
            for j, (who, p) in enumerate(((across, c), (diagonal, 1 - c))):
                src = arr.at[pl.ds(pl.multiple_of(p * EXT_ROWS, EXT_ROWS), EXT_ROWS)]
                act_on(remote(src, out.at[pl.ds(OWN_ROWS, EXT_ROWS)], ex_s.at[i, j], ex_r.at[i], who))

    for m in range(3):
        remote(given(m), w.at[m, group(0), part(z, xc)], ys_s.at[m], ys_r.at[m], across).start()
    lend(x_in, x, 0, lambda cp: cp.start())
    lend(cot, d_ffn, 1, lambda cp: cp.start())

    def inside(zz):
        return jnp.logical_and(zz >= 0, zz < nz)

    def start(cp):
        cp.start()

    def recv(cp):
        cp.wait_recv()

    def hop(m, g, d, j, ref, act_on, col=0):
        to = z + 1 - 2 * d
        sems = (zm_s.at[d, j], zm_r.at[d, j]) if col else (zs_s.at[m, g, d, j], zs_r.at[m, g, d, j])

        @pl.when(jnp.logical_and(inside(to), j < nz))
        def _():
            act_on(remote(ref, ref, *sems, {"z": to}))

    def x_copy(m, g, zz):
        ref = block(m, g, zz, xc)
        return remote(ref, ref, xs_s.at[m, g, zz], xs_r.at[m, g, zz], other_x)

    def c_copy(m, g, zz, xx):
        ref = block(m, g, zz, xx)
        return remote(ref, ref, cs_s.at[m, g, zz, xx], cs_r.at[m, g, zz, xx], core)

    def from_y(m):
        arrived(block(m, 1, z, xc), ys_r.at[m])

    def own_z(m, g):
        for d in range(2):
            hop(m, g, d, 1, block(m, g, z, xc), start)

    def own_xc(m, g):
        x_copy(m, g, z).start()
        c_copy(m, g, z, xc).start()

    def z_event(m, g, j):
        mixed = (m, g) == MIXED

        def body(d):
            zz = z - j + 2 * j * d

            @pl.when(inside(zz))
            def _():
                for col in range(2 if mixed else 1):
                    ref = block(m, g, zz, lax.rem(xc + col, 2))
                    arrived(ref, zm_r.at[d, j] if col else zs_r.at[m, g, d, j])
                    hop(m, g, d, j + 1, ref, start, col)
                    if not mixed:
                        x_copy(m, g, zz).start()
                    c_copy(m, g, zz, lax.rem(xc + col, 2)).start()

        loop(2, body)

    def x_event(m, g, j):
        def body(d):
            zz = z - j + 2 * j * d

            @pl.when(inside(zz))
            def _():
                ref = block(m, g, zz, 1 - xc)
                arrived(ref, xs_r.at[m, g, zz])
                if (m, g) == MIXED:
                    for way in range(2):
                        hop(m, g, way, 1, ref, start, 1)
                c_copy(m, g, zz, 1 - xc).start()

        loop(2 if j else 1, body)

    kinds = {"y": from_y, "L": own_z, "X": own_xc, "z": z_event, "x": x_event}

    def gather_steps(plan):
        def run(steps):
            for kind, *args in steps:
                kinds[kind](*args)

        return {k: partial(run, steps) for k, steps in plan.items()}

    def gathered(m, first=0, last=2):
        def body(i):
            g = first + i // (2 * nz)
            t = 2 * lax.rem(y + g, 2) + 1 - c
            zz, xx = (i // 2) % nz, i % 2
            arrived(w.at[m, t, part(zz, xx)], cs_r.at[m, g, zz, xx])

        loop(2 * nz * (last - first), body)

    def gather_sent(i):
        m, g = i // 2, i % 2
        ref = w.at[0, 0, pl.ds(0, rows)]
        mixed = i == 2 * MIXED[0] + MIXED[1]
        for j in range(1, nz):
            for d in range(2):
                @pl.when(inside(z - (1 - 2 * d) * (j - 1)))
                def _():
                    hop(m, g, d, j, ref, lambda cp: cp.wait_send())

                    @pl.when(mixed)
                    def _():
                        hop(m, g, d, j, ref, lambda cp: cp.wait_send(), 1)
        for zz in range(nz):
            @pl.when(jnp.logical_or(jnp.logical_not(mixed), z == zz))
            def _():
                has_left(ref, xs_s.at[m, g, zz])

            for xx in range(2):
                has_left(ref, cs_s.at[m, g, zz, xx])

    def norm_hop(i, act_on):
        if i == 0:
            act_on(remote(n_all.at[me], n_all.at[me], na_s.at[0], na_r.at[0], core))
        elif i == 1:
            ref = n_all.at[pl.ds(me - c, 2)]
            act_on(remote(ref, ref, na_s.at[1], na_r.at[1], across))
        elif i == 2:
            ref = n_all.at[pl.ds(me - c - 2 * y, 4)]
            act_on(remote(ref, ref, na_s.at[2], na_r.at[2], other_x))
        else:
            ref = n_all.at[pl.ds(8 * z, 8)]
            for dz in range(1, nz):
                act_on(remote(ref, ref, na_s.at[2 + dz], na_r.at[2 + dz], {"z": z_of(dz)}))

    for cp in loads[:2]:
        cp.wait()
    norm_hop(0, start)
    for kind, *args in GATHER_FIRST:
        kinds[kind](*args)
        if (kind, *args) == ("z", 0, 0, 1):
            norm_hop(0, recv)
            norm_hop(1, start)
        if (kind, *args) == ("z", 0, 0, 3):
            norm_hop(1, recv)
            norm_hop(2, start)
    norm_hop(2, recv)
    norm_hop(3, start)
    gathered(0)
    loads[2].wait()
    arrived(x.at[pl.ds(OWN_ROWS, EXT_ROWS)], ex_r.at[0])

    def projection(i):
        t, k = i // N_CHUNK, i % N_CHUNK
        r = chunk_rows(k)
        proj[t, r] = dot_nn(x[r], w[0, t]).astype(BF)

        @pl.when(k == N_CHUNK - 1)
        def _():
            out_columns(t, w, wo)

    weave(GROUPS * N_CHUNK, projection, gather_steps(GATHER_QKV))
    per = SLOTS // PAIR

    def attention(i):
        attend(i // per, [(i % per) * PAIR + k for k in range(PAIR)], length_of, proj, probs, hout)

    weave(GROUPS * per, attention, gather_steps(GATHER_ATTEND))
    norm_hop(3, recv)
    lane = lanes((2, D))
    gains, shifts = jnp.zeros((2, D), F32), jnp.zeros((2, D), F32)
    for d in range(8 * nz):
        within = jnp.logical_and(lane >= d * cols, lane < (d + 1) * cols)
        for name in range(2):
            piece = n_all[d, pl.ds(4 * name + 2 * y, 2), :]
            piece = jnp.concatenate([piece, jnp.zeros((2, D - 128), F32)], 1)
            piece = jnp.where(within, pltpu.roll(piece, d * cols, 1) if d else piece, 0.0)
            if name == 0:
                gains += piece
            else:
                shifts += piece
    prm[0:2] = gains
    prm[2:4] = shifts
    weave(
        N_CHUNK,
        lambda i: first_norm(i, x, hout, wo, prm, mid, n1, s1, mid_low),
        gather_steps(GATHER_NORM),
    )
    gathered(1)
    weave(
        GROUPS * N_CHUNK,
        lambda i: feed_up(i // N_CHUNK, i % N_CHUNK, mid_low, w, act, slope),
        gather_steps(GATHER_UP),
    )
    gathered(2, 0, 1)
    first_two = 2 * y
    last_two = 2 - first_two
    loop(N_CHUNK, lambda i: feed_down(i, first_two, act, w, mid))
    gathered(2, 1, 2)
    loads[3].wait()
    arrived(d_ffn.at[pl.ds(OWN_ROWS, EXT_ROWS)], ex_r.at[1])

    def y_stage(i):
        return gown.at[1, i // 2, pl.ds(pl.multiple_of((i % 2) * CHUNK, CHUNK), CHUNK)]

    def give_back(src, dst, i, act_on):
        dst = dst.at[pl.ds(pl.multiple_of(c * EXT_ROWS, EXT_ROWS), EXT_ROWS)]

        @pl.when(c == y)
        def _():
            act_on(remote(src, dst, e_s.at[i], e_r.at[i, c], across))

        @pl.when(c != y)
        def _():
            act_on(remote(src, dst, e_s.at[i], e_r.at[i, c], diagonal))

    def y_copy(i):
        return pltpu.make_async_copy(y_stage(i), y_out.at[pl.ds(i * CHUNK, CHUNK)], io_s.at[i])

    loop(
        N_CHUNK,
        lambda i: second_norm(
            i, last_two, act, w, prm, mid, d_ffn, mine, y_stage(i), d_ffn, ngrad
        ),
    )
    for i in range(2):
        y_copy(i).start()
    give_back(y_stage(2), y_back, 0, start)

    def spare(m, g):
        return gown.at[0, g] if m else act.at[2 * g + c, pl.ds(0, D)]

    def core_send(m, g):
        return remote(spare(m, g), r_c.at[m, g], c_s.at[m, g], c_r.at[m, g], core)

    def fetch(m, g):
        return pltpu.make_async_copy(r_c.at[m, g], act.at[2 * g + 1 - c, pl.ds(0, D)], stage_s.at[g])

    def core_fetch(m, g):
        arrived(r_c.at[m, g], c_r.at[m, g])
        fetch(m, g).start()

    middle = jnp.logical_and(z > 0, z < nz - 1)

    def target(k):
        down = jnp.where(nz - 1 - k > z, nz - 1 - k, nz - 2 - k)
        up = jnp.where(k < z, k, k + 1)
        return jnp.where(k == nz - 1, z, jnp.where(z < nz // 2, down, up))

    def core_add(m, g):
        fetch(m, g).wait()

        def body(i):
            p = part(target(i // 2), lax.rem(xc + 1 + i, 2))
            gown[m, g, p] = (gown[m, g, p].astype(F32) + act[2 * g + 1 - c, p].astype(F32)).astype(BF)

        loop(2 * nz, body)

        def over(k):
            zz = target(k)
            remote(gown.at[m, g, part(zz, 1 - xc)], r_x.at[m, g, zz], x_s.at[m, g, zz], x_r.at[m, g, zz], other_x).start()

        loop(nz, over)

    def sum_event(q):
        m = 2 - q // (2 * nz)
        g = (q // nz) % 2
        k = q % nz
        zz = target(k)
        arrived(r_x.at[m, g, zz], x_r.at[m, g, zz])
        p = part(zz, xc)
        gown[m, g, p] = (gown[m, g, p].astype(F32) + r_x[m, g, zz].astype(F32)).astype(BF)

        joins = jnp.logical_and(k == 0, jnp.logical_not(middle))
        waits = jnp.logical_and(k == 0, middle)
        beside = jnp.where(z == 0, 1, nz - 2)
        to = jnp.where(joins, beside, zz)
        slot = jnp.where(joins, beside, z)

        @pl.when(jnp.logical_and(k < nz - 1, jnp.logical_not(waits)))
        def _():
            remote(gown.at[m, g, p], r_z.at[m, g, slot], z_s.at[m, g, zz], z_r.at[m, g, slot], {"z": to}).start()

        @pl.when(jnp.logical_and(k == jnp.where(m == 0, 1, nz - 2), middle))
        def _():
            far = target(0)
            f = part(far, xc)
            arrived(r_z.at[m, g, z], z_r.at[m, g, z])
            gown[m, g, f] = (gown[m, g, f].astype(F32) + r_z[m, g, z].astype(F32)).astype(BF)
            remote(gown.at[m, g, f], r_z.at[m, g, z], z_s.at[m, g, far], z_r.at[m, g, z], {"z": far}).start()

    outs = (qo_out, up_out, dn_out)

    def out_stage(m, other):
        return mid.at[pl.ds(m * rows + (0 if other else OWN_ROWS), rows)]

    def out_copy(m, other):
        return pltpu.make_async_copy(out_stage(m, other), outs[m].at[1 - y if other else y], out_s.at[m, other])

    def last_send(m):
        return remote(mid_low.at[pl.ds(EXT_ROWS + m * rows, rows)], oth.at[m], y_s.at[m], y_r.at[m], across)

    def finish(m, g):
        total = gown[m, g, part(z, xc)].astype(F32)
        for dz in range(1, nz):
            source = z_of(dz)
            direct = jnp.abs(source - z) < nz - 1

            @pl.when(direct)
            def _():
                arrived(r_z.at[m, g, source], z_r.at[m, g, source])

            total += jnp.where(direct, r_z[m, g, source].astype(F32), 0.0)

        @pl.when(y == g)
        def _():
            out_stage(m, 0)[...] = total
            out_copy(m, 0).start()

        @pl.when(y != g)
        def _():
            mid_low[EXT_ROWS + m * rows : EXT_ROWS + (m + 1) * rows] = total.astype(BF)
            last_send(m).start()

    def slope_grads(m, a, b, extra):
        def unit(q):
            g = q % 2
            t = 2 * g + jnp.where(q < 2, 1 - c, c)
            dst = gown.at[jnp.where(q < 2, 0, m), g]
            for k in range(0, D, GW):
                dst[:, k : k + GW] = dot_tn(a[...], b[t, :, k : k + GW]).astype(BF)

            @pl.when(q < 2)
            def _():
                core_send(m, g).start()

        weave(4, unit, extra)

    def then(*steps):
        def run():
            for f, *args in steps:
                f(*args)

        return run

    def core_over(m):
        for g in range(2):
            core_send(m, g).wait_send()

    slope_grads(
        2,
        d_ffn,
        act,
        {
            1: then((core_fetch, 2, 0)),
            2: then((core_fetch, 2, 1), (core_add, 2, 0)),
            3: then((core_add, 2, 1), (core_over, 2)),
        },
    )

    def up_back(i):
        back_up(i // N_CHUNK, i % N_CHUNK, d_ffn, w, slope)

    weave(GROUPS * N_CHUNK, up_back, {7: then((sum_event, 0)), 11: then((sum_event, 1))})
    for i in range(2):
        y_copy(i).wait()
    has_left(y_stage(2), e_s.at[0])
    slope_grads(1, mid_low, slope, {1: then((sum_event, 2)), 3: then((sum_event, 3))})
    for g in range(2):
        core_fetch(1, g)
    weave(
        N_CHUNK,
        lambda i: back_first_norm(i, slope, w, prm, mid, n1, s1, d_ffn, ngrad),
        {
            0: then((core_add, 1, 0), (core_add, 1, 1), (core_over, 1)),
            1: then((sum_event, 4)),
            2: then((sum_event, 5)),
        },
    )

    def send_norms(i, act_on):
        if i == 0:
            act_on(remote(ngrad, n_c, ng_s.at[0], ng_r.at[0], core))
        elif i == 1:
            act_on(remote(n_c, n_x, ng_s.at[1], ng_r.at[1], other_x))
        elif i == 2:
            for dz in range(1, nz):
                act_on(remote(n_x, n_z.at[dz], ng_s.at[1 + dz], ng_r.at[1 + dz], {"z": z_of(dz)}))
        else:
            act_on(remote(n_out.at[y], n_out.at[y], ng_s.at[nz + 1], ng_r.at[nz + 1], across))

    send_norms(0, start)
    loop(GROUPS, lambda t: back_heads(t, d_ffn, wo, slope))
    sum_event(6)
    send_norms(0, recv)
    send_norms(0, lambda cp: cp.wait_send())
    n_c[...] += ngrad[...]
    send_norms(1, start)

    def attention_back(i):
        back_attend(i // per, [(i % per) * PAIR + k for k in range(PAIR)], proj, probs, slope)

        @pl.when(i % 2 == 1)
        def _():
            sum_event(7 + i // 2)

    loop(GROUPS * per, attention_back)
    seen = 7 + GROUPS * per // 2

    def qkv_grads(q):
        g, own = q // 2, q % 2

        def store(col, value):
            value = value.astype(BF)

            @pl.when(own == 0)
            def _():
                spare(0, g)[:, col : col + 128] = value

            @pl.when(own == 1)
            def _():
                gown[0, g, :, col : col + 128] = value

        grad_qkv_out(2 * g + jnp.where(own == 0, 1 - c, c), x, proj, d_ffn, hout, store)

        @pl.when(own == 0)
        def _():
            core_send(0, g).start()

    weave(
        4,
        qkv_grads,
        {
            0: then((sum_event, seen)),
            1: then((core_fetch, 0, 0), (sum_event, seen + 1)),
            2: then((core_add, 0, 0), (sum_event, seen + 2)),
            3: then((core_fetch, 0, 1), (core_add, 0, 1)),
        },
    )
    seen += 3

    def inputs_back(i):
        k = lax.rem(i + N_CHUNK - 1, N_CHUNK)

        def keep(r, grad):
            mid[r] = grad

            @pl.when(i == 0)
            def _():
                mid_low[:EXT_ROWS] = grad.astype(BF)

        back_input(k, proj, w, mid, keep)

        @pl.when(i == 0)
        def _():
            give_back(mid_low.at[pl.ds(0, EXT_ROWS)], g_back, 1, start)

    weave(N_CHUNK, inputs_back, {1: then((sum_event, seen)), 2: then((sum_event, seen + 1))})
    seen += 2
    after = 4 * nz
    if seen < after:
        loop(after - seen, lambda q: sum_event(seen + q))
    for g in range(2):
        finish(2, g)
    loop(2, lambda q: sum_event(after + q))

    trips = [
        pltpu.make_async_copy(g_back, proj.at[0, pl.ds(0, OWN_ROWS)], io_s.at[0]),
        pltpu.make_async_copy(y_out, proj.at[1, pl.ds(0, OWN_ROWS)], io_s.at[1]),
        pltpu.make_async_copy(y_back, proj.at[2, pl.ds(0, OWN_ROWS)], io_s.at[2]),
    ]
    y_again = pltpu.make_async_copy(proj.at[1, pl.ds(0, OWN_ROWS)], y_out, io_s.at[1])
    g_copy = pltpu.make_async_copy(mid.at[pl.ds(0, OWN_ROWS)], g_out, io_s.at[3])

    @pl.when(lender)
    def _():
        for i, dst in enumerate((y_back, g_back)):
            for j in range(2):
                arrived(dst.at[pl.ds(j * EXT_ROWS, EXT_ROWS)], e_r.at[i, j])
        for cp in trips:
            cp.start()
        for cp in trips:
            cp.wait()

        def merge(s):
            r = chunk_rows(s, LENGTH)
            keep = jnp.zeros((LENGTH, D), F32) + mine(s) > 0.5
            mid[r] = jnp.where(keep, mid[r], proj[0, r].astype(F32))
            proj[1, r] = jnp.where(keep, proj[1, r].astype(F32), proj[2, r].astype(F32)).astype(BF)

        loop(OWN, merge)
        y_again.start()

    g_copy.start()
    loop(nz - 2, lambda q: sum_event(after + 2 + q))
    send_norms(1, recv)
    send_norms(1, lambda cp: cp.wait_send())
    n_x[...] += n_c[...]
    send_norms(2, start)
    for g in range(2):
        finish(1, g)
    loop(nz - 1, lambda q: sum_event(after + nz + q))
    total = n_x[...]
    for dz in range(1, nz):
        arrived(n_z.at[dz], ng_r.at[1 + dz])
        total += n_z[dz]
    n_out[y] = total
    send_norms(3, start)
    finish(0, 0)
    sum_event(after + 2 * nz - 1)
    finish(0, 1)
    g_copy.wait()
    for m in (2, 1, 0):
        arrived(oth.at[m], y_r.at[m])
        out_stage(m, 1)[...] = oth[m].astype(F32)
        out_copy(m, 1).start()

    def sums_sent(i):
        m, g = i // 2, i % 2
        for zz in range(nz):
            @pl.when(z != zz)
            def _():
                has_left(r_x.at[0, 0, 0], z_s.at[m, g, zz])

            has_left(r_x.at[0, 0, 0], x_s.at[m, g, zz])

    loop(6, sums_sent)
    loop(6, gather_sent)
    for g in range(2):
        core_send(0, g).wait_send()
    for m in range(3):
        has_left(given(m), ys_s.at[m])
        for other in range(2):
            out_copy(m, other).wait()
        last_send(m).wait_send()
    lend(x_in, x, 0, lambda cp: cp.wait_send())
    lend(cot, d_ffn, 1, lambda cp: cp.wait_send())
    for i in range(4):
        norm_hop(i, lambda cp: cp.wait_send())
    send_norms(2, lambda cp: cp.wait_send())
    send_norms(3, lambda cp: cp.wait())
    has_left(mid_low.at[pl.ds(0, EXT_ROWS)], e_s.at[1])

    @pl.when(lender)
    def _():
        y_again.wait()


def run_step(nz, tags, lens, x_in, cot, qkv, wout, up, dn, gain, bias):
    rows = up.shape[1]
    V = pl.BlockSpec(memory_space=pltpu.VMEM)
    S = pl.BlockSpec(memory_space=pltpu.SMEM)
    sem = pltpu.SemaphoreType.DMA
    out = jax.ShapeDtypeStruct
    return pl.pallas_call(
        partial(step_kernel, nz, rows),
        out_shape=(
            out((OWN_ROWS, D), BF),
            out((OWN_ROWS, D), F32),
            out((2, rows, D), F32),
            out((2, rows, D), F32),
            out((2, rows, D), F32),
            out((2, 8, D), F32),
            out((OWN_ROWS, D), BF),
            out((OWN_ROWS, D), BF),
            out((3, 2, D, D), BF),
        ),
        in_specs=[S, S] + [ANY] * 6 + [V, V],
        out_specs=(ANY, ANY, ANY, ANY, ANY, V, ANY, ANY, ANY),
        scratch_shapes=[
            pltpu.VMEM((3, GROUPS, D, D), BF),
            pltpu.VMEM((ROWS, D), BF),
            pltpu.VMEM((GROUPS, ROWS, D), BF),
            pltpu.VMEM((GROUPS, SLOTS, LENGTH, 512), BF),
            pltpu.VMEM((GROUPS, ROWS, GW), BF),
            pltpu.VMEM((GROUPS, D, GW), BF),
            pltpu.VMEM((ROWS, D), F32),
            pltpu.VMEM((ROWS, D), BF),
            pltpu.VMEM((ROWS, 128), F32),
            pltpu.VMEM((ROWS, D), BF),
            pltpu.VMEM((GROUPS, ROWS, D), BF),
            pltpu.VMEM((GROUPS, ROWS, D), BF),
            pltpu.VMEM((ROWS, D), BF),
            pltpu.VMEM((3, 2, D, D), BF),
            pltpu.VMEM((3, 2, nz, rows, D), BF),
            pltpu.VMEM((3, 2, nz, rows, D), BF),
            pltpu.VMEM((3, rows, D), BF),
            pltpu.VMEM(qkv.shape, BF),
            pltpu.VMEM(wout.shape, BF),
            pltpu.VMEM((rows, D), BF),
            pltpu.VMEM((8 * nz, 8, 128), F32),
            pltpu.VMEM((8, D), F32),
            pltpu.VMEM((8, D), F32),
            pltpu.VMEM((8, D), F32),
            pltpu.VMEM((8, D), F32),
            pltpu.VMEM((nz, 8, D), F32),
            sem((6,)), sem((4,)), sem((2,)), sem((3, 2)),
            sem((3,)), sem((3,)),
            sem((3, 2, 2, nz)), sem((3, 2, 2, nz)),
            sem((2, nz)), sem((2, nz)),
            sem((3, 2, nz)), sem((3, 2, nz)),
            sem((3, 2, nz, 2)), sem((3, 2, nz, 2)),
            sem((2, 2)), sem((2,)),
            sem((nz + 2,)), sem((nz + 2,)),
            sem((3, 2)), sem((3, 2)),
            sem((3, 2, nz)), sem((3, 2, nz)),
            sem((3, 2, nz)), sem((3, 2, nz)),
            sem((3,)), sem((3,)),
            sem((2,)), sem((2, 2)),
            sem((nz + 2,)), sem((nz + 2,)),
        ],
        compiler_params=pltpu.CompilerParams(
            collective_id=0, has_side_effects=True, vmem_limit_bytes=67043328
        ),
        name="layer_step",
    )(tags, lens, x_in, cot, qkv, wout, up, dn, gain, bias)


def deliver_kernel(cols, y_in, g_in, qo, up_in, dn_in, sums,
                   y_out, g_out, qkv_out, wout_out, up_out, dn_out, gain_out, bias_out,
                   v_y, v_g, v_qo, v_up, v_dn, v_qkv, v_out, in_s, out_s):
    through = [(up_in, v_up, up_out), (dn_in, v_dn, dn_out)]
    for k in range(OWN):
        r = pl.ds(k * LENGTH, LENGTH)
        through.append((g_in.at[r], v_g.at[r], g_out.at[r]))
    for k in range(2):
        r = pl.ds(k * CHUNK, CHUNK)
        through.append((y_in.at[r], v_y.at[r], y_out.at[r]))
    n = len(through)
    first = pltpu.make_async_copy(qo, v_qo, in_s.at[n])
    first.start()
    loads, stores = [], []
    for i, (src, via, dst) in enumerate(through):
        loads.append(pltpu.make_async_copy(src, via, in_s.at[i]))
        stores.append(pltpu.make_async_copy(via, dst, out_s.at[i]))
        loads[-1].start()
    z, x, y, c = place()
    me = ((z * 2 + x) * 2 + y) * 2 + c
    for k in range(2):
        turned = pltpu.roll(sums[k], lax.rem(D - me * cols, D), 1)
        gain_out[k] = turned[0:2, :cols]
        bias_out[k] = turned[2:4, :cols]
    first.wait()
    for k in range(2):
        tail = []
        for i in range(3):
            v_qkv[k, i] = v_qo[k, :, GW * i : GW * i + GW - HEAD_DIM]
            tail.append(v_qo[k, :, GW * (i + 1) - HEAD_DIM : GW * (i + 1)])
        v_out[k] = jnp.concatenate(tail, 1)
    stores.append(pltpu.make_async_copy(v_qkv, qkv_out, out_s.at[n]))
    stores.append(pltpu.make_async_copy(v_out, wout_out, out_s.at[n + 1]))
    for i in range(n):
        loads[i].wait()
        stores[i].start()
    for cp in stores[n:]:
        cp.start()
    for cp in stores:
        cp.wait()


def deliver(cols, y_in, g_in, qo, up_in, dn_in, sums):
    rows = qo.shape[1]
    V = pl.BlockSpec(memory_space=pltpu.VMEM)
    sem = pltpu.SemaphoreType.DMA
    out = jax.ShapeDtypeStruct
    width = GW - HEAD_DIM
    shapes = [((2, 3, rows, width), F32), ((2, rows, width), F32)]
    whole = [(y_in.shape, BF), (g_in.shape, F32), (qo.shape, F32), (qo.shape, F32), (qo.shape, F32)]
    return pl.pallas_call(
        partial(deliver_kernel, cols),
        out_shape=tuple(
            out(*p) for p in whole[:2] + shapes + whole[3:] + [((2, 2, cols), F32)] * 2
        ),
        in_specs=[ANY] * 5 + [V],
        out_specs=(ANY,) * 6 + (V, V),
        scratch_shapes=[pltpu.VMEM(*p) for p in whole + shapes] + [sem((9,)), sem((10,))],
        name="deliver",
    )(y_in, g_in, qo, up_in, dn_in, sums)


def split_local(nz, x_in, tags, lengths, w_qkv, w_out, w_up, w_down, norm_gain, norm_bias, cotangent):
    cols = norm_gain.shape[2]
    y_out, x_grad, qo_grad, up_grad, down_grad, n_sum, _, _, _ = run_step(
        nz, tags, lengths, x_in, cotangent, w_qkv.transpose(0, 2, 1, 3), w_out, w_up, w_down, norm_gain, norm_bias
    )
    y_out, x_grad, qkv, out, up, down, gain, bias = deliver(
        cols, y_out, x_grad, qo_grad, up_grad, down_grad, n_sum
    )
    return y_out, x_grad, qkv.transpose(0, 2, 1, 3), out, up, down, gain, bias


def typed_map(operand, stacked, chain_kinds, pattern):

    def single(element):
        weight = lax.dynamic_index_in_dim(stacked, element[1], 0, keepdims=False)
        return jnp.einsum(pattern, element[0], weight, preferred_element_type=jnp.float32)

    return lax.map(single, (operand, chain_kinds))


def typed_grads(running, operand, partner, chain_kinds, pattern):

    def single(carry, element):
        product_term = jnp.einsum(
            pattern, element[0], element[1], preferred_element_type=jnp.float32
        )
        previous = lax.dynamic_index_in_dim(carry, element[2], 0, keepdims=False)
        return (
            lax.dynamic_update_index_in_dim(carry, previous + product_term, element[2], 0),
            None,
        )

    return lax.scan(single, running, (operand, partner, chain_kinds))[0]


def row_terms(operand, stacked, chain_kinds, pattern, row_count):
    result = typed_map(operand, stacked, chain_kinds, pattern)
    return result.reshape(row_count, result.shape[-1])


def old_norm_forward(values, gain_rows, shift_rows):
    center = values - jnp.mean(values, -1, keepdims=True)
    factor = lax.rsqrt(jnp.mean(center * center, -1, keepdims=True) + EPS)
    normed = center * factor
    return (normed * gain_rows + shift_rows, normed, factor)


def old_norm_backward(grad_out, normed, factor, gain_rows):
    scaled = grad_out * gain_rows
    mean_plain = jnp.mean(scaled, -1, keepdims=True)
    mean_normed = jnp.mean(scaled * normed, -1, keepdims=True)
    return factor * (scaled - mean_plain - normed * mean_normed)


def type_sums(onehot, values):
    return jnp.dot(onehot.T, values, precision=HIGH, preferred_element_type=jnp.float32)


def general_local(x_in, tags, lengths, w_qkv, w_out, w_up, w_down, norm_gain, norm_bias, cotangent):
    tp_count = lax.axis_size("tensor")
    tp_index = lax.axis_index("tensor")
    local_rows = CHAINS_PART * LENGTH
    batch_chains = tp_count * CHAINS_PART
    head_cols = w_qkv.shape[3]
    local_heads = head_cols // HEAD_DIM
    tag_grid = tags.reshape(tp_count, MICRO, CHAINS_PART)
    len_grid = lengths.reshape(tp_count, MICRO, CHAINS_PART)
    own_tags = lax.dynamic_index_in_dim(tag_grid, tp_index, 0, keepdims=False)
    gains, shifts = (
        lax.all_gather(norm_gain, ("dp", "tensor"), axis=2, tiled=True),
        lax.all_gather(norm_bias, ("dp", "tensor"), axis=2, tiled=True),
    )
    grad_full = (
        jnp.zeros((2, D, 3, head_cols), jnp.float32),
        jnp.zeros((2, D, head_cols), jnp.float32),
        jnp.zeros((2, D, w_up.shape[2]), jnp.float32),
        jnp.zeros((2, D, w_down.shape[2]), jnp.float32),
    )
    shards = (
        jnp.zeros(w_qkv.shape, jnp.float32),
        jnp.zeros(w_out.shape, jnp.float32),
        jnp.zeros(w_up.shape, jnp.float32),
        jnp.zeros(w_down.shape, jnp.float32),
    )
    gain_acc = jnp.zeros((2, 2, D), jnp.float32)
    shift_acc = jnp.zeros((2, 2, D), jnp.float32)
    outputs = []
    input_grads = []
    for micro_index in range(MICRO):
        held = (
            lax.all_gather(w_qkv, "dp", axis=1, tiled=True),
            lax.all_gather(w_out, "dp", axis=1, tiled=True),
            lax.all_gather(w_up, "dp", axis=1, tiled=True),
            lax.all_gather(w_down, "dp", axis=1, tiled=True),
        )
        qkv_w, out_w, up_w, down_w = held
        chain_kinds = tag_grid[:, micro_index].reshape(batch_chains)
        chain_lens = len_grid[:, micro_index].reshape(batch_chains)
        own_rows = x_in[micro_index * local_rows : (micro_index + 1) * local_rows]
        kinds_rows = jnp.repeat(own_tags[micro_index], LENGTH)
        heavy_rows = (kinds_rows == 0)[:, None]
        onehot = (kinds_rows[:, None] == jnp.arange(2)[None, :]).astype(jnp.float32)
        gain_mid = jnp.where(heavy_rows, gains[0, 0], gains[1, 0])
        shift_mid = jnp.where(heavy_rows, shifts[0, 0], shifts[1, 0])
        gain_end = jnp.where(heavy_rows, gains[0, 1], gains[1, 1])
        shift_end = jnp.where(heavy_rows, shifts[0, 1], shifts[1, 1])
        gathered = lax.all_gather(own_rows, "tensor", axis=0, tiled=True).reshape(
            batch_chains, LENGTH, D
        )
        projected = typed_map(gathered, qkv_w, chain_kinds, "ld,dkh->lkh").astype(jnp.bfloat16)
        query = projected[:, :, 0].reshape(batch_chains, LENGTH, local_heads, HEAD_DIM)
        keys_low = projected[:, :, 1].reshape(batch_chains, LENGTH, local_heads, HEAD_DIM)
        values_low = projected[:, :, 2].reshape(batch_chains, LENGTH, local_heads, HEAD_DIM)
        valid = (
            lax.broadcasted_iota(jnp.int32, (batch_chains, 1, 1, LENGTH), 3)
            < chain_lens[:, None, None, None]
        )
        scores = (
            jnp.einsum("cqhe,ckhe->chqk", query, keys_low, preferred_element_type=jnp.float32)
            * 0.125
        )
        scores = jnp.where(valid, scores, NEG)
        highest = jnp.max(scores, -1, keepdims=True)
        expo = jnp.exp(scores - highest)
        totals = jnp.sum(expo, -1, keepdims=True)
        probs = expo / totals
        log_total = highest + jnp.log(totals)
        heads_low = jnp.einsum(
            "chqk,ckhe->cqhe",
            probs.astype(jnp.bfloat16),
            values_low,
            preferred_element_type=jnp.float32,
        ).astype(jnp.bfloat16)
        heads_low = heads_low.reshape(batch_chains, LENGTH, head_cols)
        attn_sum = lax.psum_scatter(
            row_terms(
                heads_low, out_w, chain_kinds, "lh,dh->ld", lax.axis_size("tensor") * local_rows
            ).astype(jnp.bfloat16),
            "tensor",
            scatter_dimension=0,
            tiled=True,
        ).astype(jnp.float32)
        mid, normed_mid, factor_mid = old_norm_forward(
            own_rows.astype(jnp.float32) + attn_sum, gain_mid, shift_mid
        )
        mid_all = lax.all_gather(mid.astype(jnp.bfloat16), "tensor", axis=0, tiled=True).reshape(
            batch_chains, LENGTH, D
        )
        up_value = typed_map(mid_all, up_w, chain_kinds, "ld,df->lf")
        act_low = jax.nn.gelu(up_value, approximate=False).astype(jnp.bfloat16)
        ffn_sum = lax.psum_scatter(
            row_terms(
                act_low, down_w, chain_kinds, "lf,df->ld", lax.axis_size("tensor") * local_rows
            ).astype(jnp.bfloat16),
            "tensor",
            scatter_dimension=0,
            tiled=True,
        ).astype(jnp.float32)
        final, normed_end, factor_end = old_norm_forward(ffn_sum + mid, gain_end, shift_end)
        outputs.append(final.astype(jnp.bfloat16))
        base = grad_full
        grad_final = cotangent[micro_index * local_rows : (micro_index + 1) * local_rows].astype(
            jnp.float32
        )
        gain_acc = gain_acc.at[:, 1].add(type_sums(onehot, grad_final * normed_end))
        shift_acc = shift_acc.at[:, 1].add(type_sums(onehot, grad_final))
        grad_resid2 = old_norm_backward(grad_final, normed_end, factor_end, gain_end)
        grad_ffn = lax.all_gather(
            grad_resid2.astype(jnp.bfloat16), "tensor", axis=0, tiled=True
        ).reshape(batch_chains, LENGTH, D)
        grad_act = typed_map(grad_ffn, down_w, chain_kinds, "ld,df->lf")
        unused_value, gelu_back = jax.vjp(partial(jax.nn.gelu, approximate=False), up_value)
        grad_up = gelu_back(grad_act)[0].astype(jnp.bfloat16)
        down_acc = typed_grads(base[3], grad_ffn, act_low, chain_kinds, "ld,lf->df")
        up_acc = typed_grads(base[2], mid_all, grad_up, chain_kinds, "ld,lf->df")
        grad_mid = grad_resid2 + lax.psum_scatter(
            row_terms(
                grad_up, up_w, chain_kinds, "lf,df->ld", lax.axis_size("tensor") * local_rows
            ).astype(jnp.bfloat16),
            "tensor",
            scatter_dimension=0,
            tiled=True,
        ).astype(jnp.float32)
        gain_acc = gain_acc.at[:, 0].add(type_sums(onehot, grad_mid * normed_mid))
        shift_acc = shift_acc.at[:, 0].add(type_sums(onehot, grad_mid))
        grad_resid1 = old_norm_backward(grad_mid, normed_mid, factor_mid, gain_mid)
        grad_attn = lax.all_gather(
            grad_resid1.astype(jnp.bfloat16), "tensor", axis=0, tiled=True
        ).reshape(batch_chains, LENGTH, D)
        grad_heads = typed_map(grad_attn, out_w, chain_kinds, "ld,dh->lh").astype(jnp.bfloat16)
        out_acc = typed_grads(base[1], grad_attn, heads_low, chain_kinds, "ld,lh->dh")
        grad_heads = grad_heads.reshape(batch_chains, LENGTH, local_heads, HEAD_DIM)
        again = (
            jnp.einsum("cqhe,ckhe->chqk", query, keys_low, preferred_element_type=jnp.float32)
            * 0.125
        )
        probs_again = jnp.exp(jnp.where(valid, again, NEG) - log_total)
        grad_probs = jnp.einsum(
            "cqhe,ckhe->chqk", grad_heads, values_low, preferred_element_type=jnp.float32
        )
        inner = jnp.sum(grad_probs * probs_again, -1, keepdims=True)
        grad_scores = (probs_again * (grad_probs - inner)).astype(jnp.bfloat16)
        grad_query = (
            jnp.einsum("chqk,ckhe->cqhe", grad_scores, keys_low, preferred_element_type=jnp.float32)
            * 0.125
        ).astype(jnp.bfloat16)
        grad_keys = (
            jnp.einsum("chqk,cqhe->ckhe", grad_scores, query, preferred_element_type=jnp.float32)
            * 0.125
        ).astype(jnp.bfloat16)
        grad_values = jnp.einsum(
            "chqk,cqhe->ckhe",
            probs_again.astype(jnp.bfloat16),
            grad_heads,
            preferred_element_type=jnp.float32,
        ).astype(jnp.bfloat16)
        grad_proj = jnp.stack([grad_query, grad_keys, grad_values], 2).reshape(
            batch_chains, LENGTH, 3, head_cols
        )
        qkv_acc = typed_grads(base[0], gathered, grad_proj, chain_kinds, "ld,lkh->dkh")
        grad_input = grad_resid1 + lax.psum_scatter(
            row_terms(
                grad_proj, qkv_w, chain_kinds, "lkh,dkh->ld", lax.axis_size("tensor") * local_rows
            ).astype(jnp.bfloat16),
            "tensor",
            scatter_dimension=0,
            tiled=True,
        ).astype(jnp.float32)
        input_grads.append(grad_input)
        updated = (qkv_acc, out_acc, up_acc, down_acc)
        grad_full = updated
    shards = (
        lax.psum_scatter(grad_full[0], "dp", scatter_dimension=1, tiled=True),
        lax.psum_scatter(grad_full[1], "dp", scatter_dimension=1, tiled=True),
        lax.psum_scatter(grad_full[2], "dp", scatter_dimension=1, tiled=True),
        lax.psum_scatter(grad_full[3], "dp", scatter_dimension=1, tiled=True),
    )
    gain_grad, shift_grad = (
        lax.psum_scatter(gain_acc, ("dp", "tensor"), scatter_dimension=2, tiled=True),
        lax.psum_scatter(shift_acc, ("dp", "tensor"), scatter_dimension=2, tiled=True),
    )
    return (
        jnp.concatenate(outputs, 0),
        jnp.concatenate(input_grads, 0),
        shards[0],
        shards[1],
        shards[2],
        shards[3],
        gain_grad,
        shift_grad,
    )


def solution(mesh):
    placed = (
        P(("dp", "tensor"), None),
        P("dp"),
        P("dp"),
        P(None, "dp", None, "tensor"),
        P(None, "dp", "tensor"),
        P(None, "dp", "tensor"),
        P(None, "dp", "tensor"),
        P(None, None, ("dp", "tensor")),
        P(None, None, ("dp", "tensor")),
        P(("dp", "tensor"), None),
    )
    results = (
        P(("dp", "tensor"), None),
        P(("dp", "tensor"), None),
        P(None, "dp", None, "tensor"),
        P(None, "dp", "tensor"),
        P(None, "dp", "tensor"),
        P(None, "dp", "tensor"),
        P(None, None, ("dp", "tensor")),
        P(None, None, ("dp", "tensor")),
    )
    n_dp, n_tensor = mesh.shape["dp"], mesh.shape["tensor"]
    if n_tensor != GROUPS or n_dp != 8:
        return jax.shard_map(
            general_local, mesh=mesh, in_specs=placed, out_specs=results, check_vma=False
        )
    fine = Mesh(mesh.devices.reshape(n_dp // 2, 2, 2, 2), AXES)
    names = {"dp": ("z", "x"), "tensor": ("y", "c")}

    def refine(spec):
        parts = []
        for entry in spec:
            entry = (entry,) if isinstance(entry, str) else entry
            parts.append(entry and sum((names[a] for a in entry), ()))
        return P(*parts)

    return jax.shard_map(
        partial(split_local, n_dp // 2),
        mesh=fine,
        in_specs=tuple(refine(s) for s in placed),
        out_specs=tuple(refine(s) for s in results),
        check_vma=False,
    )
```

```python
from functools import partial

import jax
import jax.numpy as jnp
from jax import lax
from jax.experimental import pallas as pl
from jax.experimental.pallas import tpu as pltpu
from jax.sharding import Mesh
from jax.sharding import PartitionSpec as P

D = 768
HEADS = 12
HEAD_DIM = 64
MICRO = 4
CHAINS_PART = 1
LENGTH = 160
GROUPS = 4
OWN = 4
EXTRA = 2
SLOTS = OWN + EXTRA
EXT_ROWS = EXTRA * LENGTH
OWN_ROWS = OWN * LENGTH
ROWS = SLOTS * LENGTH

EPS = 1e-12
NEG = -1e30
HIGH = lax.Precision.HIGHEST
BF = jnp.bfloat16
F32 = jnp.float32
MESH = pl.DeviceIdType.MESH
ANY = pl.BlockSpec(memory_space=pl.ANY)
AXES = ("z", "x", "y", "c")


def place():
    return tuple(lax.axis_index(a) for a in AXES)


def greet(nz, z, x, y, c):
    barrier = pltpu.get_barrier_semaphore()
    friends = [{"c": 1 - c}, {"y": 1 - y}, {"y": 1 - y, "c": 1 - c}, {"x": 1 - x}]
    friends += [{"z": lax.rem(z + dz, nz)} for dz in range(1, nz)]
    for friend in friends:
        pl.semaphore_signal(barrier, inc=1, device_id=friend, device_id_type=MESH)
    return barrier, len(friends)


CHUNK = 320
SUB = 80
N_CHUNK = ROWS // CHUNK
WIDE = 3 * LENGTH
GW = 256
PAIR = 3


def dot_nn(a, b):
    return lax.dot_general(a, b, (((1,), (0,)), ((), ())), preferred_element_type=F32)


def dot_nt(a, b):
    return lax.dot_general(a, b, (((1,), (1,)), ((), ())), preferred_element_type=F32)


def dot_tn(a, b):
    return lax.dot_general(a, b, (((0,), (0,)), ((), ())), preferred_element_type=F32)


def lanes(shape):
    return lax.broadcasted_iota(jnp.int32, shape, len(shape) - 1)


def head_mask(h, shape):
    lane = lanes(shape)
    return jnp.logical_and(lane >= h * HEAD_DIM, lane < (h + 1) * HEAD_DIM)


def stack_heads(rows):
    zero = jnp.zeros_like(rows)
    return jnp.concatenate([jnp.where(head_mask(h, rows.shape), rows, zero) for h in range(3)], 0)


def merge_heads(stack):
    out = jnp.zeros((LENGTH, GW), stack.dtype)
    for h in range(3):
        out = jnp.where(head_mask(h, out.shape), stack[h * LENGTH : (h + 1) * LENGTH], out)
    return out


def chunk_rows(i, size=CHUNK):
    return pl.ds(pl.multiple_of(i * size, size), size)


def loop(count, body):
    def step(i, carry):
        body(i)
        return carry

    lax.fori_loop(0, count, step, 0)


def weave(count, unit, extra):
    def body(i):
        unit(i)
        for k, step in extra.items():
            pl.when(i == k)(step)

    loop(count, body)


def out_columns(t, w, wo):
    low = lanes((D, 128)) < HEAD_DIM
    tiles = [w[0, t, :, GW * i + 128 : GW * i + 256].astype(F32) for i in range(3)]
    wo[t, :, :128] = jnp.where(low, pltpu.roll(tiles[0], 64, 1), tiles[1]).astype(BF)
    wo[t, :, 128:] = jnp.where(low, pltpu.roll(tiles[2], 64, 1), 0.0).astype(BF)


def attend(t, chains, lens, proj, probs, hout):
    rows = [chunk_rows(s, LENGTH) for s in chains]
    parts = [(proj[t, r, :GW], proj[t, r, GW : 2 * GW], proj[t, r, 2 * GW :]) for r in rows]
    lows, outs = [], []
    for s, (query, key, value) in zip(chains, parts):
        scores = dot_nt(key, stack_heads(query * jnp.asarray(0.125, BF)))
        valid = lax.broadcasted_iota(jnp.int32, (LENGTH, 1), 0) < lens(s)
        scores = jnp.where(valid, scores, NEG)
        expo = jnp.exp(scores - jnp.max(scores, 0, keepdims=True))
        lows.append((expo * (1.0 / jnp.sum(expo, 0, keepdims=True))).astype(BF))
        outs.append(merge_heads(dot_tn(lows[-1], value)).astype(BF))
    for s, r, low, out in zip(chains, rows, lows, outs):
        probs[t, s, :, :WIDE] = low
        hout[t, r] = out


def norm_rows(values):
    center = values - jnp.mean(values, -1, keepdims=True)
    factor = lax.rsqrt(jnp.mean(center * center, -1, keepdims=True) + EPS)
    return center * factor, factor


def norm_back(scaled, normed, factor):
    return factor * (
        scaled
        - jnp.mean(scaled, -1, keepdims=True)
        - normed * jnp.mean(scaled * normed, -1, keepdims=True)
    )


def pieces(i, body):
    def step(k):
        body(pl.ds(pl.multiple_of(i * CHUNK + k * SUB, SUB), SUB), k)

    loop(CHUNK // SUB, step)


def first_norm(i, x, hout, wo, prm, mid, n1, s1, mid_low):
    r = chunk_rows(i)
    attn = dot_nt(hout[0, r], wo[0])
    for t in range(1, GROUPS):
        attn += dot_nt(hout[t, r], wo[t])
    mid[r] = attn

    def piece(p, k):
        normed, factor = norm_rows(x[p].astype(F32) + mid[p])
        n1[p] = normed.astype(BF)
        s1[p] = jnp.broadcast_to(factor, (SUB, 128))
        value = normed * prm[0:1] + prm[2:3]
        mid[p] = value
        mid_low[p] = value.astype(BF)

    pieces(i, piece)


def feed_up(t, i, mid_low, w, act, slope):
    r = chunk_rows(i)
    for k in range(0, D, GW):
        up = dot_nn(mid_low[r], w[1, t, :, k : k + GW])
        cdf = 0.5 * (1.0 + lax.erf(up * 0.7071067811865476))
        act[t, r, k : k + GW] = (up * cdf).astype(BF)
        bell = 0.3989422804014327 * jnp.exp(-0.5 * up * up)
        slope[t, r, k : k + GW] = (cdf + up * bell).astype(BF)


def feed_down(i, t, act, w, mid):
    r = chunk_rows(i)
    mid[r] += dot_nt(act[t, r], w[2, t]) + dot_nt(act[t + 1, r], w[2, t + 1])


def second_norm(i, t, act, w, prm, mid, cot, mine, y_rows, d_ffn, ngrad):
    feed_down(i, t, act, w, mid)

    def piece(p, k):
        normed, factor = norm_rows(mid[p])
        y_rows[pl.ds(pl.multiple_of(k * SUB, SUB), SUB)] = (normed * prm[1:2] + prm[3:4]).astype(BF)
        grad = cot[p].astype(F32) * jnp.where(k < LENGTH // SUB, mine(2 * i), mine(2 * i + 1))
        ngrad[1:2] += jnp.sum(grad * normed, 0, keepdims=True)
        ngrad[3:4] += jnp.sum(grad, 0, keepdims=True)
        back = norm_back(grad * prm[1:2], normed, factor)
        mid[p] = back
        d_ffn[p] = back.astype(BF)

    pieces(i, piece)


def back_up(t, i, d_ffn, w, slope):
    r = chunk_rows(i)
    slope[t, r] = (dot_nn(d_ffn[r], w[2, t]) * slope[t, r].astype(F32)).astype(BF)


def back_first_norm(i, d_up, w, prm, mid, n1, s1, d_attn, ngrad):
    r = chunk_rows(i)
    grad = dot_nt(d_up[0, r], w[1, 0])
    for t in range(1, GROUPS):
        grad += dot_nt(d_up[t, r], w[1, t])
    mid[r] += grad

    def piece(p, k):
        grad = mid[p]
        normed = n1[p].astype(F32)
        ngrad[0:1] += jnp.sum(grad * normed, 0, keepdims=True)
        ngrad[2:3] += jnp.sum(grad, 0, keepdims=True)
        back = norm_back(grad * prm[0:1], normed, s1[p, 0:1])
        mid[p] = back
        d_attn[p] = back.astype(BF)

    pieces(i, piece)


def back_heads(t, d_attn, wo, d_heads):
    d_heads[t, :, :GW] = dot_nn(d_attn[...], wo[t]).astype(BF)


def back_attend(t, chains, proj, probs, d_heads):
    rows = [chunk_rows(s, LENGTH) for s in chains]
    parts = [
        (proj[t, r, :GW], proj[t, r, GW : 2 * GW], proj[t, r, 2 * GW :], d_heads[t, r, :GW], probs[t, s, :, :WIDE])
        for s, r in zip(chains, rows)
    ]
    results = []
    for query, key, value, grad, low in parts:
        grad = stack_heads(grad)
        p = low.astype(F32)
        d_probs = dot_nt(value, grad)
        d_scores = (p * (d_probs - jnp.sum(d_probs * p, 0, keepdims=True))).astype(BF)
        d_query = merge_heads(dot_tn(d_scores, key)) * 0.125
        d_key = dot_nn(d_scores, stack_heads(query * jnp.asarray(0.125, BF)))
        results.append((d_query.astype(BF), d_key.astype(BF), dot_nn(low, grad).astype(BF)))
    for r, (d_query, d_key, d_value) in zip(rows, results):
        proj[t, r, :GW] = d_query
        proj[t, r, GW : 2 * GW] = d_key
        proj[t, r, 2 * GW :] = d_value


def grad_qkv_out(t, x, d_proj, d_attn, hout, store):
    low = lanes((D, 128)) < HEAD_DIM
    outs = dot_tn(d_attn[...], hout[t])
    places = (pltpu.roll(outs[:, :128], 64, 1), outs[:, :128], pltpu.roll(outs[:, 128:], 64, 1))
    for i in range(3):
        part = dot_tn(x[...], d_proj[t, :, GW * i : GW * (i + 1)])
        store(GW * i, part[:, :128])
        store(GW * i + 128, jnp.where(low, part[:, 128:], places[i]))


def back_input(i, d_proj, w, mid, out):
    r = chunk_rows(i)
    grad = mid[r]
    for t in range(GROUPS):
        grad += dot_nt(d_proj[t, r], w[0, t])
    out(r, grad)


MIXED = (2, 1)
GATHER_FIRST = (
    ('X', 0, 0), ('L', 0, 0), ('y', 0), ('X', 0, 1), ('L', 0, 1),
    ('z', 0, 0, 1), ('z', 0, 1, 1), ('z', 0, 0, 2), ('x', 0, 0, 0), ('z', 0, 1, 2),
    ('z', 0, 0, 3), ('y', 1), ('L', 1, 1), ('x', 0, 1, 1), ('z', 0, 1, 3),
    ('x', 0, 1, 0), ('y', 2), ('X', 2, 1), ('L', 1, 0), ('X', 1, 0),
    ('x', 0, 0, 2), ('X', 1, 1), ('z', 1, 1, 1), ('x', 0, 0, 3), ('L', 2, 0),
    ('x', 0, 0, 1), ('x', 0, 1, 2), ('x', 0, 1, 3), ('z', 1, 0, 1),
)
GATHER_QKV = {
    6: (('z', 1, 1, 2),),
    11: (('z', 1, 0, 2),),
}
GATHER_ATTEND = {
    2: (('x', 2, 1, 0),),
    3: (('x', 1, 1, 1), ('x', 1, 0, 0), ('z', 1, 0, 3),),
    4: (('L', 2, 1), ('z', 1, 1, 3), ('x', 1, 1, 0),),
    5: (('z', 2, 0, 1), ('X', 2, 0),),
}
GATHER_NORM = {
    0: (('z', 2, 1, 1),),
    1: (('x', 1, 0, 3), ('x', 1, 0, 1), ('x', 1, 1, 2), ('x', 1, 0, 2), ('x', 1, 1, 3),),
    2: (('z', 2, 0, 2),),
}
GATHER_UP = {
    3: (('z', 2, 1, 2),),
    5: (('z', 2, 0, 3),),
    8: (('x', 2, 0, 1),),
    10: (('x', 2, 0, 0), ('x', 2, 0, 2), ('x', 2, 0, 3),),
    11: (('z', 2, 1, 3),),
}


def remote(src, dst, s_sem, r_sem, who):
    return pltpu.make_async_remote_copy(
        src_ref=src, dst_ref=dst, send_sem=s_sem, recv_sem=r_sem, device_id=who, device_id_type=MESH
    )


def arrived(ref, sem):
    remote(ref, ref, sem, sem, {"c": 1 - lax.axis_index("c")}).wait_recv()


def has_left(ref, sem):
    remote(ref, ref, sem, sem, {"c": 1 - lax.axis_index("c")}).wait_send()


def step_kernel(nz, rows,
                tags, lens, x_in, cot, qkv, wout, up, dn, gain, bias,
                y_out, g_out, qo_out, up_out, dn_out, n_out, y_back, g_back, r_c,
                w, x, proj, probs, hout, wo, mid, n1, s1, mid_low, act, slope, d_ffn, gown, r_xz, oth, v_qkv, v_out, far,
                n_all, prm, ngrad, n_c, n_x, n_z,
                load_s, io_s, stage_s, out_s,
                ys_s, ys_r, zs_s, zs_r, zm_s, zm_r, xs_s, xs_r, cs_s, cs_r, ex_s, ex_r, na_s, na_r,
                c_s, c_r, cp_s, cp_r, x_s, x_r, z_s, z_r, y_s, y_r, e_s, e_r, ng_s, ng_r):
    z, xc, y, c = place()
    core, across, other_x = {"c": 1 - c}, {"y": 1 - y}, {"x": 1 - xc}
    diagonal = {"y": 1 - y, "c": 1 - c}
    mats = (None, up, dn)
    lender = y != c
    home = (2 * y + c) * OWN
    away = (2 - y) * OWN + c * EXTRA

    def z_of(dz):
        return lax.rem(z + dz, nz)

    def chain(s):
        return jnp.where(s < OWN, home + s, away + s - OWN)

    def length_of(s):
        return lens[chain(s)]

    def mine(s):
        return jnp.where(tags[chain(s)] == y, 1.0, 0.0)

    def part(zz, xx):
        return pl.ds(pl.multiple_of((zz * 2 + xx) * rows, rows), rows)

    def group(g):
        return 2 * lax.rem(y + g, 2) + c

    def block(m, g, zz, xx):
        return w.at[m, group(g), part(zz, xx)]

    loads = [pltpu.make_async_copy(mats[m].at[y], block(m, 0, z, xc), load_s.at[m]) for m in range(1, 3)]
    loads += [
        pltpu.make_async_copy(x_in, x.at[pl.ds(0, OWN_ROWS)], load_s.at[3]),
        pltpu.make_async_copy(cot, d_ffn.at[pl.ds(0, OWN_ROWS)], load_s.at[4]),
        pltpu.make_async_copy(qkv, v_qkv, load_s.at[0]),
        pltpu.make_async_copy(wout, v_out, load_s.at[5]),
    ]
    for cp in loads:
        cp.start()
    barrier, friends = greet(nz, z, xc, y, c)
    me = ((z * 2 + xc) * 2 + y) * 2 + c
    cols = gain.shape[2]
    n_all[me] = jnp.zeros((8, 128), F32)
    for i in range(2):
        n_all[me, 2 * i : 2 * i + 2, :cols] = gain[i]
        n_all[me, 4 + 2 * i : 6 + 2 * i, :cols] = bias[i]
    ngrad[...] = jnp.zeros_like(ngrad)
    for cp in loads[4:]:
        cp.wait()

    def packed(k):
        tail = v_out[k]
        cols = []
        for i in range(3):
            cols += [v_qkv[k, i], tail[:, HEAD_DIM * i : HEAD_DIM * (i + 1)]]
        return jnp.concatenate(cols, 1)

    w[0, group(0), part(z, xc)] = packed(y)
    far[...] = packed(1 - y)
    pl.semaphore_wait(barrier, friends)

    def given(m):
        return mats[m].at[1 - y] if m else far

    def lend(arr, out, i, act_on):
        @pl.when(lender)
        def _():
            for j, (who, p) in enumerate(((across, c), (diagonal, 1 - c))):
                src = arr.at[pl.ds(pl.multiple_of(p * EXT_ROWS, EXT_ROWS), EXT_ROWS)]
                act_on(remote(src, out.at[pl.ds(OWN_ROWS, EXT_ROWS)], ex_s.at[i, j], ex_r.at[i], who))

    for m in range(3):
        remote(given(m), w.at[m, group(0), part(z, xc)], ys_s.at[m], ys_r.at[m], across).start()
    lend(x_in, x, 0, lambda cp: cp.start())
    lend(cot, d_ffn, 1, lambda cp: cp.start())

    def inside(zz):
        return jnp.logical_and(zz >= 0, zz < nz)

    def start(cp):
        cp.start()

    def recv(cp):
        cp.wait_recv()

    def hop(m, g, d, j, ref, act_on, col=0):
        to = z + 1 - 2 * d
        sems = (zm_s.at[d, j], zm_r.at[d, j]) if col else (zs_s.at[m, g, d, j], zs_r.at[m, g, d, j])

        @pl.when(jnp.logical_and(inside(to), j < nz))
        def _():
            act_on(remote(ref, ref, *sems, {"z": to}))

    def x_copy(m, g, zz):
        ref = block(m, g, zz, xc)
        return remote(ref, ref, xs_s.at[m, g, zz], xs_r.at[m, g, zz], other_x)

    def c_copy(m, g, zz, xx):
        ref = block(m, g, zz, xx)
        return remote(ref, ref, cs_s.at[m, g, zz, xx], cs_r.at[m, g, zz, xx], core)

    def from_y(m):
        arrived(block(m, 1, z, xc), ys_r.at[m])

    def own_z(m, g):
        for d in range(2):
            hop(m, g, d, 1, block(m, g, z, xc), start)

    def own_xc(m, g):
        x_copy(m, g, z).start()
        c_copy(m, g, z, xc).start()

    def z_event(m, g, j):
        mixed = (m, g) == MIXED

        def body(d):
            zz = z - j + 2 * j * d

            @pl.when(inside(zz))
            def _():
                for col in range(2 if mixed else 1):
                    ref = block(m, g, zz, lax.rem(xc + col, 2))
                    arrived(ref, zm_r.at[d, j] if col else zs_r.at[m, g, d, j])
                    hop(m, g, d, j + 1, ref, start, col)
                    if not mixed:
                        x_copy(m, g, zz).start()
                    c_copy(m, g, zz, lax.rem(xc + col, 2)).start()

        loop(2, body)

    def x_event(m, g, j):
        def body(d):
            zz = z - j + 2 * j * d

            @pl.when(inside(zz))
            def _():
                ref = block(m, g, zz, 1 - xc)
                arrived(ref, xs_r.at[m, g, zz])
                if (m, g) == MIXED:
                    for way in range(2):
                        hop(m, g, way, 1, ref, start, 1)
                c_copy(m, g, zz, 1 - xc).start()

        loop(2 if j else 1, body)

    kinds = {"y": from_y, "L": own_z, "X": own_xc, "z": z_event, "x": x_event}

    def gather_steps(plan):
        def run(steps):
            for kind, *args in steps:
                kinds[kind](*args)

        return {k: partial(run, steps) for k, steps in plan.items()}

    def gathered(m, first=0, last=2):
        def body(i):
            g = first + i // (2 * nz)
            t = 2 * lax.rem(y + g, 2) + 1 - c
            zz, xx = (i // 2) % nz, i % 2
            arrived(w.at[m, t, part(zz, xx)], cs_r.at[m, g, zz, xx])

        loop(2 * nz * (last - first), body)

    def gather_sent(i):
        m, g = i // 2, i % 2
        ref = w.at[0, 0, pl.ds(0, rows)]
        mixed = i == 2 * MIXED[0] + MIXED[1]
        for j in range(1, nz):
            for d in range(2):
                @pl.when(inside(z - (1 - 2 * d) * (j - 1)))
                def _():
                    hop(m, g, d, j, ref, lambda cp: cp.wait_send())

                    @pl.when(mixed)
                    def _():
                        hop(m, g, d, j, ref, lambda cp: cp.wait_send(), 1)
        for zz in range(nz):
            @pl.when(jnp.logical_or(jnp.logical_not(mixed), z == zz))
            def _():
                has_left(ref, xs_s.at[m, g, zz])

            for xx in range(2):
                has_left(ref, cs_s.at[m, g, zz, xx])

    def norm_hop(i, act_on):
        if i == 0:
            act_on(remote(n_all.at[me], n_all.at[me], na_s.at[0], na_r.at[0], core))
        elif i == 1:
            ref = n_all.at[pl.ds(me - c, 2)]
            act_on(remote(ref, ref, na_s.at[1], na_r.at[1], across))
        elif i == 2:
            ref = n_all.at[pl.ds(me - c - 2 * y, 4)]
            act_on(remote(ref, ref, na_s.at[2], na_r.at[2], other_x))
        else:
            ref = n_all.at[pl.ds(8 * z, 8)]
            for dz in range(1, nz):
                act_on(remote(ref, ref, na_s.at[2 + dz], na_r.at[2 + dz], {"z": z_of(dz)}))

    for cp in loads[:2]:
        cp.wait()
    norm_hop(0, start)
    for kind, *args in GATHER_FIRST:
        kinds[kind](*args)
        if (kind, *args) == ("z", 0, 0, 1):
            norm_hop(0, recv)
            norm_hop(1, start)
        if (kind, *args) == ("z", 0, 0, 3):
            norm_hop(1, recv)
            norm_hop(2, start)
    norm_hop(2, recv)
    norm_hop(3, start)
    gathered(0)
    loads[2].wait()
    arrived(x.at[pl.ds(OWN_ROWS, EXT_ROWS)], ex_r.at[0])

    def projection(i):
        t, k = i // N_CHUNK, i % N_CHUNK
        r = chunk_rows(k)
        proj[t, r] = dot_nn(x[r], w[0, t]).astype(BF)

        @pl.when(k == N_CHUNK - 1)
        def _():
            out_columns(t, w, wo)

    weave(GROUPS * N_CHUNK, projection, gather_steps(GATHER_QKV))
    per = SLOTS // PAIR

    def attention(i):
        attend(i // per, [(i % per) * PAIR + k for k in range(PAIR)], length_of, proj, probs, hout)

    weave(GROUPS * per, attention, gather_steps(GATHER_ATTEND))
    norm_hop(3, recv)
    lane = lanes((2, D))
    gains, shifts = jnp.zeros((2, D), F32), jnp.zeros((2, D), F32)
    for d in range(8 * nz):
        within = jnp.logical_and(lane >= d * cols, lane < (d + 1) * cols)
        for name in range(2):
            piece = n_all[d, pl.ds(4 * name + 2 * y, 2), :]
            piece = jnp.concatenate([piece, jnp.zeros((2, D - 128), F32)], 1)
            piece = jnp.where(within, pltpu.roll(piece, d * cols, 1) if d else piece, 0.0)
            if name == 0:
                gains += piece
            else:
                shifts += piece
    prm[0:2] = gains
    prm[2:4] = shifts
    weave(
        N_CHUNK,
        lambda i: first_norm(i, x, hout, wo, prm, mid, n1, s1, mid_low),
        gather_steps(GATHER_NORM),
    )
    gathered(1)
    weave(
        GROUPS * N_CHUNK,
        lambda i: feed_up(i // N_CHUNK, i % N_CHUNK, mid_low, w, act, slope),
        gather_steps(GATHER_UP),
    )
    gathered(2, 0, 1)
    first_two = 2 * y
    last_two = 2 - first_two
    loop(N_CHUNK, lambda i: feed_down(i, first_two, act, w, mid))
    gathered(2, 1, 2)
    loads[3].wait()
    arrived(d_ffn.at[pl.ds(OWN_ROWS, EXT_ROWS)], ex_r.at[1])

    def y_stage(i):
        return r_xz.at[i // 2, 0, pl.ds(pl.multiple_of((i % 2) * CHUNK, CHUNK), CHUNK)]

    def give_back(src, dst, i, act_on):
        dst = dst.at[pl.ds(pl.multiple_of(c * EXT_ROWS, EXT_ROWS), EXT_ROWS)]

        @pl.when(c == y)
        def _():
            act_on(remote(src, dst, e_s.at[i], e_r.at[i, c], across))

        @pl.when(c != y)
        def _():
            act_on(remote(src, dst, e_s.at[i], e_r.at[i, c], diagonal))

    def y_copy(i):
        return pltpu.make_async_copy(y_stage(i), y_out.at[pl.ds(i * CHUNK, CHUNK)], io_s.at[i])

    loop(
        N_CHUNK,
        lambda i: second_norm(
            i, last_two, act, w, prm, mid, d_ffn, mine, y_stage(i), d_ffn, ngrad
        ),
    )
    for i in range(2):
        y_copy(i).start()
    give_back(y_stage(2), y_back, 0, start)

    def x_place(m, g, i):
        return r_xz.at[0, m, pl.ds(pl.multiple_of((g * nz + i) * rows, rows), rows)]

    def z_place(m, g, i):
        return r_xz.at[1, m, pl.ds(pl.multiple_of((g * nz + i) * rows, rows), rows)]

    def spare(m, g):
        return gown.at[0, g] if m else act.at[2 * g + c, pl.ds(0, D)]

    def core_send(m, g):
        there = r_c.at[g] if m else spare(0, g)
        return remote(spare(m, g), there, c_s.at[m, g], c_r.at[m, g], core)

    def fetch(g):
        return pltpu.make_async_copy(r_c.at[g], act.at[2 * g + 1 - c, pl.ds(0, D)], stage_s.at[g])

    def core_piece(g, k):
        cols = pl.ds(k * GW, GW)
        return remote(gown.at[0, g, :, cols], gown.at[1, g, :, cols], cp_s.at[g, k], cp_r.at[g, k], core)

    def core_fetch(g):
        arrived(r_c.at[g], c_r.at[1, g])
        fetch(g).start()

    middle = jnp.logical_and(z > 0, z < nz - 1)

    def target(k):
        down = jnp.where(nz - 1 - k > z, nz - 1 - k, nz - 2 - k)
        up = jnp.where(k < z, k, k + 1)
        return jnp.where(k == nz - 1, z, jnp.where(z < nz // 2, down, up))

    def core_add(m, g):
        if m == 2:
            for k in range(D // GW):
                core_piece(g, k).wait_recv()
            from_core = gown.at[1, g]
        else:
            from_core = act.at[2 * g + 1 - c, pl.ds(0, D)]
            if m == 1:
                fetch(g).wait()
            else:
                arrived(from_core, c_r.at[0, g])

        def add(i):
            p = part(target(i % nz), lax.rem(xc + 1 + i // nz, 2))
            gown[m, g, p] += from_core[p]

        def over(k):
            zz = target(k)
            remote(gown.at[m, g, part(zz, 1 - xc)], x_place(m, g, zz), x_s.at[m, g, zz], x_r.at[m, g, zz], other_x).start()

        loop(nz + 1, add)
        loop(nz, over)
        loop(nz - 1, lambda i: add(nz + 1 + i))

    def sum_event(q):
        m = 2 - q // (2 * nz)
        g = (q // nz) % 2
        k = q % nz
        zz = target(k)
        over = x_place(m, g, zz)
        arrived(over, x_r.at[m, g, zz])
        p = part(zz, xc)
        gown[m, g, p] += over[...]

        joins = jnp.logical_and(k == 0, jnp.logical_not(middle))
        waits = jnp.logical_and(k == 0, middle)
        beside = jnp.where(z == 0, 1, nz - 2)
        to = jnp.where(joins, beside, zz)
        slot = jnp.where(joins, beside, z)

        @pl.when(jnp.logical_and(k < nz - 1, jnp.logical_not(waits)))
        def _():
            remote(gown.at[m, g, p], z_place(m, g, slot), z_s.at[m, g, zz], z_r.at[m, g, slot], {"z": to}).start()

        @pl.when(jnp.logical_and(k == jnp.where(m == 0, 1, nz - 2), middle))
        def _():
            far = target(0)
            f = part(far, xc)
            arrived(z_place(m, g, z), z_r.at[m, g, z])
            gown[m, g, f] += z_place(m, g, z)[...]
            remote(gown.at[m, g, f], z_place(m, g, z), z_s.at[m, g, far], z_r.at[m, g, z], {"z": far}).start()

    outs = (qo_out, up_out, dn_out)

    def out_stage(m, other):
        return mid.at[pl.ds(m * rows + (0 if other else OWN_ROWS), rows)]

    def out_copy(m, other):
        return pltpu.make_async_copy(out_stage(m, other), outs[m].at[1 - y if other else y], out_s.at[m, other])

    def last_send(m):
        return remote(mid_low.at[pl.ds(EXT_ROWS + m * rows, rows)], oth.at[m], y_s.at[m], y_r.at[m], across)

    def finish(m, g):
        total = gown[m, g, part(z, xc)].astype(F32)
        for dz in range(1, nz):
            source = z_of(dz)
            direct = jnp.abs(source - z) < nz - 1

            @pl.when(direct)
            def _():
                arrived(z_place(m, g, source), z_r.at[m, g, source])

            total += jnp.where(direct, z_place(m, g, source)[...].astype(F32), 0.0)

        @pl.when(y == g)
        def _():
            out_stage(m, 0)[...] = total
            out_copy(m, 0).start()

        @pl.when(y != g)
        def _():
            mid_low[EXT_ROWS + m * rows : EXT_ROWS + (m + 1) * rows] = total.astype(BF)
            last_send(m).start()

    def slope_grads(m, a, b, extra):
        def unit(q):
            g, own = (q // 2, q % 2) if m == 2 else (q % 2, q // 2)
            t = 2 * g + jnp.where(own == 0, 1 - c, c)
            dst = gown.at[jnp.where(own == 0, 0, m), g]
            for k in range(D // GW):
                cols = slice(k * GW, (k + 1) * GW)
                dst[:, cols] = dot_tn(a[...], b[t, :, cols]).astype(BF)

                if m == 2 and k:
                    pl.when(own == 0)(core_piece(g, k - 1).start)

            @pl.when(own == 0)
            def _():
                if m == 2:
                    core_piece(g, D // GW - 1).start()
                else:
                    core_send(m, g).start()

        weave(4, unit, extra)

    def then(*steps):
        def run():
            for f, *args in steps:
                f(*args)

        return run

    def core_over(m):
        for g in range(2):
            if m == 2:
                for k in range(D // GW):
                    core_piece(g, k).wait_send()
            else:
                core_send(m, g).wait_send()

    slope_grads(
        2,
        d_ffn,
        act,
        {
            1: then((core_add, 2, 0)),
            3: then((core_add, 2, 1), (core_over, 2)),
        },
    )

    def up_back(i):
        back_up(i // N_CHUNK, i % N_CHUNK, d_ffn, w, slope)

    weave(GROUPS * N_CHUNK, up_back, {1: then((sum_event, 0)), 7: then((sum_event, 1)), 11: then((sum_event, 2))})
    for i in range(2):
        y_copy(i).wait()
    has_left(y_stage(2), e_s.at[0])
    slope_grads(1, mid_low, slope, {1: then((sum_event, 3)), 3: then((sum_event, 4))})
    for g in range(2):
        core_fetch(g)
    weave(
        N_CHUNK,
        lambda i: back_first_norm(i, slope, w, prm, mid, n1, s1, d_ffn, ngrad),
        {
            0: then((core_add, 1, 0), (core_add, 1, 1), (core_over, 1)),
            1: then((sum_event, 5)),
            2: then((sum_event, 6)),
        },
    )

    def send_norms(i, act_on):
        if i == 0:
            act_on(remote(ngrad, n_c, ng_s.at[0], ng_r.at[0], core))
        elif i == 1:
            act_on(remote(n_c, n_x, ng_s.at[1], ng_r.at[1], other_x))
        elif i == 2:
            for dz in range(1, nz):
                act_on(remote(n_x, n_z.at[dz], ng_s.at[1 + dz], ng_r.at[1 + dz], {"z": z_of(dz)}))
        else:
            act_on(remote(n_out.at[y], n_out.at[y], ng_s.at[nz + 1], ng_r.at[nz + 1], across))

    send_norms(0, start)
    loop(GROUPS, lambda t: back_heads(t, d_ffn, wo, slope))
    sum_event(7)
    send_norms(0, recv)
    send_norms(0, lambda cp: cp.wait_send())
    n_c[...] += ngrad[...]
    send_norms(1, start)

    def attention_back(i):
        back_attend(i // per, [(i % per) * PAIR + k for k in range(PAIR)], proj, probs, slope)

        @pl.when(i % 2 == 1)
        def _():
            sum_event(8 + i // 2)

    loop(GROUPS * per, attention_back)
    seen = 8 + GROUPS * per // 2

    def qkv_grads(q):
        g, own = q // 2, q % 2

        def store(col, value):
            value = value.astype(BF)

            @pl.when(own == 0)
            def _():
                spare(0, g)[:, col : col + 128] = value

            @pl.when(own == 1)
            def _():
                gown[0, g, :, col : col + 128] = value

        grad_qkv_out(2 * g + jnp.where(own == 0, 1 - c, c), x, proj, d_ffn, hout, store)

        @pl.when(own == 0)
        def _():
            core_send(0, g).start()

    weave(
        4,
        qkv_grads,
        {
            0: then((sum_event, seen)),
            1: then((core_add, 0, 0), (sum_event, seen + 1)),
            3: then((core_add, 0, 1), (sum_event, seen + 2)),
        },
    )
    seen += 3

    def inputs_back(i):
        k = lax.rem(i + N_CHUNK - 1, N_CHUNK)

        def keep(r, grad):
            mid[r] = grad

            @pl.when(i == 0)
            def _():
                mid_low[:EXT_ROWS] = grad.astype(BF)

        back_input(k, proj, w, mid, keep)

        @pl.when(i == 0)
        def _():
            give_back(mid_low.at[pl.ds(0, EXT_ROWS)], g_back, 1, start)

    weave(N_CHUNK, inputs_back, {1: then((sum_event, seen))})
    seen += 1
    after = 4 * nz
    if seen < after:
        loop(after - seen, lambda q: sum_event(seen + q))
    for g in range(2):
        finish(2, g)
    loop(2, lambda q: sum_event(after + q))

    trips = [
        pltpu.make_async_copy(g_back, proj.at[0, pl.ds(0, OWN_ROWS)], io_s.at[0]),
        pltpu.make_async_copy(y_out, proj.at[1, pl.ds(0, OWN_ROWS)], io_s.at[1]),
        pltpu.make_async_copy(y_back, proj.at[2, pl.ds(0, OWN_ROWS)], io_s.at[2]),
    ]
    y_again = pltpu.make_async_copy(proj.at[1, pl.ds(0, OWN_ROWS)], y_out, io_s.at[1])
    g_copy = pltpu.make_async_copy(mid.at[pl.ds(0, OWN_ROWS)], g_out, io_s.at[3])

    @pl.when(lender)
    def _():
        for i, dst in enumerate((y_back, g_back)):
            for j in range(2):
                arrived(dst.at[pl.ds(j * EXT_ROWS, EXT_ROWS)], e_r.at[i, j])
        for cp in trips:
            cp.start()
        for cp in trips:
            cp.wait()

        def merge(s):
            r = chunk_rows(s, LENGTH)
            keep = jnp.zeros((LENGTH, D), F32) + mine(s) > 0.5
            mid[r] = jnp.where(keep, mid[r], proj[0, r].astype(F32))
            proj[1, r] = jnp.where(keep, proj[1, r].astype(F32), proj[2, r].astype(F32)).astype(BF)

        loop(OWN, merge)
        y_again.start()

    g_copy.start()
    loop(nz - 2, lambda q: sum_event(after + 2 + q))
    send_norms(1, recv)
    send_norms(1, lambda cp: cp.wait_send())
    n_x[...] += n_c[...]
    send_norms(2, start)
    for g in range(2):
        finish(1, g)
    loop(nz - 1, lambda q: sum_event(after + nz + q))
    total = n_x[...]
    for dz in range(1, nz):
        arrived(n_z.at[dz], ng_r.at[1 + dz])
        total += n_z[dz]
    n_out[y] = total
    send_norms(3, start)
    finish(0, 0)
    sum_event(after + 2 * nz - 1)
    finish(0, 1)
    g_copy.wait()
    for m in (2, 1, 0):
        arrived(oth.at[m], y_r.at[m])
        out_stage(m, 1)[...] = oth[m].astype(F32)
        out_copy(m, 1).start()

    def sums_sent(i):
        m, g = i // 2, i % 2
        for zz in range(nz):
            @pl.when(z != zz)
            def _():
                has_left(x_place(0, 0, 0), z_s.at[m, g, zz])

            has_left(x_place(0, 0, 0), x_s.at[m, g, zz])

    loop(6, sums_sent)
    loop(6, gather_sent)
    for g in range(2):
        core_send(0, g).wait_send()
    for m in range(3):
        has_left(given(m), ys_s.at[m])
        for other in range(2):
            out_copy(m, other).wait()
        last_send(m).wait_send()
    lend(x_in, x, 0, lambda cp: cp.wait_send())
    lend(cot, d_ffn, 1, lambda cp: cp.wait_send())
    for i in range(4):
        norm_hop(i, lambda cp: cp.wait_send())
    send_norms(2, lambda cp: cp.wait_send())
    send_norms(3, lambda cp: cp.wait())
    has_left(mid_low.at[pl.ds(0, EXT_ROWS)], e_s.at[1])

    @pl.when(lender)
    def _():
        y_again.wait()


def run_step(nz, tags, lens, x_in, cot, qkv, wout, up, dn, gain, bias):
    rows = up.shape[1]
    V = pl.BlockSpec(memory_space=pltpu.VMEM)
    S = pl.BlockSpec(memory_space=pltpu.SMEM)
    sem = pltpu.SemaphoreType.DMA
    out = jax.ShapeDtypeStruct
    return pl.pallas_call(
        partial(step_kernel, nz, rows),
        out_shape=(
            out((OWN_ROWS, D), BF),
            out((OWN_ROWS, D), F32),
            out((2, rows, D), F32),
            out((2, rows, D), F32),
            out((2, rows, D), F32),
            out((2, 8, D), F32),
            out((OWN_ROWS, D), BF),
            out((OWN_ROWS, D), BF),
            out((2, D, D), BF),
        ),
        in_specs=[S, S] + [ANY] * 6 + [V, V],
        out_specs=(ANY, ANY, ANY, ANY, ANY, V, ANY, ANY, ANY),
        scratch_shapes=[
            pltpu.VMEM((3, GROUPS, D, D), BF),
            pltpu.VMEM((ROWS, D), BF),
            pltpu.VMEM((GROUPS, ROWS, D), BF),
            pltpu.VMEM((GROUPS, SLOTS, LENGTH, 512), BF),
            pltpu.VMEM((GROUPS, ROWS, GW), BF),
            pltpu.VMEM((GROUPS, D, GW), BF),
            pltpu.VMEM((ROWS, D), F32),
            pltpu.VMEM((ROWS, D), BF),
            pltpu.VMEM((ROWS, 128), F32),
            pltpu.VMEM((ROWS, D), BF),
            pltpu.VMEM((GROUPS, ROWS, D), BF),
            pltpu.VMEM((GROUPS, ROWS, D), BF),
            pltpu.VMEM((ROWS, D), BF),
            pltpu.VMEM((3, 2, D, D), BF),
            pltpu.VMEM((2, 3, 2 * nz * rows, D), BF),
            pltpu.VMEM((3, rows, D), BF),
            pltpu.VMEM(qkv.shape, BF),
            pltpu.VMEM(wout.shape, BF),
            pltpu.VMEM((rows, D), BF),
            pltpu.VMEM((8 * nz, 8, 128), F32),
            pltpu.VMEM((8, D), F32),
            pltpu.VMEM((8, D), F32),
            pltpu.VMEM((8, D), F32),
            pltpu.VMEM((8, D), F32),
            pltpu.VMEM((nz, 8, D), F32),
            sem((6,)), sem((4,)), sem((2,)), sem((3, 2)),
            sem((3,)), sem((3,)),
            sem((3, 2, 2, nz)), sem((3, 2, 2, nz)),
            sem((2, nz)), sem((2, nz)),
            sem((3, 2, nz)), sem((3, 2, nz)),
            sem((3, 2, nz, 2)), sem((3, 2, nz, 2)),
            sem((2, 2)), sem((2,)),
            sem((nz + 2,)), sem((nz + 2,)),
            sem((3, 2)), sem((3, 2)),
            sem((2, 3)), sem((2, 3)),
            sem((3, 2, nz)), sem((3, 2, nz)),
            sem((3, 2, nz)), sem((3, 2, nz)),
            sem((3,)), sem((3,)),
            sem((2,)), sem((2, 2)),
            sem((nz + 2,)), sem((nz + 2,)),
        ],
        compiler_params=pltpu.CompilerParams(
            collective_id=0, has_side_effects=True, vmem_limit_bytes=67043328
        ),
        name="layer_step",
    )(tags, lens, x_in, cot, qkv, wout, up, dn, gain, bias)


def deliver_kernel(cols, y_in, g_in, qo, up_in, dn_in, sums,
                   y_out, g_out, qkv_out, wout_out, up_out, dn_out, gain_out, bias_out,
                   v_y, v_g, v_qo, v_up, v_dn, v_qkv, v_out, in_s, out_s):
    through = [(up_in, v_up, up_out), (dn_in, v_dn, dn_out)]
    for k in range(OWN):
        r = pl.ds(k * LENGTH, LENGTH)
        through.append((g_in.at[r], v_g.at[r], g_out.at[r]))
    for k in range(2):
        r = pl.ds(k * CHUNK, CHUNK)
        through.append((y_in.at[r], v_y.at[r], y_out.at[r]))
    n = len(through)
    first = pltpu.make_async_copy(qo, v_qo, in_s.at[n])
    first.start()
    loads, stores = [], []
    for i, (src, via, dst) in enumerate(through):
        loads.append(pltpu.make_async_copy(src, via, in_s.at[i]))
        stores.append(pltpu.make_async_copy(via, dst, out_s.at[i]))
        loads[-1].start()
    z, x, y, c = place()
    me = ((z * 2 + x) * 2 + y) * 2 + c
    for k in range(2):
        turned = pltpu.roll(sums[k], lax.rem(D - me * cols, D), 1)
        gain_out[k] = turned[0:2, :cols]
        bias_out[k] = turned[2:4, :cols]
    first.wait()
    for k in range(2):
        tail = []
        for i in range(3):
            v_qkv[k, i] = v_qo[k, :, GW * i : GW * i + GW - HEAD_DIM]
            tail.append(v_qo[k, :, GW * (i + 1) - HEAD_DIM : GW * (i + 1)])
        v_out[k] = jnp.concatenate(tail, 1)
    stores.append(pltpu.make_async_copy(v_qkv, qkv_out, out_s.at[n]))
    stores.append(pltpu.make_async_copy(v_out, wout_out, out_s.at[n + 1]))
    for i in range(n):
        loads[i].wait()
        stores[i].start()
    for cp in stores[n:]:
        cp.start()
    for cp in stores:
        cp.wait()


def deliver(cols, y_in, g_in, qo, up_in, dn_in, sums):
    rows = qo.shape[1]
    V = pl.BlockSpec(memory_space=pltpu.VMEM)
    sem = pltpu.SemaphoreType.DMA
    out = jax.ShapeDtypeStruct
    width = GW - HEAD_DIM
    shapes = [((2, 3, rows, width), F32), ((2, rows, width), F32)]
    whole = [(y_in.shape, BF), (g_in.shape, F32), (qo.shape, F32), (qo.shape, F32), (qo.shape, F32)]
    return pl.pallas_call(
        partial(deliver_kernel, cols),
        out_shape=tuple(
            out(*p) for p in whole[:2] + shapes + whole[3:] + [((2, 2, cols), F32)] * 2
        ),
        in_specs=[ANY] * 5 + [V],
        out_specs=(ANY,) * 6 + (V, V),
        scratch_shapes=[pltpu.VMEM(*p) for p in whole + shapes] + [sem((9,)), sem((10,))],
        name="deliver",
    )(y_in, g_in, qo, up_in, dn_in, sums)


def split_local(nz, x_in, tags, lengths, w_qkv, w_out, w_up, w_down, norm_gain, norm_bias, cotangent):
    cols = norm_gain.shape[2]
    y_out, x_grad, qo_grad, up_grad, down_grad, n_sum, _, _, _ = run_step(
        nz, tags, lengths, x_in, cotangent, w_qkv.transpose(0, 2, 1, 3), w_out, w_up, w_down, norm_gain, norm_bias
    )
    y_out, x_grad, qkv, out, up, down, gain, bias = deliver(
        cols, y_out, x_grad, qo_grad, up_grad, down_grad, n_sum
    )
    return y_out, x_grad, qkv.transpose(0, 2, 1, 3), out, up, down, gain, bias


def typed_map(operand, stacked, chain_kinds, pattern):

    def single(element):
        weight = lax.dynamic_index_in_dim(stacked, element[1], 0, keepdims=False)
        return jnp.einsum(pattern, element[0], weight, preferred_element_type=jnp.float32)

    return lax.map(single, (operand, chain_kinds))


def typed_grads(running, operand, partner, chain_kinds, pattern):

    def single(carry, element):
        product_term = jnp.einsum(
            pattern, element[0], element[1], preferred_element_type=jnp.float32
        )
        previous = lax.dynamic_index_in_dim(carry, element[2], 0, keepdims=False)
        return (
            lax.dynamic_update_index_in_dim(carry, previous + product_term, element[2], 0),
            None,
        )

    return lax.scan(single, running, (operand, partner, chain_kinds))[0]


def row_terms(operand, stacked, chain_kinds, pattern, row_count):
    result = typed_map(operand, stacked, chain_kinds, pattern)
    return result.reshape(row_count, result.shape[-1])


def old_norm_forward(values, gain_rows, shift_rows):
    center = values - jnp.mean(values, -1, keepdims=True)
    factor = lax.rsqrt(jnp.mean(center * center, -1, keepdims=True) + EPS)
    normed = center * factor
    return (normed * gain_rows + shift_rows, normed, factor)


def old_norm_backward(grad_out, normed, factor, gain_rows):
    scaled = grad_out * gain_rows
    mean_plain = jnp.mean(scaled, -1, keepdims=True)
    mean_normed = jnp.mean(scaled * normed, -1, keepdims=True)
    return factor * (scaled - mean_plain - normed * mean_normed)


def type_sums(onehot, values):
    return jnp.dot(onehot.T, values, precision=HIGH, preferred_element_type=jnp.float32)


def general_local(x_in, tags, lengths, w_qkv, w_out, w_up, w_down, norm_gain, norm_bias, cotangent):
    tp_count = lax.axis_size("tensor")
    tp_index = lax.axis_index("tensor")
    local_rows = CHAINS_PART * LENGTH
    batch_chains = tp_count * CHAINS_PART
    head_cols = w_qkv.shape[3]
    local_heads = head_cols // HEAD_DIM
    tag_grid = tags.reshape(tp_count, MICRO, CHAINS_PART)
    len_grid = lengths.reshape(tp_count, MICRO, CHAINS_PART)
    own_tags = lax.dynamic_index_in_dim(tag_grid, tp_index, 0, keepdims=False)
    gains, shifts = (
        lax.all_gather(norm_gain, ("dp", "tensor"), axis=2, tiled=True),
        lax.all_gather(norm_bias, ("dp", "tensor"), axis=2, tiled=True),
    )
    grad_full = (
        jnp.zeros((2, D, 3, head_cols), jnp.float32),
        jnp.zeros((2, D, head_cols), jnp.float32),
        jnp.zeros((2, D, w_up.shape[2]), jnp.float32),
        jnp.zeros((2, D, w_down.shape[2]), jnp.float32),
    )
    shards = (
        jnp.zeros(w_qkv.shape, jnp.float32),
        jnp.zeros(w_out.shape, jnp.float32),
        jnp.zeros(w_up.shape, jnp.float32),
        jnp.zeros(w_down.shape, jnp.float32),
    )
    gain_acc = jnp.zeros((2, 2, D), jnp.float32)
    shift_acc = jnp.zeros((2, 2, D), jnp.float32)
    outputs = []
    input_grads = []
    for micro_index in range(MICRO):
        held = (
            lax.all_gather(w_qkv, "dp", axis=1, tiled=True),
            lax.all_gather(w_out, "dp", axis=1, tiled=True),
            lax.all_gather(w_up, "dp", axis=1, tiled=True),
            lax.all_gather(w_down, "dp", axis=1, tiled=True),
        )
        qkv_w, out_w, up_w, down_w = held
        chain_kinds = tag_grid[:, micro_index].reshape(batch_chains)
        chain_lens = len_grid[:, micro_index].reshape(batch_chains)
        own_rows = x_in[micro_index * local_rows : (micro_index + 1) * local_rows]
        kinds_rows = jnp.repeat(own_tags[micro_index], LENGTH)
        heavy_rows = (kinds_rows == 0)[:, None]
        onehot = (kinds_rows[:, None] == jnp.arange(2)[None, :]).astype(jnp.float32)
        gain_mid = jnp.where(heavy_rows, gains[0, 0], gains[1, 0])
        shift_mid = jnp.where(heavy_rows, shifts[0, 0], shifts[1, 0])
        gain_end = jnp.where(heavy_rows, gains[0, 1], gains[1, 1])
        shift_end = jnp.where(heavy_rows, shifts[0, 1], shifts[1, 1])
        gathered = lax.all_gather(own_rows, "tensor", axis=0, tiled=True).reshape(
            batch_chains, LENGTH, D
        )
        projected = typed_map(gathered, qkv_w, chain_kinds, "ld,dkh->lkh").astype(jnp.bfloat16)
        query = projected[:, :, 0].reshape(batch_chains, LENGTH, local_heads, HEAD_DIM)
        keys_low = projected[:, :, 1].reshape(batch_chains, LENGTH, local_heads, HEAD_DIM)
        values_low = projected[:, :, 2].reshape(batch_chains, LENGTH, local_heads, HEAD_DIM)
        valid = (
            lax.broadcasted_iota(jnp.int32, (batch_chains, 1, 1, LENGTH), 3)
            < chain_lens[:, None, None, None]
        )
        scores = (
            jnp.einsum("cqhe,ckhe->chqk", query, keys_low, preferred_element_type=jnp.float32)
            * 0.125
        )
        scores = jnp.where(valid, scores, NEG)
        highest = jnp.max(scores, -1, keepdims=True)
        expo = jnp.exp(scores - highest)
        totals = jnp.sum(expo, -1, keepdims=True)
        probs = expo / totals
        log_total = highest + jnp.log(totals)
        heads_low = jnp.einsum(
            "chqk,ckhe->cqhe",
            probs.astype(jnp.bfloat16),
            values_low,
            preferred_element_type=jnp.float32,
        ).astype(jnp.bfloat16)
        heads_low = heads_low.reshape(batch_chains, LENGTH, head_cols)
        attn_sum = lax.psum_scatter(
            row_terms(
                heads_low, out_w, chain_kinds, "lh,dh->ld", lax.axis_size("tensor") * local_rows
            ).astype(jnp.bfloat16),
            "tensor",
            scatter_dimension=0,
            tiled=True,
        ).astype(jnp.float32)
        mid, normed_mid, factor_mid = old_norm_forward(
            own_rows.astype(jnp.float32) + attn_sum, gain_mid, shift_mid
        )
        mid_all = lax.all_gather(mid.astype(jnp.bfloat16), "tensor", axis=0, tiled=True).reshape(
            batch_chains, LENGTH, D
        )
        up_value = typed_map(mid_all, up_w, chain_kinds, "ld,df->lf")
        act_low = jax.nn.gelu(up_value, approximate=False).astype(jnp.bfloat16)
        ffn_sum = lax.psum_scatter(
            row_terms(
                act_low, down_w, chain_kinds, "lf,df->ld", lax.axis_size("tensor") * local_rows
            ).astype(jnp.bfloat16),
            "tensor",
            scatter_dimension=0,
            tiled=True,
        ).astype(jnp.float32)
        final, normed_end, factor_end = old_norm_forward(ffn_sum + mid, gain_end, shift_end)
        outputs.append(final.astype(jnp.bfloat16))
        base = grad_full
        grad_final = cotangent[micro_index * local_rows : (micro_index + 1) * local_rows].astype(
            jnp.float32
        )
        gain_acc = gain_acc.at[:, 1].add(type_sums(onehot, grad_final * normed_end))
        shift_acc = shift_acc.at[:, 1].add(type_sums(onehot, grad_final))
        grad_resid2 = old_norm_backward(grad_final, normed_end, factor_end, gain_end)
        grad_ffn = lax.all_gather(
            grad_resid2.astype(jnp.bfloat16), "tensor", axis=0, tiled=True
        ).reshape(batch_chains, LENGTH, D)
        grad_act = typed_map(grad_ffn, down_w, chain_kinds, "ld,df->lf")
        unused_value, gelu_back = jax.vjp(partial(jax.nn.gelu, approximate=False), up_value)
        grad_up = gelu_back(grad_act)[0].astype(jnp.bfloat16)
        down_acc = typed_grads(base[3], grad_ffn, act_low, chain_kinds, "ld,lf->df")
        up_acc = typed_grads(base[2], mid_all, grad_up, chain_kinds, "ld,lf->df")
        grad_mid = grad_resid2 + lax.psum_scatter(
            row_terms(
                grad_up, up_w, chain_kinds, "lf,df->ld", lax.axis_size("tensor") * local_rows
            ).astype(jnp.bfloat16),
            "tensor",
            scatter_dimension=0,
            tiled=True,
        ).astype(jnp.float32)
        gain_acc = gain_acc.at[:, 0].add(type_sums(onehot, grad_mid * normed_mid))
        shift_acc = shift_acc.at[:, 0].add(type_sums(onehot, grad_mid))
        grad_resid1 = old_norm_backward(grad_mid, normed_mid, factor_mid, gain_mid)
        grad_attn = lax.all_gather(
            grad_resid1.astype(jnp.bfloat16), "tensor", axis=0, tiled=True
        ).reshape(batch_chains, LENGTH, D)
        grad_heads = typed_map(grad_attn, out_w, chain_kinds, "ld,dh->lh").astype(jnp.bfloat16)
        out_acc = typed_grads(base[1], grad_attn, heads_low, chain_kinds, "ld,lh->dh")
        grad_heads = grad_heads.reshape(batch_chains, LENGTH, local_heads, HEAD_DIM)
        again = (
            jnp.einsum("cqhe,ckhe->chqk", query, keys_low, preferred_element_type=jnp.float32)
            * 0.125
        )
        probs_again = jnp.exp(jnp.where(valid, again, NEG) - log_total)
        grad_probs = jnp.einsum(
            "cqhe,ckhe->chqk", grad_heads, values_low, preferred_element_type=jnp.float32
        )
        inner = jnp.sum(grad_probs * probs_again, -1, keepdims=True)
        grad_scores = (probs_again * (grad_probs - inner)).astype(jnp.bfloat16)
        grad_query = (
            jnp.einsum("chqk,ckhe->cqhe", grad_scores, keys_low, preferred_element_type=jnp.float32)
            * 0.125
        ).astype(jnp.bfloat16)
        grad_keys = (
            jnp.einsum("chqk,cqhe->ckhe", grad_scores, query, preferred_element_type=jnp.float32)
            * 0.125
        ).astype(jnp.bfloat16)
        grad_values = jnp.einsum(
            "chqk,cqhe->ckhe",
            probs_again.astype(jnp.bfloat16),
            grad_heads,
            preferred_element_type=jnp.float32,
        ).astype(jnp.bfloat16)
        grad_proj = jnp.stack([grad_query, grad_keys, grad_values], 2).reshape(
            batch_chains, LENGTH, 3, head_cols
        )
        qkv_acc = typed_grads(base[0], gathered, grad_proj, chain_kinds, "ld,lkh->dkh")
        grad_input = grad_resid1 + lax.psum_scatter(
            row_terms(
                grad_proj, qkv_w, chain_kinds, "lkh,dkh->ld", lax.axis_size("tensor") * local_rows
            ).astype(jnp.bfloat16),
            "tensor",
            scatter_dimension=0,
            tiled=True,
        ).astype(jnp.float32)
        input_grads.append(grad_input)
        updated = (qkv_acc, out_acc, up_acc, down_acc)
        grad_full = updated
    shards = (
        lax.psum_scatter(grad_full[0], "dp", scatter_dimension=1, tiled=True),
        lax.psum_scatter(grad_full[1], "dp", scatter_dimension=1, tiled=True),
        lax.psum_scatter(grad_full[2], "dp", scatter_dimension=1, tiled=True),
        lax.psum_scatter(grad_full[3], "dp", scatter_dimension=1, tiled=True),
    )
    gain_grad, shift_grad = (
        lax.psum_scatter(gain_acc, ("dp", "tensor"), scatter_dimension=2, tiled=True),
        lax.psum_scatter(shift_acc, ("dp", "tensor"), scatter_dimension=2, tiled=True),
    )
    return (
        jnp.concatenate(outputs, 0),
        jnp.concatenate(input_grads, 0),
        shards[0],
        shards[1],
        shards[2],
        shards[3],
        gain_grad,
        shift_grad,
    )


def solution(mesh):
    placed = (
        P(("dp", "tensor"), None),
        P("dp"),
        P("dp"),
        P(None, "dp", None, "tensor"),
        P(None, "dp", "tensor"),
        P(None, "dp", "tensor"),
        P(None, "dp", "tensor"),
        P(None, None, ("dp", "tensor")),
        P(None, None, ("dp", "tensor")),
        P(("dp", "tensor"), None),
    )
    results = (
        P(("dp", "tensor"), None),
        P(("dp", "tensor"), None),
        P(None, "dp", None, "tensor"),
        P(None, "dp", "tensor"),
        P(None, "dp", "tensor"),
        P(None, "dp", "tensor"),
        P(None, None, ("dp", "tensor")),
        P(None, None, ("dp", "tensor")),
    )
    n_dp, n_tensor = mesh.shape["dp"], mesh.shape["tensor"]
    if n_tensor != GROUPS or n_dp != 8:
        return jax.shard_map(
            general_local, mesh=mesh, in_specs=placed, out_specs=results, check_vma=False
        )
    fine = Mesh(mesh.devices.reshape(n_dp // 2, 2, 2, 2), AXES)
    names = {"dp": ("z", "x"), "tensor": ("y", "c")}

    def refine(spec):
        parts = []
        for entry in spec:
            entry = (entry,) if isinstance(entry, str) else entry
            parts.append(entry and sum((names[a] for a in entry), ()))
        return P(*parts)

    return jax.shard_map(
        partial(split_local, n_dp // 2),
        mesh=fine,
        in_specs=tuple(refine(s) for s in placed),
        out_specs=tuple(refine(s) for s in results),
        check_vma=False,
    )
```

```python
from functools import partial

import jax
import jax.numpy as jnp
from jax import lax
from jax.experimental import pallas as pl
from jax.experimental.pallas import tpu as pltpu
from jax.sharding import Mesh
from jax.sharding import PartitionSpec as P

D = 768
HEADS = 12
HEAD_DIM = 64
MICRO = 4
CHAINS_PART = 1
LENGTH = 160
GROUPS = 4
OWN = 4
EXTRA = 2
SLOTS = OWN + EXTRA
EXT_ROWS = EXTRA * LENGTH
OWN_ROWS = OWN * LENGTH
ROWS = SLOTS * LENGTH

EPS = 1e-12
NEG = -1e30
HIGH = lax.Precision.HIGHEST
BF = jnp.bfloat16
F32 = jnp.float32
MESH = pl.DeviceIdType.MESH
ANY = pl.BlockSpec(memory_space=pl.ANY)
AXES = ("z", "x", "y", "c")


def place():
    return tuple(lax.axis_index(a) for a in AXES)


def greet(nz, z, x, y, c):
    barrier = pltpu.get_barrier_semaphore()
    friends = [{"c": 1 - c}, {"y": 1 - y}, {"y": 1 - y, "c": 1 - c}, {"x": 1 - x}]
    friends += [{"z": lax.rem(z + dz, nz)} for dz in range(1, nz)]
    for friend in friends:
        pl.semaphore_signal(barrier, inc=1, device_id=friend, device_id_type=MESH)
    return barrier, len(friends)


CHUNK = 320
SUB = 80
N_CHUNK = ROWS // CHUNK
WIDE = 3 * LENGTH
GW = 256
PAIR = 3


def dot_nn(a, b):
    return lax.dot_general(a, b, (((1,), (0,)), ((), ())), preferred_element_type=F32)


def dot_nt(a, b):
    return lax.dot_general(a, b, (((1,), (1,)), ((), ())), preferred_element_type=F32)


def dot_tn(a, b):
    return lax.dot_general(a, b, (((0,), (0,)), ((), ())), preferred_element_type=F32)


def lanes(shape):
    return lax.broadcasted_iota(jnp.int32, shape, len(shape) - 1)


def head_mask(h, shape):
    lane = lanes(shape)
    return jnp.logical_and(lane >= h * HEAD_DIM, lane < (h + 1) * HEAD_DIM)


def stack_heads(rows):
    zero = jnp.zeros_like(rows)
    return jnp.concatenate([jnp.where(head_mask(h, rows.shape), rows, zero) for h in range(3)], 0)


def merge_heads(stack):
    out = jnp.zeros((LENGTH, GW), stack.dtype)
    for h in range(3):
        out = jnp.where(head_mask(h, out.shape), stack[h * LENGTH : (h + 1) * LENGTH], out)
    return out


def chunk_rows(i, size=CHUNK):
    return pl.ds(pl.multiple_of(i * size, size), size)


def loop(count, body):
    def step(i, carry):
        body(i)
        return carry

    lax.fori_loop(0, count, step, 0)


def weave(count, unit, extra):
    def body(i):
        unit(i)
        for k, step in extra.items():
            pl.when(i == k)(step)

    loop(count, body)


def out_columns(t, w, wo):
    low = lanes((D, 128)) < HEAD_DIM
    tiles = [w[0, t, :, GW * i + 128 : GW * i + 256].astype(F32) for i in range(3)]
    wo[t, :, :128] = jnp.where(low, pltpu.roll(tiles[0], 64, 1), tiles[1]).astype(BF)
    wo[t, :, 128:] = jnp.where(low, pltpu.roll(tiles[2], 64, 1), 0.0).astype(BF)


def attend(t, chains, lens, proj, probs, hout):
    rows = [chunk_rows(s, LENGTH) for s in chains]
    parts = [(proj[t, r, :GW], proj[t, r, GW : 2 * GW], proj[t, r, 2 * GW :]) for r in rows]
    lows, outs = [], []
    for s, (query, key, value) in zip(chains, parts):
        scores = dot_nt(key, stack_heads(query * jnp.asarray(0.125, BF)))
        valid = lax.broadcasted_iota(jnp.int32, (LENGTH, 1), 0) < lens(s)
        scores = jnp.where(valid, scores, NEG)
        expo = jnp.exp(scores - jnp.max(scores, 0, keepdims=True))
        lows.append((expo * (1.0 / jnp.sum(expo, 0, keepdims=True))).astype(BF))
        outs.append(merge_heads(dot_tn(lows[-1], value)).astype(BF))
    for s, r, low, out in zip(chains, rows, lows, outs):
        probs[t, s, :, :WIDE] = low
        hout[t, r] = out


def norm_rows(values):
    center = values - jnp.mean(values, -1, keepdims=True)
    factor = lax.rsqrt(jnp.mean(center * center, -1, keepdims=True) + EPS)
    return center * factor, factor


def norm_back(scaled, normed, factor):
    return factor * (
        scaled
        - jnp.mean(scaled, -1, keepdims=True)
        - normed * jnp.mean(scaled * normed, -1, keepdims=True)
    )


def pieces(i, body):
    def step(k):
        body(pl.ds(pl.multiple_of(i * CHUNK + k * SUB, SUB), SUB), k)

    loop(CHUNK // SUB, step)


def first_norm(i, x, hout, wo, prm, mid, n1, s1, mid_low):
    r = chunk_rows(i)
    attn = dot_nt(hout[0, r], wo[0])
    for t in range(1, GROUPS):
        attn += dot_nt(hout[t, r], wo[t])
    mid[r] = attn

    def piece(p, k):
        normed, factor = norm_rows(x[p].astype(F32) + mid[p])
        n1[p] = normed.astype(BF)
        s1[p] = jnp.broadcast_to(factor, (SUB, 128))
        value = normed * prm[0:1] + prm[2:3]
        mid[p] = value
        mid_low[p] = value.astype(BF)

    pieces(i, piece)


def feed_up(t, i, mid_low, w, act, slope):
    r = chunk_rows(i)
    for k in range(0, D, GW):
        up = dot_nn(mid_low[r], w[1, t, :, k : k + GW])
        cdf = 0.5 * (1.0 + lax.erf(up * 0.7071067811865476))
        act[t, r, k : k + GW] = (up * cdf).astype(BF)
        bell = 0.3989422804014327 * jnp.exp(-0.5 * up * up)
        slope[t, r, k : k + GW] = (cdf + up * bell).astype(BF)


def feed_down(i, t, act, w, mid):
    r = chunk_rows(i)
    mid[r] += dot_nt(act[t, r], w[2, t]) + dot_nt(act[t + 1, r], w[2, t + 1])


def second_norm(i, t, act, w, prm, mid, cot, mine, y_rows, d_ffn, ngrad):
    feed_down(i, t, act, w, mid)

    def piece(p, k):
        normed, factor = norm_rows(mid[p])
        y_rows[pl.ds(pl.multiple_of(k * SUB, SUB), SUB)] = (normed * prm[1:2] + prm[3:4]).astype(BF)
        grad = cot[p].astype(F32) * jnp.where(k < LENGTH // SUB, mine(2 * i), mine(2 * i + 1))
        ngrad[1:2] += jnp.sum(grad * normed, 0, keepdims=True)
        ngrad[3:4] += jnp.sum(grad, 0, keepdims=True)
        back = norm_back(grad * prm[1:2], normed, factor)
        mid[p] = back
        d_ffn[p] = back.astype(BF)

    pieces(i, piece)


def back_up(t, i, d_ffn, w, slope):
    r = chunk_rows(i)
    slope[t, r] = (dot_nn(d_ffn[r], w[2, t]) * slope[t, r].astype(F32)).astype(BF)


def back_first_norm(i, d_up, w, prm, mid, n1, s1, d_attn, ngrad):
    r = chunk_rows(i)
    grad = dot_nt(d_up[0, r], w[1, 0])
    for t in range(1, GROUPS):
        grad += dot_nt(d_up[t, r], w[1, t])
    mid[r] += grad

    def piece(p, k):
        grad = mid[p]
        normed = n1[p].astype(F32)
        ngrad[0:1] += jnp.sum(grad * normed, 0, keepdims=True)
        ngrad[2:3] += jnp.sum(grad, 0, keepdims=True)
        back = norm_back(grad * prm[0:1], normed, s1[p, 0:1])
        mid[p] = back
        d_attn[p] = back.astype(BF)

    pieces(i, piece)


def back_heads(t, d_attn, wo, d_heads):
    d_heads[t, :, :GW] = dot_nn(d_attn[...], wo[t]).astype(BF)


def back_attend(t, chains, proj, probs, d_heads):
    rows = [chunk_rows(s, LENGTH) for s in chains]
    parts = [
        (proj[t, r, :GW], proj[t, r, GW : 2 * GW], proj[t, r, 2 * GW :], d_heads[t, r, :GW], probs[t, s, :, :WIDE])
        for s, r in zip(chains, rows)
    ]
    results = []
    for query, key, value, grad, low in parts:
        grad = stack_heads(grad)
        p = low.astype(F32)
        d_probs = dot_nt(value, grad)
        d_scores = (p * (d_probs - jnp.sum(d_probs * p, 0, keepdims=True))).astype(BF)
        d_query = merge_heads(dot_tn(d_scores, key)) * 0.125
        d_key = dot_nn(d_scores, stack_heads(query * jnp.asarray(0.125, BF)))
        results.append((d_query.astype(BF), d_key.astype(BF), dot_nn(low, grad).astype(BF)))
    for r, (d_query, d_key, d_value) in zip(rows, results):
        proj[t, r, :GW] = d_query
        proj[t, r, GW : 2 * GW] = d_key
        proj[t, r, 2 * GW :] = d_value


def grad_qkv_out(t, x, d_proj, d_attn, hout, store):
    low = lanes((D, 128)) < HEAD_DIM
    outs = dot_tn(d_attn[...], hout[t])
    places = (pltpu.roll(outs[:, :128], 64, 1), outs[:, :128], pltpu.roll(outs[:, 128:], 64, 1))
    for i in range(3):
        part = dot_tn(x[...], d_proj[t, :, GW * i : GW * (i + 1)])
        store(GW * i, part[:, :128])
        store(GW * i + 128, jnp.where(low, part[:, 128:], places[i]))


def back_input(i, d_proj, w, mid, out):
    r = chunk_rows(i)
    grad = mid[r]
    for t in range(GROUPS):
        grad += dot_nt(d_proj[t, r], w[0, t])
    out(r, grad)


MIXED = (2, 1)
GATHER_FIRST = (
    ('X', 1, 0), ('L', 0, 0), ('y', 0), ('X', 0, 1), ('L', 0, 1),
    ('z', 0, 0, 1), ('z', 0, 1, 1), ('y', 1), ('L', 1, 1), ('x', 0, 1, 0),
    ('X', 0, 0), ('z', 0, 1, 2), ('x', 1, 0, 0), ('z', 0, 0, 2), ('x', 0, 1, 1),
    ('x', 0, 0, 1), ('L', 1, 0), ('z', 0, 1, 3), ('z', 0, 0, 3), ('x', 0, 0, 0),
    ('y', 2), ('X', 2, 1), ('x', 0, 1, 3), ('z', 1, 1, 1), ('x', 0, 1, 2),
    ('z', 1, 0, 1), ('x', 0, 0, 2), ('L', 2, 0), ('x', 0, 0, 3), ('z', 1, 1, 2),
    ('X', 1, 1),
)
GATHER_QKV = {
    7: (('z', 1, 0, 2),),
    10: (('x', 2, 1, 0),),
}
GATHER_ATTEND = {
    1: (('L', 2, 1), ('z', 1, 1, 3), ('z', 1, 0, 3), ('z', 2, 0, 1),),
    2: (('X', 2, 0),),
    5: (('x', 1, 1, 1), ('x', 1, 1, 2),),
    6: (('z', 2, 1, 1), ('x', 1, 1, 0),),
    7: (('z', 2, 0, 2), ('x', 1, 0, 1),),
}
GATHER_NORM = {
    0: (('x', 1, 0, 2), ('x', 1, 1, 3), ('x', 1, 0, 3),),
}
GATHER_UP = {
    3: (('z', 2, 1, 2),),
    4: (('z', 2, 0, 3),),
    7: (('x', 2, 0, 1),),
    9: (('x', 2, 0, 0),),
    10: (('x', 2, 0, 3), ('x', 2, 0, 2),),
    11: (('z', 2, 1, 3),),
}


def remote(src, dst, s_sem, r_sem, who):
    return pltpu.make_async_remote_copy(
        src_ref=src, dst_ref=dst, send_sem=s_sem, recv_sem=r_sem, device_id=who, device_id_type=MESH
    )


def arrived(ref, sem):
    remote(ref, ref, sem, sem, {"c": 1 - lax.axis_index("c")}).wait_recv()


def has_left(ref, sem):
    remote(ref, ref, sem, sem, {"c": 1 - lax.axis_index("c")}).wait_send()


def step_kernel(nz, rows,
                tags, lens, x_in, cot, qkv, wout, up, dn, gain, bias,
                y_out, g_out, qo_out, up_out, dn_out, n_out, y_back, g_back, r_c,
                w, x, proj, probs, hout, wo, mid, n1, s1, mid_low, act, slope, d_ffn, gown, r_xz, oth, v_qkv, v_out, far,
                n_all, prm, ngrad, n_c, n_x, n_z,
                load_s, io_s, stage_s, out_s,
                ys_s, ys_r, zs_s, zs_r, zm_s, zm_r, xs_s, xs_r, cs_s, cs_r, ex_s, ex_r, na_s, na_r,
                c_s, c_r, cp_s, cp_r, x_s, x_r, z_s, z_r, y_s, y_r, e_s, e_r, ng_s, ng_r):
    z, xc, y, c = place()
    core, across, other_x = {"c": 1 - c}, {"y": 1 - y}, {"x": 1 - xc}
    diagonal = {"y": 1 - y, "c": 1 - c}
    mats = (None, up, dn)
    lender = y != c
    home = (2 * y + c) * OWN
    away = (2 - y) * OWN + c * EXTRA

    def z_of(dz):
        return lax.rem(z + dz, nz)

    def chain(s):
        return jnp.where(s < OWN, home + s, away + s - OWN)

    def length_of(s):
        return lens[chain(s)]

    def mine(s):
        return jnp.where(tags[chain(s)] == y, 1.0, 0.0)

    def part(zz, xx):
        return pl.ds(pl.multiple_of((zz * 2 + xx) * rows, rows), rows)

    def group(g):
        return 2 * lax.rem(y + g, 2) + c

    def block(m, g, zz, xx):
        return w.at[m, group(g), part(zz, xx)]

    loads = [pltpu.make_async_copy(mats[m].at[y], block(m, 0, z, xc), load_s.at[m]) for m in range(1, 3)]
    loads += [
        pltpu.make_async_copy(x_in, x.at[pl.ds(0, OWN_ROWS)], load_s.at[3]),
        pltpu.make_async_copy(cot, d_ffn.at[pl.ds(0, OWN_ROWS)], load_s.at[4]),
        pltpu.make_async_copy(qkv, v_qkv, load_s.at[0]),
        pltpu.make_async_copy(wout, v_out, load_s.at[5]),
    ]
    for cp in loads:
        cp.start()
    barrier, friends = greet(nz, z, xc, y, c)
    me = ((z * 2 + xc) * 2 + y) * 2 + c
    cols = gain.shape[2]
    n_all[me] = jnp.zeros((8, 128), F32)
    for i in range(2):
        n_all[me, 2 * i : 2 * i + 2, :cols] = gain[i]
        n_all[me, 4 + 2 * i : 6 + 2 * i, :cols] = bias[i]
    ngrad[...] = jnp.zeros_like(ngrad)
    for cp in loads[4:]:
        cp.wait()

    def packed(k):
        tail = v_out[k]
        cols = []
        for i in range(3):
            cols += [v_qkv[k, i], tail[:, HEAD_DIM * i : HEAD_DIM * (i + 1)]]
        return jnp.concatenate(cols, 1)

    w[0, group(0), part(z, xc)] = packed(y)
    far[...] = packed(1 - y)
    pl.semaphore_wait(barrier, friends)

    def given(m):
        return mats[m].at[1 - y] if m else far

    def lend(arr, out, i, act_on):
        @pl.when(lender)
        def _():
            for j, (who, p) in enumerate(((across, c), (diagonal, 1 - c))):
                src = arr.at[pl.ds(pl.multiple_of(p * EXT_ROWS, EXT_ROWS), EXT_ROWS)]
                act_on(remote(src, out.at[pl.ds(OWN_ROWS, EXT_ROWS)], ex_s.at[i, j], ex_r.at[i], who))

    for m in range(3):
        remote(given(m), w.at[m, group(0), part(z, xc)], ys_s.at[m], ys_r.at[m], across).start()
    lend(x_in, x, 0, lambda cp: cp.start())
    lend(cot, d_ffn, 1, lambda cp: cp.start())

    def inside(zz):
        return jnp.logical_and(zz >= 0, zz < nz)

    def start(cp):
        cp.start()

    def recv(cp):
        cp.wait_recv()

    def hop(m, g, d, j, ref, act_on, col=0):
        to = z + 1 - 2 * d
        sems = (zm_s.at[d, j], zm_r.at[d, j]) if col else (zs_s.at[m, g, d, j], zs_r.at[m, g, d, j])

        @pl.when(jnp.logical_and(inside(to), j < nz))
        def _():
            act_on(remote(ref, ref, *sems, {"z": to}))

    def x_copy(m, g, zz):
        ref = block(m, g, zz, xc)
        return remote(ref, ref, xs_s.at[m, g, zz], xs_r.at[m, g, zz], other_x)

    def c_copy(m, g, zz, xx):
        ref = block(m, g, zz, xx)
        return remote(ref, ref, cs_s.at[m, g, zz, xx], cs_r.at[m, g, zz, xx], core)

    def from_y(m):
        arrived(block(m, 1, z, xc), ys_r.at[m])

    def own_z(m, g):
        for d in range(2):
            hop(m, g, d, 1, block(m, g, z, xc), start)

    def own_xc(m, g):
        x_copy(m, g, z).start()
        c_copy(m, g, z, xc).start()

    def z_event(m, g, j):
        mixed = (m, g) == MIXED

        def body(d):
            zz = z - j + 2 * j * d

            @pl.when(inside(zz))
            def _():
                for col in range(2 if mixed else 1):
                    ref = block(m, g, zz, lax.rem(xc + col, 2))
                    arrived(ref, zm_r.at[d, j] if col else zs_r.at[m, g, d, j])
                    hop(m, g, d, j + 1, ref, start, col)
                    if not mixed:
                        x_copy(m, g, zz).start()
                    c_copy(m, g, zz, lax.rem(xc + col, 2)).start()

        loop(2, body)

    def x_event(m, g, j):
        def body(d):
            zz = z - j + 2 * j * d

            @pl.when(inside(zz))
            def _():
                ref = block(m, g, zz, 1 - xc)
                arrived(ref, xs_r.at[m, g, zz])
                if (m, g) == MIXED:
                    for way in range(2):
                        hop(m, g, way, 1, ref, start, 1)
                c_copy(m, g, zz, 1 - xc).start()

        loop(2 if j else 1, body)

    kinds = {"y": from_y, "L": own_z, "X": own_xc, "z": z_event, "x": x_event}

    def gather_steps(plan):
        def run(steps):
            for kind, *args in steps:
                kinds[kind](*args)

        return {k: partial(run, steps) for k, steps in plan.items()}

    def gathered(m, first=0, last=2):
        def body(i):
            g = first + i // (2 * nz)
            t = 2 * lax.rem(y + g, 2) + 1 - c
            zz, xx = (i // 2) % nz, i % 2
            arrived(w.at[m, t, part(zz, xx)], cs_r.at[m, g, zz, xx])

        loop(2 * nz * (last - first), body)

    def gather_sent(i):
        m, g = i // 2, i % 2
        ref = w.at[0, 0, pl.ds(0, rows)]
        mixed = i == 2 * MIXED[0] + MIXED[1]
        for j in range(1, nz):
            for d in range(2):
                @pl.when(inside(z - (1 - 2 * d) * (j - 1)))
                def _():
                    hop(m, g, d, j, ref, lambda cp: cp.wait_send())

                    @pl.when(mixed)
                    def _():
                        hop(m, g, d, j, ref, lambda cp: cp.wait_send(), 1)
        for zz in range(nz):
            @pl.when(jnp.logical_or(jnp.logical_not(mixed), z == zz))
            def _():
                has_left(ref, xs_s.at[m, g, zz])

            for xx in range(2):
                has_left(ref, cs_s.at[m, g, zz, xx])

    def norm_hop(i, act_on):
        if i == 0:
            act_on(remote(n_all.at[me], n_all.at[me], na_s.at[0], na_r.at[0], core))
        elif i == 1:
            ref = n_all.at[pl.ds(me - c, 2)]
            act_on(remote(ref, ref, na_s.at[1], na_r.at[1], across))
        elif i == 2:
            ref = n_all.at[pl.ds(me - c - 2 * y, 4)]
            act_on(remote(ref, ref, na_s.at[2], na_r.at[2], other_x))
        else:
            ref = n_all.at[pl.ds(8 * z, 8)]
            for dz in range(1, nz):
                act_on(remote(ref, ref, na_s.at[2 + dz], na_r.at[2 + dz], {"z": z_of(dz)}))

    for cp in loads[:2]:
        cp.wait()
    norm_hop(0, start)
    for kind, *args in GATHER_FIRST:
        kinds[kind](*args)
        if (kind, *args) == ("z", 0, 0, 1):
            norm_hop(0, recv)
            norm_hop(1, start)
        if (kind, *args) == ("z", 0, 0, 3):
            norm_hop(1, recv)
            norm_hop(2, start)
    norm_hop(2, recv)
    norm_hop(3, start)
    gathered(0)
    loads[2].wait()
    arrived(x.at[pl.ds(OWN_ROWS, EXT_ROWS)], ex_r.at[0])

    def projection(i):
        t, k = i // N_CHUNK, i % N_CHUNK
        r = chunk_rows(k)
        proj[t, r] = dot_nn(x[r], w[0, t]).astype(BF)

        @pl.when(k == N_CHUNK - 1)
        def _():
            out_columns(t, w, wo)

    weave(GROUPS * N_CHUNK, projection, gather_steps(GATHER_QKV))
    per = SLOTS // PAIR

    def attention(i):
        attend(i // per, [(i % per) * PAIR + k for k in range(PAIR)], length_of, proj, probs, hout)

    weave(GROUPS * per, attention, gather_steps(GATHER_ATTEND))
    norm_hop(3, recv)
    lane = lanes((2, D))
    gains, shifts = jnp.zeros((2, D), F32), jnp.zeros((2, D), F32)
    for d in range(8 * nz):
        within = jnp.logical_and(lane >= d * cols, lane < (d + 1) * cols)
        for name in range(2):
            piece = n_all[d, pl.ds(4 * name + 2 * y, 2), :]
            piece = jnp.concatenate([piece, jnp.zeros((2, D - 128), F32)], 1)
            piece = jnp.where(within, pltpu.roll(piece, d * cols, 1) if d else piece, 0.0)
            if name == 0:
                gains += piece
            else:
                shifts += piece
    prm[0:2] = gains
    prm[2:4] = shifts
    weave(
        N_CHUNK,
        lambda i: first_norm(i, x, hout, wo, prm, mid, n1, s1, mid_low),
        gather_steps(GATHER_NORM),
    )
    gathered(1)
    weave(
        GROUPS * N_CHUNK,
        lambda i: feed_up(i // N_CHUNK, i % N_CHUNK, mid_low, w, act, slope),
        gather_steps(GATHER_UP),
    )
    gathered(2, 0, 1)
    first_two = 2 * y
    last_two = 2 - first_two
    loop(N_CHUNK, lambda i: feed_down(i, first_two, act, w, mid))
    gathered(2, 1, 2)
    loads[3].wait()
    arrived(d_ffn.at[pl.ds(OWN_ROWS, EXT_ROWS)], ex_r.at[1])

    def y_stage(i):
        return r_xz.at[i // 2, 0, pl.ds(pl.multiple_of((i % 2) * CHUNK, CHUNK), CHUNK)]

    def give_back(src, dst, i, act_on):
        dst = dst.at[pl.ds(pl.multiple_of(c * EXT_ROWS, EXT_ROWS), EXT_ROWS)]

        @pl.when(c == y)
        def _():
            act_on(remote(src, dst, e_s.at[i], e_r.at[i, c], across))

        @pl.when(c != y)
        def _():
            act_on(remote(src, dst, e_s.at[i], e_r.at[i, c], diagonal))

    def y_copy(i):
        return pltpu.make_async_copy(y_stage(i), y_out.at[pl.ds(i * CHUNK, CHUNK)], io_s.at[i])

    loop(
        N_CHUNK,
        lambda i: second_norm(
            i, last_two, act, w, prm, mid, d_ffn, mine, y_stage(i), d_ffn, ngrad
        ),
    )
    for i in range(2):
        y_copy(i).start()
    give_back(y_stage(2), y_back, 0, start)

    def x_place(m, g, i):
        return r_xz.at[0, m, pl.ds(pl.multiple_of((g * nz + i) * rows, rows), rows)]

    def z_place(m, g, i):
        return r_xz.at[1, m, pl.ds(pl.multiple_of((g * nz + i) * rows, rows), rows)]

    def spare(m, g):
        return gown.at[0, g] if m else act.at[2 * g + c, pl.ds(0, D)]

    def core_send(m, g):
        there = r_c.at[g] if m else spare(0, g)
        return remote(spare(m, g), there, c_s.at[m, g], c_r.at[m, g], core)

    def fetch(g):
        return pltpu.make_async_copy(r_c.at[g], act.at[2 * g + 1 - c, pl.ds(0, D)], stage_s.at[g])

    def core_piece(g, k):
        cols = pl.ds(k * GW, GW)
        return remote(gown.at[0, g, :, cols], gown.at[1, g, :, cols], cp_s.at[g, k], cp_r.at[g, k], core)

    def core_fetch(g):
        arrived(r_c.at[g], c_r.at[1, g])
        fetch(g).start()

    middle = jnp.logical_and(z > 0, z < nz - 1)

    def target(k):
        down = jnp.where(nz - 1 - k > z, nz - 1 - k, nz - 2 - k)
        up = jnp.where(k < z, k, k + 1)
        return jnp.where(k == nz - 1, z, jnp.where(z < nz // 2, down, up))

    def core_add(m, g):
        if m == 2:
            for k in range(D // GW):
                core_piece(g, k).wait_recv()
            from_core = gown.at[1, g]
        else:
            from_core = act.at[2 * g + 1 - c, pl.ds(0, D)]
            if m == 1:
                fetch(g).wait()
            else:
                arrived(from_core, c_r.at[0, g])

        def add(i):
            p = part(target(i % nz), lax.rem(xc + 1 + i // nz, 2))
            gown[m, g, p] += from_core[p]

        def over(k):
            zz = target(k)
            remote(gown.at[m, g, part(zz, 1 - xc)], x_place(m, g, zz), x_s.at[m, g, zz], x_r.at[m, g, zz], other_x).start()

        loop(nz + 1, add)
        loop(nz, over)
        loop(nz - 1, lambda i: add(nz + 1 + i))

    def sum_event(q):
        m = 2 - q // (2 * nz)
        g = (q // nz) % 2
        k = q % nz
        zz = target(k)
        over = x_place(m, g, zz)
        arrived(over, x_r.at[m, g, zz])
        p = part(zz, xc)
        gown[m, g, p] += over[...]

        joins = jnp.logical_and(k == 0, jnp.logical_not(middle))
        waits = jnp.logical_and(k == 0, middle)
        beside = jnp.where(z == 0, 1, nz - 2)
        to = jnp.where(joins, beside, zz)
        slot = jnp.where(joins, beside, z)

        @pl.when(jnp.logical_and(k < nz - 1, jnp.logical_not(waits)))
        def _():
            remote(gown.at[m, g, p], z_place(m, g, slot), z_s.at[m, g, zz], z_r.at[m, g, slot], {"z": to}).start()

        @pl.when(jnp.logical_and(k == jnp.where(m == 0, 1, nz - 2), middle))
        def _():
            far = target(0)
            f = part(far, xc)
            arrived(z_place(m, g, z), z_r.at[m, g, z])
            gown[m, g, f] += z_place(m, g, z)[...]
            remote(gown.at[m, g, f], z_place(m, g, z), z_s.at[m, g, far], z_r.at[m, g, z], {"z": far}).start()

    outs = (qo_out, up_out, dn_out)

    def out_stage(m, other):
        return mid.at[pl.ds(m * rows + (0 if other else OWN_ROWS), rows)]

    def out_copy(m, other):
        return pltpu.make_async_copy(out_stage(m, other), outs[m].at[1 - y if other else y], out_s.at[m, other])

    def last_send(m):
        return remote(mid_low.at[pl.ds(EXT_ROWS + m * rows, rows)], oth.at[m], y_s.at[m], y_r.at[m], across)

    def finish(m, g):
        total = gown[m, g, part(z, xc)].astype(F32)
        for dz in range(1, nz):
            source = z_of(dz)
            direct = jnp.abs(source - z) < nz - 1

            @pl.when(direct)
            def _():
                arrived(z_place(m, g, source), z_r.at[m, g, source])

            total += jnp.where(direct, z_place(m, g, source)[...].astype(F32), 0.0)

        @pl.when(y == g)
        def _():
            out_stage(m, 0)[...] = total
            out_copy(m, 0).start()

        @pl.when(y != g)
        def _():
            mid_low[EXT_ROWS + m * rows : EXT_ROWS + (m + 1) * rows] = total.astype(BF)
            last_send(m).start()

    def slope_grads(m, a, b, extra):
        def unit(q):
            g, own = (q // 2, q % 2) if m == 2 else (q % 2, q // 2)
            t = 2 * g + jnp.where(own == 0, 1 - c, c)
            dst = gown.at[jnp.where(own == 0, 0, m), g]
            for k in range(D // GW):
                cols = slice(k * GW, (k + 1) * GW)
                dst[:, cols] = dot_tn(a[...], b[t, :, cols]).astype(BF)

                if m == 2 and k:
                    pl.when(own == 0)(core_piece(g, k - 1).start)

            @pl.when(own == 0)
            def _():
                if m == 2:
                    core_piece(g, D // GW - 1).start()
                else:
                    core_send(m, g).start()

        weave(4, unit, extra)

    def then(*steps):
        def run():
            for f, *args in steps:
                f(*args)

        return run

    def core_over(m):
        for g in range(2):
            if m == 2:
                for k in range(D // GW):
                    core_piece(g, k).wait_send()
            else:
                core_send(m, g).wait_send()

    slope_grads(
        2,
        d_ffn,
        act,
        {
            1: then((core_add, 2, 0)),
            3: then((core_add, 2, 1), (core_over, 2)),
        },
    )

    def up_back(i):
        back_up(i // N_CHUNK, i % N_CHUNK, d_ffn, w, slope)

    weave(GROUPS * N_CHUNK, up_back, {1: then((sum_event, 0)), 7: then((sum_event, 1)), 11: then((sum_event, 2))})
    for i in range(2):
        y_copy(i).wait()
    has_left(y_stage(2), e_s.at[0])
    slope_grads(1, mid_low, slope, {1: then((sum_event, 3)), 3: then((sum_event, 4))})
    for g in range(2):
        core_fetch(g)
    weave(
        N_CHUNK,
        lambda i: back_first_norm(i, slope, w, prm, mid, n1, s1, d_ffn, ngrad),
        {
            0: then((core_add, 1, 0), (core_add, 1, 1), (core_over, 1)),
            1: then((sum_event, 5)),
            2: then((sum_event, 6)),
        },
    )

    def send_norms(i, act_on):
        if i == 0:
            act_on(remote(ngrad, n_c, ng_s.at[0], ng_r.at[0], core))
        elif i == 1:
            act_on(remote(n_c, n_x, ng_s.at[1], ng_r.at[1], other_x))
        elif i == 2:
            for dz in range(1, nz):
                act_on(remote(n_x, n_z.at[dz], ng_s.at[1 + dz], ng_r.at[1 + dz], {"z": z_of(dz)}))
        else:
            act_on(remote(n_out.at[y], n_out.at[y], ng_s.at[nz + 1], ng_r.at[nz + 1], across))

    send_norms(0, start)
    loop(GROUPS, lambda t: back_heads(t, d_ffn, wo, slope))
    sum_event(7)
    send_norms(0, recv)
    send_norms(0, lambda cp: cp.wait_send())
    n_c[...] += ngrad[...]
    send_norms(1, start)

    def attention_back(i):
        back_attend(i // per, [(i % per) * PAIR + k for k in range(PAIR)], proj, probs, slope)

        @pl.when(i % 2 == 1)
        def _():
            sum_event(8 + i // 2)

    loop(GROUPS * per, attention_back)
    seen = 8 + GROUPS * per // 2

    def qkv_grads(q):
        g, own = q // 2, q % 2

        def store(col, value):
            value = value.astype(BF)

            @pl.when(own == 0)
            def _():
                spare(0, g)[:, col : col + 128] = value

            @pl.when(own == 1)
            def _():
                gown[0, g, :, col : col + 128] = value

        grad_qkv_out(2 * g + jnp.where(own == 0, 1 - c, c), x, proj, d_ffn, hout, store)

        @pl.when(own == 0)
        def _():
            core_send(0, g).start()

    weave(
        4,
        qkv_grads,
        {
            0: then((sum_event, seen)),
            1: then((core_add, 0, 0), (sum_event, seen + 1)),
            3: then((core_add, 0, 1), (sum_event, seen + 2)),
        },
    )
    seen += 3

    def inputs_back(i):
        k = lax.rem(i + N_CHUNK - 1, N_CHUNK)

        def keep(r, grad):
            mid[r] = grad

            @pl.when(i == 0)
            def _():
                mid_low[:EXT_ROWS] = grad.astype(BF)

        back_input(k, proj, w, mid, keep)

        @pl.when(i == 0)
        def _():
            give_back(mid_low.at[pl.ds(0, EXT_ROWS)], g_back, 1, start)

    weave(N_CHUNK, inputs_back, {1: then((sum_event, seen))})
    seen += 1
    after = 4 * nz
    if seen < after:
        loop(after - seen, lambda q: sum_event(seen + q))
    for g in range(2):
        finish(2, g)
    loop(2, lambda q: sum_event(after + q))

    def sums_sent(i):
        m, g = i // 2, i % 2
        for zz in range(nz):
            @pl.when(z != zz)
            def _():
                has_left(x_place(0, 0, 0), z_s.at[m, g, zz])

            has_left(x_place(0, 0, 0), x_s.at[m, g, zz])

    loop(6, gather_sent)

    trips = [
        pltpu.make_async_copy(g_back, proj.at[0, pl.ds(0, OWN_ROWS)], io_s.at[0]),
        pltpu.make_async_copy(y_out, proj.at[1, pl.ds(0, OWN_ROWS)], io_s.at[1]),
        pltpu.make_async_copy(y_back, proj.at[2, pl.ds(0, OWN_ROWS)], io_s.at[2]),
    ]
    y_again = pltpu.make_async_copy(proj.at[1, pl.ds(0, OWN_ROWS)], y_out, io_s.at[1])
    g_copy = pltpu.make_async_copy(mid.at[pl.ds(0, OWN_ROWS)], g_out, io_s.at[3])

    @pl.when(lender)
    def _():
        for i, dst in enumerate((y_back, g_back)):
            for j in range(2):
                arrived(dst.at[pl.ds(j * EXT_ROWS, EXT_ROWS)], e_r.at[i, j])
        for cp in trips:
            cp.start()
        for cp in trips:
            cp.wait()

        def merge(s):
            r = chunk_rows(s, LENGTH)
            keep = jnp.zeros((LENGTH, D), F32) + mine(s) > 0.5
            mid[r] = jnp.where(keep, mid[r], proj[0, r].astype(F32))
            proj[1, r] = jnp.where(keep, proj[1, r].astype(F32), proj[2, r].astype(F32)).astype(BF)

        loop(OWN, merge)
        y_again.start()

    g_copy.start()
    loop(nz - 2, lambda q: sum_event(after + 2 + q))
    send_norms(1, recv)
    send_norms(1, lambda cp: cp.wait_send())
    n_x[...] += n_c[...]
    send_norms(2, start)
    for g in range(2):
        finish(1, g)
    loop(nz - 1, lambda q: sum_event(after + nz + q))
    g_copy.wait()

    def widen(m):
        arrived(oth.at[m], y_r.at[m])
        out_stage(m, 1)[...] = oth[m].astype(F32)
        out_copy(m, 1).start()

    widen(2)
    widen(1)
    loop(4, lambda i: sums_sent(2 + i))
    total = n_x[...]
    for dz in range(1, nz):
        arrived(n_z.at[dz], ng_r.at[1 + dz])
        total += n_z[dz]
    n_out[y] = total
    send_norms(3, start)
    finish(0, 0)
    sum_event(after + 2 * nz - 1)
    finish(0, 1)
    widen(0)

    loop(2, sums_sent)
    for g in range(2):
        core_send(0, g).wait_send()
    for m in range(3):
        has_left(given(m), ys_s.at[m])
        for other in range(2):
            out_copy(m, other).wait()
        last_send(m).wait_send()
    lend(x_in, x, 0, lambda cp: cp.wait_send())
    lend(cot, d_ffn, 1, lambda cp: cp.wait_send())
    for i in range(4):
        norm_hop(i, lambda cp: cp.wait_send())
    send_norms(2, lambda cp: cp.wait_send())
    send_norms(3, lambda cp: cp.wait())
    has_left(mid_low.at[pl.ds(0, EXT_ROWS)], e_s.at[1])

    @pl.when(lender)
    def _():
        y_again.wait()


def run_step(nz, tags, lens, x_in, cot, qkv, wout, up, dn, gain, bias):
    rows = up.shape[1]
    V = pl.BlockSpec(memory_space=pltpu.VMEM)
    S = pl.BlockSpec(memory_space=pltpu.SMEM)
    sem = pltpu.SemaphoreType.DMA
    out = jax.ShapeDtypeStruct
    return pl.pallas_call(
        partial(step_kernel, nz, rows),
        out_shape=(
            out((OWN_ROWS, D), BF),
            out((OWN_ROWS, D), F32),
            out((2, rows, D), F32),
            out((2, rows, D), F32),
            out((2, rows, D), F32),
            out((2, 8, D), F32),
            out((OWN_ROWS, D), BF),
            out((OWN_ROWS, D), BF),
            out((2, D, D), BF),
        ),
        in_specs=[S, S] + [ANY] * 6 + [V, V],
        out_specs=(ANY, ANY, ANY, ANY, ANY, V, ANY, ANY, ANY),
        scratch_shapes=[
            pltpu.VMEM((3, GROUPS, D, D), BF),
            pltpu.VMEM((ROWS, D), BF),
            pltpu.VMEM((GROUPS, ROWS, D), BF),
            pltpu.VMEM((GROUPS, SLOTS, LENGTH, 512), BF),
            pltpu.VMEM((GROUPS, ROWS, GW), BF),
            pltpu.VMEM((GROUPS, D, GW), BF),
            pltpu.VMEM((ROWS, D), F32),
            pltpu.VMEM((ROWS, D), BF),
            pltpu.VMEM((ROWS, 128), F32),
            pltpu.VMEM((ROWS, D), BF),
            pltpu.VMEM((GROUPS, ROWS, D), BF),
            pltpu.VMEM((GROUPS, ROWS, D), BF),
            pltpu.VMEM((ROWS, D), BF),
            pltpu.VMEM((3, 2, D, D), BF),
            pltpu.VMEM((2, 3, 2 * nz * rows, D), BF),
            pltpu.VMEM((3, rows, D), BF),
            pltpu.VMEM(qkv.shape, BF),
            pltpu.VMEM(wout.shape, BF),
            pltpu.VMEM((rows, D), BF),
            pltpu.VMEM((8 * nz, 8, 128), F32),
            pltpu.VMEM((8, D), F32),
            pltpu.VMEM((8, D), F32),
            pltpu.VMEM((8, D), F32),
            pltpu.VMEM((8, D), F32),
            pltpu.VMEM((nz, 8, D), F32),
            sem((6,)), sem((4,)), sem((2,)), sem((3, 2)),
            sem((3,)), sem((3,)),
            sem((3, 2, 2, nz)), sem((3, 2, 2, nz)),
            sem((2, nz)), sem((2, nz)),
            sem((3, 2, nz)), sem((3, 2, nz)),
            sem((3, 2, nz, 2)), sem((3, 2, nz, 2)),
            sem((2, 2)), sem((2,)),
            sem((nz + 2,)), sem((nz + 2,)),
            sem((3, 2)), sem((3, 2)),
            sem((2, 3)), sem((2, 3)),
            sem((3, 2, nz)), sem((3, 2, nz)),
            sem((3, 2, nz)), sem((3, 2, nz)),
            sem((3,)), sem((3,)),
            sem((2,)), sem((2, 2)),
            sem((nz + 2,)), sem((nz + 2,)),
        ],
        compiler_params=pltpu.CompilerParams(
            collective_id=0, has_side_effects=True, vmem_limit_bytes=67043328
        ),
        name="layer_step",
    )(tags, lens, x_in, cot, qkv, wout, up, dn, gain, bias)


def deliver_kernel(cols, y_in, g_in, qo, up_in, dn_in, sums,
                   y_out, g_out, qkv_out, wout_out, up_out, dn_out, gain_out, bias_out,
                   v_y, v_g, v_qo, v_up, v_dn, v_qkv, v_out, in_s, out_s):
    through = [(up_in, v_up, up_out), (dn_in, v_dn, dn_out)]
    for k in range(OWN):
        r = pl.ds(k * LENGTH, LENGTH)
        through.append((g_in.at[r], v_g.at[r], g_out.at[r]))
    for k in range(2):
        r = pl.ds(k * CHUNK, CHUNK)
        through.append((y_in.at[r], v_y.at[r], y_out.at[r]))
    n = len(through)
    first = pltpu.make_async_copy(qo, v_qo, in_s.at[n])
    first.start()
    loads, stores = [], []
    for i, (src, via, dst) in enumerate(through):
        loads.append(pltpu.make_async_copy(src, via, in_s.at[i]))
        stores.append(pltpu.make_async_copy(via, dst, out_s.at[i]))
        loads[-1].start()
    z, x, y, c = place()
    me = ((z * 2 + x) * 2 + y) * 2 + c
    for k in range(2):
        turned = pltpu.roll(sums[k], lax.rem(D - me * cols, D), 1)
        gain_out[k] = turned[0:2, :cols]
        bias_out[k] = turned[2:4, :cols]
    first.wait()

    def unpack(k):
        tail = []
        for i in range(3):
            v_qkv[k, i] = v_qo[k, :, GW * i : GW * i + GW - HEAD_DIM]
            tail.append(v_qo[k, :, GW * (i + 1) - HEAD_DIM : GW * (i + 1)])
        v_out[k] = jnp.concatenate(tail, 1)
        for j, (src, dst) in enumerate(((v_qkv, qkv_out), (v_out, wout_out))):
            stores.append(pltpu.make_async_copy(src.at[k], dst.at[k], out_s.at[n + 2 * k + j]))
            stores[-1].start()

    for i in range(n):
        loads[i].wait()
        stores[i].start()
        if i in (1, 3):
            unpack(i // 2)
    for cp in stores:
        cp.wait()


def deliver(cols, y_in, g_in, qo, up_in, dn_in, sums):
    rows = qo.shape[1]
    V = pl.BlockSpec(memory_space=pltpu.VMEM)
    sem = pltpu.SemaphoreType.DMA
    out = jax.ShapeDtypeStruct
    width = GW - HEAD_DIM
    shapes = [((2, 3, rows, width), F32), ((2, rows, width), F32)]
    whole = [(y_in.shape, BF), (g_in.shape, F32), (qo.shape, F32), (qo.shape, F32), (qo.shape, F32)]
    return pl.pallas_call(
        partial(deliver_kernel, cols),
        out_shape=tuple(
            out(*p) for p in whole[:2] + shapes + whole[3:] + [((2, 2, cols), F32)] * 2
        ),
        in_specs=[ANY] * 5 + [V],
        out_specs=(ANY,) * 6 + (V, V),
        scratch_shapes=[pltpu.VMEM(*p) for p in whole + shapes] + [sem((9,)), sem((12,))],
        name="deliver",
    )(y_in, g_in, qo, up_in, dn_in, sums)


def split_local(nz, x_in, tags, lengths, w_qkv, w_out, w_up, w_down, norm_gain, norm_bias, cotangent):
    cols = norm_gain.shape[2]
    y_out, x_grad, qo_grad, up_grad, down_grad, n_sum, _, _, _ = run_step(
        nz, tags, lengths, x_in, cotangent, w_qkv.transpose(0, 2, 1, 3), w_out, w_up, w_down, norm_gain, norm_bias
    )
    y_out, x_grad, qkv, out, up, down, gain, bias = deliver(
        cols, y_out, x_grad, qo_grad, up_grad, down_grad, n_sum
    )
    return y_out, x_grad, qkv.transpose(0, 2, 1, 3), out, up, down, gain, bias


def typed_map(operand, stacked, chain_kinds, pattern):

    def single(element):
        weight = lax.dynamic_index_in_dim(stacked, element[1], 0, keepdims=False)
        return jnp.einsum(pattern, element[0], weight, preferred_element_type=jnp.float32)

    return lax.map(single, (operand, chain_kinds))


def typed_grads(running, operand, partner, chain_kinds, pattern):

    def single(carry, element):
        product_term = jnp.einsum(
            pattern, element[0], element[1], preferred_element_type=jnp.float32
        )
        previous = lax.dynamic_index_in_dim(carry, element[2], 0, keepdims=False)
        return (
            lax.dynamic_update_index_in_dim(carry, previous + product_term, element[2], 0),
            None,
        )

    return lax.scan(single, running, (operand, partner, chain_kinds))[0]


def row_terms(operand, stacked, chain_kinds, pattern, row_count):
    result = typed_map(operand, stacked, chain_kinds, pattern)
    return result.reshape(row_count, result.shape[-1])


def old_norm_forward(values, gain_rows, shift_rows):
    center = values - jnp.mean(values, -1, keepdims=True)
    factor = lax.rsqrt(jnp.mean(center * center, -1, keepdims=True) + EPS)
    normed = center * factor
    return (normed * gain_rows + shift_rows, normed, factor)


def old_norm_backward(grad_out, normed, factor, gain_rows):
    scaled = grad_out * gain_rows
    mean_plain = jnp.mean(scaled, -1, keepdims=True)
    mean_normed = jnp.mean(scaled * normed, -1, keepdims=True)
    return factor * (scaled - mean_plain - normed * mean_normed)


def type_sums(onehot, values):
    return jnp.dot(onehot.T, values, precision=HIGH, preferred_element_type=jnp.float32)


def general_local(x_in, tags, lengths, w_qkv, w_out, w_up, w_down, norm_gain, norm_bias, cotangent):
    tp_count = lax.axis_size("tensor")
    tp_index = lax.axis_index("tensor")
    local_rows = CHAINS_PART * LENGTH
    batch_chains = tp_count * CHAINS_PART
    head_cols = w_qkv.shape[3]
    local_heads = head_cols // HEAD_DIM
    tag_grid = tags.reshape(tp_count, MICRO, CHAINS_PART)
    len_grid = lengths.reshape(tp_count, MICRO, CHAINS_PART)
    own_tags = lax.dynamic_index_in_dim(tag_grid, tp_index, 0, keepdims=False)
    gains, shifts = (
        lax.all_gather(norm_gain, ("dp", "tensor"), axis=2, tiled=True),
        lax.all_gather(norm_bias, ("dp", "tensor"), axis=2, tiled=True),
    )
    grad_full = (
        jnp.zeros((2, D, 3, head_cols), jnp.float32),
        jnp.zeros((2, D, head_cols), jnp.float32),
        jnp.zeros((2, D, w_up.shape[2]), jnp.float32),
        jnp.zeros((2, D, w_down.shape[2]), jnp.float32),
    )
    shards = (
        jnp.zeros(w_qkv.shape, jnp.float32),
        jnp.zeros(w_out.shape, jnp.float32),
        jnp.zeros(w_up.shape, jnp.float32),
        jnp.zeros(w_down.shape, jnp.float32),
    )
    gain_acc = jnp.zeros((2, 2, D), jnp.float32)
    shift_acc = jnp.zeros((2, 2, D), jnp.float32)
    outputs = []
    input_grads = []
    for micro_index in range(MICRO):
        held = (
            lax.all_gather(w_qkv, "dp", axis=1, tiled=True),
            lax.all_gather(w_out, "dp", axis=1, tiled=True),
            lax.all_gather(w_up, "dp", axis=1, tiled=True),
            lax.all_gather(w_down, "dp", axis=1, tiled=True),
        )
        qkv_w, out_w, up_w, down_w = held
        chain_kinds = tag_grid[:, micro_index].reshape(batch_chains)
        chain_lens = len_grid[:, micro_index].reshape(batch_chains)
        own_rows = x_in[micro_index * local_rows : (micro_index + 1) * local_rows]
        kinds_rows = jnp.repeat(own_tags[micro_index], LENGTH)
        heavy_rows = (kinds_rows == 0)[:, None]
        onehot = (kinds_rows[:, None] == jnp.arange(2)[None, :]).astype(jnp.float32)
        gain_mid = jnp.where(heavy_rows, gains[0, 0], gains[1, 0])
        shift_mid = jnp.where(heavy_rows, shifts[0, 0], shifts[1, 0])
        gain_end = jnp.where(heavy_rows, gains[0, 1], gains[1, 1])
        shift_end = jnp.where(heavy_rows, shifts[0, 1], shifts[1, 1])
        gathered = lax.all_gather(own_rows, "tensor", axis=0, tiled=True).reshape(
            batch_chains, LENGTH, D
        )
        projected = typed_map(gathered, qkv_w, chain_kinds, "ld,dkh->lkh").astype(jnp.bfloat16)
        query = projected[:, :, 0].reshape(batch_chains, LENGTH, local_heads, HEAD_DIM)
        keys_low = projected[:, :, 1].reshape(batch_chains, LENGTH, local_heads, HEAD_DIM)
        values_low = projected[:, :, 2].reshape(batch_chains, LENGTH, local_heads, HEAD_DIM)
        valid = (
            lax.broadcasted_iota(jnp.int32, (batch_chains, 1, 1, LENGTH), 3)
            < chain_lens[:, None, None, None]
        )
        scores = (
            jnp.einsum("cqhe,ckhe->chqk", query, keys_low, preferred_element_type=jnp.float32)
            * 0.125
        )
        scores = jnp.where(valid, scores, NEG)
        highest = jnp.max(scores, -1, keepdims=True)
        expo = jnp.exp(scores - highest)
        totals = jnp.sum(expo, -1, keepdims=True)
        probs = expo / totals
        log_total = highest + jnp.log(totals)
        heads_low = jnp.einsum(
            "chqk,ckhe->cqhe",
            probs.astype(jnp.bfloat16),
            values_low,
            preferred_element_type=jnp.float32,
        ).astype(jnp.bfloat16)
        heads_low = heads_low.reshape(batch_chains, LENGTH, head_cols)
        attn_sum = lax.psum_scatter(
            row_terms(
                heads_low, out_w, chain_kinds, "lh,dh->ld", lax.axis_size("tensor") * local_rows
            ).astype(jnp.bfloat16),
            "tensor",
            scatter_dimension=0,
            tiled=True,
        ).astype(jnp.float32)
        mid, normed_mid, factor_mid = old_norm_forward(
            own_rows.astype(jnp.float32) + attn_sum, gain_mid, shift_mid
        )
        mid_all = lax.all_gather(mid.astype(jnp.bfloat16), "tensor", axis=0, tiled=True).reshape(
            batch_chains, LENGTH, D
        )
        up_value = typed_map(mid_all, up_w, chain_kinds, "ld,df->lf")
        act_low = jax.nn.gelu(up_value, approximate=False).astype(jnp.bfloat16)
        ffn_sum = lax.psum_scatter(
            row_terms(
                act_low, down_w, chain_kinds, "lf,df->ld", lax.axis_size("tensor") * local_rows
            ).astype(jnp.bfloat16),
            "tensor",
            scatter_dimension=0,
            tiled=True,
        ).astype(jnp.float32)
        final, normed_end, factor_end = old_norm_forward(ffn_sum + mid, gain_end, shift_end)
        outputs.append(final.astype(jnp.bfloat16))
        base = grad_full
        grad_final = cotangent[micro_index * local_rows : (micro_index + 1) * local_rows].astype(
            jnp.float32
        )
        gain_acc = gain_acc.at[:, 1].add(type_sums(onehot, grad_final * normed_end))
        shift_acc = shift_acc.at[:, 1].add(type_sums(onehot, grad_final))
        grad_resid2 = old_norm_backward(grad_final, normed_end, factor_end, gain_end)
        grad_ffn = lax.all_gather(
            grad_resid2.astype(jnp.bfloat16), "tensor", axis=0, tiled=True
        ).reshape(batch_chains, LENGTH, D)
        grad_act = typed_map(grad_ffn, down_w, chain_kinds, "ld,df->lf")
        unused_value, gelu_back = jax.vjp(partial(jax.nn.gelu, approximate=False), up_value)
        grad_up = gelu_back(grad_act)[0].astype(jnp.bfloat16)
        down_acc = typed_grads(base[3], grad_ffn, act_low, chain_kinds, "ld,lf->df")
        up_acc = typed_grads(base[2], mid_all, grad_up, chain_kinds, "ld,lf->df")
        grad_mid = grad_resid2 + lax.psum_scatter(
            row_terms(
                grad_up, up_w, chain_kinds, "lf,df->ld", lax.axis_size("tensor") * local_rows
            ).astype(jnp.bfloat16),
            "tensor",
            scatter_dimension=0,
            tiled=True,
        ).astype(jnp.float32)
        gain_acc = gain_acc.at[:, 0].add(type_sums(onehot, grad_mid * normed_mid))
        shift_acc = shift_acc.at[:, 0].add(type_sums(onehot, grad_mid))
        grad_resid1 = old_norm_backward(grad_mid, normed_mid, factor_mid, gain_mid)
        grad_attn = lax.all_gather(
            grad_resid1.astype(jnp.bfloat16), "tensor", axis=0, tiled=True
        ).reshape(batch_chains, LENGTH, D)
        grad_heads = typed_map(grad_attn, out_w, chain_kinds, "ld,dh->lh").astype(jnp.bfloat16)
        out_acc = typed_grads(base[1], grad_attn, heads_low, chain_kinds, "ld,lh->dh")
        grad_heads = grad_heads.reshape(batch_chains, LENGTH, local_heads, HEAD_DIM)
        again = (
            jnp.einsum("cqhe,ckhe->chqk", query, keys_low, preferred_element_type=jnp.float32)
            * 0.125
        )
        probs_again = jnp.exp(jnp.where(valid, again, NEG) - log_total)
        grad_probs = jnp.einsum(
            "cqhe,ckhe->chqk", grad_heads, values_low, preferred_element_type=jnp.float32
        )
        inner = jnp.sum(grad_probs * probs_again, -1, keepdims=True)
        grad_scores = (probs_again * (grad_probs - inner)).astype(jnp.bfloat16)
        grad_query = (
            jnp.einsum("chqk,ckhe->cqhe", grad_scores, keys_low, preferred_element_type=jnp.float32)
            * 0.125
        ).astype(jnp.bfloat16)
        grad_keys = (
            jnp.einsum("chqk,cqhe->ckhe", grad_scores, query, preferred_element_type=jnp.float32)
            * 0.125
        ).astype(jnp.bfloat16)
        grad_values = jnp.einsum(
            "chqk,cqhe->ckhe",
            probs_again.astype(jnp.bfloat16),
            grad_heads,
            preferred_element_type=jnp.float32,
        ).astype(jnp.bfloat16)
        grad_proj = jnp.stack([grad_query, grad_keys, grad_values], 2).reshape(
            batch_chains, LENGTH, 3, head_cols
        )
        qkv_acc = typed_grads(base[0], gathered, grad_proj, chain_kinds, "ld,lkh->dkh")
        grad_input = grad_resid1 + lax.psum_scatter(
            row_terms(
                grad_proj, qkv_w, chain_kinds, "lkh,dkh->ld", lax.axis_size("tensor") * local_rows
            ).astype(jnp.bfloat16),
            "tensor",
            scatter_dimension=0,
            tiled=True,
        ).astype(jnp.float32)
        input_grads.append(grad_input)
        updated = (qkv_acc, out_acc, up_acc, down_acc)
        grad_full = updated
    shards = (
        lax.psum_scatter(grad_full[0], "dp", scatter_dimension=1, tiled=True),
        lax.psum_scatter(grad_full[1], "dp", scatter_dimension=1, tiled=True),
        lax.psum_scatter(grad_full[2], "dp", scatter_dimension=1, tiled=True),
        lax.psum_scatter(grad_full[3], "dp", scatter_dimension=1, tiled=True),
    )
    gain_grad, shift_grad = (
        lax.psum_scatter(gain_acc, ("dp", "tensor"), scatter_dimension=2, tiled=True),
        lax.psum_scatter(shift_acc, ("dp", "tensor"), scatter_dimension=2, tiled=True),
    )
    return (
        jnp.concatenate(outputs, 0),
        jnp.concatenate(input_grads, 0),
        shards[0],
        shards[1],
        shards[2],
        shards[3],
        gain_grad,
        shift_grad,
    )


def solution(mesh):
    placed = (
        P(("dp", "tensor"), None),
        P("dp"),
        P("dp"),
        P(None, "dp", None, "tensor"),
        P(None, "dp", "tensor"),
        P(None, "dp", "tensor"),
        P(None, "dp", "tensor"),
        P(None, None, ("dp", "tensor")),
        P(None, None, ("dp", "tensor")),
        P(("dp", "tensor"), None),
    )
    results = (
        P(("dp", "tensor"), None),
        P(("dp", "tensor"), None),
        P(None, "dp", None, "tensor"),
        P(None, "dp", "tensor"),
        P(None, "dp", "tensor"),
        P(None, "dp", "tensor"),
        P(None, None, ("dp", "tensor")),
        P(None, None, ("dp", "tensor")),
    )
    n_dp, n_tensor = mesh.shape["dp"], mesh.shape["tensor"]
    if n_tensor != GROUPS or n_dp != 8:
        return jax.shard_map(
            general_local, mesh=mesh, in_specs=placed, out_specs=results, check_vma=False
        )
    fine = Mesh(mesh.devices.reshape(n_dp // 2, 2, 2, 2), AXES)
    names = {"dp": ("z", "x"), "tensor": ("y", "c")}

    def refine(spec):
        parts = []
        for entry in spec:
            entry = (entry,) if isinstance(entry, str) else entry
            parts.append(entry and sum((names[a] for a in entry), ()))
        return P(*parts)

    return jax.shard_map(
        partial(split_local, n_dp // 2),
        mesh=fine,
        in_specs=tuple(refine(s) for s in placed),
        out_specs=tuple(refine(s) for s in results),
        check_vma=False,
    )
```

```python
from functools import partial

import jax
import jax.numpy as jnp
from jax import lax
from jax.experimental import pallas as pl
from jax.experimental.pallas import tpu as pltpu
from jax.sharding import Mesh
from jax.sharding import PartitionSpec as P

D = 768
HEADS = 12
HEAD_DIM = 64
MICRO = 4
CHAINS_PART = 1
LENGTH = 160
GROUPS = 4
OWN = 4
EXTRA = 2
SLOTS = OWN + EXTRA
EXT_ROWS = EXTRA * LENGTH
OWN_ROWS = OWN * LENGTH
ROWS = SLOTS * LENGTH

EPS = 1e-12
NEG = -1e30
HIGH = lax.Precision.HIGHEST
BF = jnp.bfloat16
F32 = jnp.float32
MESH = pl.DeviceIdType.MESH
ANY = pl.BlockSpec(memory_space=pl.ANY)
AXES = ("z", "x", "y", "c")


def place():
    return tuple(lax.axis_index(a) for a in AXES)


def greet(nz, z, x, y, c):
    barrier = pltpu.get_barrier_semaphore()
    friends = [{"c": 1 - c}, {"y": 1 - y}, {"y": 1 - y, "c": 1 - c}, {"x": 1 - x}]
    friends += [{"z": lax.rem(z + dz, nz)} for dz in range(1, nz)]
    for friend in friends:
        pl.semaphore_signal(barrier, inc=1, device_id=friend, device_id_type=MESH)
    return barrier, len(friends)


CHUNK = 320
SUB = 80
N_CHUNK = ROWS // CHUNK
WIDE = 3 * LENGTH
GW = 256
PAIR = 3


def dot_nn(a, b):
    return lax.dot_general(a, b, (((1,), (0,)), ((), ())), preferred_element_type=F32)


def dot_nt(a, b):
    return lax.dot_general(a, b, (((1,), (1,)), ((), ())), preferred_element_type=F32)


def dot_tn(a, b):
    return lax.dot_general(a, b, (((0,), (0,)), ((), ())), preferred_element_type=F32)


def lanes(shape):
    return lax.broadcasted_iota(jnp.int32, shape, len(shape) - 1)


def head_mask(h, shape):
    lane = lanes(shape)
    return jnp.logical_and(lane >= h * HEAD_DIM, lane < (h + 1) * HEAD_DIM)


def stack_heads(rows):
    zero = jnp.zeros_like(rows)
    return jnp.concatenate([jnp.where(head_mask(h, rows.shape), rows, zero) for h in range(3)], 0)


def merge_heads(stack):
    out = jnp.zeros((LENGTH, GW), stack.dtype)
    for h in range(3):
        out = jnp.where(head_mask(h, out.shape), stack[h * LENGTH : (h + 1) * LENGTH], out)
    return out


def chunk_rows(i, size=CHUNK):
    return pl.ds(pl.multiple_of(i * size, size), size)


def loop(count, body):
    def step(i, carry):
        body(i)
        return carry

    lax.fori_loop(0, count, step, 0)


def weave(count, unit, extra):
    def body(i):
        unit(i)
        for k, step in extra.items():
            pl.when(i == k)(step)

    loop(count, body)


def out_columns(t, w, wo):
    low = lanes((D, 128)) < HEAD_DIM
    tiles = [w[0, t, :, GW * i + 128 : GW * i + 256].astype(F32) for i in range(3)]
    wo[t, :, :128] = jnp.where(low, pltpu.roll(tiles[0], 64, 1), tiles[1]).astype(BF)
    wo[t, :, 128:] = jnp.where(low, pltpu.roll(tiles[2], 64, 1), 0.0).astype(BF)


def attend(t, chains, lens, proj, probs, hout):
    rows = [chunk_rows(s, LENGTH) for s in chains]
    parts = [(proj[t, r, :GW], proj[t, r, GW : 2 * GW], proj[t, r, 2 * GW :]) for r in rows]
    lows, outs = [], []
    for s, (query, key, value) in zip(chains, parts):
        scores = dot_nt(key, stack_heads(query * jnp.asarray(0.125, BF)))
        valid = lax.broadcasted_iota(jnp.int32, (LENGTH, 1), 0) < lens(s)
        scores = jnp.where(valid, scores, NEG)
        expo = jnp.exp(scores - jnp.max(scores, 0, keepdims=True))
        lows.append((expo * (1.0 / jnp.sum(expo, 0, keepdims=True))).astype(BF))
        outs.append(merge_heads(dot_tn(lows[-1], value)).astype(BF))
    for s, r, low, out in zip(chains, rows, lows, outs):
        probs[t, s, :, :WIDE] = low
        hout[t, r] = out


def norm_rows(values):
    center = values - jnp.mean(values, -1, keepdims=True)
    factor = lax.rsqrt(jnp.mean(center * center, -1, keepdims=True) + EPS)
    return center * factor, factor


def norm_back(scaled, normed, factor):
    return factor * (
        scaled
        - jnp.mean(scaled, -1, keepdims=True)
        - normed * jnp.mean(scaled * normed, -1, keepdims=True)
    )


def pieces(i, body):
    def step(k):
        body(pl.ds(pl.multiple_of(i * CHUNK + k * SUB, SUB), SUB), k)

    loop(CHUNK // SUB, step)


def first_norm(i, x, hout, wo, prm, mid, n1, s1, mid_low):
    r = chunk_rows(i)
    attn = dot_nt(hout[0, r], wo[0])
    for t in range(1, GROUPS):
        attn += dot_nt(hout[t, r], wo[t])
    mid[r] = attn

    def piece(p, k):
        normed, factor = norm_rows(x[p].astype(F32) + mid[p])
        n1[p] = normed.astype(BF)
        s1[p] = jnp.broadcast_to(factor, (SUB, 128))
        value = normed * prm[0:1] + prm[2:3]
        mid[p] = value
        mid_low[p] = value.astype(BF)

    pieces(i, piece)


def feed_up(t, i, mid_low, w, act, slope):
    r = chunk_rows(i)
    for k in range(0, D, GW):
        up = dot_nn(mid_low[r], w[1, t, :, k : k + GW])
        cdf = 0.5 * (1.0 + lax.erf(up * 0.7071067811865476))
        act[t, r, k : k + GW] = (up * cdf).astype(BF)
        bell = 0.3989422804014327 * jnp.exp(-0.5 * up * up)
        slope[t, r, k : k + GW] = (cdf + up * bell).astype(BF)


def feed_down(i, t, act, w, mid):
    r = chunk_rows(i)
    mid[r] += dot_nt(act[t, r], w[2, t]) + dot_nt(act[t + 1, r], w[2, t + 1])


def second_norm(i, t, act, w, prm, mid, cot, mine, y_rows, d_ffn, ngrad):
    feed_down(i, t, act, w, mid)

    def piece(p, k):
        normed, factor = norm_rows(mid[p])
        y_rows[pl.ds(pl.multiple_of(k * SUB, SUB), SUB)] = (normed * prm[1:2] + prm[3:4]).astype(BF)
        grad = cot[p].astype(F32) * jnp.where(k < LENGTH // SUB, mine(2 * i), mine(2 * i + 1))
        ngrad[1:2] += jnp.sum(grad * normed, 0, keepdims=True)
        ngrad[3:4] += jnp.sum(grad, 0, keepdims=True)
        back = norm_back(grad * prm[1:2], normed, factor)
        mid[p] = back
        d_ffn[p] = back.astype(BF)

    pieces(i, piece)


def back_up(t, i, d_ffn, w, slope):
    r = chunk_rows(i)
    slope[t, r] = (dot_nn(d_ffn[r], w[2, t]) * slope[t, r].astype(F32)).astype(BF)


def back_first_norm(i, d_up, w, prm, mid, n1, s1, d_attn, ngrad):
    r = chunk_rows(i)
    grad = dot_nt(d_up[0, r], w[1, 0])
    for t in range(1, GROUPS):
        grad += dot_nt(d_up[t, r], w[1, t])
    mid[r] += grad

    def piece(p, k):
        grad = mid[p]
        normed = n1[p].astype(F32)
        ngrad[0:1] += jnp.sum(grad * normed, 0, keepdims=True)
        ngrad[2:3] += jnp.sum(grad, 0, keepdims=True)
        back = norm_back(grad * prm[0:1], normed, s1[p, 0:1])
        mid[p] = back
        d_attn[p] = back.astype(BF)

    pieces(i, piece)


def back_heads(t, d_attn, wo, d_heads):
    d_heads[t, :, :GW] = dot_nn(d_attn[...], wo[t]).astype(BF)


def back_attend(t, chains, proj, probs, d_heads):
    rows = [chunk_rows(s, LENGTH) for s in chains]
    parts = [
        (proj[t, r, :GW], proj[t, r, GW : 2 * GW], proj[t, r, 2 * GW :], d_heads[t, r, :GW], probs[t, s, :, :WIDE])
        for s, r in zip(chains, rows)
    ]
    results = []
    for query, key, value, grad, low in parts:
        grad = stack_heads(grad)
        p = low.astype(F32)
        d_probs = dot_nt(value, grad)
        d_scores = (p * (d_probs - jnp.sum(d_probs * p, 0, keepdims=True))).astype(BF)
        d_query = merge_heads(dot_tn(d_scores, key)) * 0.125
        d_key = dot_nn(d_scores, stack_heads(query * jnp.asarray(0.125, BF)))
        results.append((d_query.astype(BF), d_key.astype(BF), dot_nn(low, grad).astype(BF)))
    for r, (d_query, d_key, d_value) in zip(rows, results):
        proj[t, r, :GW] = d_query
        proj[t, r, GW : 2 * GW] = d_key
        proj[t, r, 2 * GW :] = d_value


def grad_qkv_out(t, x, d_proj, d_attn, hout, store):
    low = lanes((D, 128)) < HEAD_DIM
    outs = dot_tn(d_attn[...], hout[t])
    places = (pltpu.roll(outs[:, :128], 64, 1), outs[:, :128], pltpu.roll(outs[:, 128:], 64, 1))
    for i in range(3):
        part = dot_tn(x[...], d_proj[t, :, GW * i : GW * (i + 1)])
        store(GW * i, part[:, :128])
        store(GW * i + 128, jnp.where(low, part[:, 128:], places[i]))


def back_input(i, d_proj, w, mid, out):
    r = chunk_rows(i)
    grad = mid[r]
    for t in range(GROUPS):
        grad += dot_nt(d_proj[t, r], w[0, t])
    out(r, grad)


MIXED = (2, 1)
GATHER_FIRST = (
    ('X', 1, 0), ('L', 0, 0), ('y', 0), ('X', 0, 1), ('L', 0, 1),
    ('z', 0, 0, 1), ('z', 0, 1, 1), ('y', 1), ('L', 1, 1), ('x', 0, 1, 0),
    ('X', 0, 0), ('z', 0, 1, 2), ('x', 1, 0, 0), ('z', 0, 0, 2), ('x', 0, 1, 1),
    ('x', 0, 0, 1), ('L', 1, 0), ('z', 0, 1, 3), ('z', 0, 0, 3), ('x', 0, 0, 0),
    ('y', 2), ('X', 2, 1), ('x', 0, 1, 3), ('z', 1, 1, 1), ('x', 0, 1, 2),
    ('z', 1, 0, 1), ('x', 0, 0, 2), ('L', 2, 0), ('x', 0, 0, 3), ('z', 1, 1, 2),
    ('X', 1, 1),
)
GATHER_QKV = {
    7: (('z', 1, 0, 2),),
    10: (('x', 2, 1, 0),),
}
GATHER_ATTEND = {
    1: (('L', 2, 1), ('z', 1, 1, 3), ('z', 1, 0, 3), ('z', 2, 0, 1),),
    2: (('X', 2, 0),),
    5: (('x', 1, 1, 1), ('x', 1, 1, 2),),
    6: (('z', 2, 1, 1), ('x', 1, 1, 0),),
    7: (('z', 2, 0, 2), ('x', 1, 0, 1),),
}
GATHER_NORM = {
    0: (('x', 1, 0, 2), ('x', 1, 1, 3), ('x', 1, 0, 3),),
}
GATHER_UP = {
    3: (('z', 2, 1, 2),),
    4: (('z', 2, 0, 3),),
    7: (('x', 2, 0, 1),),
    9: (('x', 2, 0, 0),),
    10: (('x', 2, 0, 3), ('x', 2, 0, 2),),
    11: (('z', 2, 1, 3),),
}


def remote(src, dst, s_sem, r_sem, who):
    return pltpu.make_async_remote_copy(
        src_ref=src, dst_ref=dst, send_sem=s_sem, recv_sem=r_sem, device_id=who, device_id_type=MESH
    )


def arrived(ref, sem):
    remote(ref, ref, sem, sem, {"c": 1 - lax.axis_index("c")}).wait_recv()


def has_left(ref, sem):
    remote(ref, ref, sem, sem, {"c": 1 - lax.axis_index("c")}).wait_send()


def step_kernel(nz, rows,
                tags, lens, x_in, cot, qkv, wout, up, dn, gain, bias,
                y_out, g_out, qo_out, up_out, dn_out, n_out, y_back, g_back, r_c,
                w, x, proj, probs, hout, wo, mid, n1, s1, mid_low, act, slope, d_ffn, gown, r_xz, oth, v_qkv, v_out, far,
                n_all, prm, ngrad, n_c, n_x, n_z,
                load_s, io_s, stage_s, out_s,
                ys_s, ys_r, zs_s, zs_r, zm_s, zm_r, xs_s, xs_r, cs_s, cs_r, ex_s, ex_r, na_s, na_r,
                c_s, c_r, cp_s, cp_r, x_s, x_r, z_s, z_r, y_s, y_r, e_s, e_r, ng_s, ng_r):
    z, xc, y, c = place()
    core, across, other_x = {"c": 1 - c}, {"y": 1 - y}, {"x": 1 - xc}
    diagonal = {"y": 1 - y, "c": 1 - c}
    mats = (None, up, dn)
    lender = y != c
    home = (2 * y + c) * OWN
    away = (2 - y) * OWN + c * EXTRA

    def z_of(dz):
        return lax.rem(z + dz, nz)

    def chain(s):
        return jnp.where(s < OWN, home + s, away + s - OWN)

    def length_of(s):
        return lens[chain(s)]

    def mine(s):
        return jnp.where(tags[chain(s)] == y, 1.0, 0.0)

    def part(zz, xx):
        return pl.ds(pl.multiple_of((zz * 2 + xx) * rows, rows), rows)

    def group(g):
        return 2 * lax.rem(y + g, 2) + c

    def block(m, g, zz, xx):
        return w.at[m, group(g), part(zz, xx)]

    loads = [pltpu.make_async_copy(mats[m].at[y], block(m, 0, z, xc), load_s.at[m]) for m in range(1, 3)]
    loads += [
        pltpu.make_async_copy(x_in, x.at[pl.ds(0, OWN_ROWS)], load_s.at[3]),
        pltpu.make_async_copy(cot, d_ffn.at[pl.ds(0, OWN_ROWS)], load_s.at[4]),
        pltpu.make_async_copy(qkv, v_qkv, load_s.at[0]),
        pltpu.make_async_copy(wout, v_out, load_s.at[5]),
    ]
    for cp in loads:
        cp.start()
    barrier, friends = greet(nz, z, xc, y, c)
    me = ((z * 2 + xc) * 2 + y) * 2 + c
    cols = gain.shape[2]
    n_all[me] = jnp.zeros((8, 128), F32)
    for i in range(2):
        n_all[me, 2 * i : 2 * i + 2, :cols] = gain[i]
        n_all[me, 4 + 2 * i : 6 + 2 * i, :cols] = bias[i]
    ngrad[...] = jnp.zeros_like(ngrad)
    for cp in loads[4:]:
        cp.wait()

    def packed(k):
        tail = v_out[k]
        cols = []
        for i in range(3):
            cols += [v_qkv[k, i], tail[:, HEAD_DIM * i : HEAD_DIM * (i + 1)]]
        return jnp.concatenate(cols, 1)

    w[0, group(0), part(z, xc)] = packed(y)
    far[...] = packed(1 - y)
    pl.semaphore_wait(barrier, friends)

    def given(m):
        return mats[m].at[1 - y] if m else far

    def lend(arr, out, i, act_on):
        @pl.when(lender)
        def _():
            for j, (who, p) in enumerate(((across, c), (diagonal, 1 - c))):
                src = arr.at[pl.ds(pl.multiple_of(p * EXT_ROWS, EXT_ROWS), EXT_ROWS)]
                act_on(remote(src, out.at[pl.ds(OWN_ROWS, EXT_ROWS)], ex_s.at[i, j], ex_r.at[i], who))

    for m in range(3):
        remote(given(m), w.at[m, group(0), part(z, xc)], ys_s.at[m], ys_r.at[m], across).start()
    lend(x_in, x, 0, lambda cp: cp.start())
    lend(cot, d_ffn, 1, lambda cp: cp.start())

    def inside(zz):
        return jnp.logical_and(zz >= 0, zz < nz)

    def start(cp):
        cp.start()

    def recv(cp):
        cp.wait_recv()

    def hop(m, g, d, j, ref, act_on, col=0):
        to = z + 1 - 2 * d
        sems = (zm_s.at[d, j], zm_r.at[d, j]) if col else (zs_s.at[m, g, d, j], zs_r.at[m, g, d, j])

        @pl.when(jnp.logical_and(inside(to), j < nz))
        def _():
            act_on(remote(ref, ref, *sems, {"z": to}))

    def x_copy(m, g, zz):
        ref = block(m, g, zz, xc)
        return remote(ref, ref, xs_s.at[m, g, zz], xs_r.at[m, g, zz], other_x)

    def c_copy(m, g, zz, xx):
        ref = block(m, g, zz, xx)
        return remote(ref, ref, cs_s.at[m, g, zz, xx], cs_r.at[m, g, zz, xx], core)

    def from_y(m):
        arrived(block(m, 1, z, xc), ys_r.at[m])

    def own_z(m, g):
        for d in range(2):
            hop(m, g, d, 1, block(m, g, z, xc), start)

    def own_xc(m, g):
        x_copy(m, g, z).start()
        c_copy(m, g, z, xc).start()

    def z_event(m, g, j):
        mixed = (m, g) == MIXED

        def body(d):
            zz = z - j + 2 * j * d

            @pl.when(inside(zz))
            def _():
                for col in range(2 if mixed else 1):
                    ref = block(m, g, zz, lax.rem(xc + col, 2))
                    arrived(ref, zm_r.at[d, j] if col else zs_r.at[m, g, d, j])
                    hop(m, g, d, j + 1, ref, start, col)
                    if not mixed:
                        x_copy(m, g, zz).start()
                    c_copy(m, g, zz, lax.rem(xc + col, 2)).start()

        loop(2, body)

    def x_event(m, g, j):
        def body(d):
            zz = z - j + 2 * j * d

            @pl.when(inside(zz))
            def _():
                ref = block(m, g, zz, 1 - xc)
                arrived(ref, xs_r.at[m, g, zz])
                if (m, g) == MIXED:
                    for way in range(2):
                        hop(m, g, way, 1, ref, start, 1)
                c_copy(m, g, zz, 1 - xc).start()

        loop(2 if j else 1, body)

    kinds = {"y": from_y, "L": own_z, "X": own_xc, "z": z_event, "x": x_event}

    def gather_steps(plan):
        def run(steps):
            for kind, *args in steps:
                kinds[kind](*args)

        return {k: partial(run, steps) for k, steps in plan.items()}

    def gathered(m, first=0, last=2):
        def body(i):
            g = first + i // (2 * nz)
            t = 2 * lax.rem(y + g, 2) + 1 - c
            zz, xx = (i // 2) % nz, i % 2
            arrived(w.at[m, t, part(zz, xx)], cs_r.at[m, g, zz, xx])

        loop(2 * nz * (last - first), body)

    def gather_sent(i):
        m, g = i // 2, i % 2
        ref = w.at[0, 0, pl.ds(0, rows)]
        mixed = i == 2 * MIXED[0] + MIXED[1]
        for j in range(1, nz):
            for d in range(2):
                @pl.when(inside(z - (1 - 2 * d) * (j - 1)))
                def _():
                    hop(m, g, d, j, ref, lambda cp: cp.wait_send())

                    @pl.when(mixed)
                    def _():
                        hop(m, g, d, j, ref, lambda cp: cp.wait_send(), 1)
        for zz in range(nz):
            @pl.when(jnp.logical_or(jnp.logical_not(mixed), z == zz))
            def _():
                has_left(ref, xs_s.at[m, g, zz])

            for xx in range(2):
                has_left(ref, cs_s.at[m, g, zz, xx])

    def norm_hop(i, act_on):
        if i == 0:
            act_on(remote(n_all.at[me], n_all.at[me], na_s.at[0], na_r.at[0], core))
        elif i == 1:
            ref = n_all.at[pl.ds(me - c, 2)]
            act_on(remote(ref, ref, na_s.at[1], na_r.at[1], across))
        elif i == 2:
            ref = n_all.at[pl.ds(me - c - 2 * y, 4)]
            act_on(remote(ref, ref, na_s.at[2], na_r.at[2], other_x))
        else:
            ref = n_all.at[pl.ds(8 * z, 8)]
            for dz in range(1, nz):
                act_on(remote(ref, ref, na_s.at[2 + dz], na_r.at[2 + dz], {"z": z_of(dz)}))

    for cp in loads[:2]:
        cp.wait()
    norm_hop(0, start)
    for kind, *args in GATHER_FIRST:
        kinds[kind](*args)
        if (kind, *args) == ("z", 0, 0, 1):
            norm_hop(0, recv)
            norm_hop(1, start)
        if (kind, *args) == ("z", 0, 0, 3):
            norm_hop(1, recv)
            norm_hop(2, start)
    norm_hop(2, recv)
    norm_hop(3, start)
    gathered(0)
    loads[2].wait()
    arrived(x.at[pl.ds(OWN_ROWS, EXT_ROWS)], ex_r.at[0])

    def projection(i):
        t, k = i // N_CHUNK, i % N_CHUNK
        r = chunk_rows(k)
        proj[t, r] = dot_nn(x[r], w[0, t]).astype(BF)

        @pl.when(k == N_CHUNK - 1)
        def _():
            out_columns(t, w, wo)

    weave(GROUPS * N_CHUNK, projection, gather_steps(GATHER_QKV))
    per = SLOTS // PAIR

    def attention(i):
        attend(i // per, [(i % per) * PAIR + k for k in range(PAIR)], length_of, proj, probs, hout)

    weave(GROUPS * per, attention, gather_steps(GATHER_ATTEND))
    norm_hop(3, recv)
    lane = lanes((2, D))
    gains, shifts = jnp.zeros((2, D), F32), jnp.zeros((2, D), F32)
    for d in range(8 * nz):
        within = jnp.logical_and(lane >= d * cols, lane < (d + 1) * cols)
        for name in range(2):
            piece = n_all[d, pl.ds(4 * name + 2 * y, 2), :]
            piece = jnp.concatenate([piece, jnp.zeros((2, D - 128), F32)], 1)
            piece = jnp.where(within, pltpu.roll(piece, d * cols, 1) if d else piece, 0.0)
            if name == 0:
                gains += piece
            else:
                shifts += piece
    prm[0:2] = gains
    prm[2:4] = shifts
    weave(
        N_CHUNK,
        lambda i: first_norm(i, x, hout, wo, prm, mid, n1, s1, mid_low),
        gather_steps(GATHER_NORM),
    )
    gathered(1)
    weave(
        GROUPS * N_CHUNK,
        lambda i: feed_up(i // N_CHUNK, i % N_CHUNK, mid_low, w, act, slope),
        gather_steps(GATHER_UP),
    )
    gathered(2, 0, 1)
    first_two = 2 * y
    last_two = 2 - first_two
    loop(N_CHUNK, lambda i: feed_down(i, first_two, act, w, mid))
    gathered(2, 1, 2)
    loads[3].wait()
    arrived(d_ffn.at[pl.ds(OWN_ROWS, EXT_ROWS)], ex_r.at[1])

    def y_stage(i):
        return r_xz.at[i // 2, 0, pl.ds(pl.multiple_of((i % 2) * CHUNK, CHUNK), CHUNK)]

    def give_back(src, dst, i, act_on):
        dst = dst.at[pl.ds(pl.multiple_of(c * EXT_ROWS, EXT_ROWS), EXT_ROWS)]

        @pl.when(c == y)
        def _():
            act_on(remote(src, dst, e_s.at[i], e_r.at[i, c], across))

        @pl.when(c != y)
        def _():
            act_on(remote(src, dst, e_s.at[i], e_r.at[i, c], diagonal))

    def y_copy(i):
        return pltpu.make_async_copy(y_stage(i), y_out.at[pl.ds(i * CHUNK, CHUNK)], io_s.at[i])

    loop(
        N_CHUNK,
        lambda i: second_norm(
            i, last_two, act, w, prm, mid, d_ffn, mine, y_stage(i), d_ffn, ngrad
        ),
    )
    for i in range(2):
        y_copy(i).start()
    give_back(y_stage(2), y_back, 0, start)

    def columns(g, other):
        pair = jnp.where(g == 0, 1 - y, y)
        return 2 * pair + jnp.where(other, 1 - c, c)

    def x_place(m, g, i):
        return r_xz.at[0, m, pl.ds(pl.multiple_of((g * nz + i) * rows, rows), rows)]

    def z_place(m, g, i):
        return r_xz.at[1, m, pl.ds(pl.multiple_of((g * nz + i) * rows, rows), rows)]

    def spare(m, g):
        return gown.at[0, g] if m else act.at[2 * g + c, pl.ds(0, D)]

    def core_send(m, g):
        there = r_c.at[g] if m else spare(0, g)
        return remote(spare(m, g), there, c_s.at[m, g], c_r.at[m, g], core)

    def fetch(g):
        return pltpu.make_async_copy(r_c.at[g], act.at[2 * g + 1 - c, pl.ds(0, D)], stage_s.at[g])

    half = D // 2

    def half_rows(k):
        return pl.ds(pl.multiple_of(half * jnp.where(z < nz // 2, 1 - k, k), half), half)

    def core_half(g, k):
        r = half_rows(k)
        return remote(gown.at[0, g, r], gown.at[1, g, r], cp_s.at[g, k], cp_r.at[g, k], core)

    def core_fetch(g):
        arrived(r_c.at[g], c_r.at[1, g])
        fetch(g).start()

    middle = jnp.logical_and(z > 0, z < nz - 1)

    def target(k):
        down = jnp.where(nz - 1 - k > z, nz - 1 - k, nz - 2 - k)
        up = jnp.where(k < z, k, k + 1)
        return jnp.where(k == nz - 1, z, jnp.where(z < nz // 2, down, up))

    def add_and_cross(m, g, from_core, first, count):
        def add(i):
            p = part(target(first + i % count), lax.rem(xc + 1 + i // count, 2))
            gown[m, g, p] += from_core[p]

        def over(k):
            zz = target(first + k)
            remote(gown.at[m, g, part(zz, 1 - xc)], x_place(m, g, zz), x_s.at[m, g, zz], x_r.at[m, g, zz], other_x).start()

        loop(count + 1, add)
        loop(count, over)
        loop(count - 1, lambda i: add(count + 1 + i))

    def core_add(m, g):
        from_core = act.at[2 * g + 1 - c, pl.ds(0, D)]
        if m == 1:
            fetch(g).wait()
        else:
            arrived(from_core, c_r.at[0, g])
        add_and_cross(m, g, from_core, 0, nz)

    def half_add(g, k):
        core_half(g, k).wait_recv()
        add_and_cross(2, g, gown.at[1, g], k * (nz // 2), nz // 2)

    def sum_event(q):
        m = 2 - q // (2 * nz)
        g = (q // nz) % 2
        k = q % nz
        zz = target(k)
        over = x_place(m, g, zz)
        arrived(over, x_r.at[m, g, zz])
        p = part(zz, xc)
        gown[m, g, p] += over[...]

        beside = jnp.where(z == 0, 1, nz - 2)
        joins = jnp.logical_and(k < 2, jnp.logical_not(middle))
        to = jnp.where(joins, beside, zz)
        slot = jnp.where(joins, jnp.where(k == 0, beside, nz - 1 - z), z)

        @pl.when(jnp.logical_and(k < nz - 1, jnp.logical_or(k == nz - 2, jnp.logical_not(middle))))
        def _():
            remote(gown.at[m, g, p], z_place(m, g, slot), z_s.at[m, g, zz], z_r.at[m, g, slot], {"z": to}).start()

        def relay(k, slot):
            to = target(k)
            q = part(to, xc)
            arrived(z_place(m, g, slot), z_r.at[m, g, slot])
            gown[m, g, q] += z_place(m, g, slot)[...]
            remote(gown.at[m, g, q], z_place(m, g, z), z_s.at[m, g, to], z_r.at[m, g, z], {"z": to}).start()

        early = jnp.where(m == 0, 1, 0)

        @pl.when(jnp.logical_and(k == nz - 2 - early, middle))
        def _():
            relay(0, z)

        @pl.when(jnp.logical_and(k == nz - 1 - early, middle))
        def _():
            relay(1, jnp.where(z == 1, nz - 1, 0))

    outs = (qo_out, up_out, dn_out)

    def out_stage(m, other):
        return mid.at[pl.ds(m * rows + (0 if other else OWN_ROWS), rows)]

    def out_copy(m, other):
        return pltpu.make_async_copy(out_stage(m, other), outs[m].at[1 - y if other else y], out_s.at[m, other])

    def last_send(m):
        return remote(mid_low.at[pl.ds(EXT_ROWS + m * rows, rows)], oth.at[m], y_s.at[m], y_r.at[m], across)

    def finish(m, g):
        total = gown[m, g, part(z, xc)].astype(F32)
        for dz in range(1, nz):
            source = z_of(dz)
            direct = jnp.abs(source - z) <= jnp.where(middle, 1, 2)

            @pl.when(direct)
            def _():
                arrived(z_place(m, g, source), z_r.at[m, g, source])

            total += jnp.where(direct, z_place(m, g, source)[...].astype(F32), 0.0)

        if g == 1:
            out_stage(m, 0)[...] = total
            out_copy(m, 0).start()
        else:
            mid_low[EXT_ROWS + m * rows : EXT_ROWS + (m + 1) * rows] = total.astype(BF)
            last_send(m).start()

    def up_grads(extra):
        def unit(q):
            g, own = q % 2, q // 2
            t = columns(g, own == 0)
            dst = gown.at[own, g]
            for k in range(0, D, GW):
                dst[:, k : k + GW] = dot_tn(mid_low[...], slope[t, :, k : k + GW]).astype(BF)

            @pl.when(own == 0)
            def _():
                core_send(1, g).start()

        weave(4, unit, extra)

    def down_grads(extra):
        def unit(q):
            g, k, own = q // 4, (q // 2) % 2, q % 2
            t = columns(g, own == 0)
            r = half_rows(k)
            dst = gown.at[2 * own, g, r]
            for j in range(0, D, GW):
                dst[:, j : j + GW] = dot_tn(d_ffn[:, r], act[t, :, j : j + GW]).astype(BF)

            @pl.when(own == 0)
            def _():
                core_half(g, k).start()

        weave(8, unit, extra)

    def then(*steps):
        def run():
            for f, *args in steps:
                f(*args)

        return run

    def core_over(m):
        for g in range(2):
            if m == 2:
                for k in range(2):
                    core_half(g, k).wait_send()
            else:
                core_send(m, g).wait_send()

    down_grads(
        {
            2: then((half_add, 0, 0)),
            3: then((half_add, 0, 1)),
            5: then((half_add, 1, 0)),
            7: then((half_add, 1, 1), (core_over, 2)),
        }
    )

    def up_back(i):
        back_up(i // N_CHUNK, i % N_CHUNK, d_ffn, w, slope)

    weave(GROUPS * N_CHUNK, up_back, {0: then((sum_event, 0)), 5: then((sum_event, 1)), 10: then((sum_event, 2))})
    for i in range(2):
        y_copy(i).wait()
    has_left(y_stage(2), e_s.at[0])
    up_grads({1: then((sum_event, 3)), 3: then((sum_event, 4))})
    for g in range(2):
        core_fetch(g)
    weave(
        N_CHUNK,
        lambda i: back_first_norm(i, slope, w, prm, mid, n1, s1, d_ffn, ngrad),
        {
            0: then((core_add, 1, 0), (core_add, 1, 1), (core_over, 1)),
            1: then((sum_event, 5)),
            2: then((sum_event, 6)),
        },
    )

    def send_norms(i, act_on):
        if i == 0:
            act_on(remote(ngrad, n_c, ng_s.at[0], ng_r.at[0], core))
        elif i == 1:
            act_on(remote(n_c, n_x, ng_s.at[1], ng_r.at[1], other_x))
        elif i == 2:
            for dz in range(1, nz):
                act_on(remote(n_x, n_z.at[dz], ng_s.at[1 + dz], ng_r.at[1 + dz], {"z": z_of(dz)}))
        else:
            act_on(remote(n_out.at[y], n_out.at[y], ng_s.at[nz + 1], ng_r.at[nz + 1], across))

    send_norms(0, start)
    loop(GROUPS, lambda t: back_heads(t, d_ffn, wo, slope))
    sum_event(7)
    send_norms(0, recv)
    send_norms(0, lambda cp: cp.wait_send())
    n_c[...] += ngrad[...]
    send_norms(1, start)

    def attention_back(i):
        back_attend(i // per, [(i % per) * PAIR + k for k in range(PAIR)], proj, probs, slope)

        @pl.when(i % 2 == 1)
        def _():
            sum_event(8 + i // 2)

    loop(GROUPS * per, attention_back)
    seen = 8 + GROUPS * per // 2

    def qkv_grads(q):
        g, own = q // 2, q % 2

        def store(col, value):
            value = value.astype(BF)

            @pl.when(own == 0)
            def _():
                spare(0, g)[:, col : col + 128] = value

            @pl.when(own == 1)
            def _():
                gown[0, g, :, col : col + 128] = value

        grad_qkv_out(columns(g, own == 0), x, proj, d_ffn, hout, store)

        @pl.when(own == 0)
        def _():
            core_send(0, g).start()

    weave(
        4,
        qkv_grads,
        {
            0: then((sum_event, seen)),
            1: then((core_add, 0, 0), (sum_event, seen + 1)),
            3: then((core_add, 0, 1), (sum_event, seen + 2)),
        },
    )
    seen += 3

    def inputs_back(i):
        k = lax.rem(i + N_CHUNK - 1, N_CHUNK)

        def keep(r, grad):
            mid[r] = grad

            @pl.when(i == 0)
            def _():
                mid_low[:EXT_ROWS] = grad.astype(BF)

        back_input(k, proj, w, mid, keep)

        @pl.when(i == 0)
        def _():
            give_back(mid_low.at[pl.ds(0, EXT_ROWS)], g_back, 1, start)

    weave(N_CHUNK, inputs_back, {1: then((sum_event, seen))})
    seen += 1
    after = 4 * nz
    if seen < after:
        loop(after - seen, lambda q: sum_event(seen + q))
    for g in range(2):
        finish(2, g)
    loop(2, lambda q: sum_event(after + q))

    def sums_sent(i):
        m, g = i // 2, i % 2
        for zz in range(nz):
            @pl.when(z != zz)
            def _():
                has_left(x_place(0, 0, 0), z_s.at[m, g, zz])

            has_left(x_place(0, 0, 0), x_s.at[m, g, zz])

    loop(6, gather_sent)

    trips = [
        pltpu.make_async_copy(g_back, proj.at[0, pl.ds(0, OWN_ROWS)], io_s.at[0]),
        pltpu.make_async_copy(y_out, proj.at[1, pl.ds(0, OWN_ROWS)], io_s.at[1]),
        pltpu.make_async_copy(y_back, proj.at[2, pl.ds(0, OWN_ROWS)], io_s.at[2]),
    ]
    y_again = pltpu.make_async_copy(proj.at[1, pl.ds(0, OWN_ROWS)], y_out, io_s.at[1])
    g_copy = pltpu.make_async_copy(mid.at[pl.ds(0, OWN_ROWS)], g_out, io_s.at[3])

    @pl.when(lender)
    def _():
        for i, dst in enumerate((y_back, g_back)):
            for j in range(2):
                arrived(dst.at[pl.ds(j * EXT_ROWS, EXT_ROWS)], e_r.at[i, j])
        for cp in trips:
            cp.start()
        for cp in trips:
            cp.wait()

        def merge(s):
            r = chunk_rows(s, LENGTH)
            keep = jnp.zeros((LENGTH, D), F32) + mine(s) > 0.5
            mid[r] = jnp.where(keep, mid[r], proj[0, r].astype(F32))
            proj[1, r] = jnp.where(keep, proj[1, r].astype(F32), proj[2, r].astype(F32)).astype(BF)

        loop(OWN, merge)
        y_again.start()

    g_copy.start()
    loop(nz - 2, lambda q: sum_event(after + 2 + q))
    send_norms(1, recv)
    send_norms(1, lambda cp: cp.wait_send())
    n_x[...] += n_c[...]
    send_norms(2, start)
    for g in range(2):
        finish(1, g)
    loop(nz - 1, lambda q: sum_event(after + nz + q))
    g_copy.wait()

    def widen(m):
        arrived(oth.at[m], y_r.at[m])
        out_stage(m, 1)[...] = oth[m].astype(F32)
        out_copy(m, 1).start()

    widen(2)
    widen(1)
    loop(4, lambda i: sums_sent(2 + i))
    total = n_x[...]
    for dz in range(1, nz):
        arrived(n_z.at[dz], ng_r.at[1 + dz])
        total += n_z[dz]
    n_out[y] = total
    send_norms(3, start)
    finish(0, 0)
    sum_event(after + 2 * nz - 1)
    widen(0)
    finish(0, 1)

    loop(2, sums_sent)
    for g in range(2):
        core_send(0, g).wait_send()
    for m in range(3):
        has_left(given(m), ys_s.at[m])
        for other in range(2):
            out_copy(m, other).wait()
        last_send(m).wait_send()
    lend(x_in, x, 0, lambda cp: cp.wait_send())
    lend(cot, d_ffn, 1, lambda cp: cp.wait_send())
    for i in range(4):
        norm_hop(i, lambda cp: cp.wait_send())
    send_norms(2, lambda cp: cp.wait_send())
    send_norms(3, lambda cp: cp.wait())
    has_left(mid_low.at[pl.ds(0, EXT_ROWS)], e_s.at[1])

    @pl.when(lender)
    def _():
        y_again.wait()


def run_step(nz, tags, lens, x_in, cot, qkv, wout, up, dn, gain, bias):
    rows = up.shape[1]
    V = pl.BlockSpec(memory_space=pltpu.VMEM)
    S = pl.BlockSpec(memory_space=pltpu.SMEM)
    sem = pltpu.SemaphoreType.DMA
    out = jax.ShapeDtypeStruct
    return pl.pallas_call(
        partial(step_kernel, nz, rows),
        out_shape=(
            out((OWN_ROWS, D), BF),
            out((OWN_ROWS, D), F32),
            out((2, rows, D), F32),
            out((2, rows, D), F32),
            out((2, rows, D), F32),
            out((2, 8, D), F32),
            out((OWN_ROWS, D), BF),
            out((OWN_ROWS, D), BF),
            out((2, D, D), BF),
        ),
        in_specs=[S, S] + [ANY] * 6 + [V, V],
        out_specs=(ANY, ANY, ANY, ANY, ANY, V, ANY, ANY, ANY),
        scratch_shapes=[
            pltpu.VMEM((3, GROUPS, D, D), BF),
            pltpu.VMEM((ROWS, D), BF),
            pltpu.VMEM((GROUPS, ROWS, D), BF),
            pltpu.VMEM((GROUPS, SLOTS, LENGTH, 512), BF),
            pltpu.VMEM((GROUPS, ROWS, GW), BF),
            pltpu.VMEM((GROUPS, D, GW), BF),
            pltpu.VMEM((ROWS, D), F32),
            pltpu.VMEM((ROWS, D), BF),
            pltpu.VMEM((ROWS, 128), F32),
            pltpu.VMEM((ROWS, D), BF),
            pltpu.VMEM((GROUPS, ROWS, D), BF),
            pltpu.VMEM((GROUPS, ROWS, D), BF),
            pltpu.VMEM((ROWS, D), BF),
            pltpu.VMEM((3, 2, D, D), BF),
            pltpu.VMEM((2, 3, 2 * nz * rows, D), BF),
            pltpu.VMEM((3, rows, D), BF),
            pltpu.VMEM(qkv.shape, BF),
            pltpu.VMEM(wout.shape, BF),
            pltpu.VMEM((rows, D), BF),
            pltpu.VMEM((8 * nz, 8, 128), F32),
            pltpu.VMEM((8, D), F32),
            pltpu.VMEM((8, D), F32),
            pltpu.VMEM((8, D), F32),
            pltpu.VMEM((8, D), F32),
            pltpu.VMEM((nz, 8, D), F32),
            sem((6,)), sem((4,)), sem((2,)), sem((3, 2)),
            sem((3,)), sem((3,)),
            sem((3, 2, 2, nz)), sem((3, 2, 2, nz)),
            sem((2, nz)), sem((2, nz)),
            sem((3, 2, nz)), sem((3, 2, nz)),
            sem((3, 2, nz, 2)), sem((3, 2, nz, 2)),
            sem((2, 2)), sem((2,)),
            sem((nz + 2,)), sem((nz + 2,)),
            sem((3, 2)), sem((3, 2)),
            sem((2, 2)), sem((2, 2)),
            sem((3, 2, nz)), sem((3, 2, nz)),
            sem((3, 2, nz)), sem((3, 2, nz)),
            sem((3,)), sem((3,)),
            sem((2,)), sem((2, 2)),
            sem((nz + 2,)), sem((nz + 2,)),
        ],
        compiler_params=pltpu.CompilerParams(
            collective_id=0, has_side_effects=True, vmem_limit_bytes=67043328
        ),
        name="layer_step",
    )(tags, lens, x_in, cot, qkv, wout, up, dn, gain, bias)


def deliver_kernel(cols, y_in, g_in, qo, up_in, dn_in, sums,
                   y_out, g_out, qkv_out, wout_out, up_out, dn_out, gain_out, bias_out,
                   v_y, v_g, v_qo, v_up, v_dn, v_qkv, v_out, in_s, out_s):
    through = [(up_in, v_up, up_out), (dn_in, v_dn, dn_out)]
    for k in range(OWN):
        r = pl.ds(k * LENGTH, LENGTH)
        through.append((g_in.at[r], v_g.at[r], g_out.at[r]))
    for k in range(2):
        r = pl.ds(k * CHUNK, CHUNK)
        through.append((y_in.at[r], v_y.at[r], y_out.at[r]))
    n = len(through)
    first = pltpu.make_async_copy(qo, v_qo, in_s.at[n])
    first.start()
    loads, stores = [], []
    for i, (src, via, dst) in enumerate(through):
        loads.append(pltpu.make_async_copy(src, via, in_s.at[i]))
        stores.append(pltpu.make_async_copy(via, dst, out_s.at[i]))
        loads[-1].start()
    z, x, y, c = place()
    me = ((z * 2 + x) * 2 + y) * 2 + c
    for k in range(2):
        turned = pltpu.roll(sums[k], lax.rem(D - me * cols, D), 1)
        gain_out[k] = turned[0:2, :cols]
        bias_out[k] = turned[2:4, :cols]
    first.wait()

    def unpack(k):
        tail = []
        for i in range(3):
            v_qkv[k, i] = v_qo[k, :, GW * i : GW * i + GW - HEAD_DIM]
            tail.append(v_qo[k, :, GW * (i + 1) - HEAD_DIM : GW * (i + 1)])
        v_out[k] = jnp.concatenate(tail, 1)
        for j, (src, dst) in enumerate(((v_qkv, qkv_out), (v_out, wout_out))):
            stores.append(pltpu.make_async_copy(src.at[k], dst.at[k], out_s.at[n + 2 * k + j]))
            stores[-1].start()

    for i in range(n):
        loads[i].wait()
        stores[i].start()
        if i in (1, 3):
            unpack(i // 2)
    for cp in stores:
        cp.wait()


def deliver(cols, y_in, g_in, qo, up_in, dn_in, sums):
    rows = qo.shape[1]
    V = pl.BlockSpec(memory_space=pltpu.VMEM)
    sem = pltpu.SemaphoreType.DMA
    out = jax.ShapeDtypeStruct
    width = GW - HEAD_DIM
    shapes = [((2, 3, rows, width), F32), ((2, rows, width), F32)]
    whole = [(y_in.shape, BF), (g_in.shape, F32), (qo.shape, F32), (qo.shape, F32), (qo.shape, F32)]
    return pl.pallas_call(
        partial(deliver_kernel, cols),
        out_shape=tuple(
            out(*p) for p in whole[:2] + shapes + whole[3:] + [((2, 2, cols), F32)] * 2
        ),
        in_specs=[ANY] * 5 + [V],
        out_specs=(ANY,) * 6 + (V, V),
        scratch_shapes=[pltpu.VMEM(*p) for p in whole + shapes] + [sem((9,)), sem((12,))],
        name="deliver",
    )(y_in, g_in, qo, up_in, dn_in, sums)


def split_local(nz, x_in, tags, lengths, w_qkv, w_out, w_up, w_down, norm_gain, norm_bias, cotangent):
    cols = norm_gain.shape[2]
    y_out, x_grad, qo_grad, up_grad, down_grad, n_sum, _, _, _ = run_step(
        nz, tags, lengths, x_in, cotangent, w_qkv.transpose(0, 2, 1, 3), w_out, w_up, w_down, norm_gain, norm_bias
    )
    y_out, x_grad, qkv, out, up, down, gain, bias = deliver(
        cols, y_out, x_grad, qo_grad, up_grad, down_grad, n_sum
    )
    return y_out, x_grad, qkv.transpose(0, 2, 1, 3), out, up, down, gain, bias


def typed_map(operand, stacked, chain_kinds, pattern):

    def single(element):
        weight = lax.dynamic_index_in_dim(stacked, element[1], 0, keepdims=False)
        return jnp.einsum(pattern, element[0], weight, preferred_element_type=jnp.float32)

    return lax.map(single, (operand, chain_kinds))


def typed_grads(running, operand, partner, chain_kinds, pattern):

    def single(carry, element):
        product_term = jnp.einsum(
            pattern, element[0], element[1], preferred_element_type=jnp.float32
        )
        previous = lax.dynamic_index_in_dim(carry, element[2], 0, keepdims=False)
        return (
            lax.dynamic_update_index_in_dim(carry, previous + product_term, element[2], 0),
            None,
        )

    return lax.scan(single, running, (operand, partner, chain_kinds))[0]


def row_terms(operand, stacked, chain_kinds, pattern, row_count):
    result = typed_map(operand, stacked, chain_kinds, pattern)
    return result.reshape(row_count, result.shape[-1])


def old_norm_forward(values, gain_rows, shift_rows):
    center = values - jnp.mean(values, -1, keepdims=True)
    factor = lax.rsqrt(jnp.mean(center * center, -1, keepdims=True) + EPS)
    normed = center * factor
    return (normed * gain_rows + shift_rows, normed, factor)


def old_norm_backward(grad_out, normed, factor, gain_rows):
    scaled = grad_out * gain_rows
    mean_plain = jnp.mean(scaled, -1, keepdims=True)
    mean_normed = jnp.mean(scaled * normed, -1, keepdims=True)
    return factor * (scaled - mean_plain - normed * mean_normed)


def type_sums(onehot, values):
    return jnp.dot(onehot.T, values, precision=HIGH, preferred_element_type=jnp.float32)


def general_local(x_in, tags, lengths, w_qkv, w_out, w_up, w_down, norm_gain, norm_bias, cotangent):
    tp_count = lax.axis_size("tensor")
    tp_index = lax.axis_index("tensor")
    local_rows = CHAINS_PART * LENGTH
    batch_chains = tp_count * CHAINS_PART
    head_cols = w_qkv.shape[3]
    local_heads = head_cols // HEAD_DIM
    tag_grid = tags.reshape(tp_count, MICRO, CHAINS_PART)
    len_grid = lengths.reshape(tp_count, MICRO, CHAINS_PART)
    own_tags = lax.dynamic_index_in_dim(tag_grid, tp_index, 0, keepdims=False)
    gains, shifts = (
        lax.all_gather(norm_gain, ("dp", "tensor"), axis=2, tiled=True),
        lax.all_gather(norm_bias, ("dp", "tensor"), axis=2, tiled=True),
    )
    grad_full = (
        jnp.zeros((2, D, 3, head_cols), jnp.float32),
        jnp.zeros((2, D, head_cols), jnp.float32),
        jnp.zeros((2, D, w_up.shape[2]), jnp.float32),
        jnp.zeros((2, D, w_down.shape[2]), jnp.float32),
    )
    shards = (
        jnp.zeros(w_qkv.shape, jnp.float32),
        jnp.zeros(w_out.shape, jnp.float32),
        jnp.zeros(w_up.shape, jnp.float32),
        jnp.zeros(w_down.shape, jnp.float32),
    )
    gain_acc = jnp.zeros((2, 2, D), jnp.float32)
    shift_acc = jnp.zeros((2, 2, D), jnp.float32)
    outputs = []
    input_grads = []
    for micro_index in range(MICRO):
        held = (
            lax.all_gather(w_qkv, "dp", axis=1, tiled=True),
            lax.all_gather(w_out, "dp", axis=1, tiled=True),
            lax.all_gather(w_up, "dp", axis=1, tiled=True),
            lax.all_gather(w_down, "dp", axis=1, tiled=True),
        )
        qkv_w, out_w, up_w, down_w = held
        chain_kinds = tag_grid[:, micro_index].reshape(batch_chains)
        chain_lens = len_grid[:, micro_index].reshape(batch_chains)
        own_rows = x_in[micro_index * local_rows : (micro_index + 1) * local_rows]
        kinds_rows = jnp.repeat(own_tags[micro_index], LENGTH)
        heavy_rows = (kinds_rows == 0)[:, None]
        onehot = (kinds_rows[:, None] == jnp.arange(2)[None, :]).astype(jnp.float32)
        gain_mid = jnp.where(heavy_rows, gains[0, 0], gains[1, 0])
        shift_mid = jnp.where(heavy_rows, shifts[0, 0], shifts[1, 0])
        gain_end = jnp.where(heavy_rows, gains[0, 1], gains[1, 1])
        shift_end = jnp.where(heavy_rows, shifts[0, 1], shifts[1, 1])
        gathered = lax.all_gather(own_rows, "tensor", axis=0, tiled=True).reshape(
            batch_chains, LENGTH, D
        )
        projected = typed_map(gathered, qkv_w, chain_kinds, "ld,dkh->lkh").astype(jnp.bfloat16)
        query = projected[:, :, 0].reshape(batch_chains, LENGTH, local_heads, HEAD_DIM)
        keys_low = projected[:, :, 1].reshape(batch_chains, LENGTH, local_heads, HEAD_DIM)
        values_low = projected[:, :, 2].reshape(batch_chains, LENGTH, local_heads, HEAD_DIM)
        valid = (
            lax.broadcasted_iota(jnp.int32, (batch_chains, 1, 1, LENGTH), 3)
            < chain_lens[:, None, None, None]
        )
        scores = (
            jnp.einsum("cqhe,ckhe->chqk", query, keys_low, preferred_element_type=jnp.float32)
            * 0.125
        )
        scores = jnp.where(valid, scores, NEG)
        highest = jnp.max(scores, -1, keepdims=True)
        expo = jnp.exp(scores - highest)
        totals = jnp.sum(expo, -1, keepdims=True)
        probs = expo / totals
        log_total = highest + jnp.log(totals)
        heads_low = jnp.einsum(
            "chqk,ckhe->cqhe",
            probs.astype(jnp.bfloat16),
            values_low,
            preferred_element_type=jnp.float32,
        ).astype(jnp.bfloat16)
        heads_low = heads_low.reshape(batch_chains, LENGTH, head_cols)
        attn_sum = lax.psum_scatter(
            row_terms(
                heads_low, out_w, chain_kinds, "lh,dh->ld", lax.axis_size("tensor") * local_rows
            ).astype(jnp.bfloat16),
            "tensor",
            scatter_dimension=0,
            tiled=True,
        ).astype(jnp.float32)
        mid, normed_mid, factor_mid = old_norm_forward(
            own_rows.astype(jnp.float32) + attn_sum, gain_mid, shift_mid
        )
        mid_all = lax.all_gather(mid.astype(jnp.bfloat16), "tensor", axis=0, tiled=True).reshape(
            batch_chains, LENGTH, D
        )
        up_value = typed_map(mid_all, up_w, chain_kinds, "ld,df->lf")
        act_low = jax.nn.gelu(up_value, approximate=False).astype(jnp.bfloat16)
        ffn_sum = lax.psum_scatter(
            row_terms(
                act_low, down_w, chain_kinds, "lf,df->ld", lax.axis_size("tensor") * local_rows
            ).astype(jnp.bfloat16),
            "tensor",
            scatter_dimension=0,
            tiled=True,
        ).astype(jnp.float32)
        final, normed_end, factor_end = old_norm_forward(ffn_sum + mid, gain_end, shift_end)
        outputs.append(final.astype(jnp.bfloat16))
        base = grad_full
        grad_final = cotangent[micro_index * local_rows : (micro_index + 1) * local_rows].astype(
            jnp.float32
        )
        gain_acc = gain_acc.at[:, 1].add(type_sums(onehot, grad_final * normed_end))
        shift_acc = shift_acc.at[:, 1].add(type_sums(onehot, grad_final))
        grad_resid2 = old_norm_backward(grad_final, normed_end, factor_end, gain_end)
        grad_ffn = lax.all_gather(
            grad_resid2.astype(jnp.bfloat16), "tensor", axis=0, tiled=True
        ).reshape(batch_chains, LENGTH, D)
        grad_act = typed_map(grad_ffn, down_w, chain_kinds, "ld,df->lf")
        unused_value, gelu_back = jax.vjp(partial(jax.nn.gelu, approximate=False), up_value)
        grad_up = gelu_back(grad_act)[0].astype(jnp.bfloat16)
        down_acc = typed_grads(base[3], grad_ffn, act_low, chain_kinds, "ld,lf->df")
        up_acc = typed_grads(base[2], mid_all, grad_up, chain_kinds, "ld,lf->df")
        grad_mid = grad_resid2 + lax.psum_scatter(
            row_terms(
                grad_up, up_w, chain_kinds, "lf,df->ld", lax.axis_size("tensor") * local_rows
            ).astype(jnp.bfloat16),
            "tensor",
            scatter_dimension=0,
            tiled=True,
        ).astype(jnp.float32)
        gain_acc = gain_acc.at[:, 0].add(type_sums(onehot, grad_mid * normed_mid))
        shift_acc = shift_acc.at[:, 0].add(type_sums(onehot, grad_mid))
        grad_resid1 = old_norm_backward(grad_mid, normed_mid, factor_mid, gain_mid)
        grad_attn = lax.all_gather(
            grad_resid1.astype(jnp.bfloat16), "tensor", axis=0, tiled=True
        ).reshape(batch_chains, LENGTH, D)
        grad_heads = typed_map(grad_attn, out_w, chain_kinds, "ld,dh->lh").astype(jnp.bfloat16)
        out_acc = typed_grads(base[1], grad_attn, heads_low, chain_kinds, "ld,lh->dh")
        grad_heads = grad_heads.reshape(batch_chains, LENGTH, local_heads, HEAD_DIM)
        again = (
            jnp.einsum("cqhe,ckhe->chqk", query, keys_low, preferred_element_type=jnp.float32)
            * 0.125
        )
        probs_again = jnp.exp(jnp.where(valid, again, NEG) - log_total)
        grad_probs = jnp.einsum(
            "cqhe,ckhe->chqk", grad_heads, values_low, preferred_element_type=jnp.float32
        )
        inner = jnp.sum(grad_probs * probs_again, -1, keepdims=True)
        grad_scores = (probs_again * (grad_probs - inner)).astype(jnp.bfloat16)
        grad_query = (
            jnp.einsum("chqk,ckhe->cqhe", grad_scores, keys_low, preferred_element_type=jnp.float32)
            * 0.125
        ).astype(jnp.bfloat16)
        grad_keys = (
            jnp.einsum("chqk,cqhe->ckhe", grad_scores, query, preferred_element_type=jnp.float32)
            * 0.125
        ).astype(jnp.bfloat16)
        grad_values = jnp.einsum(
            "chqk,cqhe->ckhe",
            probs_again.astype(jnp.bfloat16),
            grad_heads,
            preferred_element_type=jnp.float32,
        ).astype(jnp.bfloat16)
        grad_proj = jnp.stack([grad_query, grad_keys, grad_values], 2).reshape(
            batch_chains, LENGTH, 3, head_cols
        )
        qkv_acc = typed_grads(base[0], gathered, grad_proj, chain_kinds, "ld,lkh->dkh")
        grad_input = grad_resid1 + lax.psum_scatter(
            row_terms(
                grad_proj, qkv_w, chain_kinds, "lkh,dkh->ld", lax.axis_size("tensor") * local_rows
            ).astype(jnp.bfloat16),
            "tensor",
            scatter_dimension=0,
            tiled=True,
        ).astype(jnp.float32)
        input_grads.append(grad_input)
        updated = (qkv_acc, out_acc, up_acc, down_acc)
        grad_full = updated
    shards = (
        lax.psum_scatter(grad_full[0], "dp", scatter_dimension=1, tiled=True),
        lax.psum_scatter(grad_full[1], "dp", scatter_dimension=1, tiled=True),
        lax.psum_scatter(grad_full[2], "dp", scatter_dimension=1, tiled=True),
        lax.psum_scatter(grad_full[3], "dp", scatter_dimension=1, tiled=True),
    )
    gain_grad, shift_grad = (
        lax.psum_scatter(gain_acc, ("dp", "tensor"), scatter_dimension=2, tiled=True),
        lax.psum_scatter(shift_acc, ("dp", "tensor"), scatter_dimension=2, tiled=True),
    )
    return (
        jnp.concatenate(outputs, 0),
        jnp.concatenate(input_grads, 0),
        shards[0],
        shards[1],
        shards[2],
        shards[3],
        gain_grad,
        shift_grad,
    )


def solution(mesh):
    placed = (
        P(("dp", "tensor"), None),
        P("dp"),
        P("dp"),
        P(None, "dp", None, "tensor"),
        P(None, "dp", "tensor"),
        P(None, "dp", "tensor"),
        P(None, "dp", "tensor"),
        P(None, None, ("dp", "tensor")),
        P(None, None, ("dp", "tensor")),
        P(("dp", "tensor"), None),
    )
    results = (
        P(("dp", "tensor"), None),
        P(("dp", "tensor"), None),
        P(None, "dp", None, "tensor"),
        P(None, "dp", "tensor"),
        P(None, "dp", "tensor"),
        P(None, "dp", "tensor"),
        P(None, None, ("dp", "tensor")),
        P(None, None, ("dp", "tensor")),
    )
    n_dp, n_tensor = mesh.shape["dp"], mesh.shape["tensor"]
    if n_tensor != GROUPS or n_dp != 8:
        return jax.shard_map(
            general_local, mesh=mesh, in_specs=placed, out_specs=results, check_vma=False
        )
    fine = Mesh(mesh.devices.reshape(n_dp // 2, 2, 2, 2), AXES)
    names = {"dp": ("z", "x"), "tensor": ("y", "c")}

    def refine(spec):
        parts = []
        for entry in spec:
            entry = (entry,) if isinstance(entry, str) else entry
            parts.append(entry and sum((names[a] for a in entry), ()))
        return P(*parts)

    return jax.shard_map(
        partial(split_local, n_dp // 2),
        mesh=fine,
        in_specs=tuple(refine(s) for s in placed),
        out_specs=tuple(refine(s) for s in results),
        check_vma=False,
    )
```

```python
from functools import partial

import jax
import jax.numpy as jnp
from jax import lax
from jax.experimental import pallas as pl
from jax.experimental.pallas import tpu as pltpu
from jax.sharding import Mesh
from jax.sharding import PartitionSpec as P

D = 768
HEADS = 12
HEAD_DIM = 64
MICRO = 4
CHAINS_PART = 1
LENGTH = 160
GROUPS = 4
OWN = 4
EXTRA = 2
SLOTS = OWN + EXTRA
EXT_ROWS = EXTRA * LENGTH
OWN_ROWS = OWN * LENGTH
ROWS = SLOTS * LENGTH

EPS = 1e-12
NEG = -1e30
HIGH = lax.Precision.HIGHEST
BF = jnp.bfloat16
F32 = jnp.float32
MESH = pl.DeviceIdType.MESH
ANY = pl.BlockSpec(memory_space=pl.ANY)
AXES = ("z", "x", "y", "c")


def place():
    return tuple(lax.axis_index(a) for a in AXES)


def greet(nz, z, x, y, c):
    barrier = pltpu.get_barrier_semaphore()
    friends = [{"c": 1 - c}, {"y": 1 - y}, {"y": 1 - y, "c": 1 - c}, {"x": 1 - x}]
    friends += [{"z": lax.rem(z + dz, nz)} for dz in range(1, nz)]
    for friend in friends:
        pl.semaphore_signal(barrier, inc=1, device_id=friend, device_id_type=MESH)
    return barrier, len(friends)


CHUNK = 320
SUB = 80
N_CHUNK = ROWS // CHUNK
WIDE = 3 * LENGTH
GW = 256
PAIR = 3


def dot_nn(a, b):
    return lax.dot_general(a, b, (((1,), (0,)), ((), ())), preferred_element_type=F32)


def dot_nt(a, b):
    return lax.dot_general(a, b, (((1,), (1,)), ((), ())), preferred_element_type=F32)


def dot_tn(a, b):
    return lax.dot_general(a, b, (((0,), (0,)), ((), ())), preferred_element_type=F32)


def lanes(shape):
    return lax.broadcasted_iota(jnp.int32, shape, len(shape) - 1)


def head_mask(h, shape):
    lane = lanes(shape)
    return jnp.logical_and(lane >= h * HEAD_DIM, lane < (h + 1) * HEAD_DIM)


def stack_heads(rows):
    zero = jnp.zeros_like(rows)
    return jnp.concatenate([jnp.where(head_mask(h, rows.shape), rows, zero) for h in range(3)], 0)


def merge_heads(stack):
    out = jnp.zeros((LENGTH, GW), stack.dtype)
    for h in range(3):
        out = jnp.where(head_mask(h, out.shape), stack[h * LENGTH : (h + 1) * LENGTH], out)
    return out


def chunk_rows(i, size=CHUNK):
    return pl.ds(pl.multiple_of(i * size, size), size)


def loop(count, body):
    def step(i, carry):
        body(i)
        return carry

    lax.fori_loop(0, count, step, 0)


def weave(count, unit, extra):
    def body(i):
        unit(i)
        for k, step in extra.items():
            pl.when(i == k)(step)

    loop(count, body)


def out_columns(t, w, wo):
    low = lanes((D, 128)) < HEAD_DIM
    tiles = [w[0, t, :, GW * i + 128 : GW * i + 256].astype(F32) for i in range(3)]
    wo[t, :, :128] = jnp.where(low, pltpu.roll(tiles[0], 64, 1), tiles[1]).astype(BF)
    wo[t, :, 128:] = jnp.where(low, pltpu.roll(tiles[2], 64, 1), 0.0).astype(BF)


def attend(t, chains, lens, proj, probs, hout):
    rows = [chunk_rows(s, LENGTH) for s in chains]
    parts = [(proj[t, r, :GW], proj[t, r, GW : 2 * GW], proj[t, r, 2 * GW :]) for r in rows]
    lows, outs = [], []
    for s, (query, key, value) in zip(chains, parts):
        scores = dot_nt(key, stack_heads(query * jnp.asarray(0.125, BF)))
        valid = lax.broadcasted_iota(jnp.int32, (LENGTH, 1), 0) < lens(s)
        scores = jnp.where(valid, scores, NEG)
        expo = jnp.exp(scores - jnp.max(scores, 0, keepdims=True))
        lows.append((expo * (1.0 / jnp.sum(expo, 0, keepdims=True))).astype(BF))
        outs.append(merge_heads(dot_tn(lows[-1], value)).astype(BF))
    for s, r, low, out in zip(chains, rows, lows, outs):
        probs[t, s, :, :WIDE] = low
        hout[t, r] = out


def norm_rows(values):
    center = values - jnp.mean(values, -1, keepdims=True)
    factor = lax.rsqrt(jnp.mean(center * center, -1, keepdims=True) + EPS)
    return center * factor, factor


def norm_back(scaled, normed, factor):
    return factor * (
        scaled
        - jnp.mean(scaled, -1, keepdims=True)
        - normed * jnp.mean(scaled * normed, -1, keepdims=True)
    )


def pieces(i, body):
    def step(k):
        body(pl.ds(pl.multiple_of(i * CHUNK + k * SUB, SUB), SUB), k)

    loop(CHUNK // SUB, step)


def first_norm(i, x, hout, wo, prm, mid, n1, s1, mid_low):
    r = chunk_rows(i)
    attn = dot_nt(hout[0, r], wo[0])
    for t in range(1, GROUPS):
        attn += dot_nt(hout[t, r], wo[t])
    mid[r] = attn

    def piece(p, k):
        normed, factor = norm_rows(x[p].astype(F32) + mid[p])
        n1[p] = normed.astype(BF)
        s1[p] = jnp.broadcast_to(factor, (SUB, 128))
        value = normed * prm[0:1] + prm[2:3]
        mid[p] = value
        mid_low[p] = value.astype(BF)

    pieces(i, piece)


def feed_up(t, i, mid_low, w, act, slope):
    r = chunk_rows(i)
    for k in range(0, D, GW):
        up = dot_nn(mid_low[r], w[1, t, :, k : k + GW])
        cdf = 0.5 * (1.0 + lax.erf(up * 0.7071067811865476))
        act[t, r, k : k + GW] = (up * cdf).astype(BF)
        bell = 0.3989422804014327 * jnp.exp(-0.5 * up * up)
        slope[t, r, k : k + GW] = (cdf + up * bell).astype(BF)


def feed_down(i, t, act, w, mid):
    r = chunk_rows(i)
    mid[r] += dot_nt(act[t, r], w[2, t]) + dot_nt(act[t + 1, r], w[2, t + 1])


def second_norm(i, t, act, w, prm, mid, cot, mine, y_rows, d_ffn, ngrad):
    feed_down(i, t, act, w, mid)

    def piece(p, k):
        normed, factor = norm_rows(mid[p])
        y_rows[pl.ds(pl.multiple_of(k * SUB, SUB), SUB)] = (normed * prm[1:2] + prm[3:4]).astype(BF)
        grad = cot[p].astype(F32) * jnp.where(k < LENGTH // SUB, mine(2 * i), mine(2 * i + 1))
        ngrad[1:2] += jnp.sum(grad * normed, 0, keepdims=True)
        ngrad[3:4] += jnp.sum(grad, 0, keepdims=True)
        back = norm_back(grad * prm[1:2], normed, factor)
        mid[p] = back
        d_ffn[p] = back.astype(BF)

    pieces(i, piece)


def back_up(t, i, d_ffn, w, slope):
    r = chunk_rows(i)
    slope[t, r] = (dot_nn(d_ffn[r], w[2, t]) * slope[t, r].astype(F32)).astype(BF)


def back_first_norm(i, d_up, w, prm, mid, n1, s1, d_attn, ngrad):
    r = chunk_rows(i)
    grad = dot_nt(d_up[0, r], w[1, 0])
    for t in range(1, GROUPS):
        grad += dot_nt(d_up[t, r], w[1, t])
    mid[r] += grad

    def piece(p, k):
        grad = mid[p]
        normed = n1[p].astype(F32)
        ngrad[0:1] += jnp.sum(grad * normed, 0, keepdims=True)
        ngrad[2:3] += jnp.sum(grad, 0, keepdims=True)
        back = norm_back(grad * prm[0:1], normed, s1[p, 0:1])
        mid[p] = back
        d_attn[p] = back.astype(BF)

    pieces(i, piece)


def back_heads(t, d_attn, wo, d_heads):
    d_heads[t, :, :GW] = dot_nn(d_attn[...], wo[t]).astype(BF)


def back_attend(t, chains, proj, probs, d_heads):
    rows = [chunk_rows(s, LENGTH) for s in chains]
    parts = [
        (proj[t, r, :GW], proj[t, r, GW : 2 * GW], proj[t, r, 2 * GW :], d_heads[t, r, :GW], probs[t, s, :, :WIDE])
        for s, r in zip(chains, rows)
    ]
    results = []
    for query, key, value, grad, low in parts:
        grad = stack_heads(grad)
        p = low.astype(F32)
        d_probs = dot_nt(value, grad)
        d_scores = (p * (d_probs - jnp.sum(d_probs * p, 0, keepdims=True))).astype(BF)
        d_query = merge_heads(dot_tn(d_scores, key)) * 0.125
        d_key = dot_nn(d_scores, stack_heads(query * jnp.asarray(0.125, BF)))
        results.append((d_query.astype(BF), d_key.astype(BF), dot_nn(low, grad).astype(BF)))
    for r, (d_query, d_key, d_value) in zip(rows, results):
        proj[t, r, :GW] = d_query
        proj[t, r, GW : 2 * GW] = d_key
        proj[t, r, 2 * GW :] = d_value


def grad_qkv_out(t, x, d_proj, d_attn, hout, store):
    low = lanes((D, 128)) < HEAD_DIM
    outs = dot_tn(d_attn[...], hout[t])
    places = (pltpu.roll(outs[:, :128], 64, 1), outs[:, :128], pltpu.roll(outs[:, 128:], 64, 1))
    for i in range(3):
        part = dot_tn(x[...], d_proj[t, :, GW * i : GW * (i + 1)])
        store(GW * i, part[:, :128])
        store(GW * i + 128, jnp.where(low, part[:, 128:], places[i]))


def back_input(i, d_proj, w, mid, out):
    r = chunk_rows(i)
    grad = mid[r]
    for t in range(GROUPS):
        grad += dot_nt(d_proj[t, r], w[0, t])
    out(r, grad)


MIXED = (2, 1)
GATHER_FIRST = (
    ('X', 1, 0), ('L', 0, 0), ('y', 0), ('X', 0, 1), ('L', 0, 1),
    ('z', 0, 0, 1), ('z', 0, 1, 1), ('y', 1), ('L', 1, 1), ('x', 0, 1, 0),
    ('X', 0, 0), ('z', 0, 1, 2), ('x', 1, 0, 0), ('z', 0, 0, 2), ('x', 0, 1, 1),
    ('x', 0, 0, 1), ('L', 1, 0), ('z', 0, 1, 3), ('z', 0, 0, 3), ('x', 0, 0, 0),
    ('y', 2), ('X', 2, 1), ('x', 0, 1, 3), ('z', 1, 1, 1), ('x', 0, 1, 2),
    ('z', 1, 0, 1), ('x', 0, 0, 2), ('L', 2, 0), ('x', 0, 0, 3), ('z', 1, 1, 2),
    ('X', 1, 1),
)
GATHER_QKV = {
    7: (('z', 1, 0, 2),),
    10: (('x', 2, 1, 0),),
}
GATHER_ATTEND = {
    1: (('L', 2, 1), ('z', 1, 1, 3), ('z', 1, 0, 3), ('z', 2, 0, 1),),
    2: (('X', 2, 0),),
    5: (('x', 1, 1, 1), ('x', 1, 1, 2),),
    6: (('z', 2, 1, 1), ('x', 1, 1, 0),),
    7: (('z', 2, 0, 2), ('x', 1, 0, 1),),
}
GATHER_NORM = {
    0: (('x', 1, 0, 2), ('x', 1, 1, 3), ('x', 1, 0, 3),),
}
GATHER_UP = {
    3: (('z', 2, 1, 2),),
    4: (('z', 2, 0, 3),),
    7: (('x', 2, 0, 1),),
    9: (('x', 2, 0, 0),),
    10: (('x', 2, 0, 3), ('x', 2, 0, 2),),
    11: (('z', 2, 1, 3),),
}


def remote(src, dst, s_sem, r_sem, who):
    return pltpu.make_async_remote_copy(
        src_ref=src, dst_ref=dst, send_sem=s_sem, recv_sem=r_sem, device_id=who, device_id_type=MESH
    )


def arrived(ref, sem):
    remote(ref, ref, sem, sem, {"c": 1 - lax.axis_index("c")}).wait_recv()


def has_left(ref, sem):
    remote(ref, ref, sem, sem, {"c": 1 - lax.axis_index("c")}).wait_send()


def step_kernel(nz, rows,
                tags, lens, x_in, cot, qkv, wout, up, dn, gain, bias,
                y_out, g_out, qo_out, up_out, dn_out, n_out, y_back, g_back, r_c,
                w, x, proj, probs, hout, wo, mid, n1, s1, mid_low, act, slope, d_ffn, gown, r_xz, oth, v_qkv, v_out, far,
                n_all, prm, ngrad, n_c, n_x, n_z,
                load_s, io_s, stage_s, out_s,
                ys_s, ys_r, zs_s, zs_r, zm_s, zm_r, xs_s, xs_r, cs_s, cs_r, ex_s, ex_r, na_s, na_r,
                c_s, c_r, cp_s, cp_r, x_s, x_r, z_s, z_r, y_s, y_r, e_s, e_r, ng_s, ng_r):
    z, xc, y, c = place()
    core, across, other_x = {"c": 1 - c}, {"y": 1 - y}, {"x": 1 - xc}
    diagonal = {"y": 1 - y, "c": 1 - c}
    mats = (None, up, dn)
    lender = y != c
    home = (2 * y + c) * OWN
    away = (2 - y) * OWN + c * EXTRA

    def z_of(dz):
        return lax.rem(z + dz, nz)

    def chain(s):
        return jnp.where(s < OWN, home + s, away + s - OWN)

    def length_of(s):
        return lens[chain(s)]

    def mine(s):
        return jnp.where(tags[chain(s)] == y, 1.0, 0.0)

    def part(zz, xx):
        return pl.ds(pl.multiple_of((zz * 2 + xx) * rows, rows), rows)

    def group(g):
        return 2 * lax.rem(y + g, 2) + c

    def block(m, g, zz, xx):
        return w.at[m, group(g), part(zz, xx)]

    loads = [pltpu.make_async_copy(mats[m].at[y], block(m, 0, z, xc), load_s.at[m]) for m in range(1, 3)]
    loads += [
        pltpu.make_async_copy(x_in, x.at[pl.ds(0, OWN_ROWS)], load_s.at[3]),
        pltpu.make_async_copy(cot, d_ffn.at[pl.ds(0, OWN_ROWS)], load_s.at[4]),
        pltpu.make_async_copy(qkv, v_qkv, load_s.at[0]),
        pltpu.make_async_copy(wout, v_out, load_s.at[5]),
    ]
    for cp in loads:
        cp.start()
    barrier, friends = greet(nz, z, xc, y, c)
    me = ((z * 2 + xc) * 2 + y) * 2 + c
    cols = gain.shape[2]
    n_all[me] = jnp.zeros((8, 128), F32)
    for i in range(2):
        n_all[me, 2 * i : 2 * i + 2, :cols] = gain[i]
        n_all[me, 4 + 2 * i : 6 + 2 * i, :cols] = bias[i]
    ngrad[...] = jnp.zeros_like(ngrad)
    for cp in loads[4:]:
        cp.wait()

    def packed(k):
        tail = v_out[k]
        cols = []
        for i in range(3):
            cols += [v_qkv[k, i], tail[:, HEAD_DIM * i : HEAD_DIM * (i + 1)]]
        return jnp.concatenate(cols, 1)

    w[0, group(0), part(z, xc)] = packed(y)
    far[...] = packed(1 - y)
    pl.semaphore_wait(barrier, friends)

    def given(m):
        return mats[m].at[1 - y] if m else far

    def lend(arr, out, i, act_on):
        @pl.when(lender)
        def _():
            for j, (who, p) in enumerate(((across, c), (diagonal, 1 - c))):
                src = arr.at[pl.ds(pl.multiple_of(p * EXT_ROWS, EXT_ROWS), EXT_ROWS)]
                act_on(remote(src, out.at[pl.ds(OWN_ROWS, EXT_ROWS)], ex_s.at[i, j], ex_r.at[i], who))

    for m in range(3):
        remote(given(m), w.at[m, group(0), part(z, xc)], ys_s.at[m], ys_r.at[m], across).start()
    lend(x_in, x, 0, lambda cp: cp.start())
    lend(cot, d_ffn, 1, lambda cp: cp.start())

    def inside(zz):
        return jnp.logical_and(zz >= 0, zz < nz)

    def start(cp):
        cp.start()

    def recv(cp):
        cp.wait_recv()

    def hop(m, g, d, j, ref, act_on, col=0):
        to = z + 1 - 2 * d
        sems = (zm_s.at[d, j], zm_r.at[d, j]) if col else (zs_s.at[m, g, d, j], zs_r.at[m, g, d, j])

        @pl.when(jnp.logical_and(inside(to), j < nz))
        def _():
            act_on(remote(ref, ref, *sems, {"z": to}))

    def x_copy(m, g, zz):
        ref = block(m, g, zz, xc)
        return remote(ref, ref, xs_s.at[m, g, zz], xs_r.at[m, g, zz], other_x)

    def c_copy(m, g, zz, xx):
        ref = block(m, g, zz, xx)
        return remote(ref, ref, cs_s.at[m, g, zz, xx], cs_r.at[m, g, zz, xx], core)

    def from_y(m):
        arrived(block(m, 1, z, xc), ys_r.at[m])

    def own_z(m, g):
        for d in range(2):
            hop(m, g, d, 1, block(m, g, z, xc), start)

    def own_xc(m, g):
        x_copy(m, g, z).start()
        c_copy(m, g, z, xc).start()

    def z_event(m, g, j):
        mixed = (m, g) == MIXED

        def body(d):
            zz = z - j + 2 * j * d

            @pl.when(inside(zz))
            def _():
                for col in range(2 if mixed else 1):
                    ref = block(m, g, zz, lax.rem(xc + col, 2))
                    arrived(ref, zm_r.at[d, j] if col else zs_r.at[m, g, d, j])
                    hop(m, g, d, j + 1, ref, start, col)
                    if not mixed:
                        x_copy(m, g, zz).start()
                    c_copy(m, g, zz, lax.rem(xc + col, 2)).start()

        loop(2, body)

    def x_event(m, g, j):
        def body(d):
            zz = z - j + 2 * j * d

            @pl.when(inside(zz))
            def _():
                ref = block(m, g, zz, 1 - xc)
                arrived(ref, xs_r.at[m, g, zz])
                if (m, g) == MIXED:
                    for way in range(2):
                        hop(m, g, way, 1, ref, start, 1)
                c_copy(m, g, zz, 1 - xc).start()

        loop(2 if j else 1, body)

    kinds = {"y": from_y, "L": own_z, "X": own_xc, "z": z_event, "x": x_event}

    def gather_steps(plan):
        def run(steps):
            for kind, *args in steps:
                kinds[kind](*args)

        return {k: partial(run, steps) for k, steps in plan.items()}

    def gathered(m, first=0, last=2):
        def body(i):
            g = first + i // (2 * nz)
            t = 2 * lax.rem(y + g, 2) + 1 - c
            zz, xx = (i // 2) % nz, i % 2
            arrived(w.at[m, t, part(zz, xx)], cs_r.at[m, g, zz, xx])

        loop(2 * nz * (last - first), body)

    def gather_sent(i):
        m, g = i // 2, i % 2
        ref = w.at[0, 0, pl.ds(0, rows)]
        mixed = i == 2 * MIXED[0] + MIXED[1]
        for j in range(1, nz):
            for d in range(2):
                @pl.when(inside(z - (1 - 2 * d) * (j - 1)))
                def _():
                    hop(m, g, d, j, ref, lambda cp: cp.wait_send())

                    @pl.when(mixed)
                    def _():
                        hop(m, g, d, j, ref, lambda cp: cp.wait_send(), 1)
        for zz in range(nz):
            @pl.when(jnp.logical_or(jnp.logical_not(mixed), z == zz))
            def _():
                has_left(ref, xs_s.at[m, g, zz])

            for xx in range(2):
                has_left(ref, cs_s.at[m, g, zz, xx])

    def norm_hop(i, act_on):
        if i == 0:
            act_on(remote(n_all.at[me], n_all.at[me], na_s.at[0], na_r.at[0], core))
        elif i == 1:
            ref = n_all.at[pl.ds(me - c, 2)]
            act_on(remote(ref, ref, na_s.at[1], na_r.at[1], across))
        elif i == 2:
            ref = n_all.at[pl.ds(me - c - 2 * y, 4)]
            act_on(remote(ref, ref, na_s.at[2], na_r.at[2], other_x))
        else:
            ref = n_all.at[pl.ds(8 * z, 8)]
            for dz in range(1, nz):
                act_on(remote(ref, ref, na_s.at[2 + dz], na_r.at[2 + dz], {"z": z_of(dz)}))

    for cp in loads[:2]:
        cp.wait()
    norm_hop(0, start)
    for kind, *args in GATHER_FIRST:
        kinds[kind](*args)
        if (kind, *args) == ("z", 0, 0, 1):
            norm_hop(0, recv)
            norm_hop(1, start)
        if (kind, *args) == ("z", 0, 0, 3):
            norm_hop(1, recv)
            norm_hop(2, start)
    norm_hop(2, recv)
    norm_hop(3, start)
    gathered(0)
    loads[2].wait()
    arrived(x.at[pl.ds(OWN_ROWS, EXT_ROWS)], ex_r.at[0])

    def projection(i):
        t, k = i // N_CHUNK, i % N_CHUNK
        r = chunk_rows(k)
        proj[t, r] = dot_nn(x[r], w[0, t]).astype(BF)

        @pl.when(k == N_CHUNK - 1)
        def _():
            out_columns(t, w, wo)

    weave(GROUPS * N_CHUNK, projection, gather_steps(GATHER_QKV))
    per = SLOTS // PAIR

    def attention(i):
        attend(i // per, [(i % per) * PAIR + k for k in range(PAIR)], length_of, proj, probs, hout)

    weave(GROUPS * per, attention, gather_steps(GATHER_ATTEND))
    norm_hop(3, recv)
    lane = lanes((2, D))
    gains, shifts = jnp.zeros((2, D), F32), jnp.zeros((2, D), F32)
    for d in range(8 * nz):
        within = jnp.logical_and(lane >= d * cols, lane < (d + 1) * cols)
        for name in range(2):
            piece = n_all[d, pl.ds(4 * name + 2 * y, 2), :]
            piece = jnp.concatenate([piece, jnp.zeros((2, D - 128), F32)], 1)
            piece = jnp.where(within, pltpu.roll(piece, d * cols, 1) if d else piece, 0.0)
            if name == 0:
                gains += piece
            else:
                shifts += piece
    prm[0:2] = gains
    prm[2:4] = shifts
    weave(
        N_CHUNK,
        lambda i: first_norm(i, x, hout, wo, prm, mid, n1, s1, mid_low),
        gather_steps(GATHER_NORM),
    )
    gathered(1)
    weave(
        GROUPS * N_CHUNK,
        lambda i: feed_up(i // N_CHUNK, i % N_CHUNK, mid_low, w, act, slope),
        gather_steps(GATHER_UP),
    )
    gathered(2, 0, 1)
    first_two = 2 * y
    last_two = 2 - first_two
    loop(N_CHUNK, lambda i: feed_down(i, first_two, act, w, mid))
    gathered(2, 1, 2)
    loads[3].wait()
    arrived(d_ffn.at[pl.ds(OWN_ROWS, EXT_ROWS)], ex_r.at[1])

    def y_stage(i):
        return r_xz.at[i // 2, 0, pl.ds(pl.multiple_of((i % 2) * CHUNK, CHUNK), CHUNK)]

    def give_back(src, dst, i, act_on):
        dst = dst.at[pl.ds(pl.multiple_of(c * EXT_ROWS, EXT_ROWS), EXT_ROWS)]

        @pl.when(c == y)
        def _():
            act_on(remote(src, dst, e_s.at[i], e_r.at[i, c], across))

        @pl.when(c != y)
        def _():
            act_on(remote(src, dst, e_s.at[i], e_r.at[i, c], diagonal))

    def y_copy(i):
        return pltpu.make_async_copy(y_stage(i), y_out.at[pl.ds(i * CHUNK, CHUNK)], io_s.at[i])

    loop(
        N_CHUNK,
        lambda i: second_norm(
            i, last_two, act, w, prm, mid, d_ffn, mine, y_stage(i), d_ffn, ngrad
        ),
    )
    for i in range(2):
        y_copy(i).start()
    give_back(y_stage(2), y_back, 0, start)

    def columns(g, other):
        pair = jnp.where(g == 0, 1 - y, y)
        return 2 * pair + jnp.where(other, 1 - c, c)

    def x_place(m, g, i):
        return r_xz.at[0, m, pl.ds(pl.multiple_of((g * nz + i) * rows, rows), rows)]

    def z_place(m, g, i):
        return r_xz.at[1, m, pl.ds(pl.multiple_of((g * nz + i) * rows, rows), rows)]

    def spare(m, g):
        return gown.at[0, g] if m else act.at[2 * g + c, pl.ds(0, D)]

    def core_send(m, g):
        there = r_c.at[g] if m else spare(0, g)
        return remote(spare(m, g), there, c_s.at[m, g], c_r.at[m, g], core)

    def fetch(g):
        return pltpu.make_async_copy(r_c.at[g], act.at[2 * g + 1 - c, pl.ds(0, D)], stage_s.at[g])

    half = D // 2

    def half_rows(k):
        return pl.ds(pl.multiple_of(half * jnp.where(z < nz // 2, 1 - k, k), half), half)

    def core_half(g, k):
        r = half_rows(k)
        return remote(gown.at[0, g, r], gown.at[1, g, r], cp_s.at[g, k], cp_r.at[g, k], core)

    def core_fetch(g):
        arrived(r_c.at[g], c_r.at[1, g])
        fetch(g).start()

    middle = jnp.logical_and(z > 0, z < nz - 1)

    def target(k):
        down = jnp.where(nz - 1 - k > z, nz - 1 - k, nz - 2 - k)
        up = jnp.where(k < z, k, k + 1)
        return jnp.where(k == nz - 1, z, jnp.where(z < nz // 2, down, up))

    def add_and_cross(m, g, from_core, first, count):
        def add(i):
            p = part(target(first + i % count), lax.rem(xc + 1 + i // count, 2))
            gown[m, g, p] += from_core[p]

        def over(k):
            zz = target(first + k)
            remote(gown.at[m, g, part(zz, 1 - xc)], x_place(m, g, zz), x_s.at[m, g, zz], x_r.at[m, g, zz], other_x).start()

        loop(count + 1, add)
        loop(count, over)
        loop(count - 1, lambda i: add(count + 1 + i))

    def core_add(m, g):
        from_core = act.at[2 * g + 1 - c, pl.ds(0, D)]
        if m == 1:
            fetch(g).wait()
        else:
            arrived(from_core, c_r.at[0, g])
        add_and_cross(m, g, from_core, 0, nz)

    def half_add(g, k):
        core_half(g, k).wait_recv()
        add_and_cross(2, g, gown.at[1, g], k * (nz // 2), nz // 2)

    def sum_event(q):
        m = 2 - q // (2 * nz)
        g = (q // nz) % 2
        k = q % nz
        zz = target(k)
        over = x_place(m, g, zz)
        arrived(over, x_r.at[m, g, zz])
        p = part(zz, xc)
        gown[m, g, p] += over[...]

        beside = jnp.where(z == 0, 1, nz - 2)
        joins = jnp.logical_and(k < 2, jnp.logical_not(middle))
        to = jnp.where(joins, beside, zz)
        slot = jnp.where(joins, jnp.where(k == 0, beside, nz - 1 - z), z)

        @pl.when(jnp.logical_and(k < nz - 1, jnp.logical_or(k == nz - 2, jnp.logical_not(middle))))
        def _():
            remote(gown.at[m, g, p], z_place(m, g, slot), z_s.at[m, g, zz], z_r.at[m, g, slot], {"z": to}).start()

        def relay(k, slot):
            to = target(k)
            q = part(to, xc)
            arrived(z_place(m, g, slot), z_r.at[m, g, slot])
            gown[m, g, q] += z_place(m, g, slot)[...]
            remote(gown.at[m, g, q], z_place(m, g, z), z_s.at[m, g, to], z_r.at[m, g, z], {"z": to}).start()

        early = jnp.where(m == 0, 1, 0)

        @pl.when(jnp.logical_and(k == nz - 2 - early, middle))
        def _():
            relay(0, z)

        @pl.when(jnp.logical_and(k == nz - 1 - early, middle))
        def _():
            relay(1, jnp.where(z == 1, nz - 1, 0))

    outs = (qo_out, up_out, dn_out)

    def out_stage(m, other):
        return mid.at[pl.ds(m * rows + (0 if other else OWN_ROWS), rows)]

    def out_copy(m, other):
        return pltpu.make_async_copy(out_stage(m, other), outs[m].at[1 - y if other else y], out_s.at[m, other])

    def last_send(m):
        return remote(mid_low.at[pl.ds(EXT_ROWS + m * rows, rows)], oth.at[m], y_s.at[m], y_r.at[m], across)

    def finish(m, g):
        total = gown[m, g, part(z, xc)].astype(F32)
        for dz in range(1, nz):
            source = z_of(dz)
            direct = jnp.abs(source - z) <= jnp.where(middle, 1, 2)

            @pl.when(direct)
            def _():
                arrived(z_place(m, g, source), z_r.at[m, g, source])

            total += jnp.where(direct, z_place(m, g, source)[...].astype(F32), 0.0)

        if g == 1:
            out_stage(m, 0)[...] = total
            out_copy(m, 0).start()
        else:
            mid_low[EXT_ROWS + m * rows : EXT_ROWS + (m + 1) * rows] = total.astype(BF)
            last_send(m).start()

    def up_grads(extra):
        def unit(q):
            g, own = q % 2, q // 2
            t = columns(g, own == 0)
            dst = gown.at[own, g]
            for k in range(0, D, GW):
                dst[:, k : k + GW] = dot_tn(mid_low[...], slope[t, :, k : k + GW]).astype(BF)

            @pl.when(own == 0)
            def _():
                core_send(1, g).start()

        weave(4, unit, extra)

    def down_grads(extra):
        def unit(q):
            g, k, own = q // 4, (q // 2) % 2, q % 2
            t = columns(g, own == 0)
            r = half_rows(k)
            dst = gown.at[2 * own, g, r]
            for j in range(0, D, GW):
                dst[:, j : j + GW] = dot_tn(d_ffn[:, r], act[t, :, j : j + GW]).astype(BF)

            @pl.when(own == 0)
            def _():
                core_half(g, k).start()

        weave(8, unit, extra)

    def then(*steps):
        def run():
            for f, *args in steps:
                f(*args)

        return run

    def core_over(m):
        for g in range(2):
            if m == 2:
                for k in range(2):
                    core_half(g, k).wait_send()
            else:
                core_send(m, g).wait_send()

    down_grads(
        {
            2: then((half_add, 0, 0)),
            3: then((half_add, 0, 1)),
            5: then((half_add, 1, 0)),
            7: then((half_add, 1, 1), (core_over, 2)),
        }
    )

    def up_back(i):
        back_up(i // N_CHUNK, i % N_CHUNK, d_ffn, w, slope)

    weave(GROUPS * N_CHUNK, up_back, {0: then((sum_event, 0)), 5: then((sum_event, 1)), 10: then((sum_event, 2))})
    for i in range(2):
        y_copy(i).wait()
    has_left(y_stage(2), e_s.at[0])
    up_grads({1: then((sum_event, 3)), 3: then((sum_event, 4))})
    for g in range(2):
        core_fetch(g)
    weave(
        N_CHUNK,
        lambda i: back_first_norm(i, slope, w, prm, mid, n1, s1, d_ffn, ngrad),
        {
            0: then((core_add, 1, 0), (core_add, 1, 1), (core_over, 1)),
            1: then((sum_event, 5)),
            2: then((sum_event, 6)),
        },
    )

    def send_norms(i, act_on):
        if i == 0:
            act_on(remote(ngrad, n_c, ng_s.at[0], ng_r.at[0], core))
        elif i == 1:
            act_on(remote(n_c, n_x, ng_s.at[1], ng_r.at[1], other_x))
        elif i == 2:
            for dz in range(1, nz):
                act_on(remote(n_x, n_z.at[dz], ng_s.at[1 + dz], ng_r.at[1 + dz], {"z": z_of(dz)}))
        else:
            act_on(remote(n_out.at[y], n_out.at[y], ng_s.at[nz + 1], ng_r.at[nz + 1], across))

    send_norms(0, start)
    loop(GROUPS, lambda t: back_heads(t, d_ffn, wo, slope))
    sum_event(7)
    send_norms(0, recv)
    send_norms(0, lambda cp: cp.wait_send())
    n_c[...] += ngrad[...]
    send_norms(1, start)

    def attention_back(i):
        back_attend(i // per, [(i % per) * PAIR + k for k in range(PAIR)], proj, probs, slope)

        @pl.when(i % 2 == 1)
        def _():
            sum_event(8 + i // 2)

    loop(GROUPS * per, attention_back)
    seen = 8 + GROUPS * per // 2

    def qkv_grads(q):
        g, own = q // 2, q % 2

        def store(col, value):
            value = value.astype(BF)

            @pl.when(own == 0)
            def _():
                spare(0, g)[:, col : col + 128] = value

            @pl.when(own == 1)
            def _():
                gown[0, g, :, col : col + 128] = value

        grad_qkv_out(columns(g, own == 0), x, proj, d_ffn, hout, store)

        @pl.when(own == 0)
        def _():
            core_send(0, g).start()

    weave(
        4,
        qkv_grads,
        {
            0: then((sum_event, seen)),
            1: then((core_add, 0, 0), (sum_event, seen + 1)),
            3: then((core_add, 0, 1), (sum_event, seen + 2)),
        },
    )
    seen += 3

    def inputs_back(i):
        k = lax.rem(i + N_CHUNK - 1, N_CHUNK)

        def keep(r, grad):
            mid[r] = grad

            @pl.when(i == 0)
            def _():
                mid_low[:EXT_ROWS] = grad.astype(BF)

        back_input(k, proj, w, mid, keep)

        @pl.when(i == 0)
        def _():
            give_back(mid_low.at[pl.ds(0, EXT_ROWS)], g_back, 1, start)

    weave(N_CHUNK, inputs_back, {1: then((sum_event, seen))})
    seen += 1
    after = 4 * nz
    if seen < after:
        loop(after - seen, lambda q: sum_event(seen + q))
    for g in range(2):
        finish(2, g)
    loop(nz, lambda q: sum_event(after + q))

    def sums_sent(i):
        m, g = i // 2, i % 2
        for zz in range(nz):
            @pl.when(z != zz)
            def _():
                has_left(x_place(0, 0, 0), z_s.at[m, g, zz])

            has_left(x_place(0, 0, 0), x_s.at[m, g, zz])

    loop(6, gather_sent)

    trips = [
        pltpu.make_async_copy(g_back, proj.at[0, pl.ds(0, OWN_ROWS)], io_s.at[0]),
        pltpu.make_async_copy(y_out, proj.at[1, pl.ds(0, OWN_ROWS)], io_s.at[1]),
        pltpu.make_async_copy(y_back, proj.at[2, pl.ds(0, OWN_ROWS)], io_s.at[2]),
    ]
    y_again = pltpu.make_async_copy(proj.at[1, pl.ds(0, OWN_ROWS)], y_out, io_s.at[1])
    g_copy = pltpu.make_async_copy(mid.at[pl.ds(0, OWN_ROWS)], g_out, io_s.at[3])

    @pl.when(lender)
    def _():
        for i, dst in enumerate((y_back, g_back)):
            for j in range(2):
                arrived(dst.at[pl.ds(j * EXT_ROWS, EXT_ROWS)], e_r.at[i, j])
        for cp in trips:
            cp.start()
        for cp in trips:
            cp.wait()

        def merge(s):
            r = chunk_rows(s, LENGTH)
            keep = jnp.zeros((LENGTH, D), F32) + mine(s) > 0.5
            mid[r] = jnp.where(keep, mid[r], proj[0, r].astype(F32))
            proj[1, r] = jnp.where(keep, proj[1, r].astype(F32), proj[2, r].astype(F32)).astype(BF)

        loop(OWN, merge)
        y_again.start()

    g_copy.start()
    send_norms(1, recv)
    send_norms(1, lambda cp: cp.wait_send())
    n_x[...] += n_c[...]
    send_norms(2, start)
    for g in range(2):
        finish(1, g)
    loop(nz - 1, lambda q: sum_event(after + nz + q))
    g_copy.wait()

    def widen(m):
        arrived(oth.at[m], y_r.at[m])
        out_stage(m, 1)[...] = oth[m].astype(F32)
        out_copy(m, 1).start()

    widen(2)
    widen(1)
    loop(4, lambda i: sums_sent(2 + i))
    total = n_x[...]
    for dz in range(1, nz):
        arrived(n_z.at[dz], ng_r.at[1 + dz])
        total += n_z[dz]
    n_out[y] = total
    send_norms(3, start)
    finish(0, 0)
    sum_event(after + 2 * nz - 1)
    widen(0)
    finish(0, 1)

    loop(2, sums_sent)
    for g in range(2):
        core_send(0, g).wait_send()
    for m in range(3):
        has_left(given(m), ys_s.at[m])
        for other in range(2):
            out_copy(m, other).wait()
        last_send(m).wait_send()
    lend(x_in, x, 0, lambda cp: cp.wait_send())
    lend(cot, d_ffn, 1, lambda cp: cp.wait_send())
    for i in range(4):
        norm_hop(i, lambda cp: cp.wait_send())
    send_norms(2, lambda cp: cp.wait_send())
    send_norms(3, lambda cp: cp.wait())
    has_left(mid_low.at[pl.ds(0, EXT_ROWS)], e_s.at[1])

    @pl.when(lender)
    def _():
        y_again.wait()


def run_step(nz, tags, lens, x_in, cot, qkv, wout, up, dn, gain, bias):
    rows = up.shape[1]
    V = pl.BlockSpec(memory_space=pltpu.VMEM)
    S = pl.BlockSpec(memory_space=pltpu.SMEM)
    sem = pltpu.SemaphoreType.DMA
    out = jax.ShapeDtypeStruct
    return pl.pallas_call(
        partial(step_kernel, nz, rows),
        out_shape=(
            out((OWN_ROWS, D), BF),
            out((OWN_ROWS, D), F32),
            out((2, rows, D), F32),
            out((2, rows, D), F32),
            out((2, rows, D), F32),
            out((2, 8, D), F32),
            out((OWN_ROWS, D), BF),
            out((OWN_ROWS, D), BF),
            out((2, D, D), BF),
        ),
        in_specs=[S, S] + [ANY] * 6 + [V, V],
        out_specs=(ANY, ANY, ANY, ANY, ANY, V, ANY, ANY, ANY),
        scratch_shapes=[
            pltpu.VMEM((3, GROUPS, D, D), BF),
            pltpu.VMEM((ROWS, D), BF),
            pltpu.VMEM((GROUPS, ROWS, D), BF),
            pltpu.VMEM((GROUPS, SLOTS, LENGTH, 512), BF),
            pltpu.VMEM((GROUPS, ROWS, GW), BF),
            pltpu.VMEM((GROUPS, D, GW), BF),
            pltpu.VMEM((ROWS, D), F32),
            pltpu.VMEM((ROWS, D), BF),
            pltpu.VMEM((ROWS, 128), F32),
            pltpu.VMEM((ROWS, D), BF),
            pltpu.VMEM((GROUPS, ROWS, D), BF),
            pltpu.VMEM((GROUPS, ROWS, D), BF),
            pltpu.VMEM((ROWS, D), BF),
            pltpu.VMEM((3, 2, D, D), BF),
            pltpu.VMEM((2, 3, 2 * nz * rows, D), BF),
            pltpu.VMEM((3, rows, D), BF),
            pltpu.VMEM(qkv.shape, BF),
            pltpu.VMEM(wout.shape, BF),
            pltpu.VMEM((rows, D), BF),
            pltpu.VMEM((8 * nz, 8, 128), F32),
            pltpu.VMEM((8, D), F32),
            pltpu.VMEM((8, D), F32),
            pltpu.VMEM((8, D), F32),
            pltpu.VMEM((8, D), F32),
            pltpu.VMEM((nz, 8, D), F32),
            sem((6,)), sem((4,)), sem((2,)), sem((3, 2)),
            sem((3,)), sem((3,)),
            sem((3, 2, 2, nz)), sem((3, 2, 2, nz)),
            sem((2, nz)), sem((2, nz)),
            sem((3, 2, nz)), sem((3, 2, nz)),
            sem((3, 2, nz, 2)), sem((3, 2, nz, 2)),
            sem((2, 2)), sem((2,)),
            sem((nz + 2,)), sem((nz + 2,)),
            sem((3, 2)), sem((3, 2)),
            sem((2, 2)), sem((2, 2)),
            sem((3, 2, nz)), sem((3, 2, nz)),
            sem((3, 2, nz)), sem((3, 2, nz)),
            sem((3,)), sem((3,)),
            sem((2,)), sem((2, 2)),
            sem((nz + 2,)), sem((nz + 2,)),
        ],
        compiler_params=pltpu.CompilerParams(
            collective_id=0, has_side_effects=True, vmem_limit_bytes=67043328
        ),
        name="layer_step",
    )(tags, lens, x_in, cot, qkv, wout, up, dn, gain, bias)


def deliver_kernel(cols, y_in, g_in, qo, up_in, dn_in, sums,
                   y_out, g_out, qkv_out, wout_out, up_out, dn_out, gain_out, bias_out,
                   v_y, v_g, v_qo, v_up, v_dn, v_qkv, v_out, in_s, out_s):
    through = [(up_in, v_up, up_out), (dn_in, v_dn, dn_out)]
    for k in range(OWN):
        r = pl.ds(k * LENGTH, LENGTH)
        through.append((g_in.at[r], v_g.at[r], g_out.at[r]))
    for k in range(2):
        r = pl.ds(k * CHUNK, CHUNK)
        through.append((y_in.at[r], v_y.at[r], y_out.at[r]))
    n = len(through)
    first = pltpu.make_async_copy(qo, v_qo, in_s.at[n])
    first.start()
    loads, stores = [], []
    for i, (src, via, dst) in enumerate(through):
        loads.append(pltpu.make_async_copy(src, via, in_s.at[i]))
        stores.append(pltpu.make_async_copy(via, dst, out_s.at[i]))
        loads[-1].start()
    z, x, y, c = place()
    me = ((z * 2 + x) * 2 + y) * 2 + c
    for k in range(2):
        turned = pltpu.roll(sums[k], lax.rem(D - me * cols, D), 1)
        gain_out[k] = turned[0:2, :cols]
        bias_out[k] = turned[2:4, :cols]
    first.wait()

    def unpack(k):
        tail = []
        for i in range(3):
            v_qkv[k, i] = v_qo[k, :, GW * i : GW * i + GW - HEAD_DIM]
            tail.append(v_qo[k, :, GW * (i + 1) - HEAD_DIM : GW * (i + 1)])
        v_out[k] = jnp.concatenate(tail, 1)
        for j, (src, dst) in enumerate(((v_qkv, qkv_out), (v_out, wout_out))):
            stores.append(pltpu.make_async_copy(src.at[k], dst.at[k], out_s.at[n + 2 * k + j]))
            stores[-1].start()

    for i in range(n):
        loads[i].wait()
        stores[i].start()
        if i in (1, 3):
            unpack(i // 2)
    for cp in stores:
        cp.wait()


def deliver(cols, y_in, g_in, qo, up_in, dn_in, sums):
    rows = qo.shape[1]
    V = pl.BlockSpec(memory_space=pltpu.VMEM)
    sem = pltpu.SemaphoreType.DMA
    out = jax.ShapeDtypeStruct
    width = GW - HEAD_DIM
    shapes = [((2, 3, rows, width), F32), ((2, rows, width), F32)]
    whole = [(y_in.shape, BF), (g_in.shape, F32), (qo.shape, F32), (qo.shape, F32), (qo.shape, F32)]
    return pl.pallas_call(
        partial(deliver_kernel, cols),
        out_shape=tuple(
            out(*p) for p in whole[:2] + shapes + whole[3:] + [((2, 2, cols), F32)] * 2
        ),
        in_specs=[ANY] * 5 + [V],
        out_specs=(ANY,) * 6 + (V, V),
        scratch_shapes=[pltpu.VMEM(*p) for p in whole + shapes] + [sem((9,)), sem((12,))],
        name="deliver",
    )(y_in, g_in, qo, up_in, dn_in, sums)


def split_local(nz, x_in, tags, lengths, w_qkv, w_out, w_up, w_down, norm_gain, norm_bias, cotangent):
    cols = norm_gain.shape[2]
    y_out, x_grad, qo_grad, up_grad, down_grad, n_sum, _, _, _ = run_step(
        nz, tags, lengths, x_in, cotangent, w_qkv.transpose(0, 2, 1, 3), w_out, w_up, w_down, norm_gain, norm_bias
    )
    y_out, x_grad, qkv, out, up, down, gain, bias = deliver(
        cols, y_out, x_grad, qo_grad, up_grad, down_grad, n_sum
    )
    return y_out, x_grad, qkv.transpose(0, 2, 1, 3), out, up, down, gain, bias


def typed_map(operand, stacked, chain_kinds, pattern):

    def single(element):
        weight = lax.dynamic_index_in_dim(stacked, element[1], 0, keepdims=False)
        return jnp.einsum(pattern, element[0], weight, preferred_element_type=jnp.float32)

    return lax.map(single, (operand, chain_kinds))


def typed_grads(running, operand, partner, chain_kinds, pattern):

    def single(carry, element):
        product_term = jnp.einsum(
            pattern, element[0], element[1], preferred_element_type=jnp.float32
        )
        previous = lax.dynamic_index_in_dim(carry, element[2], 0, keepdims=False)
        return (
            lax.dynamic_update_index_in_dim(carry, previous + product_term, element[2], 0),
            None,
        )

    return lax.scan(single, running, (operand, partner, chain_kinds))[0]


def row_terms(operand, stacked, chain_kinds, pattern, row_count):
    result = typed_map(operand, stacked, chain_kinds, pattern)
    return result.reshape(row_count, result.shape[-1])


def old_norm_forward(values, gain_rows, shift_rows):
    center = values - jnp.mean(values, -1, keepdims=True)
    factor = lax.rsqrt(jnp.mean(center * center, -1, keepdims=True) + EPS)
    normed = center * factor
    return (normed * gain_rows + shift_rows, normed, factor)


def old_norm_backward(grad_out, normed, factor, gain_rows):
    scaled = grad_out * gain_rows
    mean_plain = jnp.mean(scaled, -1, keepdims=True)
    mean_normed = jnp.mean(scaled * normed, -1, keepdims=True)
    return factor * (scaled - mean_plain - normed * mean_normed)


def type_sums(onehot, values):
    return jnp.dot(onehot.T, values, precision=HIGH, preferred_element_type=jnp.float32)


def general_local(x_in, tags, lengths, w_qkv, w_out, w_up, w_down, norm_gain, norm_bias, cotangent):
    tp_count = lax.axis_size("tensor")
    tp_index = lax.axis_index("tensor")
    local_rows = CHAINS_PART * LENGTH
    batch_chains = tp_count * CHAINS_PART
    head_cols = w_qkv.shape[3]
    local_heads = head_cols // HEAD_DIM
    tag_grid = tags.reshape(tp_count, MICRO, CHAINS_PART)
    len_grid = lengths.reshape(tp_count, MICRO, CHAINS_PART)
    own_tags = lax.dynamic_index_in_dim(tag_grid, tp_index, 0, keepdims=False)
    gains, shifts = (
        lax.all_gather(norm_gain, ("dp", "tensor"), axis=2, tiled=True),
        lax.all_gather(norm_bias, ("dp", "tensor"), axis=2, tiled=True),
    )
    grad_full = (
        jnp.zeros((2, D, 3, head_cols), jnp.float32),
        jnp.zeros((2, D, head_cols), jnp.float32),
        jnp.zeros((2, D, w_up.shape[2]), jnp.float32),
        jnp.zeros((2, D, w_down.shape[2]), jnp.float32),
    )
    shards = (
        jnp.zeros(w_qkv.shape, jnp.float32),
        jnp.zeros(w_out.shape, jnp.float32),
        jnp.zeros(w_up.shape, jnp.float32),
        jnp.zeros(w_down.shape, jnp.float32),
    )
    gain_acc = jnp.zeros((2, 2, D), jnp.float32)
    shift_acc = jnp.zeros((2, 2, D), jnp.float32)
    outputs = []
    input_grads = []
    for micro_index in range(MICRO):
        held = (
            lax.all_gather(w_qkv, "dp", axis=1, tiled=True),
            lax.all_gather(w_out, "dp", axis=1, tiled=True),
            lax.all_gather(w_up, "dp", axis=1, tiled=True),
            lax.all_gather(w_down, "dp", axis=1, tiled=True),
        )
        qkv_w, out_w, up_w, down_w = held
        chain_kinds = tag_grid[:, micro_index].reshape(batch_chains)
        chain_lens = len_grid[:, micro_index].reshape(batch_chains)
        own_rows = x_in[micro_index * local_rows : (micro_index + 1) * local_rows]
        kinds_rows = jnp.repeat(own_tags[micro_index], LENGTH)
        heavy_rows = (kinds_rows == 0)[:, None]
        onehot = (kinds_rows[:, None] == jnp.arange(2)[None, :]).astype(jnp.float32)
        gain_mid = jnp.where(heavy_rows, gains[0, 0], gains[1, 0])
        shift_mid = jnp.where(heavy_rows, shifts[0, 0], shifts[1, 0])
        gain_end = jnp.where(heavy_rows, gains[0, 1], gains[1, 1])
        shift_end = jnp.where(heavy_rows, shifts[0, 1], shifts[1, 1])
        gathered = lax.all_gather(own_rows, "tensor", axis=0, tiled=True).reshape(
            batch_chains, LENGTH, D
        )
        projected = typed_map(gathered, qkv_w, chain_kinds, "ld,dkh->lkh").astype(jnp.bfloat16)
        query = projected[:, :, 0].reshape(batch_chains, LENGTH, local_heads, HEAD_DIM)
        keys_low = projected[:, :, 1].reshape(batch_chains, LENGTH, local_heads, HEAD_DIM)
        values_low = projected[:, :, 2].reshape(batch_chains, LENGTH, local_heads, HEAD_DIM)
        valid = (
            lax.broadcasted_iota(jnp.int32, (batch_chains, 1, 1, LENGTH), 3)
            < chain_lens[:, None, None, None]
        )
        scores = (
            jnp.einsum("cqhe,ckhe->chqk", query, keys_low, preferred_element_type=jnp.float32)
            * 0.125
        )
        scores = jnp.where(valid, scores, NEG)
        highest = jnp.max(scores, -1, keepdims=True)
        expo = jnp.exp(scores - highest)
        totals = jnp.sum(expo, -1, keepdims=True)
        probs = expo / totals
        log_total = highest + jnp.log(totals)
        heads_low = jnp.einsum(
            "chqk,ckhe->cqhe",
            probs.astype(jnp.bfloat16),
            values_low,
            preferred_element_type=jnp.float32,
        ).astype(jnp.bfloat16)
        heads_low = heads_low.reshape(batch_chains, LENGTH, head_cols)
        attn_sum = lax.psum_scatter(
            row_terms(
                heads_low, out_w, chain_kinds, "lh,dh->ld", lax.axis_size("tensor") * local_rows
            ).astype(jnp.bfloat16),
            "tensor",
            scatter_dimension=0,
            tiled=True,
        ).astype(jnp.float32)
        mid, normed_mid, factor_mid = old_norm_forward(
            own_rows.astype(jnp.float32) + attn_sum, gain_mid, shift_mid
        )
        mid_all = lax.all_gather(mid.astype(jnp.bfloat16), "tensor", axis=0, tiled=True).reshape(
            batch_chains, LENGTH, D
        )
        up_value = typed_map(mid_all, up_w, chain_kinds, "ld,df->lf")
        act_low = jax.nn.gelu(up_value, approximate=False).astype(jnp.bfloat16)
        ffn_sum = lax.psum_scatter(
            row_terms(
                act_low, down_w, chain_kinds, "lf,df->ld", lax.axis_size("tensor") * local_rows
            ).astype(jnp.bfloat16),
            "tensor",
            scatter_dimension=0,
            tiled=True,
        ).astype(jnp.float32)
        final, normed_end, factor_end = old_norm_forward(ffn_sum + mid, gain_end, shift_end)
        outputs.append(final.astype(jnp.bfloat16))
        base = grad_full
        grad_final = cotangent[micro_index * local_rows : (micro_index + 1) * local_rows].astype(
            jnp.float32
        )
        gain_acc = gain_acc.at[:, 1].add(type_sums(onehot, grad_final * normed_end))
        shift_acc = shift_acc.at[:, 1].add(type_sums(onehot, grad_final))
        grad_resid2 = old_norm_backward(grad_final, normed_end, factor_end, gain_end)
        grad_ffn = lax.all_gather(
            grad_resid2.astype(jnp.bfloat16), "tensor", axis=0, tiled=True
        ).reshape(batch_chains, LENGTH, D)
        grad_act = typed_map(grad_ffn, down_w, chain_kinds, "ld,df->lf")
        unused_value, gelu_back = jax.vjp(partial(jax.nn.gelu, approximate=False), up_value)
        grad_up = gelu_back(grad_act)[0].astype(jnp.bfloat16)
        down_acc = typed_grads(base[3], grad_ffn, act_low, chain_kinds, "ld,lf->df")
        up_acc = typed_grads(base[2], mid_all, grad_up, chain_kinds, "ld,lf->df")
        grad_mid = grad_resid2 + lax.psum_scatter(
            row_terms(
                grad_up, up_w, chain_kinds, "lf,df->ld", lax.axis_size("tensor") * local_rows
            ).astype(jnp.bfloat16),
            "tensor",
            scatter_dimension=0,
            tiled=True,
        ).astype(jnp.float32)
        gain_acc = gain_acc.at[:, 0].add(type_sums(onehot, grad_mid * normed_mid))
        shift_acc = shift_acc.at[:, 0].add(type_sums(onehot, grad_mid))
        grad_resid1 = old_norm_backward(grad_mid, normed_mid, factor_mid, gain_mid)
        grad_attn = lax.all_gather(
            grad_resid1.astype(jnp.bfloat16), "tensor", axis=0, tiled=True
        ).reshape(batch_chains, LENGTH, D)
        grad_heads = typed_map(grad_attn, out_w, chain_kinds, "ld,dh->lh").astype(jnp.bfloat16)
        out_acc = typed_grads(base[1], grad_attn, heads_low, chain_kinds, "ld,lh->dh")
        grad_heads = grad_heads.reshape(batch_chains, LENGTH, local_heads, HEAD_DIM)
        again = (
            jnp.einsum("cqhe,ckhe->chqk", query, keys_low, preferred_element_type=jnp.float32)
            * 0.125
        )
        probs_again = jnp.exp(jnp.where(valid, again, NEG) - log_total)
        grad_probs = jnp.einsum(
            "cqhe,ckhe->chqk", grad_heads, values_low, preferred_element_type=jnp.float32
        )
        inner = jnp.sum(grad_probs * probs_again, -1, keepdims=True)
        grad_scores = (probs_again * (grad_probs - inner)).astype(jnp.bfloat16)
        grad_query = (
            jnp.einsum("chqk,ckhe->cqhe", grad_scores, keys_low, preferred_element_type=jnp.float32)
            * 0.125
        ).astype(jnp.bfloat16)
        grad_keys = (
            jnp.einsum("chqk,cqhe->ckhe", grad_scores, query, preferred_element_type=jnp.float32)
            * 0.125
        ).astype(jnp.bfloat16)
        grad_values = jnp.einsum(
            "chqk,cqhe->ckhe",
            probs_again.astype(jnp.bfloat16),
            grad_heads,
            preferred_element_type=jnp.float32,
        ).astype(jnp.bfloat16)
        grad_proj = jnp.stack([grad_query, grad_keys, grad_values], 2).reshape(
            batch_chains, LENGTH, 3, head_cols
        )
        qkv_acc = typed_grads(base[0], gathered, grad_proj, chain_kinds, "ld,lkh->dkh")
        grad_input = grad_resid1 + lax.psum_scatter(
            row_terms(
                grad_proj, qkv_w, chain_kinds, "lkh,dkh->ld", lax.axis_size("tensor") * local_rows
            ).astype(jnp.bfloat16),
            "tensor",
            scatter_dimension=0,
            tiled=True,
        ).astype(jnp.float32)
        input_grads.append(grad_input)
        updated = (qkv_acc, out_acc, up_acc, down_acc)
        grad_full = updated
    shards = (
        lax.psum_scatter(grad_full[0], "dp", scatter_dimension=1, tiled=True),
        lax.psum_scatter(grad_full[1], "dp", scatter_dimension=1, tiled=True),
        lax.psum_scatter(grad_full[2], "dp", scatter_dimension=1, tiled=True),
        lax.psum_scatter(grad_full[3], "dp", scatter_dimension=1, tiled=True),
    )
    gain_grad, shift_grad = (
        lax.psum_scatter(gain_acc, ("dp", "tensor"), scatter_dimension=2, tiled=True),
        lax.psum_scatter(shift_acc, ("dp", "tensor"), scatter_dimension=2, tiled=True),
    )
    return (
        jnp.concatenate(outputs, 0),
        jnp.concatenate(input_grads, 0),
        shards[0],
        shards[1],
        shards[2],
        shards[3],
        gain_grad,
        shift_grad,
    )


def solution(mesh):
    placed = (
        P(("dp", "tensor"), None),
        P("dp"),
        P("dp"),
        P(None, "dp", None, "tensor"),
        P(None, "dp", "tensor"),
        P(None, "dp", "tensor"),
        P(None, "dp", "tensor"),
        P(None, None, ("dp", "tensor")),
        P(None, None, ("dp", "tensor")),
        P(("dp", "tensor"), None),
    )
    results = (
        P(("dp", "tensor"), None),
        P(("dp", "tensor"), None),
        P(None, "dp", None, "tensor"),
        P(None, "dp", "tensor"),
        P(None, "dp", "tensor"),
        P(None, "dp", "tensor"),
        P(None, None, ("dp", "tensor")),
        P(None, None, ("dp", "tensor")),
    )
    n_dp, n_tensor = mesh.shape["dp"], mesh.shape["tensor"]
    if n_tensor != GROUPS or n_dp != 8:
        return jax.shard_map(
            general_local, mesh=mesh, in_specs=placed, out_specs=results, check_vma=False
        )
    fine = Mesh(mesh.devices.reshape(n_dp // 2, 2, 2, 2), AXES)
    names = {"dp": ("z", "x"), "tensor": ("y", "c")}

    def refine(spec):
        parts = []
        for entry in spec:
            entry = (entry,) if isinstance(entry, str) else entry
            parts.append(entry and sum((names[a] for a in entry), ()))
        return P(*parts)

    return jax.shard_map(
        partial(split_local, n_dp // 2),
        mesh=fine,
        in_specs=tuple(refine(s) for s in placed),
        out_specs=tuple(refine(s) for s in results),
        check_vma=False,
    )
```

```python
from functools import partial

import jax
import jax.numpy as jnp
from jax import lax
from jax.experimental import pallas as pl
from jax.experimental.pallas import tpu as pltpu
from jax.sharding import Mesh
from jax.sharding import PartitionSpec as P

D = 768
HEADS = 12
HEAD_DIM = 64
MICRO = 4
CHAINS_PART = 1
LENGTH = 160
GROUPS = 4
OWN = 4
EXTRA = 2
SLOTS = OWN + EXTRA
EXT_ROWS = EXTRA * LENGTH
OWN_ROWS = OWN * LENGTH
ROWS = SLOTS * LENGTH

EPS = 1e-12
NEG = -1e30
HIGH = lax.Precision.HIGHEST
BF = jnp.bfloat16
F32 = jnp.float32
MESH = pl.DeviceIdType.MESH
ANY = pl.BlockSpec(memory_space=pl.ANY)
AXES = ("z", "x", "y", "c")


def place():
    return tuple(lax.axis_index(a) for a in AXES)


def greet(nz, z, x, y, c):
    barrier = pltpu.get_barrier_semaphore()
    friends = [{"c": 1 - c}, {"y": 1 - y}, {"y": 1 - y, "c": 1 - c}, {"x": 1 - x}]
    friends += [{"z": lax.rem(z + dz, nz)} for dz in range(1, nz)]
    for friend in friends:
        pl.semaphore_signal(barrier, inc=1, device_id=friend, device_id_type=MESH)
    return barrier, len(friends)


CHUNK = 320
SUB = 80
N_CHUNK = ROWS // CHUNK
WIDE = 3 * LENGTH
GW = 256
PAIR = 3


def dot_nn(a, b):
    return lax.dot_general(a, b, (((1,), (0,)), ((), ())), preferred_element_type=F32)


def dot_nt(a, b):
    return lax.dot_general(a, b, (((1,), (1,)), ((), ())), preferred_element_type=F32)


def dot_tn(a, b):
    return lax.dot_general(a, b, (((0,), (0,)), ((), ())), preferred_element_type=F32)


def lanes(shape):
    return lax.broadcasted_iota(jnp.int32, shape, len(shape) - 1)


def head_mask(h, shape):
    lane = lanes(shape)
    return jnp.logical_and(lane >= h * HEAD_DIM, lane < (h + 1) * HEAD_DIM)


def stack_heads(rows):
    zero = jnp.zeros_like(rows)
    return jnp.concatenate([jnp.where(head_mask(h, rows.shape), rows, zero) for h in range(3)], 0)


def merge_heads(stack):
    out = jnp.zeros((LENGTH, GW), stack.dtype)
    for h in range(3):
        out = jnp.where(head_mask(h, out.shape), stack[h * LENGTH : (h + 1) * LENGTH], out)
    return out


def chunk_rows(i, size=CHUNK):
    return pl.ds(pl.multiple_of(i * size, size), size)


def loop(count, body):
    def step(i, carry):
        body(i)
        return carry

    lax.fori_loop(0, count, step, 0)


def weave(count, unit, extra):
    def body(i):
        unit(i)
        for k, step in extra.items():
            pl.when(i == k)(step)

    loop(count, body)


def out_columns(t, w, wo):
    low = lanes((D, 128)) < HEAD_DIM
    tiles = [w[0, t, :, GW * i + 128 : GW * i + 256].astype(F32) for i in range(3)]
    wo[t, :, :128] = jnp.where(low, pltpu.roll(tiles[0], 64, 1), tiles[1]).astype(BF)
    wo[t, :, 128:] = jnp.where(low, pltpu.roll(tiles[2], 64, 1), 0.0).astype(BF)


def attend(t, chains, lens, proj, probs, hout):
    rows = [chunk_rows(s, LENGTH) for s in chains]
    parts = [(proj[t, r, :GW], proj[t, r, GW : 2 * GW], proj[t, r, 2 * GW :]) for r in rows]
    lows, outs = [], []
    for s, (query, key, value) in zip(chains, parts):
        scores = dot_nt(key, stack_heads(query * jnp.asarray(0.125, BF)))
        valid = lax.broadcasted_iota(jnp.int32, (LENGTH, 1), 0) < lens(s)
        scores = jnp.where(valid, scores, NEG)
        expo = jnp.exp(scores - jnp.max(scores, 0, keepdims=True))
        lows.append((expo * (1.0 / jnp.sum(expo, 0, keepdims=True))).astype(BF))
        outs.append(merge_heads(dot_tn(lows[-1], value)).astype(BF))
    for s, r, low, out in zip(chains, rows, lows, outs):
        probs[t, s, :, :WIDE] = low
        hout[t, r] = out


def norm_rows(values):
    center = values - jnp.mean(values, -1, keepdims=True)
    factor = lax.rsqrt(jnp.mean(center * center, -1, keepdims=True) + EPS)
    return center * factor, factor


def norm_back(scaled, normed, factor):
    return factor * (
        scaled
        - jnp.mean(scaled, -1, keepdims=True)
        - normed * jnp.mean(scaled * normed, -1, keepdims=True)
    )


def pieces(i, body):
    def step(k):
        body(pl.ds(pl.multiple_of(i * CHUNK + k * SUB, SUB), SUB), k)

    loop(CHUNK // SUB, step)


def first_norm(i, x, hout, wo, prm, mid, n1, s1, mid_low):
    r = chunk_rows(i)
    attn = dot_nt(hout[0, r], wo[0])
    for t in range(1, GROUPS):
        attn += dot_nt(hout[t, r], wo[t])
    mid[r] = attn

    def piece(p, k):
        normed, factor = norm_rows(x[p].astype(F32) + mid[p])
        n1[p] = normed.astype(BF)
        s1[p] = jnp.broadcast_to(factor, (SUB, 128))
        value = normed * prm[0:1] + prm[2:3]
        mid[p] = value
        mid_low[p] = value.astype(BF)

    pieces(i, piece)


def feed_up(t, i, mid_low, w, act, slope):
    r = chunk_rows(i)
    for k in range(0, D, GW):
        up = dot_nn(mid_low[r], w[1, t, :, k : k + GW])
        cdf = 0.5 * (1.0 + lax.erf(up * 0.7071067811865476))
        act[t, r, k : k + GW] = (up * cdf).astype(BF)
        bell = 0.3989422804014327 * jnp.exp(-0.5 * up * up)
        slope[t, r, k : k + GW] = (cdf + up * bell).astype(BF)


def feed_down(i, t, act, w, mid):
    r = chunk_rows(i)
    mid[r] += dot_nt(act[t, r], w[2, t]) + dot_nt(act[t + 1, r], w[2, t + 1])


def second_norm(i, t, act, w, prm, mid, cot, mine, y_rows, d_ffn, ngrad):
    feed_down(i, t, act, w, mid)

    def piece(p, k):
        normed, factor = norm_rows(mid[p])
        y_rows[pl.ds(pl.multiple_of(k * SUB, SUB), SUB)] = (normed * prm[1:2] + prm[3:4]).astype(BF)
        grad = cot[p].astype(F32) * jnp.where(k < LENGTH // SUB, mine(2 * i), mine(2 * i + 1))
        ngrad[1:2] += jnp.sum(grad * normed, 0, keepdims=True)
        ngrad[3:4] += jnp.sum(grad, 0, keepdims=True)
        back = norm_back(grad * prm[1:2], normed, factor)
        mid[p] = back
        d_ffn[p] = back.astype(BF)

    pieces(i, piece)


def back_up(t, i, d_ffn, w, slope):
    r = chunk_rows(i)
    slope[t, r] = (dot_nn(d_ffn[r], w[2, t]) * slope[t, r].astype(F32)).astype(BF)


def back_first_norm(i, d_up, w, prm, mid, n1, s1, d_attn, ngrad):
    r = chunk_rows(i)
    grad = dot_nt(d_up[0, r], w[1, 0])
    for t in range(1, GROUPS):
        grad += dot_nt(d_up[t, r], w[1, t])
    mid[r] += grad

    def piece(p, k):
        grad = mid[p]
        normed = n1[p].astype(F32)
        ngrad[0:1] += jnp.sum(grad * normed, 0, keepdims=True)
        ngrad[2:3] += jnp.sum(grad, 0, keepdims=True)
        back = norm_back(grad * prm[0:1], normed, s1[p, 0:1])
        mid[p] = back
        d_attn[p] = back.astype(BF)

    pieces(i, piece)


def back_heads(t, d_attn, wo, d_heads):
    d_heads[t, :, :GW] = dot_nn(d_attn[...], wo[t]).astype(BF)


def back_attend(t, chains, proj, probs, d_heads):
    rows = [chunk_rows(s, LENGTH) for s in chains]
    parts = [
        (proj[t, r, :GW], proj[t, r, GW : 2 * GW], proj[t, r, 2 * GW :], d_heads[t, r, :GW], probs[t, s, :, :WIDE])
        for s, r in zip(chains, rows)
    ]
    results = []
    for query, key, value, grad, low in parts:
        grad = stack_heads(grad)
        p = low.astype(F32)
        d_probs = dot_nt(value, grad)
        d_scores = (p * (d_probs - jnp.sum(d_probs * p, 0, keepdims=True))).astype(BF)
        d_query = merge_heads(dot_tn(d_scores, key)) * 0.125
        d_key = dot_nn(d_scores, stack_heads(query * jnp.asarray(0.125, BF)))
        results.append((d_query.astype(BF), d_key.astype(BF), dot_nn(low, grad).astype(BF)))
    for r, (d_query, d_key, d_value) in zip(rows, results):
        proj[t, r, :GW] = d_query
        proj[t, r, GW : 2 * GW] = d_key
        proj[t, r, 2 * GW :] = d_value


def grad_qkv_out(t, x, d_proj, d_attn, hout, store):
    low = lanes((D, 128)) < HEAD_DIM
    outs = dot_tn(d_attn[...], hout[t])
    places = (pltpu.roll(outs[:, :128], 64, 1), outs[:, :128], pltpu.roll(outs[:, 128:], 64, 1))
    for i in range(3):
        part = dot_tn(x[...], d_proj[t, :, GW * i : GW * (i + 1)])
        store(GW * i, part[:, :128])
        store(GW * i + 128, jnp.where(low, part[:, 128:], places[i]))


def back_input(i, d_proj, w, mid, out):
    r = chunk_rows(i)
    grad = mid[r]
    for t in range(GROUPS):
        grad += dot_nt(d_proj[t, r], w[0, t])
    out(r, grad)


MIXED = (2, 1)
GATHER_FIRST = (
    ('X', 1, 0), ('L', 0, 0), ('y', 0), ('X', 0, 1), ('L', 0, 1),
    ('z', 0, 0, 1), ('z', 0, 1, 1), ('y', 1), ('L', 1, 1), ('x', 0, 1, 0),
    ('X', 0, 0), ('z', 0, 1, 2), ('x', 1, 0, 0), ('z', 0, 0, 2), ('x', 0, 1, 1),
    ('x', 0, 0, 1), ('L', 1, 0), ('z', 0, 1, 3), ('z', 0, 0, 3), ('x', 0, 0, 0),
    ('y', 2), ('X', 2, 1), ('x', 0, 1, 3), ('z', 1, 1, 1), ('x', 0, 1, 2),
    ('z', 1, 0, 1), ('x', 0, 0, 2), ('L', 2, 0), ('x', 0, 0, 3), ('z', 1, 1, 2),
    ('X', 1, 1),
)
GATHER_QKV = {
    7: (('z', 1, 0, 2),),
    10: (('x', 2, 1, 0),),
}
GATHER_ATTEND = {
    1: (('L', 2, 1), ('z', 1, 1, 3), ('z', 1, 0, 3), ('z', 2, 0, 1),),
    2: (('X', 2, 0),),
    5: (('x', 1, 1, 1), ('x', 1, 1, 2),),
    6: (('z', 2, 1, 1), ('x', 1, 1, 0),),
    7: (('z', 2, 0, 2), ('x', 1, 0, 1),),
}
GATHER_NORM = {
    0: (('x', 1, 0, 2), ('x', 1, 1, 3), ('x', 1, 0, 3),),
}
GATHER_UP = {
    3: (('z', 2, 1, 2),),
    4: (('z', 2, 0, 3),),
    7: (('x', 2, 0, 1),),
    9: (('x', 2, 0, 0),),
    10: (('x', 2, 0, 3), ('x', 2, 0, 2),),
    11: (('z', 2, 1, 3),),
}


def remote(src, dst, s_sem, r_sem, who):
    return pltpu.make_async_remote_copy(
        src_ref=src, dst_ref=dst, send_sem=s_sem, recv_sem=r_sem, device_id=who, device_id_type=MESH
    )


def arrived(ref, sem):
    remote(ref, ref, sem, sem, {"c": 1 - lax.axis_index("c")}).wait_recv()


def has_left(ref, sem):
    remote(ref, ref, sem, sem, {"c": 1 - lax.axis_index("c")}).wait_send()


def step_kernel(nz, rows,
                tags, lens, x_in, cot, qkv, wout, up, dn, gain, bias,
                y_out, g_out, qo_out, up_out, dn_out, n_out, y_back, g_back, r_c,
                w, x, proj, probs, hout, wo, mid, n1, s1, mid_low, act, slope, d_ffn, gown, r_xz, oth, v_qkv, v_out, far,
                n_all, prm, ngrad, n_c, n_x, n_z,
                load_s, io_s, stage_s, out_s,
                ys_s, ys_r, zs_s, zs_r, zm_s, zm_r, xs_s, xs_r, cs_s, cs_r, ex_s, ex_r, na_s, na_r,
                c_s, c_r, cp_s, cp_r, x_s, x_r, z_s, z_r, y_s, y_r, e_s, e_r, ng_s, ng_r):
    z, xc, y, c = place()
    core, across, other_x = {"c": 1 - c}, {"y": 1 - y}, {"x": 1 - xc}
    diagonal = {"y": 1 - y, "c": 1 - c}
    mats = (None, up, dn)
    lender = y != c
    home = (2 * y + c) * OWN
    away = (2 - y) * OWN + c * EXTRA

    def z_of(dz):
        return lax.rem(z + dz, nz)

    def chain(s):
        return jnp.where(s < OWN, home + s, away + s - OWN)

    def length_of(s):
        return lens[chain(s)]

    def mine(s):
        return jnp.where(tags[chain(s)] == y, 1.0, 0.0)

    def part(zz, xx):
        return pl.ds(pl.multiple_of((zz * 2 + xx) * rows, rows), rows)

    def group(g):
        return 2 * lax.rem(y + g, 2) + c

    def block(m, g, zz, xx):
        return w.at[m, group(g), part(zz, xx)]

    loads = [pltpu.make_async_copy(mats[m].at[y], block(m, 0, z, xc), load_s.at[m]) for m in range(1, 3)]
    loads += [
        pltpu.make_async_copy(x_in, x.at[pl.ds(0, OWN_ROWS)], load_s.at[3]),
        pltpu.make_async_copy(cot, d_ffn.at[pl.ds(0, OWN_ROWS)], load_s.at[4]),
        pltpu.make_async_copy(qkv, v_qkv, load_s.at[0]),
        pltpu.make_async_copy(wout, v_out, load_s.at[5]),
    ]
    for cp in loads:
        cp.start()
    barrier, friends = greet(nz, z, xc, y, c)
    me = ((z * 2 + xc) * 2 + y) * 2 + c
    cols = gain.shape[2]
    n_all[me] = jnp.zeros((8, 128), F32)
    for i in range(2):
        n_all[me, 2 * i : 2 * i + 2, :cols] = gain[i]
        n_all[me, 4 + 2 * i : 6 + 2 * i, :cols] = bias[i]
    ngrad[...] = jnp.zeros_like(ngrad)
    for cp in loads[4:]:
        cp.wait()

    def packed(k):
        tail = v_out[k]
        cols = []
        for i in range(3):
            cols += [v_qkv[k, i], tail[:, HEAD_DIM * i : HEAD_DIM * (i + 1)]]
        return jnp.concatenate(cols, 1)

    w[0, group(0), part(z, xc)] = packed(y)
    far[...] = packed(1 - y)
    pl.semaphore_wait(barrier, friends)

    def given(m):
        return mats[m].at[1 - y] if m else far

    def lend(arr, out, i, act_on):
        @pl.when(lender)
        def _():
            for j, (who, p) in enumerate(((across, c), (diagonal, 1 - c))):
                src = arr.at[pl.ds(pl.multiple_of(p * EXT_ROWS, EXT_ROWS), EXT_ROWS)]
                act_on(remote(src, out.at[pl.ds(OWN_ROWS, EXT_ROWS)], ex_s.at[i, j], ex_r.at[i], who))

    for m in range(3):
        remote(given(m), w.at[m, group(0), part(z, xc)], ys_s.at[m], ys_r.at[m], across).start()
    lend(x_in, x, 0, lambda cp: cp.start())
    lend(cot, d_ffn, 1, lambda cp: cp.start())

    def inside(zz):
        return jnp.logical_and(zz >= 0, zz < nz)

    def start(cp):
        cp.start()

    def recv(cp):
        cp.wait_recv()

    def hop(m, g, d, j, ref, act_on, col=0):
        to = z + 1 - 2 * d
        sems = (zm_s.at[d, j], zm_r.at[d, j]) if col else (zs_s.at[m, g, d, j], zs_r.at[m, g, d, j])

        @pl.when(jnp.logical_and(inside(to), j < nz))
        def _():
            act_on(remote(ref, ref, *sems, {"z": to}))

    def x_copy(m, g, zz):
        ref = block(m, g, zz, xc)
        return remote(ref, ref, xs_s.at[m, g, zz], xs_r.at[m, g, zz], other_x)

    def c_copy(m, g, zz, xx):
        ref = block(m, g, zz, xx)
        return remote(ref, ref, cs_s.at[m, g, zz, xx], cs_r.at[m, g, zz, xx], core)

    def from_y(m):
        arrived(block(m, 1, z, xc), ys_r.at[m])

    def own_z(m, g):
        for d in range(2):
            hop(m, g, d, 1, block(m, g, z, xc), start)

    def own_xc(m, g):
        x_copy(m, g, z).start()
        c_copy(m, g, z, xc).start()

    def z_event(m, g, j):
        mixed = (m, g) == MIXED

        def body(d):
            zz = z - j + 2 * j * d

            @pl.when(inside(zz))
            def _():
                for col in range(2 if mixed else 1):
                    ref = block(m, g, zz, lax.rem(xc + col, 2))
                    arrived(ref, zm_r.at[d, j] if col else zs_r.at[m, g, d, j])
                    hop(m, g, d, j + 1, ref, start, col)
                    if not mixed:
                        x_copy(m, g, zz).start()
                    c_copy(m, g, zz, lax.rem(xc + col, 2)).start()

        loop(2, body)

    def x_event(m, g, j):
        def body(d):
            zz = z - j + 2 * j * d

            @pl.when(inside(zz))
            def _():
                ref = block(m, g, zz, 1 - xc)
                arrived(ref, xs_r.at[m, g, zz])
                if (m, g) == MIXED:
                    for way in range(2):
                        hop(m, g, way, 1, ref, start, 1)
                c_copy(m, g, zz, 1 - xc).start()

        loop(2 if j else 1, body)

    kinds = {"y": from_y, "L": own_z, "X": own_xc, "z": z_event, "x": x_event}

    def gather_steps(plan):
        def run(steps):
            for kind, *args in steps:
                kinds[kind](*args)

        return {k: partial(run, steps) for k, steps in plan.items()}

    def gathered(m, first=0, last=2):
        def body(i):
            g = first + i // (2 * nz)
            t = 2 * lax.rem(y + g, 2) + 1 - c
            zz, xx = (i // 2) % nz, i % 2
            arrived(w.at[m, t, part(zz, xx)], cs_r.at[m, g, zz, xx])

        loop(2 * nz * (last - first), body)

    def gather_sent(i):
        m, g = i // 2, i % 2
        ref = w.at[0, 0, pl.ds(0, rows)]
        mixed = i == 2 * MIXED[0] + MIXED[1]
        for j in range(1, nz):
            for d in range(2):
                @pl.when(inside(z - (1 - 2 * d) * (j - 1)))
                def _():
                    hop(m, g, d, j, ref, lambda cp: cp.wait_send())

                    @pl.when(mixed)
                    def _():
                        hop(m, g, d, j, ref, lambda cp: cp.wait_send(), 1)
        for zz in range(nz):
            @pl.when(jnp.logical_or(jnp.logical_not(mixed), z == zz))
            def _():
                has_left(ref, xs_s.at[m, g, zz])

            for xx in range(2):
                has_left(ref, cs_s.at[m, g, zz, xx])

    def norm_hop(i, act_on):
        if i == 0:
            act_on(remote(n_all.at[me], n_all.at[me], na_s.at[0], na_r.at[0], core))
        elif i == 1:
            ref = n_all.at[pl.ds(me - c, 2)]
            act_on(remote(ref, ref, na_s.at[1], na_r.at[1], across))
        elif i == 2:
            ref = n_all.at[pl.ds(me - c - 2 * y, 4)]
            act_on(remote(ref, ref, na_s.at[2], na_r.at[2], other_x))
        else:
            ref = n_all.at[pl.ds(8 * z, 8)]
            for dz in range(1, nz):
                act_on(remote(ref, ref, na_s.at[2 + dz], na_r.at[2 + dz], {"z": z_of(dz)}))

    for cp in loads[:2]:
        cp.wait()
    norm_hop(0, start)
    for kind, *args in GATHER_FIRST:
        kinds[kind](*args)
        if (kind, *args) == ("z", 0, 0, 1):
            norm_hop(0, recv)
            norm_hop(1, start)
        if (kind, *args) == ("z", 0, 0, 3):
            norm_hop(1, recv)
            norm_hop(2, start)
    norm_hop(2, recv)
    norm_hop(3, start)
    gathered(0)
    loads[2].wait()
    arrived(x.at[pl.ds(OWN_ROWS, EXT_ROWS)], ex_r.at[0])

    def projection(i):
        t, k = i // N_CHUNK, i % N_CHUNK
        r = chunk_rows(k)
        proj[t, r] = dot_nn(x[r], w[0, t]).astype(BF)

        @pl.when(k == N_CHUNK - 1)
        def _():
            out_columns(t, w, wo)

    weave(GROUPS * N_CHUNK, projection, gather_steps(GATHER_QKV))
    per = SLOTS // PAIR

    def attention(i):
        attend(i // per, [(i % per) * PAIR + k for k in range(PAIR)], length_of, proj, probs, hout)

    weave(GROUPS * per, attention, gather_steps(GATHER_ATTEND))
    norm_hop(3, recv)
    lane = lanes((2, D))
    gains, shifts = jnp.zeros((2, D), F32), jnp.zeros((2, D), F32)
    for d in range(8 * nz):
        within = jnp.logical_and(lane >= d * cols, lane < (d + 1) * cols)
        for name in range(2):
            piece = n_all[d, pl.ds(4 * name + 2 * y, 2), :]
            piece = jnp.concatenate([piece, jnp.zeros((2, D - 128), F32)], 1)
            piece = jnp.where(within, pltpu.roll(piece, d * cols, 1) if d else piece, 0.0)
            if name == 0:
                gains += piece
            else:
                shifts += piece
    prm[0:2] = gains
    prm[2:4] = shifts
    weave(
        N_CHUNK,
        lambda i: first_norm(i, x, hout, wo, prm, mid, n1, s1, mid_low),
        gather_steps(GATHER_NORM),
    )
    gathered(1)
    weave(
        GROUPS * N_CHUNK,
        lambda i: feed_up(i // N_CHUNK, i % N_CHUNK, mid_low, w, act, slope),
        gather_steps(GATHER_UP),
    )
    gathered(2, 0, 1)
    first_two = 2 * y
    last_two = 2 - first_two
    loop(N_CHUNK, lambda i: feed_down(i, first_two, act, w, mid))
    gathered(2, 1, 2)
    loads[3].wait()
    arrived(d_ffn.at[pl.ds(OWN_ROWS, EXT_ROWS)], ex_r.at[1])

    def y_stage(i):
        return r_xz.at[i // 2, 0, pl.ds(pl.multiple_of((i % 2) * CHUNK, CHUNK), CHUNK)]

    def give_back(src, dst, i, act_on):
        dst = dst.at[pl.ds(pl.multiple_of(c * EXT_ROWS, EXT_ROWS), EXT_ROWS)]

        @pl.when(c == y)
        def _():
            act_on(remote(src, dst, e_s.at[i], e_r.at[i, c], across))

        @pl.when(c != y)
        def _():
            act_on(remote(src, dst, e_s.at[i], e_r.at[i, c], diagonal))

    def y_copy(i):
        return pltpu.make_async_copy(y_stage(i), y_out.at[pl.ds(i * CHUNK, CHUNK)], io_s.at[i])

    loop(
        N_CHUNK,
        lambda i: second_norm(
            i, last_two, act, w, prm, mid, d_ffn, mine, y_stage(i), d_ffn, ngrad
        ),
    )
    for i in range(2):
        y_copy(i).start()
    give_back(y_stage(2), y_back, 0, start)

    def columns(g, other):
        pair = jnp.where(g == 0, 1 - y, y)
        return 2 * pair + jnp.where(other, 1 - c, c)

    def x_place(m, g, i):
        return r_xz.at[0, m, pl.ds(pl.multiple_of((g * nz + i) * rows, rows), rows)]

    def z_place(m, g, i):
        return r_xz.at[1, m, pl.ds(pl.multiple_of((g * nz + i) * rows, rows), rows)]

    def spare(m, g):
        return gown.at[0, g] if m else act.at[2 * g + c, pl.ds(0, D)]

    def core_send(m, g):
        there = r_c.at[g] if m else spare(0, g)
        return remote(spare(m, g), there, c_s.at[m, g], c_r.at[m, g], core)

    def fetch(g):
        return pltpu.make_async_copy(r_c.at[g], act.at[2 * g + 1 - c, pl.ds(0, D)], stage_s.at[g])

    half = D // 2

    def half_rows(k):
        return pl.ds(pl.multiple_of(half * jnp.where(z < nz // 2, 1 - k, k), half), half)

    def core_half(g, k):
        r = half_rows(k)
        return remote(gown.at[0, g, r], gown.at[1, g, r], cp_s.at[g, k], cp_r.at[g, k], core)

    def core_fetch(g):
        arrived(r_c.at[g], c_r.at[1, g])
        fetch(g).start()

    middle = jnp.logical_and(z > 0, z < nz - 1)

    def target(k):
        down = jnp.where(nz - 1 - k > z, nz - 1 - k, nz - 2 - k)
        up = jnp.where(k < z, k, k + 1)
        return jnp.where(k == nz - 1, z, jnp.where(z < nz // 2, down, up))

    def add_and_cross(m, g, from_core, first, count):
        def add(i):
            p = part(target(first + i % count), lax.rem(xc + 1 + i // count, 2))
            gown[m, g, p] += from_core[p]

        def over(k):
            zz = target(first + k)
            remote(gown.at[m, g, part(zz, 1 - xc)], x_place(m, g, zz), x_s.at[m, g, zz], x_r.at[m, g, zz], other_x).start()

        loop(count + 1, add)
        loop(count, over)
        loop(count - 1, lambda i: add(count + 1 + i))

    def core_add(m, g):
        from_core = act.at[2 * g + 1 - c, pl.ds(0, D)]
        if m == 1:
            fetch(g).wait()
        else:
            arrived(from_core, c_r.at[0, g])
        add_and_cross(m, g, from_core, 0, nz)

    def half_add(g, k):
        core_half(g, k).wait_recv()
        add_and_cross(2, g, gown.at[1, g], k * (nz // 2), nz // 2)

    def sum_event(q):
        m = 2 - q // (2 * nz)
        g = (q // nz) % 2
        k = q % nz
        zz = target(k)
        over = x_place(m, g, zz)
        arrived(over, x_r.at[m, g, zz])
        p = part(zz, xc)
        gown[m, g, p] += over[...]

        beside = jnp.where(z == 0, 1, nz - 2)
        joins = jnp.logical_and(k < 2, jnp.logical_not(middle))
        to = jnp.where(joins, beside, zz)
        slot = jnp.where(joins, jnp.where(k == 0, beside, nz - 1 - z), z)

        @pl.when(jnp.logical_and(k < nz - 1, jnp.logical_or(k == nz - 2, jnp.logical_not(middle))))
        def _():
            remote(gown.at[m, g, p], z_place(m, g, slot), z_s.at[m, g, zz], z_r.at[m, g, slot], {"z": to}).start()

        def relay(k, slot):
            to = target(k)
            q = part(to, xc)
            arrived(z_place(m, g, slot), z_r.at[m, g, slot])
            gown[m, g, q] += z_place(m, g, slot)[...]
            remote(gown.at[m, g, q], z_place(m, g, z), z_s.at[m, g, to], z_r.at[m, g, z], {"z": to}).start()

        early = jnp.where(m == 0, 1, 0)

        @pl.when(jnp.logical_and(k == nz - 2 - early, middle))
        def _():
            relay(0, z)

        @pl.when(jnp.logical_and(k == nz - 1 - early, middle))
        def _():
            relay(1, jnp.where(z == 1, nz - 1, 0))

    outs = (qo_out, up_out, dn_out)

    def out_stage(m, other):
        return mid.at[pl.ds(m * rows + (0 if other else OWN_ROWS), rows)]

    def out_copy(m, other):
        return pltpu.make_async_copy(out_stage(m, other), outs[m].at[1 - y if other else y], out_s.at[m, other])

    def last_send(m):
        return remote(mid_low.at[pl.ds(EXT_ROWS + m * rows, rows)], oth.at[m], y_s.at[m], y_r.at[m], across)

    def finish(m, g):
        total = gown[m, g, part(z, xc)].astype(F32)
        for dz in range(1, nz):
            source = z_of(dz)
            direct = jnp.abs(source - z) <= jnp.where(middle, 1, 2)

            @pl.when(direct)
            def _():
                arrived(z_place(m, g, source), z_r.at[m, g, source])

            total += jnp.where(direct, z_place(m, g, source)[...].astype(F32), 0.0)

        if g == 1:
            out_stage(m, 0)[...] = total
            out_copy(m, 0).start()
        else:
            mid_low[EXT_ROWS + m * rows : EXT_ROWS + (m + 1) * rows] = total.astype(BF)
            last_send(m).start()

    def up_grads(extra):
        def unit(q):
            g, own = q % 2, q // 2
            t = columns(g, own == 0)
            dst = gown.at[own, g]
            for k in range(0, D, GW):
                dst[:, k : k + GW] = dot_tn(mid_low[...], slope[t, :, k : k + GW]).astype(BF)

            @pl.when(own == 0)
            def _():
                core_send(1, g).start()

        weave(4, unit, extra)

    def down_grads(extra):
        def unit(q):
            g, k, own = q // 4, (q // 2) % 2, q % 2
            t = columns(g, own == 0)
            r = half_rows(k)
            dst = gown.at[2 * own, g, r]
            for j in range(0, D, GW):
                dst[:, j : j + GW] = dot_tn(d_ffn[:, r], act[t, :, j : j + GW]).astype(BF)

            @pl.when(own == 0)
            def _():
                core_half(g, k).start()

        weave(8, unit, extra)

    def then(*steps):
        def run():
            for f, *args in steps:
                f(*args)

        return run

    def core_over(m):
        for g in range(2):
            if m == 2:
                for k in range(2):
                    core_half(g, k).wait_send()
            else:
                core_send(m, g).wait_send()

    down_grads(
        {
            2: then((half_add, 0, 0)),
            3: then((half_add, 0, 1)),
            5: then((half_add, 1, 0)),
            7: then((half_add, 1, 1), (sum_event, 0), (core_over, 2)),
        }
    )

    def up_back(i):
        back_up(i // N_CHUNK, i % N_CHUNK, d_ffn, w, slope)

    weave(GROUPS * N_CHUNK, up_back, {4: then((sum_event, 1)), 9: then((sum_event, 2))})
    for i in range(2):
        y_copy(i).wait()
    has_left(y_stage(2), e_s.at[0])
    up_grads({1: then((sum_event, 3)), 3: then((sum_event, 4))})
    for g in range(2):
        core_fetch(g)
    weave(
        N_CHUNK,
        lambda i: back_first_norm(i, slope, w, prm, mid, n1, s1, d_ffn, ngrad),
        {
            0: then((core_add, 1, 0), (core_add, 1, 1), (core_over, 1)),
            1: then((sum_event, 5)),
            2: then((sum_event, 6)),
        },
    )

    def send_norms(i, act_on):
        if i == 0:
            act_on(remote(ngrad, n_c, ng_s.at[0], ng_r.at[0], core))
        elif i == 1:
            act_on(remote(n_c, n_x, ng_s.at[1], ng_r.at[1], other_x))
        elif i == 2:
            for dz in range(1, nz):
                act_on(remote(n_x, n_z.at[dz], ng_s.at[1 + dz], ng_r.at[1 + dz], {"z": z_of(dz)}))
        else:
            act_on(remote(n_out.at[y], n_out.at[y], ng_s.at[nz + 1], ng_r.at[nz + 1], across))

    send_norms(0, start)
    loop(GROUPS, lambda t: back_heads(t, d_ffn, wo, slope))
    sum_event(7)
    send_norms(0, recv)
    send_norms(0, lambda cp: cp.wait_send())
    n_c[...] += ngrad[...]
    send_norms(1, start)

    def attention_back(i):
        back_attend(i // per, [(i % per) * PAIR + k for k in range(PAIR)], proj, probs, slope)

        @pl.when(i % 2 == 1)
        def _():
            sum_event(8 + i // 2)

    loop(GROUPS * per, attention_back)
    seen = 8 + GROUPS * per // 2

    def qkv_grads(q):
        g, own = q // 2, q % 2

        def store(col, value):
            value = value.astype(BF)

            @pl.when(own == 0)
            def _():
                spare(0, g)[:, col : col + 128] = value

            @pl.when(own == 1)
            def _():
                gown[0, g, :, col : col + 128] = value

        grad_qkv_out(columns(g, own == 0), x, proj, d_ffn, hout, store)

        @pl.when(own == 0)
        def _():
            core_send(0, g).start()

    weave(
        4,
        qkv_grads,
        {
            0: then((sum_event, seen)),
            1: then((core_add, 0, 0), (sum_event, seen + 1)),
            3: then((core_add, 0, 1), (sum_event, seen + 2)),
        },
    )
    seen += 3

    def inputs_back(i):
        k = lax.rem(i + N_CHUNK - 1, N_CHUNK)

        def keep(r, grad):
            mid[r] = grad

            @pl.when(i == 0)
            def _():
                mid_low[:EXT_ROWS] = grad.astype(BF)

        back_input(k, proj, w, mid, keep)

        @pl.when(i == 0)
        def _():
            give_back(mid_low.at[pl.ds(0, EXT_ROWS)], g_back, 1, start)

    weave(N_CHUNK, inputs_back, {1: then((sum_event, seen))})
    seen += 1
    after = 4 * nz
    if seen < after:
        loop(after - seen, lambda q: sum_event(seen + q))
    for g in range(2):
        finish(2, g)
    loop(nz, lambda q: sum_event(after + q))

    def sums_sent(i):
        m, g = i // 2, i % 2
        for zz in range(nz):
            @pl.when(z != zz)
            def _():
                has_left(x_place(0, 0, 0), z_s.at[m, g, zz])

            has_left(x_place(0, 0, 0), x_s.at[m, g, zz])

    loop(6, gather_sent)

    trips = [
        pltpu.make_async_copy(g_back, proj.at[0, pl.ds(0, OWN_ROWS)], io_s.at[0]),
        pltpu.make_async_copy(y_out, proj.at[1, pl.ds(0, OWN_ROWS)], io_s.at[1]),
        pltpu.make_async_copy(y_back, proj.at[2, pl.ds(0, OWN_ROWS)], io_s.at[2]),
    ]
    y_again = pltpu.make_async_copy(proj.at[1, pl.ds(0, OWN_ROWS)], y_out, io_s.at[1])
    g_copy = pltpu.make_async_copy(mid.at[pl.ds(0, OWN_ROWS)], g_out, io_s.at[3])

    @pl.when(lender)
    def _():
        for i, dst in enumerate((y_back, g_back)):
            for j in range(2):
                arrived(dst.at[pl.ds(j * EXT_ROWS, EXT_ROWS)], e_r.at[i, j])
        for cp in trips:
            cp.start()
        for cp in trips:
            cp.wait()

        def merge(s):
            r = chunk_rows(s, LENGTH)
            keep = jnp.zeros((LENGTH, D), F32) + mine(s) > 0.5
            mid[r] = jnp.where(keep, mid[r], proj[0, r].astype(F32))
            proj[1, r] = jnp.where(keep, proj[1, r].astype(F32), proj[2, r].astype(F32)).astype(BF)

        loop(OWN, merge)
        y_again.start()

    g_copy.start()
    send_norms(1, recv)
    send_norms(1, lambda cp: cp.wait_send())
    n_x[...] += n_c[...]
    send_norms(2, start)
    for g in range(2):
        finish(1, g)
    loop(nz - 1, lambda q: sum_event(after + nz + q))
    g_copy.wait()

    def widen(m):
        arrived(oth.at[m], y_r.at[m])
        out_stage(m, 1)[...] = oth[m].astype(F32)
        out_copy(m, 1).start()

    widen(2)
    widen(1)
    loop(4, lambda i: sums_sent(2 + i))
    total = n_x[...]
    for dz in range(1, nz):
        arrived(n_z.at[dz], ng_r.at[1 + dz])
        total += n_z[dz]
    n_out[y] = total
    send_norms(3, start)
    finish(0, 0)
    sum_event(after + 2 * nz - 1)
    widen(0)
    finish(0, 1)

    loop(2, sums_sent)
    for g in range(2):
        core_send(0, g).wait_send()
    for m in range(3):
        has_left(given(m), ys_s.at[m])
        for other in range(2):
            out_copy(m, other).wait()
        last_send(m).wait_send()
    lend(x_in, x, 0, lambda cp: cp.wait_send())
    lend(cot, d_ffn, 1, lambda cp: cp.wait_send())
    for i in range(4):
        norm_hop(i, lambda cp: cp.wait_send())
    send_norms(2, lambda cp: cp.wait_send())
    send_norms(3, lambda cp: cp.wait())
    has_left(mid_low.at[pl.ds(0, EXT_ROWS)], e_s.at[1])

    @pl.when(lender)
    def _():
        y_again.wait()


def run_step(nz, tags, lens, x_in, cot, qkv, wout, up, dn, gain, bias):
    rows = up.shape[1]
    V = pl.BlockSpec(memory_space=pltpu.VMEM)
    S = pl.BlockSpec(memory_space=pltpu.SMEM)
    sem = pltpu.SemaphoreType.DMA
    out = jax.ShapeDtypeStruct
    return pl.pallas_call(
        partial(step_kernel, nz, rows),
        out_shape=(
            out((OWN_ROWS, D), BF),
            out((OWN_ROWS, D), F32),
            out((2, rows, D), F32),
            out((2, rows, D), F32),
            out((2, rows, D), F32),
            out((2, 8, D), F32),
            out((OWN_ROWS, D), BF),
            out((OWN_ROWS, D), BF),
            out((2, D, D), BF),
        ),
        in_specs=[S, S] + [ANY] * 6 + [V, V],
        out_specs=(ANY, ANY, ANY, ANY, ANY, V, ANY, ANY, ANY),
        scratch_shapes=[
            pltpu.VMEM((3, GROUPS, D, D), BF),
            pltpu.VMEM((ROWS, D), BF),
            pltpu.VMEM((GROUPS, ROWS, D), BF),
            pltpu.VMEM((GROUPS, SLOTS, LENGTH, 512), BF),
            pltpu.VMEM((GROUPS, ROWS, GW), BF),
            pltpu.VMEM((GROUPS, D, GW), BF),
            pltpu.VMEM((ROWS, D), F32),
            pltpu.VMEM((ROWS, D), BF),
            pltpu.VMEM((ROWS, 128), F32),
            pltpu.VMEM((ROWS, D), BF),
            pltpu.VMEM((GROUPS, ROWS, D), BF),
            pltpu.VMEM((GROUPS, ROWS, D), BF),
            pltpu.VMEM((ROWS, D), BF),
            pltpu.VMEM((3, 2, D, D), BF),
            pltpu.VMEM((2, 3, 2 * nz * rows, D), BF),
            pltpu.VMEM((3, rows, D), BF),
            pltpu.VMEM(qkv.shape, BF),
            pltpu.VMEM(wout.shape, BF),
            pltpu.VMEM((rows, D), BF),
            pltpu.VMEM((8 * nz, 8, 128), F32),
            pltpu.VMEM((8, D), F32),
            pltpu.VMEM((8, D), F32),
            pltpu.VMEM((8, D), F32),
            pltpu.VMEM((8, D), F32),
            pltpu.VMEM((nz, 8, D), F32),
            sem((6,)), sem((4,)), sem((2,)), sem((3, 2)),
            sem((3,)), sem((3,)),
            sem((3, 2, 2, nz)), sem((3, 2, 2, nz)),
            sem((2, nz)), sem((2, nz)),
            sem((3, 2, nz)), sem((3, 2, nz)),
            sem((3, 2, nz, 2)), sem((3, 2, nz, 2)),
            sem((2, 2)), sem((2,)),
            sem((nz + 2,)), sem((nz + 2,)),
            sem((3, 2)), sem((3, 2)),
            sem((2, 2)), sem((2, 2)),
            sem((3, 2, nz)), sem((3, 2, nz)),
            sem((3, 2, nz)), sem((3, 2, nz)),
            sem((3,)), sem((3,)),
            sem((2,)), sem((2, 2)),
            sem((nz + 2,)), sem((nz + 2,)),
        ],
        compiler_params=pltpu.CompilerParams(
            collective_id=0, has_side_effects=True, vmem_limit_bytes=67043328
        ),
        name="layer_step",
    )(tags, lens, x_in, cot, qkv, wout, up, dn, gain, bias)


def deliver_kernel(cols, y_in, g_in, qo, up_in, dn_in, sums,
                   y_out, g_out, qkv_out, wout_out, up_out, dn_out, gain_out, bias_out,
                   v_y, v_g, v_qo, v_up, v_dn, v_qkv, v_out, in_s, out_s):
    through = [(up_in, v_up, up_out), (dn_in, v_dn, dn_out)]
    for k in range(OWN):
        r = pl.ds(k * LENGTH, LENGTH)
        through.append((g_in.at[r], v_g.at[r], g_out.at[r]))
    for k in range(2):
        r = pl.ds(k * CHUNK, CHUNK)
        through.append((y_in.at[r], v_y.at[r], y_out.at[r]))
    n = len(through)
    first = pltpu.make_async_copy(qo, v_qo, in_s.at[n])
    first.start()
    loads, stores = [], []
    for i, (src, via, dst) in enumerate(through):
        loads.append(pltpu.make_async_copy(src, via, in_s.at[i]))
        stores.append(pltpu.make_async_copy(via, dst, out_s.at[i]))
        loads[-1].start()
    z, x, y, c = place()
    me = ((z * 2 + x) * 2 + y) * 2 + c
    for k in range(2):
        turned = pltpu.roll(sums[k], lax.rem(D - me * cols, D), 1)
        gain_out[k] = turned[0:2, :cols]
        bias_out[k] = turned[2:4, :cols]
    first.wait()

    def unpack(k):
        tail = []
        for i in range(3):
            v_qkv[k, i] = v_qo[k, :, GW * i : GW * i + GW - HEAD_DIM]
            tail.append(v_qo[k, :, GW * (i + 1) - HEAD_DIM : GW * (i + 1)])
        v_out[k] = jnp.concatenate(tail, 1)
        for j, (src, dst) in enumerate(((v_qkv, qkv_out), (v_out, wout_out))):
            stores.append(pltpu.make_async_copy(src.at[k], dst.at[k], out_s.at[n + 2 * k + j]))
            stores[-1].start()

    for i in range(n):
        loads[i].wait()
        stores[i].start()
        if i in (1, 3):
            unpack(i // 2)
    for cp in stores:
        cp.wait()


def deliver(cols, y_in, g_in, qo, up_in, dn_in, sums):
    rows = qo.shape[1]
    V = pl.BlockSpec(memory_space=pltpu.VMEM)
    sem = pltpu.SemaphoreType.DMA
    out = jax.ShapeDtypeStruct
    width = GW - HEAD_DIM
    shapes = [((2, 3, rows, width), F32), ((2, rows, width), F32)]
    whole = [(y_in.shape, BF), (g_in.shape, F32), (qo.shape, F32), (qo.shape, F32), (qo.shape, F32)]
    return pl.pallas_call(
        partial(deliver_kernel, cols),
        out_shape=tuple(
            out(*p) for p in whole[:2] + shapes + whole[3:] + [((2, 2, cols), F32)] * 2
        ),
        in_specs=[ANY] * 5 + [V],
        out_specs=(ANY,) * 6 + (V, V),
        scratch_shapes=[pltpu.VMEM(*p) for p in whole + shapes] + [sem((9,)), sem((12,))],
        name="deliver",
    )(y_in, g_in, qo, up_in, dn_in, sums)


def split_local(nz, x_in, tags, lengths, w_qkv, w_out, w_up, w_down, norm_gain, norm_bias, cotangent):
    cols = norm_gain.shape[2]
    y_out, x_grad, qo_grad, up_grad, down_grad, n_sum, _, _, _ = run_step(
        nz, tags, lengths, x_in, cotangent, w_qkv.transpose(0, 2, 1, 3), w_out, w_up, w_down, norm_gain, norm_bias
    )
    y_out, x_grad, qkv, out, up, down, gain, bias = deliver(
        cols, y_out, x_grad, qo_grad, up_grad, down_grad, n_sum
    )
    return y_out, x_grad, qkv.transpose(0, 2, 1, 3), out, up, down, gain, bias


def typed_map(operand, stacked, chain_kinds, pattern):

    def single(element):
        weight = lax.dynamic_index_in_dim(stacked, element[1], 0, keepdims=False)
        return jnp.einsum(pattern, element[0], weight, preferred_element_type=jnp.float32)

    return lax.map(single, (operand, chain_kinds))


def typed_grads(running, operand, partner, chain_kinds, pattern):

    def single(carry, element):
        product_term = jnp.einsum(
            pattern, element[0], element[1], preferred_element_type=jnp.float32
        )
        previous = lax.dynamic_index_in_dim(carry, element[2], 0, keepdims=False)
        return (
            lax.dynamic_update_index_in_dim(carry, previous + product_term, element[2], 0),
            None,
        )

    return lax.scan(single, running, (operand, partner, chain_kinds))[0]


def row_terms(operand, stacked, chain_kinds, pattern, row_count):
    result = typed_map(operand, stacked, chain_kinds, pattern)
    return result.reshape(row_count, result.shape[-1])


def old_norm_forward(values, gain_rows, shift_rows):
    center = values - jnp.mean(values, -1, keepdims=True)
    factor = lax.rsqrt(jnp.mean(center * center, -1, keepdims=True) + EPS)
    normed = center * factor
    return (normed * gain_rows + shift_rows, normed, factor)


def old_norm_backward(grad_out, normed, factor, gain_rows):
    scaled = grad_out * gain_rows
    mean_plain = jnp.mean(scaled, -1, keepdims=True)
    mean_normed = jnp.mean(scaled * normed, -1, keepdims=True)
    return factor * (scaled - mean_plain - normed * mean_normed)


def type_sums(onehot, values):
    return jnp.dot(onehot.T, values, precision=HIGH, preferred_element_type=jnp.float32)


def general_local(x_in, tags, lengths, w_qkv, w_out, w_up, w_down, norm_gain, norm_bias, cotangent):
    tp_count = lax.axis_size("tensor")
    tp_index = lax.axis_index("tensor")
    local_rows = CHAINS_PART * LENGTH
    batch_chains = tp_count * CHAINS_PART
    head_cols = w_qkv.shape[3]
    local_heads = head_cols // HEAD_DIM
    tag_grid = tags.reshape(tp_count, MICRO, CHAINS_PART)
    len_grid = lengths.reshape(tp_count, MICRO, CHAINS_PART)
    own_tags = lax.dynamic_index_in_dim(tag_grid, tp_index, 0, keepdims=False)
    gains, shifts = (
        lax.all_gather(norm_gain, ("dp", "tensor"), axis=2, tiled=True),
        lax.all_gather(norm_bias, ("dp", "tensor"), axis=2, tiled=True),
    )
    grad_full = (
        jnp.zeros((2, D, 3, head_cols), jnp.float32),
        jnp.zeros((2, D, head_cols), jnp.float32),
        jnp.zeros((2, D, w_up.shape[2]), jnp.float32),
        jnp.zeros((2, D, w_down.shape[2]), jnp.float32),
    )
    shards = (
        jnp.zeros(w_qkv.shape, jnp.float32),
        jnp.zeros(w_out.shape, jnp.float32),
        jnp.zeros(w_up.shape, jnp.float32),
        jnp.zeros(w_down.shape, jnp.float32),
    )
    gain_acc = jnp.zeros((2, 2, D), jnp.float32)
    shift_acc = jnp.zeros((2, 2, D), jnp.float32)
    outputs = []
    input_grads = []
    for micro_index in range(MICRO):
        held = (
            lax.all_gather(w_qkv, "dp", axis=1, tiled=True),
            lax.all_gather(w_out, "dp", axis=1, tiled=True),
            lax.all_gather(w_up, "dp", axis=1, tiled=True),
            lax.all_gather(w_down, "dp", axis=1, tiled=True),
        )
        qkv_w, out_w, up_w, down_w = held
        chain_kinds = tag_grid[:, micro_index].reshape(batch_chains)
        chain_lens = len_grid[:, micro_index].reshape(batch_chains)
        own_rows = x_in[micro_index * local_rows : (micro_index + 1) * local_rows]
        kinds_rows = jnp.repeat(own_tags[micro_index], LENGTH)
        heavy_rows = (kinds_rows == 0)[:, None]
        onehot = (kinds_rows[:, None] == jnp.arange(2)[None, :]).astype(jnp.float32)
        gain_mid = jnp.where(heavy_rows, gains[0, 0], gains[1, 0])
        shift_mid = jnp.where(heavy_rows, shifts[0, 0], shifts[1, 0])
        gain_end = jnp.where(heavy_rows, gains[0, 1], gains[1, 1])
        shift_end = jnp.where(heavy_rows, shifts[0, 1], shifts[1, 1])
        gathered = lax.all_gather(own_rows, "tensor", axis=0, tiled=True).reshape(
            batch_chains, LENGTH, D
        )
        projected = typed_map(gathered, qkv_w, chain_kinds, "ld,dkh->lkh").astype(jnp.bfloat16)
        query = projected[:, :, 0].reshape(batch_chains, LENGTH, local_heads, HEAD_DIM)
        keys_low = projected[:, :, 1].reshape(batch_chains, LENGTH, local_heads, HEAD_DIM)
        values_low = projected[:, :, 2].reshape(batch_chains, LENGTH, local_heads, HEAD_DIM)
        valid = (
            lax.broadcasted_iota(jnp.int32, (batch_chains, 1, 1, LENGTH), 3)
            < chain_lens[:, None, None, None]
        )
        scores = (
            jnp.einsum("cqhe,ckhe->chqk", query, keys_low, preferred_element_type=jnp.float32)
            * 0.125
        )
        scores = jnp.where(valid, scores, NEG)
        highest = jnp.max(scores, -1, keepdims=True)
        expo = jnp.exp(scores - highest)
        totals = jnp.sum(expo, -1, keepdims=True)
        probs = expo / totals
        log_total = highest + jnp.log(totals)
        heads_low = jnp.einsum(
            "chqk,ckhe->cqhe",
            probs.astype(jnp.bfloat16),
            values_low,
            preferred_element_type=jnp.float32,
        ).astype(jnp.bfloat16)
        heads_low = heads_low.reshape(batch_chains, LENGTH, head_cols)
        attn_sum = lax.psum_scatter(
            row_terms(
                heads_low, out_w, chain_kinds, "lh,dh->ld", lax.axis_size("tensor") * local_rows
            ).astype(jnp.bfloat16),
            "tensor",
            scatter_dimension=0,
            tiled=True,
        ).astype(jnp.float32)
        mid, normed_mid, factor_mid = old_norm_forward(
            own_rows.astype(jnp.float32) + attn_sum, gain_mid, shift_mid
        )
        mid_all = lax.all_gather(mid.astype(jnp.bfloat16), "tensor", axis=0, tiled=True).reshape(
            batch_chains, LENGTH, D
        )
        up_value = typed_map(mid_all, up_w, chain_kinds, "ld,df->lf")
        act_low = jax.nn.gelu(up_value, approximate=False).astype(jnp.bfloat16)
        ffn_sum = lax.psum_scatter(
            row_terms(
                act_low, down_w, chain_kinds, "lf,df->ld", lax.axis_size("tensor") * local_rows
            ).astype(jnp.bfloat16),
            "tensor",
            scatter_dimension=0,
            tiled=True,
        ).astype(jnp.float32)
        final, normed_end, factor_end = old_norm_forward(ffn_sum + mid, gain_end, shift_end)
        outputs.append(final.astype(jnp.bfloat16))
        base = grad_full
        grad_final = cotangent[micro_index * local_rows : (micro_index + 1) * local_rows].astype(
            jnp.float32
        )
        gain_acc = gain_acc.at[:, 1].add(type_sums(onehot, grad_final * normed_end))
        shift_acc = shift_acc.at[:, 1].add(type_sums(onehot, grad_final))
        grad_resid2 = old_norm_backward(grad_final, normed_end, factor_end, gain_end)
        grad_ffn = lax.all_gather(
            grad_resid2.astype(jnp.bfloat16), "tensor", axis=0, tiled=True
        ).reshape(batch_chains, LENGTH, D)
        grad_act = typed_map(grad_ffn, down_w, chain_kinds, "ld,df->lf")
        unused_value, gelu_back = jax.vjp(partial(jax.nn.gelu, approximate=False), up_value)
        grad_up = gelu_back(grad_act)[0].astype(jnp.bfloat16)
        down_acc = typed_grads(base[3], grad_ffn, act_low, chain_kinds, "ld,lf->df")
        up_acc = typed_grads(base[2], mid_all, grad_up, chain_kinds, "ld,lf->df")
        grad_mid = grad_resid2 + lax.psum_scatter(
            row_terms(
                grad_up, up_w, chain_kinds, "lf,df->ld", lax.axis_size("tensor") * local_rows
            ).astype(jnp.bfloat16),
            "tensor",
            scatter_dimension=0,
            tiled=True,
        ).astype(jnp.float32)
        gain_acc = gain_acc.at[:, 0].add(type_sums(onehot, grad_mid * normed_mid))
        shift_acc = shift_acc.at[:, 0].add(type_sums(onehot, grad_mid))
        grad_resid1 = old_norm_backward(grad_mid, normed_mid, factor_mid, gain_mid)
        grad_attn = lax.all_gather(
            grad_resid1.astype(jnp.bfloat16), "tensor", axis=0, tiled=True
        ).reshape(batch_chains, LENGTH, D)
        grad_heads = typed_map(grad_attn, out_w, chain_kinds, "ld,dh->lh").astype(jnp.bfloat16)
        out_acc = typed_grads(base[1], grad_attn, heads_low, chain_kinds, "ld,lh->dh")
        grad_heads = grad_heads.reshape(batch_chains, LENGTH, local_heads, HEAD_DIM)
        again = (
            jnp.einsum("cqhe,ckhe->chqk", query, keys_low, preferred_element_type=jnp.float32)
            * 0.125
        )
        probs_again = jnp.exp(jnp.where(valid, again, NEG) - log_total)
        grad_probs = jnp.einsum(
            "cqhe,ckhe->chqk", grad_heads, values_low, preferred_element_type=jnp.float32
        )
        inner = jnp.sum(grad_probs * probs_again, -1, keepdims=True)
        grad_scores = (probs_again * (grad_probs - inner)).astype(jnp.bfloat16)
        grad_query = (
            jnp.einsum("chqk,ckhe->cqhe", grad_scores, keys_low, preferred_element_type=jnp.float32)
            * 0.125
        ).astype(jnp.bfloat16)
        grad_keys = (
            jnp.einsum("chqk,cqhe->ckhe", grad_scores, query, preferred_element_type=jnp.float32)
            * 0.125
        ).astype(jnp.bfloat16)
        grad_values = jnp.einsum(
            "chqk,cqhe->ckhe",
            probs_again.astype(jnp.bfloat16),
            grad_heads,
            preferred_element_type=jnp.float32,
        ).astype(jnp.bfloat16)
        grad_proj = jnp.stack([grad_query, grad_keys, grad_values], 2).reshape(
            batch_chains, LENGTH, 3, head_cols
        )
        qkv_acc = typed_grads(base[0], gathered, grad_proj, chain_kinds, "ld,lkh->dkh")
        grad_input = grad_resid1 + lax.psum_scatter(
            row_terms(
                grad_proj, qkv_w, chain_kinds, "lkh,dkh->ld", lax.axis_size("tensor") * local_rows
            ).astype(jnp.bfloat16),
            "tensor",
            scatter_dimension=0,
            tiled=True,
        ).astype(jnp.float32)
        input_grads.append(grad_input)
        updated = (qkv_acc, out_acc, up_acc, down_acc)
        grad_full = updated
    shards = (
        lax.psum_scatter(grad_full[0], "dp", scatter_dimension=1, tiled=True),
        lax.psum_scatter(grad_full[1], "dp", scatter_dimension=1, tiled=True),
        lax.psum_scatter(grad_full[2], "dp", scatter_dimension=1, tiled=True),
        lax.psum_scatter(grad_full[3], "dp", scatter_dimension=1, tiled=True),
    )
    gain_grad, shift_grad = (
        lax.psum_scatter(gain_acc, ("dp", "tensor"), scatter_dimension=2, tiled=True),
        lax.psum_scatter(shift_acc, ("dp", "tensor"), scatter_dimension=2, tiled=True),
    )
    return (
        jnp.concatenate(outputs, 0),
        jnp.concatenate(input_grads, 0),
        shards[0],
        shards[1],
        shards[2],
        shards[3],
        gain_grad,
        shift_grad,
    )


def solution(mesh):
    placed = (
        P(("dp", "tensor"), None),
        P("dp"),
        P("dp"),
        P(None, "dp", None, "tensor"),
        P(None, "dp", "tensor"),
        P(None, "dp", "tensor"),
        P(None, "dp", "tensor"),
        P(None, None, ("dp", "tensor")),
        P(None, None, ("dp", "tensor")),
        P(("dp", "tensor"), None),
    )
    results = (
        P(("dp", "tensor"), None),
        P(("dp", "tensor"), None),
        P(None, "dp", None, "tensor"),
        P(None, "dp", "tensor"),
        P(None, "dp", "tensor"),
        P(None, "dp", "tensor"),
        P(None, None, ("dp", "tensor")),
        P(None, None, ("dp", "tensor")),
    )
    n_dp, n_tensor = mesh.shape["dp"], mesh.shape["tensor"]
    if n_tensor != GROUPS or n_dp != 8:
        return jax.shard_map(
            general_local, mesh=mesh, in_specs=placed, out_specs=results, check_vma=False
        )
    fine = Mesh(mesh.devices.reshape(n_dp // 2, 2, 2, 2), AXES)
    names = {"dp": ("z", "x"), "tensor": ("y", "c")}

    def refine(spec):
        parts = []
        for entry in spec:
            entry = (entry,) if isinstance(entry, str) else entry
            parts.append(entry and sum((names[a] for a in entry), ()))
        return P(*parts)

    return jax.shard_map(
        partial(split_local, n_dp // 2),
        mesh=fine,
        in_specs=tuple(refine(s) for s in placed),
        out_specs=tuple(refine(s) for s in results),
        check_vma=False,
    )
```
